128 devices in a mesh: ctx: 32 (over z, x, core), exp: 4 (over y).
Axes of the slice: x: 4, y: 4, z: 4, core: 2. Of those that a mesh axis runs over, the one named last changes fastest.
Arguments:
- queries: bfloat16 [16384, 6144], P('ctx', 'exp'), may hold values from -0.52734375 to 0.52734375
- key_vectors: bfloat16 [16384, 6144], P('ctx', 'exp'), may hold values from -6 to 6
- values: bfloat16 [16384, 6144], P('ctx', 'exp'), may hold values from -6 to 6
- log_decay: float32 [16384, 48], P('ctx', 'exp'), may hold values from -1 to 0, as said below
- out_gate: bfloat16 [16384, 6144], P(('ctx', 'exp')), may hold values from -6 to 6
- residual: bfloat16 [16384, 6144], P(('ctx', 'exp')), may hold values from -6 to 6
- attn_gain: float32 [6144], replicated, may hold values from 0.1 to 1.9
- moe_gain: float32 [6144], replicated, may hold values from 0.1 to 1.9
- expert_ids: int32 [16384, 2], P(('ctx', 'exp')), may hold values from 0 to 31, as said below
- route_weights: float32 [16384, 2], P(('ctx', 'exp')), may hold values from 0.5 to 1.5
- w_gate: bfloat16 [4, 6144, 9216], P('exp', None, 'ctx'), may hold values from -0.078125 to 0.078125
- w_up: bfloat16 [4, 6144, 9216], P('exp', None, 'ctx'), may hold values from -0.078125 to 0.078125
- w_down: bfloat16 [4, 9216, 6144], P('exp', 'ctx'), may hold values from -0.0625 to 0.0625
Outputs:
- hidden: bfloat16 [16384, 6144], P(('ctx', 'exp'))
- moe_out: bfloat16 [16384, 6144], P(('ctx', 'exp'))
The draws below stay inside these ranges and needn't reach their ends.
Inputs may be any that keep to these rules, and one draw needn't show every extreme that they name: `expert_ids`: each token names two different experts, at most one of them below 4. The 128 rows of one device name each expert below 4 at most 4 times; in every draw one expert is named exactly 4 times by every device of some index of ctx. `log_decay`: every entry is negative.
All inputs are finite; a program needn't handle non-finite values.
Results may differ from the reference program's by a relative error of at most 0.03.
Values may be sent and summed in bfloat16 or wider, within the bound.
No kernel may reach another device: no remote copies, remote signals or barrier semaphores. Data moves between devices by JAX's collectives and lax.ppermute only.
A program may use at most 128 MiB of HBM per device.

```python
import math
import jax
import jax.numpy as jnp
from jax import lax

D = 6144
HEADS = 48
HEAD_DIM = 128
FF = 9216
ALL_EXPERTS = 32
CAP = 4
TOK_DEV = 128
EXPERTS = 4
TOK_CTX = 512
CONTEXT_LENGTH = 16384
UNITS_DEV = 288
N_CTX = 32


def draw_expert_ids(key, part):
    derived_seed_list = jax.random.split(jax.random.fold_in(key, 11), 7)
    block_count = CONTEXT_LENGTH // TOK_DEV
    levels = jnp.minimum(jax.random.permutation(derived_seed_list[0], EXPERTS), 2)
    shifts = jnp.minimum(jax.random.randint(derived_seed_list[1], (block_count, EXPERTS), 0, 2) + levels[None, :], 2)
    groups = jnp.arange(block_count) // (TOK_CTX // TOK_DEV)
    chosen_group = jax.random.randint(derived_seed_list[2], (), 0, CONTEXT_LENGTH // TOK_CTX)
    forced = (groups == chosen_group)[:, None] & (levels == 0)[None, :]
    shifts = jnp.where(forced, 0, shifts)
    counts = jnp.maximum(jnp.right_shift(jnp.full((block_count, EXPERTS), CAP, jnp.int32), shifts.astype(jnp.int32)), 1)
    offsets = jnp.cumsum(counts, axis=1) - counts
    orders = jax.vmap(lambda subkey: jax.random.permutation(subkey, TOK_DEV))(jax.random.split(derived_seed_list[3], block_count))
    ranks = jnp.argsort(orders, axis=1).astype(jnp.int32)
    within = (ranks[:, :, None] >= offsets[:, None, :]) & (ranks[:, :, None] < (offsets + counts)[:, None, :])
    has_held = jnp.any(within, axis=2)
    held_id = jnp.sum(within.astype(jnp.int32) * jnp.arange(EXPERTS, dtype=jnp.int32), axis=2)
    spares = jax.random.randint(derived_seed_list[4], (block_count, TOK_DEV), EXPERTS, ALL_EXPERTS)
    stride = jax.random.randint(derived_seed_list[5], (block_count, TOK_DEV), 1, ALL_EXPERTS - EXPERTS)
    first_id = jnp.where(has_held, held_id, spares)
    second_id = jnp.where(has_held, spares, EXPERTS + (spares - EXPERTS + stride) % (ALL_EXPERTS - EXPERTS))
    flips = jax.random.randint(derived_seed_list[6], (block_count, TOK_DEV), 0, 2)
    column_one = jnp.where(flips == 1, second_id, first_id)
    column_two = jnp.where(flips == 1, first_id, second_id)
    return jnp.stack([column_one, column_two], axis=-1).reshape(CONTEXT_LENGTH, 2).astype(jnp.int32)


def draw_log_decay(key, part):
    derived_seed_list = jax.random.split(jax.random.fold_in(key, 23), 7)
    quick_head = jax.random.randint(derived_seed_list[0], (HEADS,), 0, 8) < 4
    quick_rate = jnp.exp(jax.random.uniform(derived_seed_list[1], (HEADS,), jnp.float32, math.log(0.02), math.log(0.05)))
    slow_rate = jnp.exp(jax.random.uniform(derived_seed_list[2], (HEADS,), jnp.float32, math.log(0.05), math.log(0.5))) / CONTEXT_LENGTH
    base_rate = jnp.where(quick_head, quick_rate, slow_rate)
    per_block = jnp.exp(jax.random.uniform(derived_seed_list[3], (CONTEXT_LENGTH // TOK_CTX, 1, HEADS), jnp.float32, math.log(0.5), math.log(2.0)))
    per_position = jnp.exp(jax.random.uniform(derived_seed_list[4], (CONTEXT_LENGTH // TOK_CTX, TOK_CTX, HEADS), jnp.float32, math.log(0.5), math.log(2.0)))
    fading_speeds = (base_rate[None, None, :] * per_block * per_position).reshape(CONTEXT_LENGTH, HEADS)
    spike_indices = jax.random.randint(derived_seed_list[5], (3,), 0, CONTEXT_LENGTH)
    objective_scores = jax.random.uniform(derived_seed_list[6], (3, HEADS), jnp.float32, 0.2, 0.5)
    place_along_text = jnp.arange(CONTEXT_LENGTH)
    fading_spikes = jnp.sum(jnp.where(place_along_text[None, :, None] == spike_indices[:, None, None], -jnp.log(1.0 - objective_scores)[:, None, :], 0.0), axis=0)
    return -(fading_speeds + fading_spikes)


def steps_of(rng, extent, cuts, smallest, largest):
    level = 1.0
    for axis_at, blocks in cuts:
        draws = jax.random.uniform(jax.random.fold_in(jax.random.fold_in(rng, 6), axis_at), (blocks,), jnp.float32, smallest / len(cuts), largest / len(cuts))
        level = level * jnp.repeat(jnp.exp(draws), extent[axis_at] // blocks).reshape((-1,) + (1,) * (len(extent) - 1 - axis_at))
    return level


def normal_values(key, extent, scale, bound, shards=(), kind=jnp.bfloat16):
    level = steps_of(key, extent, shards, -0.22, 0.18) if shards else 1.0
    array = jax.random.normal(key, extent, jnp.float32) * scale * level
    return jnp.minimum(jnp.maximum(array, -bound), bound).astype(kind)


def setup_inputs(seed: int = 0) -> dict:
    key_list = jax.random.split(jax.random.key(seed), 14)
    queries = normal_values(key_list[0], (CONTEXT_LENGTH, D), (HEAD_DIM ** -0.5), 0.52734375, ((0, 32), (1, 4)))
    key_vectors = normal_values(key_list[1], (CONTEXT_LENGTH, D), 1.0, 6.0, ((0, 32), (1, 4)))
    values = normal_values(key_list[2], (CONTEXT_LENGTH, D), 1.0, 6.0, ((0, 32), (1, 4)))
    log_decay = draw_log_decay(jax.random.fold_in(key_list[13], 71), 0)
    out_gate = normal_values(key_list[4], (CONTEXT_LENGTH, D), 1.5, 6.0, ((0, 128),))
    residual = normal_values(key_list[5], (CONTEXT_LENGTH, D), 1.0, 6.0, ((0, 128),))
    attn_gain = jnp.clip(1.0 + 0.18 * jax.random.normal(key_list[6], (D,), jnp.float32), 0.1, 1.9)
    moe_gain = jnp.clip(1.0 + 0.18 * jax.random.normal(key_list[7], (D,), jnp.float32), 0.1, 1.9)
    expert_ids = draw_expert_ids(jax.random.fold_in(key_list[13], 71), 0)
    route_weights = jnp.clip(0.5 + 1.0 * jax.random.uniform(key_list[9], (CONTEXT_LENGTH, 2), jnp.float32) ** steps_of(key_list[9], (CONTEXT_LENGTH, 2), ((0, 128),), -0.2, 0.2), 0.5, 1.5)
    w_gate = normal_values(key_list[10], (EXPERTS, D, FF), D ** -0.5, 0.078125, ((0, 4), (2, 32)))
    w_up = normal_values(key_list[11], (EXPERTS, D, FF), D ** -0.5, 0.078125, ((0, 4), (2, 32)))
    w_down = normal_values(key_list[12], (EXPERTS, FF, D), FF ** -0.5, 0.0625, ((0, 4), (1, 32)))
    return dict(queries=queries, key_vectors=key_vectors, values=values, log_decay=log_decay, out_gate=out_gate, residual=residual, attn_gain=attn_gain, moe_gain=moe_gain, expert_ids=expert_ids, route_weights=route_weights, w_gate=w_gate, w_up=w_up, w_down=w_down)


def attend_block(block_query, block_key, block_value, block_cum, carry_state):
    total_rows = block_query.shape[0]
    block_size = min(512, total_rows)
    highest = lax.Precision.HIGHEST

    def query_part(block_index):
        offset = block_index * block_size
        query_now = lax.dynamic_slice_in_dim(block_query, offset, block_size, 0).astype(jnp.float32)
        cum_now = lax.dynamic_slice_in_dim(block_cum, offset, block_size, 0)
        scores = jnp.einsum('thd,shd->hts', query_now, block_key.astype(jnp.float32), precision=highest)
        log_gap = cum_now.T[:, :, None] - block_cum.T[:, None, :]
        causal = (offset + jnp.arange(block_size))[:, None] >= jnp.arange(total_rows)[None, :]
        decay_now = jnp.where(causal[None], jnp.exp(jnp.minimum(log_gap, 0.0)), 0.0)
        weights = (scores * decay_now).astype(jnp.bfloat16)
        inside = jnp.einsum('hts,shd->thd', weights.astype(jnp.float32), block_value.astype(jnp.float32), precision=highest)
        scaled = query_now * jnp.exp(cum_now)[:, :, None]
        carried_part = jnp.einsum('thd,hde->the', scaled, carry_state, precision=highest)
        return (inside + carried_part).astype(jnp.bfloat16)
    return lax.map(query_part, jnp.arange(total_rows // block_size))

def reference(queries, key_vectors, values, log_decay, out_gate, residual, attn_gain, moe_gain, expert_ids, route_weights, w_gate, w_up, w_down):
    highest = lax.Precision.HIGHEST
    block_count = CONTEXT_LENGTH // TOK_CTX
    query_blocks = queries.reshape(block_count, TOK_CTX, HEADS, HEAD_DIM)
    key_blocks = key_vectors.reshape(block_count, TOK_CTX, HEADS, HEAD_DIM)
    value_blocks = values.reshape(block_count, TOK_CTX, HEADS, HEAD_DIM)
    cumulative = jnp.cumsum(log_decay.reshape(block_count, TOK_CTX, HEADS), axis=1)

    def block_step(carry_state, inputs_now):
        block_query, block_key, block_value, block_cum = inputs_now
        output_now = attend_block(block_query, block_key, block_value, block_cum, carry_state)
        final_cum = block_cum[-1]
        weighted_keys = block_key.astype(jnp.float32) * jnp.exp(final_cum[None, :] - block_cum)[:, :, None]
        local_state = jnp.einsum('shd,she->hde', weighted_keys, block_value.astype(jnp.float32), precision=highest)
        next_state = jnp.exp(final_cum)[:, None, None] * carry_state + local_state
        return (next_state, output_now)
    start_state = jnp.zeros((HEADS, HEAD_DIM, HEAD_DIM), jnp.float32)
    _, block_outputs = lax.scan(block_step, start_state, (query_blocks, key_blocks, value_blocks, cumulative))
    attention = block_outputs.reshape(CONTEXT_LENGTH, D)
    attn_f32 = attention.astype(jnp.float32)
    attn_norm = attn_f32 * lax.rsqrt(lax.optimization_barrier(jnp.mean(attn_f32 * attn_f32, axis=-1, keepdims=True)) + 1e-05) * attn_gain
    hidden = (residual.astype(jnp.float32) + attn_norm * jax.nn.sigmoid(out_gate.astype(jnp.float32))).astype(jnp.bfloat16)
    hidden_f32 = hidden.astype(jnp.float32)
    normed = (hidden_f32 * lax.rsqrt(lax.optimization_barrier(jnp.mean(hidden_f32 * hidden_f32, axis=-1, keepdims=True)) + 1e-05) * moe_gain).astype(jnp.bfloat16)
    slot_total = CONTEXT_LENGTH // TOK_DEV * CAP

    def one_expert(expert):
        naming = expert_ids == expert
        selected = jnp.any(naming, axis=1)
        weight_row = lax.optimization_barrier(jnp.sum(jnp.where(naming, route_weights, 0.0), axis=1))
        picked = jnp.argsort(jnp.where(selected, 0, 1).astype(jnp.int32), stable=True)[:slot_total].astype(jnp.int32)
        picked_rows = normed[picked]
        gate_part = jnp.dot(picked_rows, w_gate[expert], preferred_element_type=jnp.float32)
        up_part = jnp.dot(picked_rows, w_up[expert], preferred_element_type=jnp.float32)
        activations = (jax.nn.silu(gate_part) * up_part).astype(jnp.bfloat16)
        down_matrix = w_down[expert]

        def add_slice(running, slice_index):
            act_slice = lax.dynamic_slice_in_dim(activations, slice_index * UNITS_DEV, UNITS_DEV, 1)
            down_slice = lax.dynamic_slice_in_dim(down_matrix, slice_index * UNITS_DEV, UNITS_DEV, 0)
            product = jnp.dot(act_slice, down_slice, preferred_element_type=jnp.float32)
            return (running + lax.optimization_barrier(product.astype(jnp.bfloat16)).astype(jnp.float32), None)
        summed, _ = lax.scan(add_slice, jnp.zeros((slot_total, D), jnp.float32), jnp.arange(N_CTX, dtype=jnp.int32))
        expert_rows = lax.optimization_barrier(summed.astype(jnp.bfloat16)).astype(jnp.float32)
        contribution = jnp.where(selected[picked][:, None], weight_row[picked][:, None] * expert_rows, 0.0)
        return (picked, contribution)
    picked_all, contributions = lax.map(one_expert, jnp.arange(EXPERTS, dtype=jnp.int32))
    moe_sum = jnp.zeros((CONTEXT_LENGTH, D), jnp.float32).at[picked_all.reshape(-1)].add(contributions.reshape(-1, D))
    return (hidden, moe_sum.astype(jnp.bfloat16))
```

```python
import functools

import jax
import jax.numpy as jnp
from jax import lax
from jax.experimental import pallas as pl
from jax.experimental.pallas import tpu as pltpu
from jax.sharding import Mesh, PartitionSpec as P

HEAD_DIM = 128
CAP = 4
EPS = 1e-05
F32 = jnp.float32
BF16 = jnp.bfloat16
HIGHEST = lax.Precision.HIGHEST
CTX = ("z", "x", "core")
VMEM_LIMIT = 48 * 1024 * 1024


def iota(shape, dim):
    return lax.broadcasted_iota(jnp.int32, shape, dim)


def params(**kw):
    return pltpu.CompilerParams(vmem_limit_bytes=VMEM_LIMIT, **kw)


def cost(flops, bytes_accessed):
    return pl.CostEstimate(flops=flops, bytes_accessed=bytes_accessed, transcendentals=0)


def state_kernel(k_ref, v_ref, ld_ref, cum_ref, cumt_ref, msg_ref):
    rows, heads = ld_ref.shape
    per = heads * HEAD_DIM // 32
    ld = ld_ref[...]
    tri = (iota((rows, rows), 0) >= iota((rows, rows), 1)).astype(F32)
    cum = jnp.dot(tri, ld, precision=HIGHEST, preferred_element_type=F32)
    cum_ref[...] = cum
    cumt_ref[...] = lax.dot_general(
        ld, tri, (((0,), (1,)), ((), ())), precision=HIGHEST, preferred_element_type=F32
    )
    final = cum[rows - 1 : rows, :]
    fade = jnp.exp(final - cum)
    decay = jnp.exp(final)
    row16 = iota((16, HEAD_DIM), 0)
    tiles = []
    for h in range(heads):
        cols = slice(h * HEAD_DIM, (h + 1) * HEAD_DIM)
        wk = (k_ref[:, cols].astype(F32) * fade[:, h : h + 1]).astype(BF16)
        state = lax.dot_general(
            wk, v_ref[:, cols], (((0,), (0,)), ((), ())), preferred_element_type=F32
        ).astype(BF16)
        row = h * HEAD_DIM
        while row < (h + 1) * HEAD_DIM:
            part, at = row // per, row % per
            take = min(per - at, (h + 1) * HEAD_DIM - row)
            lo = row - h * HEAD_DIM
            msg_ref[part, at : at + take, :] = state[lo : lo + take, :]
            row += take
        whole = jnp.broadcast_to(decay[:, h : h + 1], (16, HEAD_DIM))
        high = whole.astype(BF16).astype(F32)
        tiles.append((high, whole - high))
    for part in range(32):
        first = per * part // HEAD_DIM
        last = (per * part + per - 1) // HEAD_DIM
        tile = jnp.where(
            row16 == 0,
            tiles[first][0],
            jnp.where(
                row16 == 1, tiles[first][1], jnp.where(row16 == 2, tiles[last][0], tiles[last][1])
            ),
        )
        msg_ref[part, per : per + 16, :] = tile.astype(BF16)


def local_states(k, v, ld):
    rows, width = k.shape
    heads = ld.shape[1]
    per = heads * HEAD_DIM // 32
    return pl.pallas_call(
        state_kernel,
        out_shape=(
            jax.ShapeDtypeStruct((rows, heads), F32),
            jax.ShapeDtypeStruct((heads, rows), F32),
            jax.ShapeDtypeStruct((32, per + 16, HEAD_DIM), BF16),
        ),
        compiler_params=params(),
        cost_estimate=cost(2 * rows * width * HEAD_DIM, 4 * rows * width),
        name="local_states",
    )(k, v, ld)


def scan_kernel(split_ref, in_ref, out_ref):
    parts, per, width = out_ref.shape
    first_rows = iota((per, width), 0) < split_ref[0]
    state = jnp.zeros((per, width), F32)
    for b in range(parts):
        out_ref[b, :, :] = state.astype(BF16)
        if b + 1 < parts:
            tail = in_ref[b, per : per + 16, :].astype(F32)
            d0 = tail[0:1, :] + tail[1:2, :]
            d1 = tail[2:3, :] + tail[3:4, :]
            decay = jnp.where(first_rows, d0, d1)
            state = decay * state + in_ref[b, 0:per, :].astype(F32)


def scan_blocks(msg, part):
    parts, tall, width = msg.shape
    per = tall - 16
    split = (HEAD_DIM - (per * part) % HEAD_DIM).astype(jnp.int32).reshape(1)
    return pl.pallas_call(
        scan_kernel,
        out_shape=jax.ShapeDtypeStruct((parts, per, width), BF16),
        in_specs=[
            pl.BlockSpec(memory_space=pltpu.SMEM),
            pl.BlockSpec(memory_space=pltpu.VMEM),
        ],
        out_specs=pl.BlockSpec(memory_space=pltpu.VMEM),
        compiler_params=params(),
        cost_estimate=cost(1000000, 1000000),
        name="scan_blocks",
    )(split, msg)


def inside_kernel(group, q_ref, k_ref, v_ref, cum_ref, cumt_ref, inside_ref, qs_ref):
    rows, heads = cum_ref.shape
    lane = iota((rows, heads), 1)
    cum = cum_ref[...]
    causal = iota((HEAD_DIM, HEAD_DIM), 0) >= iota((HEAD_DIM, HEAD_DIM), 1)
    for j in range(group):
        h = pl.program_id(0) * group + j
        cols = slice(j * HEAD_DIM, (j + 1) * HEAD_DIM)
        col = jnp.sum(jnp.where(lane == h, cum, 0.0), axis=1, keepdims=True)
        row = cumt_ref[pl.ds(h, 1), :]
        q = q_ref[:, cols]
        k = k_ref[:, cols]
        v = v_ref[:, cols]
        qs_ref[:, cols] = (q.astype(F32) * jnp.exp(col)).astype(BF16)
        for i in range(rows // HEAD_DIM):
            lo, hi = i * HEAD_DIM, (i + 1) * HEAD_DIM
            qi = q[lo:hi]
            ci = col[lo:hi]
            s = lax.dot_general(
                qi, k[lo:hi], (((1,), (1,)), ((), ())), preferred_element_type=F32
            )
            gap = jnp.minimum(ci - row[:, lo:hi], 0.0)
            w = jnp.where(causal, s * jnp.exp(gap), 0.0).astype(BF16)
            total = jnp.dot(w, v[lo:hi], preferred_element_type=F32)
            if i:
                s = lax.dot_general(
                    qi, k[:lo], (((1,), (1,)), ((), ())), preferred_element_type=F32
                )
                w = (s * jnp.exp(jnp.minimum(ci - row[:, :lo], 0.0))).astype(BF16)
                total = total + jnp.dot(w, v[:lo], preferred_element_type=F32)
            inside_ref[lo:hi, cols] = total


def inside_blocks(q, k, v, cum, cumt, group=3):
    rows, width = q.shape
    heads = cum.shape[1]
    block = pl.BlockSpec((rows, group * HEAD_DIM), lambda g: (0, g))
    return pl.pallas_call(
        functools.partial(inside_kernel, group),
        grid=(heads // group,),
        out_shape=(
            jax.ShapeDtypeStruct((rows, width), F32),
            jax.ShapeDtypeStruct((rows, width), BF16),
        ),
        in_specs=[
            block,
            block,
            block,
            pl.BlockSpec((rows, heads), lambda g: (0, 0)),
            pl.BlockSpec((heads, rows), lambda g: (0, 0)),
        ],
        out_specs=(block, block),
        compiler_params=params(),
        cost_estimate=cost(4 * rows * rows * width, 12 * rows * width),
        name="inside_blocks",
    )(q, k, v, cum, cumt)


def carried_kernel(group, inside_ref, qs_ref, state_ref, place_ref, att_ref, sel_ref):
    for j in range(group):
        cols = slice(j * HEAD_DIM, (j + 1) * HEAD_DIM)
        att = (
            inside_ref[:, cols]
            + jnp.dot(qs_ref[:, cols], state_ref[j], preferred_element_type=F32)
        ).astype(BF16)
        att_ref[:, cols] = att
        sel_ref[:, cols] = jnp.dot(
            place_ref[...], att, preferred_element_type=F32
        ).astype(BF16)


def carried_blocks(inside, qs, state, place, group=3):
    rows, width = inside.shape
    heads = width // HEAD_DIM
    chosen = place.shape[0]
    block = pl.BlockSpec((rows, group * HEAD_DIM), lambda g: (0, g))
    return pl.pallas_call(
        functools.partial(carried_kernel, group),
        grid=(heads // group,),
        out_shape=(
            jax.ShapeDtypeStruct((rows, width), BF16),
            jax.ShapeDtypeStruct((chosen, width), BF16),
        ),
        in_specs=[
            block,
            block,
            pl.BlockSpec((group, HEAD_DIM, HEAD_DIM), lambda g: (g, 0, 0)),
            pl.BlockSpec((chosen, rows), lambda g: (0, 0)),
        ],
        out_specs=(block, pl.BlockSpec((chosen, group * HEAD_DIM), lambda g: (0, g))),
        compiler_params=params(),
        cost_estimate=cost(4 * rows * width * HEAD_DIM, 8 * rows * width),
        name="carried_blocks",
    )(inside, qs, state, place)


def members(ids, held):
    return jnp.concatenate(
        [
            ((ids[0:1, :] == e) | (ids[1:2, :] == e)).astype(F32)
            for e in range(held)
        ],
        axis=0,
    )


def place_kernel(ids_ref, place_ref):
    sources, _, tokens = ids_ref.shape
    held = sources
    total = sources * tokens
    ids = jnp.concatenate([ids_ref[j] for j in range(sources)], axis=1)
    m = members(ids, held)
    before = iota((total, total), 0)
    after = iota((total, total), 1)
    upto = ((before <= after) & (before // tokens == after // tokens)).astype(BF16)
    rank = jnp.dot(m.astype(BF16), upto, preferred_element_type=F32) - 1.0
    rows = sources * CAP
    r = iota((rows, total), 0)
    t = iota((rows, total), 1)
    here = (t // tokens == r // CAP).astype(F32)
    slot = (r % CAP).astype(F32)
    for e in range(held):
        hit = jnp.where(rank[e : e + 1, :] == slot, m[e : e + 1, :] * here, 0.0)
        place_ref[e * rows : (e + 1) * rows, :] = hit.astype(BF16)


def place_rows(ids):
    sources, _, tokens = ids.shape
    return pl.pallas_call(
        place_kernel,
        out_shape=jax.ShapeDtypeStruct((sources * sources * CAP, sources * tokens), BF16),
        compiler_params=params(),
        cost_estimate=cost(1000000, 200000),
        name="place_rows",
    )(ids)


def route_kernel(ids_ref, res_ref, gate_ref, out_ref, place_ref):
    held = out_ref.shape[0]
    tokens = ids_ref.shape[1]
    m = members(ids_ref[...], held)
    upto = (iota((tokens, tokens), 0) <= iota((tokens, tokens), 1)).astype(BF16)
    rank = jnp.dot(m.astype(BF16), upto, preferred_element_type=F32) - 1.0
    slot = iota((CAP, tokens), 0).astype(F32)
    for e in range(held):
        hit = jnp.where(rank[e : e + 1, :] == slot, m[e : e + 1, :], 0.0)
        place_ref[e * CAP : (e + 1) * CAP, :] = hit
        chosen = hit.astype(BF16)
        out_ref[e, 0:CAP, :] = jnp.dot(
            chosen, res_ref[...], preferred_element_type=F32
        ).astype(BF16)
        out_ref[e, CAP : 2 * CAP, :] = jnp.dot(
            chosen, gate_ref[...], preferred_element_type=F32
        ).astype(BF16)


def route_rows(ids, residual, out_gate, held):
    tokens, width = residual.shape
    return pl.pallas_call(
        route_kernel,
        out_shape=(
            jax.ShapeDtypeStruct((held, 2 * CAP, width), BF16),
            jax.ShapeDtypeStruct((held * CAP, tokens), F32),
        ),
        compiler_params=params(),
        cost_estimate=cost(64 * tokens * width, 5 * tokens * width),
        name="route_rows",
    )(ids, residual, out_gate)


def gated(att, res, gate, attn_gain):
    norm = att * lax.rsqrt(jnp.mean(att * att, axis=-1, keepdims=True) + EPS) * attn_gain
    return (res + norm * jax.nn.sigmoid(gate)).astype(BF16)


def routed_norm_kernel(att_ref, rg_ref, ag_ref, mg_ref, one_ref, two_ref):
    sources, rows, _ = att_ref.shape
    att = jnp.concatenate([att_ref[s].astype(F32) for s in range(sources)], axis=1)
    rg = [rg_ref[j].astype(F32) for j in range(sources)]
    res = jnp.concatenate([a[0:CAP] for a in rg], axis=0)
    gate = jnp.concatenate([a[CAP : 2 * CAP] for a in rg], axis=0)
    hidden = gated(att, res, gate, ag_ref[...]).astype(F32)
    normed = (
        hidden * lax.rsqrt(jnp.mean(hidden * hidden, axis=-1, keepdims=True) + EPS) * mg_ref[...]
    ).astype(BF16)
    half = normed.shape[1] // 2
    for s in range(one_ref.shape[0]):
        one_ref[s] = normed[:, :half]
        two_ref[s] = normed[:, half:]


def routed_norm(att, rg, attn_gain, moe_gain, copies):
    sources, rows, part = att.shape
    width = sources * part
    return pl.pallas_call(
        routed_norm_kernel,
        out_shape=(
            jax.ShapeDtypeStruct((copies, rows, width // 2), BF16),
            jax.ShapeDtypeStruct((copies, rows, width // 2), BF16),
        ),
        compiler_params=params(),
        cost_estimate=cost(20 * rows * width, 20 * rows * width),
        name="routed_norm",
    )(att, rg, attn_gain, moe_gain)


def hidden_kernel(att_ref, res_ref, gate_ref, ag_ref, out_ref):
    sources = att_ref.shape[0]
    att = jnp.concatenate([att_ref[s].astype(F32) for s in range(sources)], axis=1)
    out_ref[...] = gated(att, res_ref[...].astype(F32), gate_ref[...].astype(F32), ag_ref[...])


def hidden_rows(att, residual, out_gate, attn_gain, tile=32):
    sources, rows, part = att.shape
    width = sources * part
    block = pl.BlockSpec((tile, width), lambda i: (i, 0))
    return pl.pallas_call(
        hidden_kernel,
        grid=(rows // tile,),
        out_shape=jax.ShapeDtypeStruct((rows, width), BF16),
        in_specs=[
            pl.BlockSpec((sources, tile, part), lambda i: (0, i, 0)),
            block,
            block,
            pl.BlockSpec((1, width), lambda i: (0, 0)),
        ],
        out_specs=block,
        compiler_params=params(),
        cost_estimate=cost(20 * rows * width, 8 * rows * width),
        name="hidden_rows",
    )(att, residual, out_gate, attn_gain)


def expert_kernel(
    ksteps, nsteps, one_ref, two_ref, wg_ref, wu_ref, wd_ref, o1_ref, o2_ref, gate_acc, up_acc, act
):
    step = pl.program_id(0)
    nz, nx, rows, _ = one_ref.shape
    depth = one_ref.shape[3]

    def accumulate(lhs, first):
        g = jnp.dot(lhs, wg_ref[0], preferred_element_type=F32)
        u = jnp.dot(lhs, wu_ref[0], preferred_element_type=F32)
        if first:
            gate_acc[...] = g
            up_acc[...] = u
        else:
            gate_acc[...] += g
            up_acc[...] += u

    half = ksteps // 2
    for s in range(ksteps):

        @pl.when(step == s)
        def _():
            if s < half:
                lhs = one_ref[...].reshape(nz * nx * rows, depth)
            else:
                lhs = jnp.concatenate(
                    [two_ref[x, z] for z in range(nz) for x in range(nx)], axis=0
                )
            accumulate(lhs, s == 0)
            if s == ksteps - 1:
                g = gate_acc[...]
                act[...] = (g * jax.nn.sigmoid(g) * up_acc[...]).astype(BF16)

    @pl.when(step >= ksteps)
    def _():
        out = jnp.dot(act[...], wd_ref[0], preferred_element_type=F32).astype(BF16)

        @pl.when(step < ksteps + nsteps // 2)
        def _():
            o1_ref[...] = out.reshape(o1_ref.shape)

        @pl.when(step >= ksteps + nsteps // 2)
        def _():
            for z in range(nz):
                for x in range(nx):
                    at = (z * nx + x) * rows
                    o2_ref[x, z] = out[at : at + rows]


def expert_rows(one, two, w_gate, w_up, w_down, ksteps=4, nsteps=4):
    nz, nx, rows, half = one.shape
    units = w_gate.shape[2]
    depth = 2 * half // ksteps
    wide = 2 * half // nsteps
    kh, nh = ksteps // 2, nsteps // 2
    count = nz * nx * rows

    def k_at(i):
        return jnp.minimum(i, ksteps - 1)

    def n_at(i):
        return jnp.maximum(i - ksteps, 0)

    return pl.pallas_call(
        functools.partial(expert_kernel, ksteps, nsteps),
        grid=(ksteps + nsteps,),
        out_shape=(
            jax.ShapeDtypeStruct((nz, nx, rows, half), BF16),
            jax.ShapeDtypeStruct((nx, nz, rows, half), BF16),
        ),
        in_specs=[
            pl.BlockSpec((nz, nx, rows, depth), lambda i: (0, 0, 0, jnp.minimum(i, kh - 1))),
            pl.BlockSpec(
                (nx, nz, rows, depth), lambda i: (0, 0, 0, jnp.clip(i - kh, 0, kh - 1))
            ),
            pl.BlockSpec((1, depth, units), lambda i: (0, k_at(i), 0)),
            pl.BlockSpec((1, depth, units), lambda i: (0, k_at(i), 0)),
            pl.BlockSpec((1, units, wide), lambda i: (0, 0, n_at(i))),
        ],
        out_specs=(
            pl.BlockSpec((nz, nx, rows, wide), lambda i: (0, 0, 0, jnp.minimum(n_at(i), nh - 1))),
            pl.BlockSpec(
                (nx, nz, rows, wide), lambda i: (0, 0, 0, jnp.clip(n_at(i) - nh, 0, nh - 1))
            ),
        ),
        scratch_shapes=[
            pltpu.VMEM((count, units), F32),
            pltpu.VMEM((count, units), F32),
            pltpu.VMEM((count, units), BF16),
        ],
        compiler_params=params(),
        cost_estimate=cost(12 * count * half * units, 12 * half * units + 8 * count * half),
        name="expert_rows",
    )(one, two, w_gate, w_up, w_down)


def combine_kernel(place_ref, rows_ref, ids_ref, weights_ref, out_ref):
    held = rows_ref.shape[0]
    rows = jnp.concatenate([rows_ref[e].astype(F32) for e in range(held)], axis=0).astype(BF16)
    back = lax.dot_general(
        place_ref[...].astype(BF16), rows, (((0,), (0,)), ((), ())), preferred_element_type=F32
    )
    chosen = jnp.sum(
        jnp.where(ids_ref[...] < held, weights_ref[...], 0.0), axis=1, keepdims=True
    )
    out_ref[...] = (back * chosen).astype(BF16)


def combine_rows(place, rows, ids, weights):
    tokens = ids.shape[0]
    width = rows.shape[2]
    return pl.pallas_call(
        combine_kernel,
        out_shape=jax.ShapeDtypeStruct((tokens, width), BF16),
        compiler_params=params(),
        cost_estimate=cost(32 * tokens * width, 2 * tokens * width),
        name="combine_rows",
    )(place, rows, ids, weights)


def swap(a, axis):
    n = lax.axis_size(axis)
    return lax.ppermute(a, axis, [(i, (i + 1) % n) for i in range(n)])


def exchange(a, axis):
    return lax.all_to_all(a, axis, split_axis=0, concat_axis=0, tiled=True)


def local(
    queries,
    key_vectors,
    values,
    log_decay,
    out_gate,
    residual,
    attn_gain,
    moe_gain,
    expert_ids,
    route_weights,
    w_gate,
    w_up,
    w_down,
):
    held = lax.axis_size("exp")
    nz, nx = lax.axis_size("z"), lax.axis_size("x")
    rows, width = queries.shape
    heads = log_decay.shape[1]
    tokens = residual.shape[0]
    attn_gain = attn_gain.reshape(1, -1)
    moe_gain = moe_gain.reshape(1, -1)
    ids = expert_ids.T

    cum, cumt, msg = local_states(key_vectors, values, log_decay)
    sent = exchange(msg, CTX)
    prior = scan_blocks(sent, lax.axis_index(CTX))
    state = exchange(prior, CTX).reshape(heads, HEAD_DIM, HEAD_DIM)

    all_ids = lax.all_gather(ids, "exp", axis=0)
    place = place_rows(all_ids)
    rg, place_own = route_rows(ids, residual, out_gate, held)
    rg = exchange(rg, "exp")
    inside, qs = inside_blocks(queries, key_vectors, values, cum, cumt)

    attention, routed = carried_blocks(inside, qs, state, place)
    routed = exchange(routed.reshape(held, held * CAP, width), "exp")
    one, two = routed_norm(routed, rg, attn_gain, moe_gain, nx)

    one = exchange(one, "x")
    two = exchange(two, "z")
    one = exchange(jnp.broadcast_to(one[None], (nz,) + one.shape), "z")
    two = exchange(jnp.broadcast_to(two[None], (nx,) + two.shape), "x")
    one_far, two_far = swap(one, "core"), swap(two, "core")

    here1, here2 = expert_rows(one, two, w_gate, w_up, w_down)
    far1, far2 = expert_rows(one_far, two_far, w_gate, w_up, w_down)
    far1, far2 = swap(far1, "core"), swap(far2, "core")

    def total(parts):
        return jnp.sum(parts.astype(F32), axis=0).astype(BF16)

    sum1 = (here1.astype(F32) + far1.astype(F32)).astype(BF16)
    sum2 = (here2.astype(F32) + far2.astype(F32)).astype(BF16)
    sum1 = total(exchange(sum1, "z"))
    sum2 = total(exchange(sum2, "x"))
    sum1 = total(exchange(sum1, "x"))
    sum2 = total(exchange(sum2, "z"))
    back = jnp.concatenate([sum1, sum2], axis=1).reshape(held, CAP, -1)
    back = exchange(back, "exp")
    moe_out = combine_rows(place_own, back, expert_ids, route_weights)

    whole = exchange(attention.reshape(held, tokens, width), "exp")
    hidden = hidden_rows(whole, residual, out_gate, attn_gain)
    return (hidden, moe_out)


def solution(mesh):
    cube = Mesh(mesh.devices.reshape(4, 4, 2, 4), ("z", "x", "core", "exp"))
    both = CTX + ("exp",)
    in_specs = (
        P(CTX, "exp"),
        P(CTX, "exp"),
        P(CTX, "exp"),
        P(CTX, "exp"),
        P(both, None),
        P(both, None),
        P(),
        P(),
        P(both, None),
        P(both, None),
        P("exp", None, CTX),
        P("exp", None, CTX),
        P("exp", CTX, None),
    )
    out_specs = (P(both, None), P(both, None))
    return jax.shard_map(local, mesh=cube, in_specs=in_specs, out_specs=out_specs, check_vma=False)
```

```python
import functools

import jax
import jax.numpy as jnp
from jax import lax
from jax.experimental import pallas as pl
from jax.experimental.pallas import tpu as pltpu
from jax.sharding import Mesh, PartitionSpec as P

HEAD_DIM = 128
CAP = 4
EPS = 1e-05
F32 = jnp.float32
BF16 = jnp.bfloat16
HIGHEST = lax.Precision.HIGHEST
CTX = ("z", "x", "core")
VMEM_LIMIT = 60 * 1024 * 1024


def iota(shape, dim):
    return lax.broadcasted_iota(jnp.int32, shape, dim)


def params(**kw):
    return pltpu.CompilerParams(vmem_limit_bytes=VMEM_LIMIT, **kw)


def cost(flops, bytes_accessed):
    return pl.CostEstimate(flops=flops, bytes_accessed=bytes_accessed, transcendentals=0)


def running_sum(ld, axis):
    rows = ld.shape[1]
    a, b = iota((rows, rows), 0), iota((rows, rows), 1)
    ones = (a >= b).astype(BF16)
    total = None
    rest = ld
    for _ in range(3):
        part = rest.astype(BF16)
        rest = rest - part.astype(F32)
        pair = (ones, part) if axis == 0 else (part, ones)
        term = lax.dot_general(*pair, (((1,), (1,)), ((), ())), preferred_element_type=F32)
        total = term if total is None else total + term
    return total


def column(table, h):
    lane = iota(table.shape, 1)
    return jnp.sum(jnp.where(lane == h, table, 0.0), axis=1, keepdims=True)


def state_kernel(group, k_ref, v_ref, ld_ref, cum_ref, msg_ref, fade_ref, decay_ref):
    heads, rows = ld_ref.shape
    per = heads * HEAD_DIM // 32
    parts = group * HEAD_DIM // per
    g = pl.program_id(0)

    @pl.when(g == 0)
    def _():
        cum = running_sum(ld_ref[...], 0)
        cum_ref[...] = cum
        final = cum[rows - 1 : rows, :]
        fade_ref[...] = jnp.exp(final - cum)
        decay_ref[...] = jnp.broadcast_to(jnp.exp(final), decay_ref.shape)

    fade = fade_ref[...]
    decay = decay_ref[...]
    row16 = iota((16, HEAD_DIM), 0)
    tiles = []
    for j in range(group):
        h = g * group + j
        cols = slice(j * HEAD_DIM, (j + 1) * HEAD_DIM)
        wk = (k_ref[:, cols].astype(F32) * column(fade, h)).astype(BF16)
        state = lax.dot_general(
            wk, v_ref[:, cols], (((0,), (0,)), ((), ())), preferred_element_type=F32
        ).astype(BF16)
        row = j * HEAD_DIM
        while row < (j + 1) * HEAD_DIM:
            part, at = row // per, row % per
            take = min(per - at, (j + 1) * HEAD_DIM - row)
            lo = row - j * HEAD_DIM
            msg_ref[part, at : at + take, :] = state[lo : lo + take, :]
            row += take
        whole = jnp.broadcast_to(column(decay, h), (16, HEAD_DIM))
        high = whole.astype(BF16).astype(F32)
        tiles.append((high, whole - high))
    for part in range(parts):
        first = per * part // HEAD_DIM
        last = (per * part + per - 1) // HEAD_DIM
        tile = jnp.where(
            row16 == 0,
            tiles[first][0],
            jnp.where(
                row16 == 1, tiles[first][1], jnp.where(row16 == 2, tiles[last][0], tiles[last][1])
            ),
        )
        msg_ref[part, per : per + 16, :] = tile.astype(BF16)


def local_states(k, v, ld, group=3):
    rows, width = k.shape
    heads = ld.shape[0]
    per = heads * HEAD_DIM // 32
    parts = group * HEAD_DIM // per
    block = pl.BlockSpec((rows, group * HEAD_DIM), lambda g: (0, g))
    return pl.pallas_call(
        functools.partial(state_kernel, group),
        grid=(heads // group,),
        out_shape=(
            jax.ShapeDtypeStruct((rows, heads), F32),
            jax.ShapeDtypeStruct((32, per + 16, HEAD_DIM), BF16),
        ),
        in_specs=[block, block, pl.BlockSpec((heads, rows), lambda g: (0, 0))],
        out_specs=(
            pl.BlockSpec((rows, heads), lambda g: (0, 0)),
            pl.BlockSpec((parts, per + 16, HEAD_DIM), lambda g: (g, 0, 0)),
        ),
        scratch_shapes=[pltpu.VMEM((rows, heads), F32), pltpu.VMEM((16, heads), F32)],
        compiler_params=params(),
        cost_estimate=cost(2 * rows * width * HEAD_DIM, 4 * rows * width),
        name="local_states",
    )(k, v, ld)


def scan_kernel(split_ref, in_ref, out_ref):
    parts, per, width = out_ref.shape
    first_rows = iota((per, width), 0) < split_ref[0]
    state = jnp.zeros((per, width), F32)
    for b in range(parts):
        out_ref[b, :, :] = state.astype(BF16)
        if b + 1 < parts:
            tail = in_ref[b, per : per + 16, :].astype(F32)
            d0 = tail[0:1, :] + tail[1:2, :]
            d1 = tail[2:3, :] + tail[3:4, :]
            decay = jnp.where(first_rows, d0, d1)
            state = decay * state + in_ref[b, 0:per, :].astype(F32)


def scan_blocks(msg, part):
    parts, tall, width = msg.shape
    per = tall - 16
    split = (HEAD_DIM - (per * part) % HEAD_DIM).astype(jnp.int32).reshape(1)
    return pl.pallas_call(
        scan_kernel,
        out_shape=jax.ShapeDtypeStruct((parts, per, width), BF16),
        in_specs=[
            pl.BlockSpec(memory_space=pltpu.SMEM),
            pl.BlockSpec(memory_space=pltpu.VMEM),
        ],
        out_specs=pl.BlockSpec(memory_space=pltpu.VMEM),
        compiler_params=params(),
        cost_estimate=cost(1000000, 1000000),
        name="scan_blocks",
    )(split, msg)


def inside_kernel(group, q_ref, k_ref, v_ref, cum_ref, ld_ref, inside_ref, qs_ref, cumt_ref):
    rows, heads = cum_ref.shape

    @pl.when(pl.program_id(0) == 0)
    def _():
        cumt_ref[...] = running_sum(ld_ref[...], 1)

    cum = cum_ref[...]
    causal = iota((HEAD_DIM, HEAD_DIM), 0) >= iota((HEAD_DIM, HEAD_DIM), 1)
    for j in range(group):
        h = pl.program_id(0) * group + j
        cols = slice(j * HEAD_DIM, (j + 1) * HEAD_DIM)
        col = column(cum, h)
        row = cumt_ref[pl.ds(h, 1), :]
        q = q_ref[:, cols]
        k = k_ref[:, cols]
        v = v_ref[:, cols]
        qs_ref[:, cols] = (q.astype(F32) * jnp.exp(col)).astype(BF16)
        for i in range(rows // HEAD_DIM):
            lo, hi = i * HEAD_DIM, (i + 1) * HEAD_DIM
            qi = q[lo:hi]
            ci = col[lo:hi]
            s = lax.dot_general(
                qi, k[lo:hi], (((1,), (1,)), ((), ())), preferred_element_type=F32
            )
            gap = jnp.minimum(ci - row[:, lo:hi], 0.0)
            w = jnp.where(causal, s * jnp.exp(gap), 0.0).astype(BF16)
            total = jnp.dot(w, v[lo:hi], preferred_element_type=F32)
            if i:
                s = lax.dot_general(
                    qi, k[:lo], (((1,), (1,)), ((), ())), preferred_element_type=F32
                )
                w = (s * jnp.exp(jnp.minimum(ci - row[:, :lo], 0.0))).astype(BF16)
                total = total + jnp.dot(w, v[:lo], preferred_element_type=F32)
            inside_ref[lo:hi, cols] = total


def inside_blocks(q, k, v, cum, ld, group=3):
    rows, width = q.shape
    heads = cum.shape[1]
    block = pl.BlockSpec((rows, group * HEAD_DIM), lambda g: (0, g))
    return pl.pallas_call(
        functools.partial(inside_kernel, group),
        grid=(heads // group,),
        out_shape=(
            jax.ShapeDtypeStruct((rows, width), F32),
            jax.ShapeDtypeStruct((rows, width), BF16),
        ),
        in_specs=[
            block,
            block,
            block,
            pl.BlockSpec((rows, heads), lambda g: (0, 0)),
            pl.BlockSpec((heads, rows), lambda g: (0, 0)),
        ],
        out_specs=(block, block),
        scratch_shapes=[pltpu.VMEM((heads, rows), F32)],
        compiler_params=params(),
        cost_estimate=cost(4 * rows * rows * width, 12 * rows * width),
        name="inside_blocks",
    )(q, k, v, cum, ld)


def carried_kernel(group, inside_ref, qs_ref, state_ref, place_ref, att_ref, sel_ref):
    for j in range(group):
        cols = slice(j * HEAD_DIM, (j + 1) * HEAD_DIM)
        att = (
            inside_ref[:, cols]
            + jnp.dot(qs_ref[:, cols], state_ref[j], preferred_element_type=F32)
        ).astype(BF16)
        att_ref[:, cols] = att
        sel_ref[:, cols] = jnp.dot(
            place_ref[...], att, preferred_element_type=F32
        ).astype(BF16)


def carried_blocks(inside, qs, state, place, group=3):
    rows, width = inside.shape
    heads = width // HEAD_DIM
    chosen = place.shape[0]
    block = pl.BlockSpec((rows, group * HEAD_DIM), lambda g: (0, g))
    return pl.pallas_call(
        functools.partial(carried_kernel, group),
        grid=(heads // group,),
        out_shape=(
            jax.ShapeDtypeStruct((rows, width), BF16),
            jax.ShapeDtypeStruct((chosen, width), BF16),
        ),
        in_specs=[
            block,
            block,
            pl.BlockSpec((group, HEAD_DIM, HEAD_DIM), lambda g: (g, 0, 0)),
            pl.BlockSpec((chosen, rows), lambda g: (0, 0)),
        ],
        out_specs=(block, pl.BlockSpec((chosen, group * HEAD_DIM), lambda g: (0, g))),
        compiler_params=params(),
        cost_estimate=cost(4 * rows * width * HEAD_DIM, 8 * rows * width),
        name="carried_blocks",
    )(inside, qs, state, place)


def route_kernel(me_ref, ids_ref, res_ref, gate_ref, *refs):
    outs, place_ref = refs[:-1], refs[-1]
    held = len(outs)
    tokens, width = res_ref.shape
    me = me_ref[0]
    ids = ids_ref[...]
    hits = [
        ((ids[0:1, :] == e) | (ids[1:2, :] == e)).astype(F32) for e in range(held)
    ]
    m = jnp.concatenate(hits, axis=0)
    upto = (iota((tokens, tokens), 0) <= iota((tokens, tokens), 1)).astype(BF16)
    rank = jnp.dot(m.astype(BF16), upto, preferred_element_type=F32) - 1.0
    slot = iota((CAP, tokens), 0).astype(F32)
    places = [
        jnp.where(rank[e : e + 1, :] == slot, m[e : e + 1, :], 0.0) for e in range(held)
    ]
    place = jnp.concatenate(places, axis=0)
    place_ref[...] = place
    for d in range(held):
        expert = lax.rem(me + d, held)
        mine = places[0]
        for e in range(1, held):
            mine = jnp.where(expert == e, places[e], mine)
        mine = mine.astype(BF16)
        outs[d][0:CAP, 0:width] = jnp.dot(
            mine, res_ref[...], preferred_element_type=F32
        ).astype(BF16)
        outs[d][CAP : 2 * CAP, 0:width] = jnp.dot(
            mine, gate_ref[...], preferred_element_type=F32
        ).astype(BF16)
        for n in range(2):
            outs[d][:, width + n * tokens : width + (n + 1) * tokens] = jnp.broadcast_to(
                ids[n : n + 1, :].astype(F32), (2 * CAP, tokens)
            ).astype(BF16)


def route_rows(me, ids, residual, out_gate, held):
    tokens, width = residual.shape
    whole = pl.BlockSpec(memory_space=pltpu.VMEM)
    piece = jax.ShapeDtypeStruct((2 * CAP, width + 2 * tokens), BF16)
    outs = pl.pallas_call(
        route_kernel,
        out_shape=(piece,) * held + (jax.ShapeDtypeStruct((held * CAP, tokens), F32),),
        in_specs=[pl.BlockSpec(memory_space=pltpu.SMEM), whole, whole, whole],
        out_specs=(whole,) * (held + 1),
        compiler_params=params(),
        cost_estimate=cost(64 * tokens * width, 5 * tokens * width),
        name="route_rows",
    )(me, ids, residual, out_gate)
    return outs[:-1], outs[-1]


def by_source(me, pieces, j):
    count = len(pieces)
    out = pieces[0]
    for d in range(1, count):
        out = jnp.where(lax.rem(me + count - d, count) == j, pieces[d], out)
    return out


def place_kernel(me_ref, *refs):
    pieces, place_ref = refs[:-1], refs[-1]
    held = len(pieces)
    tokens = pieces[0].shape[1] // 2
    total = held * tokens
    me = me_ref[0]
    tables = [p[...].astype(F32) for p in pieces]
    ordered = [by_source(me, tables, j) for j in range(held)]
    first = jnp.concatenate([a[0:1, :tokens] for a in ordered], axis=1)
    second = jnp.concatenate([a[0:1, tokens:] for a in ordered], axis=1)
    m = jnp.concatenate(
        [((first == float(e)) | (second == float(e))).astype(F32) for e in range(held)], axis=0
    )
    before = iota((total, total), 0)
    after = iota((total, total), 1)
    upto = ((before <= after) & (before // tokens == after // tokens)).astype(BF16)
    rank = jnp.dot(m.astype(BF16), upto, preferred_element_type=F32) - 1.0
    rows = held * CAP
    r = iota((rows, total), 0)
    t = iota((rows, total), 1)
    chunk = r // (rows // 2)
    inner = r % (rows // 2)
    source = inner // (CAP // 2)
    slot = (chunk * (CAP // 2) + inner % (CAP // 2)).astype(F32)
    here = (t // tokens == source).astype(F32)
    for e in range(held):
        hit = jnp.where(rank[e : e + 1, :] == slot, m[e : e + 1, :] * here, 0.0)
        place_ref[e * rows : (e + 1) * rows, :] = hit.astype(BF16)


def place_rows(me, pieces, tokens):
    held = len(pieces)
    width = pieces[0].shape[1] - 2 * tokens
    at = width // (2 * tokens)
    return pl.pallas_call(
        place_kernel,
        grid=(1,),
        out_shape=jax.ShapeDtypeStruct((held * held * CAP, held * tokens), BF16),
        in_specs=[pl.BlockSpec(memory_space=pltpu.SMEM)]
        + [pl.BlockSpec((2 * CAP, 2 * tokens), lambda i: (0, at))] * held,
        out_specs=pl.BlockSpec((held * held * CAP, held * tokens), lambda i: (0, 0)),
        compiler_params=params(),
        cost_estimate=cost(1000000, 200000),
        name="place_rows",
    )(me, *pieces)


def gated(att, res, gate, attn_gain):
    norm = att * lax.rsqrt(jnp.mean(att * att, axis=-1, keepdims=True) + EPS) * attn_gain
    return (res + norm * jax.nn.sigmoid(gate)).astype(BF16)


def routed_norm_kernel(me_ref, att_ref, ag_ref, mg_ref, *refs):
    pieces, one_ref, two_ref = refs[:-2], refs[-2], refs[-1]
    sources, rows, part = att_ref.shape
    width = sources * part
    me = me_ref[0]
    att = jnp.concatenate([att_ref[s].astype(F32) for s in range(sources)], axis=1)
    tables = [p[...][:, :width].astype(F32) for p in pieces]
    ordered = [by_source(me, tables, j) for j in range(sources)]
    half = CAP // 2
    res = jnp.concatenate(
        [a[c * half : (c + 1) * half] for c in range(2) for a in ordered], axis=0
    )
    gate = jnp.concatenate(
        [a[CAP + c * half : CAP + (c + 1) * half] for c in range(2) for a in ordered], axis=0
    )
    hidden = gated(att, res, gate, ag_ref[...]).astype(F32)
    normed = (
        hidden * lax.rsqrt(jnp.mean(hidden * hidden, axis=-1, keepdims=True) + EPS) * mg_ref[...]
    )
    one_ref[...] = normed[: rows // 2].astype(BF16)
    two_ref[...] = normed[rows // 2 :].astype(BF16)


def routed_norm(me, att, pieces, attn_gain, moe_gain):
    sources, rows, part = att.shape
    width = sources * part
    whole = pl.BlockSpec(memory_space=pltpu.VMEM)
    shape = jax.ShapeDtypeStruct((rows // 2, width), BF16)
    return pl.pallas_call(
        routed_norm_kernel,
        out_shape=(shape, shape),
        in_specs=[pl.BlockSpec(memory_space=pltpu.SMEM)] + [whole] * (3 + len(pieces)),
        out_specs=(whole, whole),
        compiler_params=params(),
        cost_estimate=cost(20 * rows * width, 20 * rows * width),
        name="routed_norm",
    )(me, att, attn_gain, moe_gain, *pieces)


def hidden_kernel(att_ref, res_ref, gate_ref, ag_ref, out_ref):
    sources = att_ref.shape[0]
    att = jnp.concatenate([att_ref[s].astype(F32) for s in range(sources)], axis=1)
    out_ref[...] = gated(att, res_ref[...].astype(F32), gate_ref[...].astype(F32), ag_ref[...])


def hidden_rows(att, residual, out_gate, attn_gain, tile=32):
    sources, rows, part = att.shape
    width = sources * part
    block = pl.BlockSpec((tile, width), lambda i: (i, 0))
    return pl.pallas_call(
        hidden_kernel,
        grid=(rows // tile,),
        out_shape=jax.ShapeDtypeStruct((rows, width), BF16),
        in_specs=[
            pl.BlockSpec((sources, tile, part), lambda i: (0, i, 0)),
            block,
            block,
            pl.BlockSpec((1, width), lambda i: (0, 0)),
        ],
        out_specs=block,
        compiler_params=params(),
        cost_estimate=cost(20 * rows * width, 8 * rows * width),
        name="hidden_rows",
    )(att, residual, out_gate, attn_gain)


def expert_kernel(
    ksteps, core_ref, x_ref, wg_ref, wu_ref, wd_ref, own_ref, other_ref, gate_acc, up_acc, act
):
    step = pl.program_id(0)
    chips, rows, wide = own_ref.shape
    nt = (((1,), (1,)), ((), ()))

    @pl.when(step < ksteps)
    def _():
        x = x_ref[...]
        g = lax.dot_general(wg_ref[0], x, nt, preferred_element_type=F32)
        u = lax.dot_general(wu_ref[0], x, nt, preferred_element_type=F32)

        @pl.when(step == 0)
        def _():
            gate_acc[...] = g
            up_acc[...] = u

        @pl.when(step > 0)
        def _():
            gate_acc[...] += g
            up_acc[...] += u

    @pl.when(step == ksteps - 1)
    def _():
        g = gate_acc[...]
        act[...] = (g * jax.nn.sigmoid(g) * up_acc[...]).T.astype(BF16)

    @pl.when(step >= ksteps)
    def _():
        out = jnp.dot(act[...], wd_ref[0], preferred_element_type=F32)
        out = out.reshape(chips, 2, rows, wide)
        first = core_ref[0] == 0

        @pl.when(first)
        def _():
            own_ref[...] = out[:, 0].astype(BF16)
            other_ref[...] = out[:, 1].astype(BF16)

        @pl.when(jnp.logical_not(first))
        def _():
            own_ref[...] = out[:, 1].astype(BF16)
            other_ref[...] = out[:, 0].astype(BF16)


def expert_rows(core, x, w_gate, w_up, w_down, ksteps=4, nsteps=4):
    count, width = x.shape
    units = w_gate.shape[1]
    depth, wide = width // ksteps, width // nsteps
    rows = count // 32

    def k_at(i):
        return jnp.minimum(i, ksteps - 1)

    def n_at(i):
        return jnp.maximum(i - ksteps, 0)

    return pl.pallas_call(
        functools.partial(expert_kernel, ksteps),
        grid=(ksteps + nsteps,),
        out_shape=(jax.ShapeDtypeStruct((16, rows, width), BF16),) * 2,
        in_specs=[
            pl.BlockSpec(memory_space=pltpu.SMEM),
            pl.BlockSpec((count, depth), lambda i: (0, k_at(i))),
            pl.BlockSpec((1, units, depth), lambda i: (0, 0, k_at(i))),
            pl.BlockSpec((1, units, depth), lambda i: (0, 0, k_at(i))),
            pl.BlockSpec((1, units, wide), lambda i: (0, 0, n_at(i))),
        ],
        out_specs=(pl.BlockSpec((16, rows, wide), lambda i: (0, 0, n_at(i))),) * 2,
        scratch_shapes=[
            pltpu.VMEM((units, count), F32),
            pltpu.VMEM((units, count), F32),
            pltpu.VMEM((count, units), BF16),
        ],
        compiler_params=params(),
        cost_estimate=cost(6 * count * width * units, 6 * width * units + 4 * count * width),
        name="expert_rows",
    )(core, x, w_gate, w_up, w_down)


def pair_kernel(a_ref, b_ref, out_ref):
    out_ref[...] = (a_ref[...].astype(F32) + b_ref[...].astype(F32)).astype(BF16)


def pair_sum(own, other, steps=4):
    chips, rows, width = own.shape
    wide = width // steps
    block = pl.BlockSpec((chips, rows, wide), lambda i: (0, 0, i))
    return pl.pallas_call(
        pair_kernel,
        grid=(steps,),
        out_shape=jax.ShapeDtypeStruct((chips, rows, width), BF16),
        in_specs=[block, block],
        out_specs=block,
        compiler_params=params(),
        cost_estimate=cost(chips * rows * width, 6 * chips * rows * width),
        name="pair_sum",
    )(own, other)


def chip_sum_kernel(one_ref, two_ref, out_ref):
    def total(ref):
        out = ref[0].astype(F32)
        for i in range(1, ref.shape[0]):
            out = out + ref[i].astype(F32)
        return out

    one, two = total(one_ref), total(two_ref)
    half = CAP // 2
    for j in range(out_ref.shape[0]):
        at = slice(j * half, (j + 1) * half)
        out_ref[j] = jnp.concatenate([one[at], two[at]], axis=0).astype(BF16)


def chip_sum(one, two, held, steps=4):
    chips, rows, width = one.shape
    wide = width // steps
    block = pl.BlockSpec((chips, rows, wide), lambda i: (0, 0, i))
    return pl.pallas_call(
        chip_sum_kernel,
        grid=(steps,),
        out_shape=jax.ShapeDtypeStruct((held, CAP, width), BF16),
        in_specs=[block, block],
        out_specs=pl.BlockSpec((held, CAP, wide), lambda i: (0, 0, i)),
        compiler_params=params(),
        cost_estimate=cost(2 * chips * rows * width, 4 * chips * rows * width),
        name="chip_sum",
    )(one, two)


def combine_kernel(place_ref, rows_ref, ids_ref, weights_ref, out_ref):
    held = rows_ref.shape[0]
    rows = jnp.concatenate([rows_ref[e].astype(F32) for e in range(held)], axis=0).astype(BF16)
    back = lax.dot_general(
        place_ref[...].astype(BF16), rows, (((0,), (0,)), ((), ())), preferred_element_type=F32
    )
    chosen = jnp.sum(
        jnp.where(ids_ref[...] < held, weights_ref[...], 0.0), axis=1, keepdims=True
    )
    out_ref[...] = (back * chosen).astype(BF16)


def combine_rows(place, rows, ids, weights):
    tokens = ids.shape[0]
    width = rows.shape[2]
    return pl.pallas_call(
        combine_kernel,
        out_shape=jax.ShapeDtypeStruct((tokens, width), BF16),
        compiler_params=params(),
        cost_estimate=cost(32 * tokens * width, 2 * tokens * width),
        name="combine_rows",
    )(place, rows, ids, weights)


def exchange(a, axis):
    return lax.all_to_all(a, axis, split_axis=0, concat_axis=0, tiled=True)


def shift(a, axis, by):
    n = lax.axis_size(axis)
    return lax.ppermute(a, axis, [(i, (i + by) % n) for i in range(n)])


def local(
    queries,
    key_vectors,
    values,
    log_decay,
    out_gate,
    residual,
    attn_gain,
    moe_gain,
    expert_ids,
    route_weights,
    w_gate,
    w_up,
    w_down,
):
    held = lax.axis_size("exp")
    rows, width = queries.shape
    heads = log_decay.shape[1]
    tokens = residual.shape[0]
    attn_gain = attn_gain.reshape(1, -1)
    moe_gain = moe_gain.reshape(1, -1)
    w_gate = jnp.swapaxes(w_gate, 1, 2)
    w_up = jnp.swapaxes(w_up, 1, 2)
    ids = expert_ids.T
    ld = log_decay.T
    me = lax.axis_index("exp").reshape(1)
    core = lax.axis_index("core").reshape(1)
    keep = lax.optimization_barrier

    cum, msg = local_states(key_vectors, values, ld)
    sent = exchange(msg, CTX)
    inside, qs = inside_blocks(queries, key_vectors, values, cum, ld)
    pieces, place_own = route_rows(me, ids, residual, out_gate, held)
    sent, inside, qs, pieces = keep((sent, inside, qs, pieces))
    prior = scan_blocks(sent, lax.axis_index(CTX))
    state = exchange(prior, CTX).reshape(heads, HEAD_DIM, HEAD_DIM)
    pieces = [pieces[0]] + [shift(pieces[d], "exp", d) for d in range(1, held)]
    place = place_rows(me, pieces, tokens)

    attention, routed = carried_blocks(inside, qs, state, place)
    routed = exchange(routed.reshape(held, held * CAP, width), "exp")
    one, two = routed_norm(me, routed, pieces, attn_gain, moe_gain)

    def gather(a):
        return lax.all_gather(a, CTX, axis=0).reshape(32 * a.shape[0], a.shape[1])

    attention, one, two = keep((attention, one, two))
    one, two = gather(one), gather(two)
    whole = exchange(attention.reshape(held, tokens, width), "exp")
    hidden = hidden_rows(whole, residual, out_gate, attn_gain)
    one, hidden = keep((one, hidden))

    def expert(a):
        own, other = expert_rows(core, a, w_gate, w_up, w_down)
        return pair_sum(own, shift(other, "core", 1))

    one = expert(one)
    one, two = keep((one, two))
    one = exchange(one, ("z", "x"))
    two = exchange(expert(two), ("z", "x"))
    back = exchange(chip_sum(one, two, held), "exp")
    moe_out = combine_rows(place_own, back, expert_ids, route_weights)
    return (hidden, moe_out)


def solution(mesh):
    cube = Mesh(mesh.devices.reshape(4, 4, 2, 4), ("z", "x", "core", "exp"))
    both = CTX + ("exp",)
    in_specs = (
        P(CTX, "exp"),
        P(CTX, "exp"),
        P(CTX, "exp"),
        P(CTX, "exp"),
        P(both, None),
        P(both, None),
        P(),
        P(),
        P(both, None),
        P(both, None),
        P("exp", None, CTX),
        P("exp", None, CTX),
        P("exp", CTX, None),
    )
    out_specs = (P(both, None), P(both, None))
    return jax.shard_map(local, mesh=cube, in_specs=in_specs, out_specs=out_specs, check_vma=False)
```

```python
import functools

import jax
import jax.numpy as jnp
from jax import lax
from jax.experimental import pallas as pl
from jax.experimental.pallas import tpu as pltpu
from jax.sharding import Mesh, PartitionSpec as P

HEAD_DIM = 128
CAP = 4
EPS = 1e-05
F32 = jnp.float32
BF16 = jnp.bfloat16
HIGHEST = lax.Precision.HIGHEST
CTX = ("z", "x", "core")
VMEM_LIMIT = 24 * 1024 * 1024


def iota(shape, dim):
    return lax.broadcasted_iota(jnp.int32, shape, dim)


def hbm(a):
    return pltpu.with_memory_space_constraint(a, pltpu.HBM)


def far(shape, dtype=BF16):
    return pltpu.HBM(shape, dtype)


def params(**kw):
    return pltpu.CompilerParams(vmem_limit_bytes=VMEM_LIMIT, **kw)


def cost(flops, bytes_accessed):
    return pl.CostEstimate(flops=flops, bytes_accessed=bytes_accessed, transcendentals=0)


def running_sum(ld, axis):
    rows = ld.shape[1]
    a, b = iota((rows, rows), 0), iota((rows, rows), 1)
    ones = (a >= b).astype(BF16)
    total = None
    rest = ld
    for _ in range(3):
        part = rest.astype(BF16)
        rest = rest - part.astype(F32)
        pair = (ones, part) if axis == 0 else (part, ones)
        term = lax.dot_general(*pair, (((1,), (1,)), ((), ())), preferred_element_type=F32)
        total = term if total is None else total + term
    return total


def spread(table, first, count, terms):
    n = table.shape[1]
    shape = (n, count * HEAD_DIM)
    pick = (iota(shape, 0) == first + iota(shape, 1) // HEAD_DIM).astype(BF16)
    total = None
    rest = table
    for _ in range(terms):
        part = rest.astype(BF16)
        rest = rest - part.astype(F32)
        term = jnp.dot(part, pick, preferred_element_type=F32)
        total = term if total is None else total + term
    return total


def state_kernel(group, k_ref, v_ref, ld_ref, cum_ref, msg_ref, fade_ref, decay_ref):
    heads, rows = ld_ref.shape
    per = heads * HEAD_DIM // 32
    parts = group * HEAD_DIM // per
    g = pl.program_id(0)

    @pl.when(g == 0)
    def _():
        cum = running_sum(ld_ref[...], 0)
        cum_ref[...] = cum
        final = cum[rows - 1 : rows, :]
        fade_ref[...] = jnp.exp(final - cum)
        decay_ref[...] = jnp.broadcast_to(jnp.exp(final), decay_ref.shape)

    fade = spread(fade_ref[...], g * group, group, 2)
    decay = spread(decay_ref[...], g * group, group, 2)
    row16 = iota((16, HEAD_DIM), 0)
    tiles = []
    for j in range(group):
        cols = slice(j * HEAD_DIM, (j + 1) * HEAD_DIM)
        wk = (k_ref[:, cols].astype(F32) * fade[:, cols]).astype(BF16)
        state = lax.dot_general(
            wk, v_ref[:, cols], (((0,), (0,)), ((), ())), preferred_element_type=F32
        ).astype(BF16)
        row = j * HEAD_DIM
        while row < (j + 1) * HEAD_DIM:
            part, at = row // per, row % per
            take = min(per - at, (j + 1) * HEAD_DIM - row)
            lo = row - j * HEAD_DIM
            msg_ref[part, at : at + take, :] = state[lo : lo + take, :]
            row += take
        whole = decay[:, cols]
        high = whole.astype(BF16).astype(F32)
        tiles.append((high, whole - high))
    for part in range(parts):
        first = per * part // HEAD_DIM
        last = (per * part + per - 1) // HEAD_DIM
        tile = jnp.where(
            row16 == 0,
            tiles[first][0],
            jnp.where(
                row16 == 1, tiles[first][1], jnp.where(row16 == 2, tiles[last][0], tiles[last][1])
            ),
        )
        msg_ref[part, per : per + 16, :] = tile.astype(BF16)


def local_states(k, v, ld, group=3):
    rows, width = k.shape
    heads = ld.shape[0]
    per = heads * HEAD_DIM // 32
    parts = group * HEAD_DIM // per
    block = pl.BlockSpec((rows, group * HEAD_DIM), lambda g: (0, g))
    return pl.pallas_call(
        functools.partial(state_kernel, group),
        grid=(heads // group,),
        out_shape=(
            jax.ShapeDtypeStruct((rows, heads), F32),
            far((32, per + 16, HEAD_DIM)),
        ),
        in_specs=[block, block, pl.BlockSpec((heads, rows), lambda g: (0, 0))],
        out_specs=(
            pl.BlockSpec((rows, heads), lambda g: (0, 0)),
            pl.BlockSpec((parts, per + 16, HEAD_DIM), lambda g: (g, 0, 0)),
        ),
        scratch_shapes=[pltpu.VMEM((rows, heads), F32), pltpu.VMEM((16, heads), F32)],
        compiler_params=params(),
        cost_estimate=cost(2 * rows * width * HEAD_DIM, 4 * rows * width),
        name="local_states",
    )(k, v, ld)


def scan_kernel(split_ref, in_ref, out_ref):
    parts, per, width = out_ref.shape
    first_rows = iota((per, width), 0) < split_ref[0]
    state = jnp.zeros((per, width), F32)
    for b in range(parts):
        out_ref[b, :, :] = state.astype(BF16)
        if b + 1 < parts:
            tail = in_ref[b, per : per + 16, :].astype(F32)
            d0 = tail[0:1, :] + tail[1:2, :]
            d1 = tail[2:3, :] + tail[3:4, :]
            decay = jnp.where(first_rows, d0, d1)
            state = decay * state + in_ref[b, 0:per, :].astype(F32)


def scan_blocks(msg, part):
    parts, tall, width = msg.shape
    per = tall - 16
    split = (HEAD_DIM - (per * part) % HEAD_DIM).astype(jnp.int32).reshape(1)
    return pl.pallas_call(
        scan_kernel,
        out_shape=far((parts, per, width)),
        in_specs=[
            pl.BlockSpec(memory_space=pltpu.SMEM),
            pl.BlockSpec(memory_space=pltpu.VMEM),
        ],
        out_specs=pl.BlockSpec(memory_space=pltpu.VMEM),
        compiler_params=params(),
        cost_estimate=cost(1000000, 1000000),
        name="scan_blocks",
    )(split, msg)


def inside_kernel(group, q_ref, k_ref, v_ref, cum_ref, ld_ref, inside_ref, qs_ref, cumt_ref):
    rows, heads = cum_ref.shape

    @pl.when(pl.program_id(0) == 0)
    def _():
        cumt_ref[...] = running_sum(ld_ref[...], 1)

    cum = spread(cum_ref[...], pl.program_id(0) * group, group, 3)
    causal = iota((HEAD_DIM, HEAD_DIM), 0) >= iota((HEAD_DIM, HEAD_DIM), 1)
    for j in range(group):
        h = pl.program_id(0) * group + j
        cols = slice(j * HEAD_DIM, (j + 1) * HEAD_DIM)
        col = cum[:, cols]
        row = cumt_ref[pl.ds(h, 1), :]
        q = q_ref[:, cols]
        k = k_ref[:, cols]
        v = v_ref[:, cols]
        qs_ref[:, cols] = (q.astype(F32) * jnp.exp(col)).astype(BF16)
        for i in range(rows // HEAD_DIM):
            lo, hi = i * HEAD_DIM, (i + 1) * HEAD_DIM
            qi = q[lo:hi]
            ci = col[lo:hi]
            s = lax.dot_general(
                qi, k[lo:hi], (((1,), (1,)), ((), ())), preferred_element_type=F32
            )
            gap = jnp.minimum(ci - row[:, lo:hi], 0.0)
            w = jnp.where(causal, s * jnp.exp(gap), 0.0).astype(BF16)
            total = jnp.dot(w, v[lo:hi], preferred_element_type=F32)
            if i:
                s = lax.dot_general(
                    qi, k[:lo], (((1,), (1,)), ((), ())), preferred_element_type=F32
                )
                gap = jnp.concatenate([ci] * i, axis=1) - row[:, :lo]
                w = (s * jnp.exp(jnp.minimum(gap, 0.0))).astype(BF16)
                total = total + jnp.dot(w, v[:lo], preferred_element_type=F32)
            inside_ref[lo:hi, cols] = total


def inside_blocks(q, k, v, cum, ld, group=3):
    rows, width = q.shape
    heads = cum.shape[1]
    block = pl.BlockSpec((rows, group * HEAD_DIM), lambda g: (0, g))
    return pl.pallas_call(
        functools.partial(inside_kernel, group),
        grid=(heads // group,),
        out_shape=(
            jax.ShapeDtypeStruct((rows, width), F32),
            jax.ShapeDtypeStruct((rows, width), BF16),
        ),
        in_specs=[
            block,
            block,
            block,
            pl.BlockSpec((rows, heads), lambda g: (0, 0)),
            pl.BlockSpec((heads, rows), lambda g: (0, 0)),
        ],
        out_specs=(block, block),
        scratch_shapes=[pltpu.VMEM((heads, rows), F32)],
        compiler_params=params(),
        cost_estimate=cost(4 * rows * rows * width, 12 * rows * width),
        name="inside_blocks",
    )(q, k, v, cum, ld)


def carried_kernel(group, me_ref, inside_ref, qs_ref, state_ref, place_ref, sel_ref, *refs):
    outs, att_ref = refs[:-1], refs[-1]
    held = len(outs)
    tokens = outs[0].shape[0]
    for j in range(group):
        cols = slice(j * HEAD_DIM, (j + 1) * HEAD_DIM)
        att_ref[:, cols] = (
            inside_ref[:, cols]
            + jnp.dot(qs_ref[:, cols], state_ref[j], preferred_element_type=F32)
        ).astype(BF16)
    sel_ref[...] = jnp.dot(
        place_ref[...], att_ref[...], preferred_element_type=F32
    ).astype(BF16)
    for d in range(held):
        at = pl.multiple_of(lax.rem(me_ref[0] + d, held) * tokens, tokens)
        outs[d][...] = att_ref[pl.ds(at, tokens), :]


def carried_blocks(me, inside, qs, state, place, held, group=3):
    rows, width = inside.shape
    heads = width // HEAD_DIM
    chosen = place.shape[0]
    wide = group * HEAD_DIM
    tokens = rows // held
    block = pl.BlockSpec((rows, wide), lambda g: (0, g))
    outs = pl.pallas_call(
        functools.partial(carried_kernel, group),
        grid=(heads // group,),
        out_shape=(far((chosen, width)),) + (far((tokens, width)),) * held,
        in_specs=[
            pl.BlockSpec(memory_space=pltpu.SMEM),
            block,
            block,
            pl.BlockSpec((group, HEAD_DIM, HEAD_DIM), lambda g: (g, 0, 0)),
            pl.BlockSpec((chosen, rows), lambda g: (0, 0)),
        ],
        out_specs=(pl.BlockSpec((chosen, wide), lambda g: (0, g)),)
        + (pl.BlockSpec((tokens, wide), lambda g: (0, g)),) * held,
        scratch_shapes=[pltpu.VMEM((rows, wide), BF16)],
        compiler_params=params(),
        cost_estimate=cost(4 * rows * width * HEAD_DIM, 8 * rows * width),
        name="carried_blocks",
    )(me, inside, qs, state, place)
    return outs[0], list(outs[1:])


def route_kernel(me_ref, ids_ref, res_ref, gate_ref, *refs):
    outs, place_ref = refs[:-1], refs[-1]
    held = len(outs)
    tokens, width = res_ref.shape
    me = me_ref[0]
    ids = ids_ref[...]
    hits = [
        ((ids[0:1, :] == e) | (ids[1:2, :] == e)).astype(F32) for e in range(held)
    ]
    m = jnp.concatenate(hits, axis=0)
    upto = (iota((tokens, tokens), 0) <= iota((tokens, tokens), 1)).astype(BF16)
    rank = jnp.dot(m.astype(BF16), upto, preferred_element_type=F32) - 1.0
    slot = iota((CAP, tokens), 0).astype(F32)
    places = [
        jnp.where(rank[e : e + 1, :] == slot, m[e : e + 1, :], 0.0) for e in range(held)
    ]
    place = jnp.concatenate(places, axis=0)
    place_ref[...] = place
    for d in range(held):
        expert = lax.rem(me + d, held)
        mine = places[0]
        for e in range(1, held):
            mine = jnp.where(expert == e, places[e], mine)
        mine = mine.astype(BF16)
        outs[d][0:CAP, 0:width] = jnp.dot(
            mine, res_ref[...], preferred_element_type=F32
        ).astype(BF16)
        outs[d][CAP : 2 * CAP, 0:width] = jnp.dot(
            mine, gate_ref[...], preferred_element_type=F32
        ).astype(BF16)
        for n in range(2):
            outs[d][:, width + n * tokens : width + (n + 1) * tokens] = jnp.broadcast_to(
                ids[n : n + 1, :].astype(F32), (2 * CAP, tokens)
            ).astype(BF16)


def route_rows(me, ids, residual, out_gate, held):
    tokens, width = residual.shape
    whole = pl.BlockSpec(memory_space=pltpu.VMEM)
    piece = far((2 * CAP, width + 2 * tokens))
    outs = pl.pallas_call(
        route_kernel,
        out_shape=(piece,) * held + (jax.ShapeDtypeStruct((held * CAP, tokens), F32),),
        in_specs=[pl.BlockSpec(memory_space=pltpu.SMEM), whole, whole, whole],
        out_specs=(whole,) * (held + 1),
        compiler_params=params(),
        cost_estimate=cost(64 * tokens * width, 5 * tokens * width),
        name="route_rows",
    )(me, ids, residual, out_gate)
    return outs[:-1], outs[-1]


def by_source(me, pieces, j):
    count = len(pieces)
    out = pieces[0]
    for d in range(1, count):
        out = jnp.where(lax.rem(me + count - d, count) == j, pieces[d], out)
    return out


def place_kernel(me_ref, *refs):
    pieces, place_ref = refs[:-1], refs[-1]
    held = len(pieces)
    tokens = pieces[0].shape[1] // 2
    total = held * tokens
    me = me_ref[0]
    tables = [p[...].astype(F32) for p in pieces]
    ordered = [by_source(me, tables, j) for j in range(held)]
    first = jnp.concatenate([a[0:1, :tokens] for a in ordered], axis=1)
    second = jnp.concatenate([a[0:1, tokens:] for a in ordered], axis=1)
    m = jnp.concatenate(
        [((first == float(e)) | (second == float(e))).astype(F32) for e in range(held)], axis=0
    )
    before = iota((total, total), 0)
    after = iota((total, total), 1)
    upto = ((before <= after) & (before // tokens == after // tokens)).astype(BF16)
    rank = jnp.dot(m.astype(BF16), upto, preferred_element_type=F32) - 1.0
    rows = held * CAP
    r = iota((rows, total), 0)
    t = iota((rows, total), 1)
    chunk = r // (rows // 2)
    inner = r % (rows // 2)
    source = inner // (CAP // 2)
    slot = (chunk * (CAP // 2) + inner % (CAP // 2)).astype(F32)
    here = (t // tokens == source).astype(F32)
    for e in range(held):
        hit = jnp.where(rank[e : e + 1, :] == slot, m[e : e + 1, :] * here, 0.0)
        place_ref[e * rows : (e + 1) * rows, :] = hit.astype(BF16)


def place_rows(me, pieces, tokens):
    held = len(pieces)
    width = pieces[0].shape[1] - 2 * tokens
    at = width // (2 * tokens)
    return pl.pallas_call(
        place_kernel,
        grid=(1,),
        out_shape=jax.ShapeDtypeStruct((held * held * CAP, held * tokens), BF16),
        in_specs=[pl.BlockSpec(memory_space=pltpu.SMEM)]
        + [pl.BlockSpec((2 * CAP, 2 * tokens), lambda i: (0, at))] * held,
        out_specs=pl.BlockSpec((held * held * CAP, held * tokens), lambda i: (0, 0)),
        compiler_params=params(),
        cost_estimate=cost(1000000, 200000),
        name="place_rows",
    )(me, *pieces)


def gated(att, res, gate, attn_gain):
    norm = att * lax.rsqrt(jnp.mean(att * att, axis=-1, keepdims=True) + EPS) * attn_gain
    return (res + norm * jax.nn.sigmoid(gate)).astype(BF16)


def routed_norm_kernel(me_ref, att_ref, ag_ref, mg_ref, *refs):
    pieces, one_ref, two_ref = refs[:-2], refs[-2], refs[-1]
    sources, rows, part = att_ref.shape
    width = sources * part
    me = me_ref[0]
    att = jnp.concatenate([att_ref[s].astype(F32) for s in range(sources)], axis=1)
    tables = [p[...][:, :width].astype(F32) for p in pieces]
    ordered = [by_source(me, tables, j) for j in range(sources)]
    half = CAP // 2
    res = jnp.concatenate(
        [a[c * half : (c + 1) * half] for c in range(2) for a in ordered], axis=0
    )
    gate = jnp.concatenate(
        [a[CAP + c * half : CAP + (c + 1) * half] for c in range(2) for a in ordered], axis=0
    )
    hidden = gated(att, res, gate, ag_ref[...]).astype(F32)
    normed = (
        hidden * lax.rsqrt(jnp.mean(hidden * hidden, axis=-1, keepdims=True) + EPS) * mg_ref[...]
    )
    one = normed[: rows // 2].astype(BF16)
    for i in range(one_ref.shape[0]):
        one_ref[i] = one
    two_ref[...] = normed[rows // 2 :].astype(BF16)


def routed_norm(me, att, pieces, attn_gain, moe_gain, copies):
    sources, rows, part = att.shape
    width = sources * part
    whole = pl.BlockSpec(memory_space=pltpu.VMEM)
    return pl.pallas_call(
        routed_norm_kernel,
        out_shape=(far((copies, rows // 2, width)), far((rows // 2, width))),
        in_specs=[pl.BlockSpec(memory_space=pltpu.SMEM)] + [whole] * (3 + len(pieces)),
        out_specs=(whole, whole),
        compiler_params=params(),
        cost_estimate=cost(20 * rows * width, 20 * rows * width),
        name="routed_norm",
    )(me, att, attn_gain, moe_gain, *pieces)


def hidden_kernel(me_ref, res_ref, gate_ref, ag_ref, *refs):
    pieces, out_ref = refs[:-1], refs[-1]
    me = me_ref[0]
    tables = [p[...].astype(F32) for p in pieces]
    att = jnp.concatenate([by_source(me, tables, j) for j in range(len(pieces))], axis=1)
    out_ref[...] = gated(att, res_ref[...].astype(F32), gate_ref[...].astype(F32), ag_ref[...])


def hidden_rows(me, pieces, residual, out_gate, attn_gain, tile=32):
    rows, part = pieces[0].shape
    width = len(pieces) * part
    block = pl.BlockSpec((tile, width), lambda i: (i, 0))
    return pl.pallas_call(
        hidden_kernel,
        grid=(rows // tile,),
        out_shape=jax.ShapeDtypeStruct((rows, width), BF16),
        in_specs=[
            pl.BlockSpec(memory_space=pltpu.SMEM),
            block,
            block,
            pl.BlockSpec((1, width), lambda i: (0, 0)),
        ]
        + [pl.BlockSpec((tile, part), lambda i: (i, 0))] * len(pieces),
        out_specs=block,
        compiler_params=params(),
        cost_estimate=cost(20 * rows * width, 8 * rows * width),
        name="hidden_rows",
    )(me, residual, out_gate, attn_gain, *pieces)


def act_kernel(steps, streamed, wg_hbm, wu_hbm, *refs):
    count = len(refs) - 4
    xs, (act_ref, w_ref, x_ref, sem) = refs[:count], refs[count:]
    units, width = wg_hbm.shape
    nt = (((1,), (1,)), ((), ()))
    wide = width // steps
    copies = []
    for s in range(steps):
        cols = pl.ds(s * wide, wide)
        pairs = [(wg_hbm.at[:, cols], w_ref.at[0, :, cols]), (wu_hbm.at[:, cols], w_ref.at[1, :, cols])]
        if streamed:
            pairs.append((xs[0].at[:, cols], x_ref.at[:, cols]))
        copies.append(
            [pltpu.make_async_copy(a, b, sem.at[s, n]) for n, (a, b) in enumerate(pairs)]
        )
    for group in copies:
        for c in group:
            c.start()
    sources = [x_ref] if streamed else xs
    gate = up = None
    for s in range(steps):
        cols = slice(s * wide, (s + 1) * wide)
        for c in copies[s]:
            c.wait()
        x = [r[:, cols] for r in sources]
        x = x[0] if len(x) == 1 else jnp.concatenate(x, axis=0)
        g = lax.dot_general(w_ref[0, :, cols], x, nt, preferred_element_type=F32)
        u = lax.dot_general(w_ref[1, :, cols], x, nt, preferred_element_type=F32)
        gate = g if gate is None else gate + g
        up = u if up is None else up + u
    act_ref[...] = (gate * jax.nn.sigmoid(gate) * up).T.astype(BF16)


def expert_act(xs, w_gate, w_up, steps=6):
    count = sum(x.shape[0] for x in xs)
    units, width = w_gate.shape
    whole = pl.BlockSpec(memory_space=pltpu.VMEM)
    away = pl.BlockSpec(memory_space=pl.ANY)
    streamed = len(xs) == 1
    if streamed:
        xs = (hbm(xs[0]),)
    return pl.pallas_call(
        functools.partial(act_kernel, steps, streamed),
        out_shape=jax.ShapeDtypeStruct((count, units), BF16),
        in_specs=[away, away] + [away if streamed else whole] * len(xs),
        out_specs=whole,
        scratch_shapes=[
            pltpu.VMEM((2, units, width), BF16),
            pltpu.VMEM((count, width) if streamed else (16, HEAD_DIM), BF16),
            pltpu.SemaphoreType.DMA((steps, 3)),
        ],
        compiler_params=params(),
        cost_estimate=cost(4 * count * width * units, 4 * width * units + 2 * count * width),
        name="expert_act",
    )(hbm(w_gate), hbm(w_up), *xs)


def down_kernel(steps, mixed, core_ref, act_ref, wd_hbm, own_ref, other_ref, wd_ref, sem):
    chips, rows, width = own_ref.shape
    wide = width // steps
    act = act_ref[...]
    first = core_ref[0] == 0
    copies = []
    for s in range(steps):
        cols = pl.ds(s * wide, wide)
        copies.append(pltpu.make_async_copy(wd_hbm.at[:, cols], wd_ref.at[:, cols], sem.at[s]))
    for c in copies:
        c.start()
    for s in range(steps):
        cols = slice(s * wide, (s + 1) * wide)
        copies[s].wait()
        out = jnp.dot(act, wd_ref[:, cols], preferred_element_type=F32)
        if mixed:
            out = out.reshape(chips, 2, rows, wide)
            a, b = out[:, 0].astype(BF16), out[:, 1].astype(BF16)
            own_ref[:, :, cols] = jnp.where(first, a, b)
            other_ref[:, :, cols] = jnp.where(first, b, a)
        else:
            out = out.reshape(2, chips, rows, wide).astype(BF16)
            own_ref[:, :, cols] = out[0]
            other_ref[:, :, cols] = out[1]


def expert_down(core, act, w_down, mixed, steps=6):
    count, units = act.shape
    width = w_down.shape[1]
    rows = count // 32
    whole = pl.BlockSpec(memory_space=pltpu.VMEM)
    return pl.pallas_call(
        functools.partial(down_kernel, steps, mixed),
        out_shape=(jax.ShapeDtypeStruct((16, rows, width), BF16),) * 2,
        in_specs=[
            pl.BlockSpec(memory_space=pltpu.SMEM),
            whole,
            pl.BlockSpec(memory_space=pl.ANY),
        ],
        out_specs=(whole, whole),
        scratch_shapes=[pltpu.VMEM((units, width), BF16), pltpu.SemaphoreType.DMA((steps,))],
        compiler_params=params(),
        cost_estimate=cost(2 * count * width * units, 2 * width * units + 2 * count * width),
        name="expert_down",
    )(core, act, hbm(w_down))


def pair_kernel(a_ref, b_ref, out_ref):
    out_ref[...] = (a_ref[...].astype(F32) + b_ref[...].astype(F32)).astype(BF16)


def pair_sum(own, other, steps=4):
    chips, rows, width = own.shape
    wide = width // steps
    block = pl.BlockSpec((chips, rows, wide), lambda i: (0, 0, i))
    return pl.pallas_call(
        pair_kernel,
        grid=(steps,),
        out_shape=far((chips, rows, width)),
        in_specs=[block, block],
        out_specs=block,
        compiler_params=params(),
        cost_estimate=cost(chips * rows * width, 6 * chips * rows * width),
        name="pair_sum",
    )(own, other)


def chip_sum_kernel(one_ref, two_ref, out_ref):
    def total(ref):
        out = ref[0].astype(F32)
        for i in range(1, ref.shape[0]):
            out = out + ref[i].astype(F32)
        return out

    one, two = total(one_ref), total(two_ref)
    half = CAP // 2
    for j in range(out_ref.shape[0]):
        at = slice(j * half, (j + 1) * half)
        out_ref[j] = jnp.concatenate([one[at], two[at]], axis=0).astype(BF16)


def chip_sum(one, two, held, steps=4):
    chips, rows, width = one.shape
    wide = width // steps
    block = pl.BlockSpec((chips, rows, wide), lambda i: (0, 0, i))
    return pl.pallas_call(
        chip_sum_kernel,
        grid=(steps,),
        out_shape=far((held, CAP, width)),
        in_specs=[block, block],
        out_specs=pl.BlockSpec((held, CAP, wide), lambda i: (0, 0, i)),
        compiler_params=params(),
        cost_estimate=cost(2 * chips * rows * width, 4 * chips * rows * width),
        name="chip_sum",
    )(one, two)


def combine_kernel(place_ref, rows_ref, ids_ref, weights_ref, out_ref):
    held = rows_ref.shape[0]
    rows = jnp.concatenate([rows_ref[e].astype(F32) for e in range(held)], axis=0).astype(BF16)
    back = lax.dot_general(
        place_ref[...].astype(BF16), rows, (((0,), (0,)), ((), ())), preferred_element_type=F32
    )
    chosen = jnp.sum(
        jnp.where(ids_ref[...] < held, weights_ref[...], 0.0), axis=1, keepdims=True
    )
    out_ref[...] = (back * chosen).astype(BF16)


def combine_rows(place, rows, ids, weights):
    tokens = ids.shape[0]
    width = rows.shape[2]
    return pl.pallas_call(
        combine_kernel,
        out_shape=jax.ShapeDtypeStruct((tokens, width), BF16),
        compiler_params=params(),
        cost_estimate=cost(32 * tokens * width, 2 * tokens * width),
        name="combine_rows",
    )(place, rows, ids, weights)


def exchange(a, axis):
    return lax.all_to_all(a, axis, split_axis=0, concat_axis=0, tiled=True)


def shift(a, axis, by):
    n = lax.axis_size(axis)
    return lax.ppermute(a, axis, [(i, (i + by) % n) for i in range(n)])


def local(
    queries,
    key_vectors,
    values,
    log_decay,
    out_gate,
    residual,
    attn_gain,
    moe_gain,
    expert_ids,
    route_weights,
    w_gate,
    w_up,
    w_down,
):
    held = lax.axis_size("exp")
    rows, width = queries.shape
    heads = log_decay.shape[1]
    tokens = residual.shape[0]
    attn_gain = attn_gain.reshape(1, -1)
    moe_gain = moe_gain.reshape(1, -1)
    w_gate = jnp.swapaxes(w_gate, 1, 2)[0]
    w_up = jnp.swapaxes(w_up, 1, 2)[0]
    w_down = w_down[0]
    ids = expert_ids.T
    ld = log_decay.T
    me = lax.axis_index("exp").reshape(1)
    core = lax.axis_index("core").reshape(1)
    keep = lax.optimization_barrier
    chips = lax.axis_size("z") * lax.axis_size("x")

    cum, msg = local_states(hbm(key_vectors), hbm(values), ld)
    sent = exchange(msg, CTX)
    inside, qs = inside_blocks(hbm(queries), hbm(key_vectors), hbm(values), cum, ld)
    pieces, place_own = route_rows(me, ids, hbm(residual), hbm(out_gate), held)
    sent, inside, qs, pieces = keep((sent, inside, qs, pieces))
    prior = scan_blocks(sent, lax.axis_index(CTX))
    state = exchange(prior, CTX).reshape(heads, HEAD_DIM, HEAD_DIM)
    pieces = [pieces[0]] + [shift(pieces[d], "exp", d) for d in range(1, held)]
    place = place_rows(me, pieces, tokens)

    routed, attention = carried_blocks(me, inside, qs, state, place, held)
    routed = exchange(routed.reshape(held, held * CAP, width), "exp")
    one, two = routed_norm(me, routed, pieces, attn_gain, moe_gain, chips)

    attention, two = keep((attention, two))
    two = lax.all_gather(two, CTX, axis=0).reshape(32 * two.shape[0], two.shape[1])
    one = exchange(one, ("z", "x"))
    one = one.reshape(-1, one.shape[2])
    attention = [attention[0]] + [shift(attention[d], "exp", d) for d in range(1, held)]
    one, attention = keep((one, attention))

    act = expert_act((one, shift(one, "core", 1)), w_gate, w_up)
    own, other = expert_down(core, act, w_down, False)
    one = pair_sum(own, shift(other, "core", 1))
    _, two = keep((one, two))
    one = exchange(one, ("z", "x"))
    act = expert_act((two,), w_gate, w_up)
    one, act = keep((one, act))
    own, other = expert_down(core, act, w_down, True)
    two = exchange(pair_sum(own, shift(other, "core", 1)), ("z", "x"))
    hidden = hidden_rows(me, attention, hbm(residual), hbm(out_gate), attn_gain)
    back = exchange(chip_sum(one, two, held), "exp")
    moe_out = combine_rows(place_own, back, expert_ids, route_weights)
    return (hidden, moe_out)


def solution(mesh):
    cube = Mesh(mesh.devices.reshape(4, 4, 2, 4), ("z", "x", "core", "exp"))
    both = CTX + ("exp",)
    in_specs = (
        P(CTX, "exp"),
        P(CTX, "exp"),
        P(CTX, "exp"),
        P(CTX, "exp"),
        P(both, None),
        P(both, None),
        P(),
        P(),
        P(both, None),
        P(both, None),
        P("exp", None, CTX),
        P("exp", None, CTX),
        P("exp", CTX, None),
    )
    out_specs = (P(both, None), P(both, None))
    return jax.shard_map(local, mesh=cube, in_specs=in_specs, out_specs=out_specs, check_vma=False)
```

```python
import functools

import jax
import jax.numpy as jnp
from jax import lax
from jax.experimental import pallas as pl
from jax.experimental.pallas import tpu as pltpu
from jax.sharding import Mesh, PartitionSpec as P

HEAD_DIM = 128
CAP = 4
EPS = 1e-05
F32 = jnp.float32
BF16 = jnp.bfloat16
HIGHEST = lax.Precision.HIGHEST
CTX = ("z", "x", "core")
VMEM_LIMIT = 24 * 1024 * 1024


def iota(shape, dim):
    return lax.broadcasted_iota(jnp.int32, shape, dim)


def hbm(a):
    return pltpu.with_memory_space_constraint(a, pltpu.HBM)


def far(shape, dtype=BF16):
    return pltpu.HBM(shape, dtype)


def params(**kw):
    return pltpu.CompilerParams(vmem_limit_bytes=VMEM_LIMIT, **kw)


def cost(flops, bytes_accessed):
    return pl.CostEstimate(flops=flops, bytes_accessed=bytes_accessed, transcendentals=0)


def running_sum(ld, axis):
    rows = ld.shape[1]
    a, b = iota((rows, rows), 0), iota((rows, rows), 1)
    ones = (a >= b).astype(BF16)
    total = None
    rest = ld
    for _ in range(3):
        part = rest.astype(BF16)
        rest = rest - part.astype(F32)
        pair = (ones, part) if axis == 0 else (part, ones)
        term = lax.dot_general(*pair, (((1,), (1,)), ((), ())), preferred_element_type=F32)
        total = term if total is None else total + term
    return total


def spread(table, first, count, terms):
    n = table.shape[1]
    shape = (n, count * HEAD_DIM)
    pick = (iota(shape, 0) == first + iota(shape, 1) // HEAD_DIM).astype(BF16)
    total = None
    rest = table
    for _ in range(terms):
        part = rest.astype(BF16)
        rest = rest - part.astype(F32)
        term = jnp.dot(part, pick, preferred_element_type=F32)
        total = term if total is None else total + term
    return total


def state_kernel(group, k_ref, v_ref, ld_ref, cum_ref, msg_ref, fade_ref, decay_ref):
    heads, rows = ld_ref.shape
    per = heads * HEAD_DIM // 32
    parts = group * HEAD_DIM // per
    g = pl.program_id(0)

    @pl.when(g == 0)
    def _():
        cum = running_sum(ld_ref[...], 0)
        cum_ref[...] = cum
        final = cum[rows - 1 : rows, :]
        fade_ref[...] = jnp.exp(final - cum)
        decay_ref[...] = jnp.broadcast_to(jnp.exp(final), decay_ref.shape)

    fade = spread(fade_ref[...], g * group, group, 2)
    decay = spread(decay_ref[...], g * group, group, 2)
    row16 = iota((16, HEAD_DIM), 0)
    tiles = []
    for j in range(group):
        cols = slice(j * HEAD_DIM, (j + 1) * HEAD_DIM)
        wk = (k_ref[:, cols].astype(F32) * fade[:, cols]).astype(BF16)
        state = lax.dot_general(
            wk, v_ref[:, cols], (((0,), (0,)), ((), ())), preferred_element_type=F32
        ).astype(BF16)
        row = j * HEAD_DIM
        while row < (j + 1) * HEAD_DIM:
            part, at = row // per, row % per
            take = min(per - at, (j + 1) * HEAD_DIM - row)
            lo = row - j * HEAD_DIM
            msg_ref[part, at : at + take, :] = state[lo : lo + take, :]
            row += take
        whole = decay[:, cols]
        high = whole.astype(BF16).astype(F32)
        tiles.append((high, whole - high))
    for part in range(parts):
        first = per * part // HEAD_DIM
        last = (per * part + per - 1) // HEAD_DIM
        tile = jnp.where(
            row16 == 0,
            tiles[first][0],
            jnp.where(
                row16 == 1, tiles[first][1], jnp.where(row16 == 2, tiles[last][0], tiles[last][1])
            ),
        )
        msg_ref[part, per : per + 16, :] = tile.astype(BF16)


def local_states(k, v, ld, group=3):
    rows, width = k.shape
    heads = ld.shape[0]
    per = heads * HEAD_DIM // 32
    parts = group * HEAD_DIM // per
    block = pl.BlockSpec((rows, group * HEAD_DIM), lambda g: (0, g))
    return pl.pallas_call(
        functools.partial(state_kernel, group),
        grid=(heads // group,),
        out_shape=(
            jax.ShapeDtypeStruct((rows, heads), F32),
            far((32, per + 16, HEAD_DIM)),
        ),
        in_specs=[block, block, pl.BlockSpec((heads, rows), lambda g: (0, 0))],
        out_specs=(
            pl.BlockSpec((rows, heads), lambda g: (0, 0)),
            pl.BlockSpec((parts, per + 16, HEAD_DIM), lambda g: (g, 0, 0)),
        ),
        scratch_shapes=[pltpu.VMEM((rows, heads), F32), pltpu.VMEM((16, heads), F32)],
        compiler_params=params(),
        cost_estimate=cost(2 * rows * width * HEAD_DIM, 4 * rows * width),
        name="local_states",
    )(k, v, ld)


def scan_kernel(split_ref, in_ref, out_ref):
    parts, per, width = out_ref.shape
    first_rows = iota((per, width), 0) < split_ref[0]
    state = jnp.zeros((per, width), F32)
    for b in range(parts):
        out_ref[b, :, :] = state.astype(BF16)
        if b + 1 < parts:
            tail = in_ref[b, per : per + 16, :].astype(F32)
            d0 = tail[0:1, :] + tail[1:2, :]
            d1 = tail[2:3, :] + tail[3:4, :]
            decay = jnp.where(first_rows, d0, d1)
            state = decay * state + in_ref[b, 0:per, :].astype(F32)


def scan_blocks(msg, part):
    parts, tall, width = msg.shape
    per = tall - 16
    split = (HEAD_DIM - (per * part) % HEAD_DIM).astype(jnp.int32).reshape(1)
    return pl.pallas_call(
        scan_kernel,
        out_shape=far((parts, per, width)),
        in_specs=[
            pl.BlockSpec(memory_space=pltpu.SMEM),
            pl.BlockSpec(memory_space=pltpu.VMEM),
        ],
        out_specs=pl.BlockSpec(memory_space=pltpu.VMEM),
        compiler_params=params(),
        cost_estimate=cost(1000000, 1000000),
        name="scan_blocks",
    )(split, msg)


def inside_kernel(group, q_ref, k_ref, v_ref, cum_ref, ld_ref, inside_ref, qs_ref, cumt_ref):
    rows, heads = cum_ref.shape

    @pl.when(pl.program_id(0) == 0)
    def _():
        cumt_ref[...] = running_sum(ld_ref[...], 1)

    cum = spread(cum_ref[...], pl.program_id(0) * group, group, 3)
    size = 2 * HEAD_DIM
    causal = iota((size, size), 0) >= iota((size, size), 1)
    for j in range(group):
        h = pl.program_id(0) * group + j
        cols = slice(j * HEAD_DIM, (j + 1) * HEAD_DIM)
        col = cum[:, cols]
        row = cumt_ref[pl.ds(h, 1), :]
        q = q_ref[:, cols]
        k = k_ref[:, cols]
        v = v_ref[:, cols]
        qs_ref[:, cols] = (q.astype(F32) * jnp.exp(col)).astype(BF16)
        wide = jnp.concatenate([col, col], axis=1)
        total = None
        for lo in range(0, rows, size):
            hi = lo + size
            s = lax.dot_general(
                q[lo:], k[lo:hi], (((1,), (1,)), ((), ())), preferred_element_type=F32
            )
            decay = jnp.exp(jnp.minimum(wide[lo:] - row[:, lo:hi], 0.0))
            w = s * decay
            w = jnp.concatenate([jnp.where(causal, w[:size], 0.0), w[size:]], axis=0) if (
                hi < rows
            ) else jnp.where(causal, w, 0.0)
            part = jnp.dot(w.astype(BF16), v[lo:hi], preferred_element_type=F32)
            if total is None:
                total = part
            else:
                total = jnp.concatenate([total[:lo], total[lo:] + part], axis=0)
        inside_ref[:, cols] = total


def inside_blocks(q, k, v, cum, ld, group=3):
    rows, width = q.shape
    heads = cum.shape[1]
    block = pl.BlockSpec((rows, group * HEAD_DIM), lambda g: (0, g))
    return pl.pallas_call(
        functools.partial(inside_kernel, group),
        grid=(heads // group,),
        out_shape=(
            jax.ShapeDtypeStruct((rows, width), F32),
            far((rows, width)),
        ),
        in_specs=[
            block,
            block,
            block,
            pl.BlockSpec((rows, heads), lambda g: (0, 0)),
            pl.BlockSpec((heads, rows), lambda g: (0, 0)),
        ],
        out_specs=(block, block),
        scratch_shapes=[pltpu.VMEM((heads, rows), F32)],
        compiler_params=params(),
        cost_estimate=cost(4 * rows * rows * width, 12 * rows * width),
        name="inside_blocks",
    )(q, k, v, cum, ld)


def carried_kernel(group, me_ref, inside_ref, qs_ref, state_ref, place_ref, sel_ref, *refs):
    outs, att_ref = refs[:-1], refs[-1]
    held = len(outs)
    tokens = outs[0].shape[0]
    for j in range(group):
        cols = slice(j * HEAD_DIM, (j + 1) * HEAD_DIM)
        att_ref[:, cols] = (
            inside_ref[:, cols]
            + jnp.dot(qs_ref[:, cols], state_ref[j], preferred_element_type=F32)
        ).astype(BF16)
    sel_ref[...] = jnp.dot(
        place_ref[...], att_ref[...], preferred_element_type=F32
    ).astype(BF16)
    for d in range(held):
        at = pl.multiple_of(lax.rem(me_ref[0] + d, held) * tokens, tokens)
        outs[d][...] = att_ref[pl.ds(at, tokens), :]


def carried_blocks(me, inside, qs, state, place, held, group=3):
    rows, width = inside.shape
    heads = width // HEAD_DIM
    chosen = place.shape[0]
    wide = group * HEAD_DIM
    tokens = rows // held
    block = pl.BlockSpec((rows, wide), lambda g: (0, g))
    outs = pl.pallas_call(
        functools.partial(carried_kernel, group),
        grid=(heads // group,),
        out_shape=(far((chosen, width)),) + (far((tokens, width)),) * held,
        in_specs=[
            pl.BlockSpec(memory_space=pltpu.SMEM),
            block,
            block,
            pl.BlockSpec((group, HEAD_DIM, HEAD_DIM), lambda g: (g, 0, 0)),
            pl.BlockSpec((chosen, rows), lambda g: (0, 0)),
        ],
        out_specs=(pl.BlockSpec((chosen, wide), lambda g: (0, g)),)
        + (pl.BlockSpec((tokens, wide), lambda g: (0, g)),) * held,
        scratch_shapes=[pltpu.VMEM((rows, wide), BF16)],
        compiler_params=params(),
        cost_estimate=cost(4 * rows * width * HEAD_DIM, 8 * rows * width),
        name="carried_blocks",
    )(me, inside, qs, state, place)
    return outs[0], list(outs[1:])


def route_kernel(pieces, me_ref, ids_ref, res_hbm, gate_hbm, *refs):
    outs, (place_ref, res_ref, gate_ref, sem) = refs[:-4], refs[-4:]
    held = len(outs)
    size = res_ref.shape[0] // pieces
    copies = []
    for n, (a, b) in enumerate(((res_hbm, res_ref), (gate_hbm, gate_ref))):
        for i in range(pieces):
            at = pl.ds(i * size, size)
            copies.append(pltpu.make_async_copy(a.at[at], b.at[at], sem.at[n, i]))
    for c in copies:
        c.start()
    tokens, width = res_ref.shape
    me = me_ref[0]
    ids = ids_ref[...]
    hits = [
        ((ids[0:1, :] == e) | (ids[1:2, :] == e)).astype(F32) for e in range(held)
    ]
    m = jnp.concatenate(hits, axis=0)
    upto = (iota((tokens, tokens), 0) <= iota((tokens, tokens), 1)).astype(BF16)
    rank = jnp.dot(m.astype(BF16), upto, preferred_element_type=F32) - 1.0
    slot = iota((CAP, tokens), 0).astype(F32)
    places = [
        jnp.where(rank[e : e + 1, :] == slot, m[e : e + 1, :], 0.0) for e in range(held)
    ]
    place = jnp.concatenate(places, axis=0)
    place_ref[...] = place
    for c in copies:
        c.wait()
    for d in range(held):
        expert = lax.rem(me + d, held)
        mine = places[0]
        for e in range(1, held):
            mine = jnp.where(expert == e, places[e], mine)
        mine = mine.astype(BF16)
        outs[d][0:CAP, 0:width] = jnp.dot(
            mine, res_ref[...], preferred_element_type=F32
        ).astype(BF16)
        outs[d][CAP : 2 * CAP, 0:width] = jnp.dot(
            mine, gate_ref[...], preferred_element_type=F32
        ).astype(BF16)
        for n in range(2):
            outs[d][:, width + n * tokens : width + (n + 1) * tokens] = jnp.broadcast_to(
                ids[n : n + 1, :].astype(F32), (2 * CAP, tokens)
            ).astype(BF16)


def route_rows(me, ids, residual, out_gate, held, pieces=4):
    tokens, width = residual.shape
    whole = pl.BlockSpec(memory_space=pltpu.VMEM)
    away = pl.BlockSpec(memory_space=pl.ANY)
    piece = far((2 * CAP, width + 2 * tokens))
    outs = pl.pallas_call(
        functools.partial(route_kernel, pieces),
        out_shape=(piece,) * held + (jax.ShapeDtypeStruct((held * CAP, tokens), F32),),
        in_specs=[pl.BlockSpec(memory_space=pltpu.SMEM), whole, away, away],
        out_specs=(whole,) * (held + 1),
        scratch_shapes=[
            pltpu.VMEM((tokens, width), BF16),
            pltpu.VMEM((tokens, width), BF16),
            pltpu.SemaphoreType.DMA((2, pieces)),
        ],
        compiler_params=params(),
        cost_estimate=cost(64 * tokens * width, 5 * tokens * width),
        name="route_rows",
    )(me, ids, residual, out_gate)
    return outs[:-1], outs[-1]


def by_source(me, pieces, j):
    count = len(pieces)
    out = pieces[0]
    for d in range(1, count):
        out = jnp.where(lax.rem(me + count - d, count) == j, pieces[d], out)
    return out


def place_kernel(me_ref, *refs):
    pieces, place_ref = refs[:-1], refs[-1]
    held = len(pieces)
    tokens = pieces[0].shape[1] // 2
    total = held * tokens
    me = me_ref[0]
    tables = [p[...].astype(F32) for p in pieces]
    ordered = [by_source(me, tables, j) for j in range(held)]
    first = jnp.concatenate([a[0:1, :tokens] for a in ordered], axis=1)
    second = jnp.concatenate([a[0:1, tokens:] for a in ordered], axis=1)
    m = jnp.concatenate(
        [((first == float(e)) | (second == float(e))).astype(F32) for e in range(held)], axis=0
    )
    before = iota((total, total), 0)
    after = iota((total, total), 1)
    upto = ((before <= after) & (before // tokens == after // tokens)).astype(BF16)
    rank = jnp.dot(m.astype(BF16), upto, preferred_element_type=F32) - 1.0
    rows = held * CAP
    r = iota((rows, total), 0)
    t = iota((rows, total), 1)
    chunk = r // (rows // 2)
    inner = r % (rows // 2)
    source = inner // (CAP // 2)
    slot = (chunk * (CAP // 2) + inner % (CAP // 2)).astype(F32)
    here = (t // tokens == source).astype(F32)
    for e in range(held):
        hit = jnp.where(rank[e : e + 1, :] == slot, m[e : e + 1, :] * here, 0.0)
        place_ref[e * rows : (e + 1) * rows, :] = hit.astype(BF16)


def place_rows(me, pieces, tokens):
    held = len(pieces)
    width = pieces[0].shape[1] - 2 * tokens
    at = width // (2 * tokens)
    return pl.pallas_call(
        place_kernel,
        grid=(1,),
        out_shape=far((held * held * CAP, held * tokens)),
        in_specs=[pl.BlockSpec(memory_space=pltpu.SMEM)]
        + [pl.BlockSpec((2 * CAP, 2 * tokens), lambda i: (0, at))] * held,
        out_specs=pl.BlockSpec((held * held * CAP, held * tokens), lambda i: (0, 0)),
        compiler_params=params(),
        cost_estimate=cost(1000000, 200000),
        name="place_rows",
    )(me, *pieces)


def gated(att, res, gate, attn_gain):
    norm = att * lax.rsqrt(jnp.mean(att * att, axis=-1, keepdims=True) + EPS) * attn_gain
    return (res + norm * jax.nn.sigmoid(gate)).astype(BF16)


def routed_norm_kernel(me_ref, att_ref, ag_ref, mg_ref, *refs):
    pieces, one_ref, two_ref = refs[:-2], refs[-2], refs[-1]
    sources, rows, part = att_ref.shape
    width = sources * part
    me = me_ref[0]
    att = jnp.concatenate([att_ref[s].astype(F32) for s in range(sources)], axis=1)
    tables = [p[...][:, :width].astype(F32) for p in pieces]
    ordered = [by_source(me, tables, j) for j in range(sources)]
    half = CAP // 2
    res = jnp.concatenate(
        [a[c * half : (c + 1) * half] for c in range(2) for a in ordered], axis=0
    )
    gate = jnp.concatenate(
        [a[CAP + c * half : CAP + (c + 1) * half] for c in range(2) for a in ordered], axis=0
    )
    hidden = gated(att, res, gate, ag_ref[...]).astype(F32)
    normed = (
        hidden * lax.rsqrt(jnp.mean(hidden * hidden, axis=-1, keepdims=True) + EPS) * mg_ref[...]
    )
    one = normed[: rows // 2].astype(BF16)
    for i in range(one_ref.shape[0]):
        one_ref[i] = one
    two_ref[...] = normed[rows // 2 :].astype(BF16)


def routed_norm(me, att, pieces, attn_gain, moe_gain, copies):
    sources, rows, part = att.shape
    width = sources * part
    whole = pl.BlockSpec(memory_space=pltpu.VMEM)
    return pl.pallas_call(
        routed_norm_kernel,
        out_shape=(far((copies, rows // 2, width)), far((rows // 2, width))),
        in_specs=[pl.BlockSpec(memory_space=pltpu.SMEM)] + [whole] * (3 + len(pieces)),
        out_specs=(whole, whole),
        compiler_params=params(),
        cost_estimate=cost(20 * rows * width, 20 * rows * width),
        name="routed_norm",
    )(me, att, attn_gain, moe_gain, *pieces)


def hidden_kernel(me_ref, res_ref, gate_ref, ag_ref, *refs):
    pieces, out_ref = refs[:-1], refs[-1]
    me = me_ref[0]
    tables = [p[...].astype(F32) for p in pieces]
    att = jnp.concatenate([by_source(me, tables, j) for j in range(len(pieces))], axis=1)
    out_ref[...] = gated(att, res_ref[...].astype(F32), gate_ref[...].astype(F32), ag_ref[...])


def hidden_rows(me, pieces, residual, out_gate, attn_gain, tile=32):
    rows, part = pieces[0].shape
    width = len(pieces) * part
    block = pl.BlockSpec((tile, width), lambda i: (i, 0))
    return pl.pallas_call(
        hidden_kernel,
        grid=(rows // tile,),
        out_shape=jax.ShapeDtypeStruct((rows, width), BF16),
        in_specs=[
            pl.BlockSpec(memory_space=pltpu.SMEM),
            block,
            block,
            pl.BlockSpec((1, width), lambda i: (0, 0)),
        ]
        + [pl.BlockSpec((tile, part), lambda i: (i, 0))] * len(pieces),
        out_specs=block,
        compiler_params=params(),
        cost_estimate=cost(20 * rows * width, 8 * rows * width),
        name="hidden_rows",
    )(me, residual, out_gate, attn_gain, *pieces)


def act_kernel(steps, streamed, wg_hbm, wu_hbm, *refs):
    count = len(refs) - 4
    xs, (act_ref, w_ref, x_ref, sem) = refs[:count], refs[count:]
    units, width = wg_hbm.shape
    nt = (((1,), (1,)), ((), ()))
    wide = width // steps
    copies = []
    for s in range(steps):
        cols = pl.ds(s * wide, wide)
        pairs = [(wg_hbm.at[:, cols], w_ref.at[0, :, cols]), (wu_hbm.at[:, cols], w_ref.at[1, :, cols])]
        if streamed:
            pairs.append((xs[0].at[:, cols], x_ref.at[:, cols]))
        copies.append(
            [pltpu.make_async_copy(a, b, sem.at[s, n]) for n, (a, b) in enumerate(pairs)]
        )
    for group in copies:
        for c in group:
            c.start()
    sources = [x_ref] if streamed else xs
    gate = up = None
    for s in range(steps):
        cols = slice(s * wide, (s + 1) * wide)
        for c in copies[s]:
            c.wait()
        x = [r[:, cols] for r in sources]
        x = x[0] if len(x) == 1 else jnp.concatenate(x, axis=0)
        g = lax.dot_general(w_ref[0, :, cols], x, nt, preferred_element_type=F32)
        u = lax.dot_general(w_ref[1, :, cols], x, nt, preferred_element_type=F32)
        gate = g if gate is None else gate + g
        up = u if up is None else up + u
    act_ref[...] = (gate * jax.nn.sigmoid(gate) * up).T.astype(BF16)


def expert_act(xs, w_gate, w_up, steps=6):
    count = sum(x.shape[0] for x in xs)
    units, width = w_gate.shape
    whole = pl.BlockSpec(memory_space=pltpu.VMEM)
    away = pl.BlockSpec(memory_space=pl.ANY)
    streamed = len(xs) == 1
    if streamed:
        xs = (hbm(xs[0]),)
    return pl.pallas_call(
        functools.partial(act_kernel, steps, streamed),
        out_shape=jax.ShapeDtypeStruct((count, units), BF16),
        in_specs=[away, away] + [away if streamed else whole] * len(xs),
        out_specs=whole,
        scratch_shapes=[
            pltpu.VMEM((2, units, width), BF16),
            pltpu.VMEM((count, width) if streamed else (16, HEAD_DIM), BF16),
            pltpu.SemaphoreType.DMA((steps, 3)),
        ],
        compiler_params=params(),
        cost_estimate=cost(4 * count * width * units, 4 * width * units + 2 * count * width),
        name="expert_act",
    )(hbm(w_gate), hbm(w_up), *xs)


def down_kernel(steps, mixed, core_ref, act_ref, wd_hbm, own_ref, other_ref, wd_ref, sem):
    chips, rows, width = own_ref.shape
    wide = width // steps
    act = act_ref[...]
    first = core_ref[0] == 0
    copies = []
    for s in range(steps):
        cols = pl.ds(s * wide, wide)
        copies.append(pltpu.make_async_copy(wd_hbm.at[:, cols], wd_ref.at[:, cols], sem.at[s]))
    for c in copies:
        c.start()
    for s in range(steps):
        cols = slice(s * wide, (s + 1) * wide)
        copies[s].wait()
        out = jnp.dot(act, wd_ref[:, cols], preferred_element_type=F32)
        if mixed:
            out = out.reshape(chips, 2, rows, wide)
            a, b = out[:, 0].astype(BF16), out[:, 1].astype(BF16)
            own_ref[:, :, cols] = jnp.where(first, a, b)
            other_ref[:, :, cols] = jnp.where(first, b, a)
        else:
            out = out.reshape(2, chips, rows, wide).astype(BF16)
            own_ref[:, :, cols] = out[0]
            other_ref[:, :, cols] = out[1]


def expert_down(core, act, w_down, mixed, steps=6):
    count, units = act.shape
    width = w_down.shape[1]
    rows = count // 32
    whole = pl.BlockSpec(memory_space=pltpu.VMEM)
    return pl.pallas_call(
        functools.partial(down_kernel, steps, mixed),
        out_shape=(jax.ShapeDtypeStruct((16, rows, width), BF16),) * 2,
        in_specs=[
            pl.BlockSpec(memory_space=pltpu.SMEM),
            whole,
            pl.BlockSpec(memory_space=pl.ANY),
        ],
        out_specs=(whole, whole),
        scratch_shapes=[pltpu.VMEM((units, width), BF16), pltpu.SemaphoreType.DMA((steps,))],
        compiler_params=params(),
        cost_estimate=cost(2 * count * width * units, 2 * width * units + 2 * count * width),
        name="expert_down",
    )(core, act, hbm(w_down))


def pair_kernel(a_ref, b_ref, out_ref):
    out_ref[...] = (a_ref[...].astype(F32) + b_ref[...].astype(F32)).astype(BF16)


def pair_sum(own, other, steps=4):
    chips, rows, width = own.shape
    wide = width // steps
    block = pl.BlockSpec((chips, rows, wide), lambda i: (0, 0, i))
    return pl.pallas_call(
        pair_kernel,
        grid=(steps,),
        out_shape=far((chips, rows, width)),
        in_specs=[block, block],
        out_specs=block,
        compiler_params=params(),
        cost_estimate=cost(chips * rows * width, 6 * chips * rows * width),
        name="pair_sum",
    )(own, other)


def chip_sum_kernel(one_ref, two_ref, out_ref):
    def total(ref):
        out = ref[0].astype(F32)
        for i in range(1, ref.shape[0]):
            out = out + ref[i].astype(F32)
        return out

    one, two = total(one_ref), total(two_ref)
    half = CAP // 2
    for j in range(out_ref.shape[0]):
        at = slice(j * half, (j + 1) * half)
        out_ref[j] = jnp.concatenate([one[at], two[at]], axis=0).astype(BF16)


def chip_sum(one, two, held, steps=4):
    chips, rows, width = one.shape
    wide = width // steps
    block = pl.BlockSpec((chips, rows, wide), lambda i: (0, 0, i))
    return pl.pallas_call(
        chip_sum_kernel,
        grid=(steps,),
        out_shape=far((held, CAP, width)),
        in_specs=[block, block],
        out_specs=pl.BlockSpec((held, CAP, wide), lambda i: (0, 0, i)),
        compiler_params=params(),
        cost_estimate=cost(2 * chips * rows * width, 4 * chips * rows * width),
        name="chip_sum",
    )(one, two)


def combine_kernel(place_ref, rows_ref, ids_ref, weights_ref, out_ref):
    held = rows_ref.shape[0]
    rows = jnp.concatenate([rows_ref[e].astype(F32) for e in range(held)], axis=0).astype(BF16)
    back = lax.dot_general(
        place_ref[...].astype(BF16), rows, (((0,), (0,)), ((), ())), preferred_element_type=F32
    )
    chosen = jnp.sum(
        jnp.where(ids_ref[...] < held, weights_ref[...], 0.0), axis=1, keepdims=True
    )
    out_ref[...] = (back * chosen).astype(BF16)


def combine_rows(place, rows, ids, weights):
    tokens = ids.shape[0]
    width = rows.shape[2]
    return pl.pallas_call(
        combine_kernel,
        out_shape=jax.ShapeDtypeStruct((tokens, width), BF16),
        compiler_params=params(),
        cost_estimate=cost(32 * tokens * width, 2 * tokens * width),
        name="combine_rows",
    )(place, rows, ids, weights)


def exchange(a, axis):
    return lax.all_to_all(a, axis, split_axis=0, concat_axis=0, tiled=True)


def shift(a, axis, by):
    n = lax.axis_size(axis)
    return lax.ppermute(a, axis, [(i, (i + by) % n) for i in range(n)])


def local(
    queries,
    key_vectors,
    values,
    log_decay,
    out_gate,
    residual,
    attn_gain,
    moe_gain,
    expert_ids,
    route_weights,
    w_gate,
    w_up,
    w_down,
):
    held = lax.axis_size("exp")
    rows, width = queries.shape
    heads = log_decay.shape[1]
    tokens = residual.shape[0]
    attn_gain = attn_gain.reshape(1, -1)
    moe_gain = moe_gain.reshape(1, -1)
    w_gate = jnp.swapaxes(w_gate, 1, 2)[0]
    w_up = jnp.swapaxes(w_up, 1, 2)[0]
    w_down = w_down[0]
    ids = expert_ids.T
    ld = hbm(log_decay.T)
    me = lax.axis_index("exp").reshape(1)
    core = lax.axis_index("core").reshape(1)
    keep = lax.optimization_barrier
    chips = lax.axis_size("z") * lax.axis_size("x")

    cum, msg = local_states(hbm(key_vectors), hbm(values), ld)
    sent = exchange(msg, CTX)
    inside, qs = inside_blocks(hbm(queries), hbm(key_vectors), hbm(values), cum, ld)
    pieces, place_own = route_rows(me, ids, hbm(residual), hbm(out_gate), held)
    sent, inside, qs, pieces = keep((sent, inside, qs, pieces))
    prior = scan_blocks(hbm(sent), lax.axis_index(CTX))
    state = exchange(prior, CTX).reshape(heads, HEAD_DIM, HEAD_DIM)
    pieces = [pieces[0]] + [shift(pieces[d], "exp", d) for d in range(1, held)]
    pieces = [hbm(a) for a in pieces]
    place = place_rows(me, pieces, tokens)

    routed, attention = carried_blocks(me, inside, hbm(qs), state, hbm(place), held)
    routed = exchange(routed.reshape(held, held * CAP, width), "exp")
    one, two = routed_norm(me, routed, pieces, attn_gain, moe_gain, chips)

    attention, two = keep((attention, two))
    two = lax.all_gather(two, CTX, axis=0).reshape(32 * two.shape[0], two.shape[1])
    one = exchange(one, ("z", "x"))
    one = one.reshape(-1, one.shape[2])
    attention = [attention[0]] + [shift(attention[d], "exp", d) for d in range(1, held)]
    one, attention = keep((one, attention))

    act = expert_act((one, shift(one, "core", 1)), w_gate, w_up)
    own, other = expert_down(core, act, w_down, False)
    one = pair_sum(own, shift(other, "core", 1))
    _, two = keep((one, two))
    one = exchange(one, ("z", "x"))
    act = expert_act((two,), w_gate, w_up)
    own, other = expert_down(core, act, w_down, True)
    one, other = keep((one, other))
    two = exchange(pair_sum(own, shift(other, "core", 1)), ("z", "x"))
    hidden = hidden_rows(me, attention, hbm(residual), hbm(out_gate), attn_gain)
    back = exchange(chip_sum(one, two, held), "exp")
    moe_out = combine_rows(place_own, back, expert_ids, route_weights)
    return (hidden, moe_out)


def solution(mesh):
    cube = Mesh(mesh.devices.reshape(4, 4, 2, 4), ("z", "x", "core", "exp"))
    both = CTX + ("exp",)
    in_specs = (
        P(CTX, "exp"),
        P(CTX, "exp"),
        P(CTX, "exp"),
        P(CTX, "exp"),
        P(both, None),
        P(both, None),
        P(),
        P(),
        P(both, None),
        P(both, None),
        P("exp", None, CTX),
        P("exp", None, CTX),
        P("exp", CTX, None),
    )
    out_specs = (P(both, None), P(both, None))
    return jax.shard_map(local, mesh=cube, in_specs=in_specs, out_specs=out_specs, check_vma=False)
```

```python
import functools

import jax
import jax.numpy as jnp
from jax import lax
from jax.experimental import pallas as pl
from jax.experimental.pallas import tpu as pltpu
from jax.sharding import Mesh, PartitionSpec as P

HEAD_DIM = 128
CAP = 4
EPS = 1e-05
F32 = jnp.float32
BF16 = jnp.bfloat16
HIGHEST = lax.Precision.HIGHEST
CTX = ("z", "x", "core")
VMEM_LIMIT = 24 * 1024 * 1024


def iota(shape, dim):
    return lax.broadcasted_iota(jnp.int32, shape, dim)


def hbm(a):
    return pltpu.with_memory_space_constraint(a, pltpu.HBM)


def far(shape, dtype=BF16):
    return pltpu.HBM(shape, dtype)


def params(**kw):
    return pltpu.CompilerParams(vmem_limit_bytes=VMEM_LIMIT, **kw)


def cost(flops, bytes_accessed):
    return pl.CostEstimate(flops=flops, bytes_accessed=bytes_accessed, transcendentals=0)


def running_sum(ld, axis):
    rows = ld.shape[1]
    a, b = iota((rows, rows), 0), iota((rows, rows), 1)
    ones = (a >= b).astype(BF16)
    total = None
    rest = ld
    for _ in range(3):
        part = rest.astype(BF16)
        rest = rest - part.astype(F32)
        pair = (ones, part) if axis == 0 else (part, ones)
        term = lax.dot_general(*pair, (((1,), (1,)), ((), ())), preferred_element_type=F32)
        total = term if total is None else total + term
    return total


def spread(table, first, count, terms):
    n = table.shape[1]
    shape = (n, count * HEAD_DIM)
    pick = (iota(shape, 0) == first + iota(shape, 1) // HEAD_DIM).astype(BF16)
    total = None
    rest = table
    for _ in range(terms):
        part = rest.astype(BF16)
        rest = rest - part.astype(F32)
        term = jnp.dot(part, pick, preferred_element_type=F32)
        total = term if total is None else total + term
    return total


def state_kernel(group, k_ref, v_ref, ld_ref, cum_ref, msg_ref, fade_ref, decay_ref):
    heads, rows = ld_ref.shape
    per = heads * HEAD_DIM // 32
    parts = group * HEAD_DIM // per
    g = pl.program_id(0)

    @pl.when(g == 0)
    def _():
        cum = running_sum(ld_ref[...], 0)
        cum_ref[...] = cum
        final = cum[rows - 1 : rows, :]
        fade_ref[...] = jnp.exp(final - cum)
        decay_ref[...] = jnp.broadcast_to(jnp.exp(final), decay_ref.shape)

    fade = spread(fade_ref[...], g * group, group, 2)
    decay = spread(decay_ref[...], g * group, group, 2)
    row16 = iota((16, HEAD_DIM), 0)
    tiles = []
    for j in range(group):
        cols = slice(j * HEAD_DIM, (j + 1) * HEAD_DIM)
        wk = (k_ref[:, cols].astype(F32) * fade[:, cols]).astype(BF16)
        state = lax.dot_general(
            wk, v_ref[:, cols], (((0,), (0,)), ((), ())), preferred_element_type=F32
        ).astype(BF16)
        row = j * HEAD_DIM
        while row < (j + 1) * HEAD_DIM:
            part, at = row // per, row % per
            take = min(per - at, (j + 1) * HEAD_DIM - row)
            lo = row - j * HEAD_DIM
            msg_ref[part, at : at + take, :] = state[lo : lo + take, :]
            row += take
        whole = decay[:, cols]
        high = whole.astype(BF16).astype(F32)
        tiles.append((high, whole - high))
    for part in range(parts):
        first = per * part // HEAD_DIM
        last = (per * part + per - 1) // HEAD_DIM
        tile = jnp.where(
            row16 == 0,
            tiles[first][0],
            jnp.where(
                row16 == 1, tiles[first][1], jnp.where(row16 == 2, tiles[last][0], tiles[last][1])
            ),
        )
        msg_ref[part, per : per + 16, :] = tile.astype(BF16)


def local_states(k, v, ld, group=3):
    rows, width = k.shape
    heads = ld.shape[0]
    per = heads * HEAD_DIM // 32
    parts = group * HEAD_DIM // per
    block = pl.BlockSpec((rows, group * HEAD_DIM), lambda g: (0, g))
    return pl.pallas_call(
        functools.partial(state_kernel, group),
        grid=(heads // group,),
        out_shape=(
            jax.ShapeDtypeStruct((rows, heads), F32),
            far((32, per + 16, HEAD_DIM)),
        ),
        in_specs=[block, block, pl.BlockSpec((heads, rows), lambda g: (0, 0))],
        out_specs=(
            pl.BlockSpec((rows, heads), lambda g: (0, 0)),
            pl.BlockSpec((parts, per + 16, HEAD_DIM), lambda g: (g, 0, 0)),
        ),
        scratch_shapes=[pltpu.VMEM((rows, heads), F32), pltpu.VMEM((16, heads), F32)],
        compiler_params=params(),
        cost_estimate=cost(2 * rows * width * HEAD_DIM, 4 * rows * width),
        name="local_states",
    )(k, v, ld)


def scan_kernel(split_ref, in_ref, out_ref):
    parts, per, width = out_ref.shape
    first_rows = iota((per, width), 0) < split_ref[0]
    state = jnp.zeros((per, width), F32)
    for b in range(parts):
        out_ref[b, :, :] = state.astype(BF16)
        if b + 1 < parts:
            tail = in_ref[b, per : per + 16, :].astype(F32)
            d0 = tail[0:1, :] + tail[1:2, :]
            d1 = tail[2:3, :] + tail[3:4, :]
            decay = jnp.where(first_rows, d0, d1)
            state = decay * state + in_ref[b, 0:per, :].astype(F32)


def scan_blocks(msg, part):
    parts, tall, width = msg.shape
    per = tall - 16
    split = (HEAD_DIM - (per * part) % HEAD_DIM).astype(jnp.int32).reshape(1)
    return pl.pallas_call(
        scan_kernel,
        out_shape=far((parts, per, width)),
        in_specs=[
            pl.BlockSpec(memory_space=pltpu.SMEM),
            pl.BlockSpec(memory_space=pltpu.VMEM),
        ],
        out_specs=pl.BlockSpec(memory_space=pltpu.VMEM),
        compiler_params=params(),
        cost_estimate=cost(1000000, 1000000),
        name="scan_blocks",
    )(split, msg)


def inside_kernel(group, q_ref, k_ref, v_ref, cum_ref, ld_ref, inside_ref, qs_ref, cumt_ref):
    rows, heads = cum_ref.shape

    @pl.when(pl.program_id(0) == 0)
    def _():
        cumt_ref[...] = running_sum(ld_ref[...], 1)

    cum = spread(cum_ref[...], pl.program_id(0) * group, group, 3)
    size = 2 * HEAD_DIM
    causal = iota((size, size), 0) >= iota((size, size), 1)
    for j in range(group):
        h = pl.program_id(0) * group + j
        cols = slice(j * HEAD_DIM, (j + 1) * HEAD_DIM)
        col = cum[:, cols]
        row = cumt_ref[pl.ds(h, 1), :]
        q = q_ref[:, cols]
        k = k_ref[:, cols]
        v = v_ref[:, cols]
        qs_ref[:, cols] = (q.astype(F32) * jnp.exp(col)).astype(BF16)
        wide = jnp.concatenate([col, col], axis=1)
        total = None
        for lo in range(0, rows, size):
            hi = lo + size
            s = lax.dot_general(
                q[lo:], k[lo:hi], (((1,), (1,)), ((), ())), preferred_element_type=F32
            )
            decay = jnp.exp(jnp.minimum(wide[lo:] - row[:, lo:hi], 0.0))
            w = s * decay
            w = jnp.concatenate([jnp.where(causal, w[:size], 0.0), w[size:]], axis=0) if (
                hi < rows
            ) else jnp.where(causal, w, 0.0)
            part = jnp.dot(w.astype(BF16), v[lo:hi], preferred_element_type=F32)
            if total is None:
                total = part
            else:
                total = jnp.concatenate([total[:lo], total[lo:] + part], axis=0)
        inside_ref[:, cols] = total


def inside_blocks(q, k, v, cum, ld, group=3):
    rows, width = q.shape
    heads = cum.shape[1]
    block = pl.BlockSpec((rows, group * HEAD_DIM), lambda g: (0, g))
    return pl.pallas_call(
        functools.partial(inside_kernel, group),
        grid=(heads // group,),
        out_shape=(
            jax.ShapeDtypeStruct((rows, width), F32),
            far((rows, width)),
        ),
        in_specs=[
            block,
            block,
            block,
            pl.BlockSpec((rows, heads), lambda g: (0, 0)),
            pl.BlockSpec((heads, rows), lambda g: (0, 0)),
        ],
        out_specs=(block, block),
        scratch_shapes=[pltpu.VMEM((heads, rows), F32)],
        compiler_params=params(),
        cost_estimate=cost(4 * rows * rows * width, 12 * rows * width),
        name="inside_blocks",
    )(q, k, v, cum, ld)


def carried_kernel(group, me_ref, inside_ref, qs_ref, state_ref, place_ref, sel_ref, *refs):
    outs, att_ref = refs[:-1], refs[-1]
    held = len(outs)
    tokens = outs[0].shape[0]
    for j in range(group):
        cols = slice(j * HEAD_DIM, (j + 1) * HEAD_DIM)
        att_ref[:, cols] = (
            inside_ref[:, cols]
            + jnp.dot(qs_ref[:, cols], state_ref[j], preferred_element_type=F32)
        ).astype(BF16)
    sel_ref[...] = jnp.dot(
        place_ref[...], att_ref[...], preferred_element_type=F32
    ).astype(BF16)
    for d in range(held):
        at = pl.multiple_of(lax.rem(me_ref[0] + d, held) * tokens, tokens)
        outs[d][...] = att_ref[pl.ds(at, tokens), :]


def carried_blocks(me, inside, qs, state, place, held, group=3):
    rows, width = inside.shape
    heads = width // HEAD_DIM
    chosen = place.shape[0]
    wide = group * HEAD_DIM
    tokens = rows // held
    block = pl.BlockSpec((rows, wide), lambda g: (0, g))
    outs = pl.pallas_call(
        functools.partial(carried_kernel, group),
        grid=(heads // group,),
        out_shape=(far((chosen, width)),) + (far((tokens, width)),) * held,
        in_specs=[
            pl.BlockSpec(memory_space=pltpu.SMEM),
            block,
            block,
            pl.BlockSpec((group, HEAD_DIM, HEAD_DIM), lambda g: (g, 0, 0)),
            pl.BlockSpec((chosen, rows), lambda g: (0, 0)),
        ],
        out_specs=(pl.BlockSpec((chosen, wide), lambda g: (0, g)),)
        + (pl.BlockSpec((tokens, wide), lambda g: (0, g)),) * held,
        scratch_shapes=[pltpu.VMEM((rows, wide), BF16)],
        compiler_params=params(),
        cost_estimate=cost(4 * rows * width * HEAD_DIM, 8 * rows * width),
        name="carried_blocks",
    )(me, inside, qs, state, place)
    return outs[0], list(outs[1:])


def route_kernel(pieces, me_ref, ids_ref, res_hbm, gate_hbm, *refs):
    outs, (place_ref, res_ref, gate_ref, sem) = refs[:-4], refs[-4:]
    held = len(outs)
    size = res_ref.shape[0] // pieces
    copies = []
    for n, (a, b) in enumerate(((res_hbm, res_ref), (gate_hbm, gate_ref))):
        for i in range(pieces):
            at = pl.ds(i * size, size)
            copies.append(pltpu.make_async_copy(a.at[at], b.at[at], sem.at[n, i]))
    for c in copies:
        c.start()
    tokens, width = res_ref.shape
    me = me_ref[0]
    ids = ids_ref[...]
    hits = [
        ((ids[0:1, :] == e) | (ids[1:2, :] == e)).astype(F32) for e in range(held)
    ]
    m = jnp.concatenate(hits, axis=0)
    upto = (iota((tokens, tokens), 0) <= iota((tokens, tokens), 1)).astype(BF16)
    rank = jnp.dot(m.astype(BF16), upto, preferred_element_type=F32) - 1.0
    slot = iota((CAP, tokens), 0).astype(F32)
    places = [
        jnp.where(rank[e : e + 1, :] == slot, m[e : e + 1, :], 0.0) for e in range(held)
    ]
    place = jnp.concatenate(places, axis=0)
    place_ref[...] = place
    for c in copies:
        c.wait()
    for d in range(held):
        expert = lax.rem(me + d, held)
        mine = places[0]
        for e in range(1, held):
            mine = jnp.where(expert == e, places[e], mine)
        mine = mine.astype(BF16)
        outs[d][0:CAP, 0:width] = jnp.dot(
            mine, res_ref[...], preferred_element_type=F32
        ).astype(BF16)
        outs[d][CAP : 2 * CAP, 0:width] = jnp.dot(
            mine, gate_ref[...], preferred_element_type=F32
        ).astype(BF16)
        for n in range(2):
            outs[d][:, width + n * tokens : width + (n + 1) * tokens] = jnp.broadcast_to(
                ids[n : n + 1, :].astype(F32), (2 * CAP, tokens)
            ).astype(BF16)


def route_rows(me, ids, residual, out_gate, held, pieces=4):
    tokens, width = residual.shape
    whole = pl.BlockSpec(memory_space=pltpu.VMEM)
    away = pl.BlockSpec(memory_space=pl.ANY)
    piece = far((2 * CAP, width + 2 * tokens))
    outs = pl.pallas_call(
        functools.partial(route_kernel, pieces),
        out_shape=(piece,) * held + (jax.ShapeDtypeStruct((held * CAP, tokens), F32),),
        in_specs=[pl.BlockSpec(memory_space=pltpu.SMEM), whole, away, away],
        out_specs=(whole,) * (held + 1),
        scratch_shapes=[
            pltpu.VMEM((tokens, width), BF16),
            pltpu.VMEM((tokens, width), BF16),
            pltpu.SemaphoreType.DMA((2, pieces)),
        ],
        compiler_params=params(),
        cost_estimate=cost(64 * tokens * width, 5 * tokens * width),
        name="route_rows",
    )(me, ids, residual, out_gate)
    return outs[:-1], outs[-1]


def by_source(me, pieces, j):
    count = len(pieces)
    out = pieces[0]
    for d in range(1, count):
        out = jnp.where(lax.rem(me + count - d, count) == j, pieces[d], out)
    return out


def place_kernel(me_ref, *refs):
    pieces, place_ref = refs[:-1], refs[-1]
    held = len(pieces)
    tokens = pieces[0].shape[1] // 2
    total = held * tokens
    me = me_ref[0]
    tables = [p[...].astype(F32) for p in pieces]
    ordered = [by_source(me, tables, j) for j in range(held)]
    first = jnp.concatenate([a[0:1, :tokens] for a in ordered], axis=1)
    second = jnp.concatenate([a[0:1, tokens:] for a in ordered], axis=1)
    m = jnp.concatenate(
        [((first == float(e)) | (second == float(e))).astype(F32) for e in range(held)], axis=0
    )
    before = iota((total, total), 0)
    after = iota((total, total), 1)
    upto = ((before <= after) & (before // tokens == after // tokens)).astype(BF16)
    rank = jnp.dot(m.astype(BF16), upto, preferred_element_type=F32) - 1.0
    rows = held * CAP
    r = iota((rows, total), 0)
    t = iota((rows, total), 1)
    chunk = r // (rows // 2)
    inner = r % (rows // 2)
    source = inner // (CAP // 2)
    slot = (chunk * (CAP // 2) + inner % (CAP // 2)).astype(F32)
    here = (t // tokens == source).astype(F32)
    for e in range(held):
        hit = jnp.where(rank[e : e + 1, :] == slot, m[e : e + 1, :] * here, 0.0)
        place_ref[e * rows : (e + 1) * rows, :] = hit.astype(BF16)


def place_rows(me, pieces, tokens):
    held = len(pieces)
    width = pieces[0].shape[1] - 2 * tokens
    at = width // (2 * tokens)
    return pl.pallas_call(
        place_kernel,
        grid=(1,),
        out_shape=far((held * held * CAP, held * tokens)),
        in_specs=[pl.BlockSpec(memory_space=pltpu.SMEM)]
        + [pl.BlockSpec((2 * CAP, 2 * tokens), lambda i: (0, at))] * held,
        out_specs=pl.BlockSpec((held * held * CAP, held * tokens), lambda i: (0, 0)),
        compiler_params=params(),
        cost_estimate=cost(1000000, 200000),
        name="place_rows",
    )(me, *pieces)


def gated(att, res, gate, attn_gain):
    norm = att * lax.rsqrt(jnp.mean(att * att, axis=-1, keepdims=True) + EPS) * attn_gain
    return (res + norm * jax.nn.sigmoid(gate)).astype(BF16)


def routed_norm_kernel(me_ref, att_ref, ag_ref, mg_ref, *refs):
    pieces, one_ref, two_ref = refs[:-2], refs[-2], refs[-1]
    sources, rows, part = att_ref.shape
    width = sources * part
    me = me_ref[0]
    att = jnp.concatenate([att_ref[s].astype(F32) for s in range(sources)], axis=1)
    tables = [p[...][:, :width].astype(F32) for p in pieces]
    ordered = [by_source(me, tables, j) for j in range(sources)]
    half = CAP // 2
    res = jnp.concatenate(
        [a[c * half : (c + 1) * half] for c in range(2) for a in ordered], axis=0
    )
    gate = jnp.concatenate(
        [a[CAP + c * half : CAP + (c + 1) * half] for c in range(2) for a in ordered], axis=0
    )
    hidden = gated(att, res, gate, ag_ref[...]).astype(F32)
    normed = (
        hidden * lax.rsqrt(jnp.mean(hidden * hidden, axis=-1, keepdims=True) + EPS) * mg_ref[...]
    )
    one = normed[: rows // 2].astype(BF16)
    for i in range(one_ref.shape[0]):
        one_ref[i] = one
    two_ref[...] = normed[rows // 2 :].astype(BF16)


def routed_norm(me, att, pieces, attn_gain, moe_gain, copies):
    sources, rows, part = att.shape
    width = sources * part
    whole = pl.BlockSpec(memory_space=pltpu.VMEM)
    return pl.pallas_call(
        routed_norm_kernel,
        out_shape=(far((copies, rows // 2, width)), far((rows // 2, width))),
        in_specs=[pl.BlockSpec(memory_space=pltpu.SMEM)] + [whole] * (3 + len(pieces)),
        out_specs=(whole, whole),
        compiler_params=params(),
        cost_estimate=cost(20 * rows * width, 20 * rows * width),
        name="routed_norm",
    )(me, att, attn_gain, moe_gain, *pieces)


def hidden_kernel(me_ref, res_ref, gate_ref, ag_ref, *refs):
    pieces, out_ref = refs[:-1], refs[-1]
    me = me_ref[0]
    tables = [p[...].astype(F32) for p in pieces]
    att = jnp.concatenate([by_source(me, tables, j) for j in range(len(pieces))], axis=1)
    out_ref[...] = gated(att, res_ref[...].astype(F32), gate_ref[...].astype(F32), ag_ref[...])


def hidden_rows(me, pieces, residual, out_gate, attn_gain, tile=32):
    rows, part = pieces[0].shape
    width = len(pieces) * part
    block = pl.BlockSpec((tile, width), lambda i: (i, 0))
    return pl.pallas_call(
        hidden_kernel,
        grid=(rows // tile,),
        out_shape=jax.ShapeDtypeStruct((rows, width), BF16),
        in_specs=[
            pl.BlockSpec(memory_space=pltpu.SMEM),
            block,
            block,
            pl.BlockSpec((1, width), lambda i: (0, 0)),
        ]
        + [pl.BlockSpec((tile, part), lambda i: (i, 0))] * len(pieces),
        out_specs=block,
        compiler_params=params(),
        cost_estimate=cost(20 * rows * width, 8 * rows * width),
        name="hidden_rows",
    )(me, residual, out_gate, attn_gain, *pieces)


def act_kernel(steps, wg_hbm, wu_hbm, *refs):
    xs, (act_ref, w_ref, sem) = refs[:-3], refs[-3:]
    units, width = wg_hbm.shape
    nt = (((1,), (1,)), ((), ()))
    wide = width // steps
    copies = []
    for s in range(steps):
        cols = pl.ds(s * wide, wide)
        for n, a in enumerate((wg_hbm, wu_hbm)):
            copies.append(
                pltpu.make_async_copy(a.at[:, cols], w_ref.at[n, :, cols], sem.at[s, n])
            )
    for c in copies:
        c.start()
    gate = up = None
    for s in range(steps):
        cols = slice(s * wide, (s + 1) * wide)
        copies[2 * s].wait()
        copies[2 * s + 1].wait()
        x = jnp.concatenate([r[:, cols] for r in xs], axis=0)
        g = lax.dot_general(w_ref[0, :, cols], x, nt, preferred_element_type=F32)
        u = lax.dot_general(w_ref[1, :, cols], x, nt, preferred_element_type=F32)
        gate = g if gate is None else gate + g
        up = u if up is None else up + u
    act_ref[...] = (gate * jax.nn.sigmoid(gate) * up).T.astype(BF16)


def expert_act(xs, w_gate, w_up, steps=6):
    count = sum(x.shape[0] for x in xs)
    units, width = w_gate.shape
    whole = pl.BlockSpec(memory_space=pltpu.VMEM)
    away = pl.BlockSpec(memory_space=pl.ANY)
    return pl.pallas_call(
        functools.partial(act_kernel, steps),
        out_shape=jax.ShapeDtypeStruct((count, units), BF16),
        in_specs=[away, away] + [whole] * len(xs),
        out_specs=whole,
        scratch_shapes=[
            pltpu.VMEM((2, units, width), BF16),
            pltpu.SemaphoreType.DMA((steps, 2)),
        ],
        compiler_params=params(),
        cost_estimate=cost(4 * count * width * units, 4 * width * units + 2 * count * width),
        name="expert_act",
    )(hbm(w_gate), hbm(w_up), *xs)


def down_kernel(steps, act_ref, wd_hbm, *refs):
    outs, (wd_ref, sem) = refs[:-2], refs[-2:]
    chips, rows, width = outs[0].shape
    wide = width // steps
    act = act_ref[...]
    copies = []
    for s in range(steps):
        cols = pl.ds(s * wide, wide)
        copies.append(pltpu.make_async_copy(wd_hbm.at[:, cols], wd_ref.at[:, cols], sem.at[s]))
    for c in copies:
        c.start()
    for s in range(steps):
        cols = slice(s * wide, (s + 1) * wide)
        copies[s].wait()
        out = jnp.dot(act, wd_ref[:, cols], preferred_element_type=F32)
        out = out.reshape(len(outs), chips, rows, wide).astype(BF16)
        for n, ref in enumerate(outs):
            ref[:, :, cols] = out[n]


def expert_down(act, w_down, chips, rows, steps=6):
    count, units = act.shape
    width = w_down.shape[1]
    pieces = count // (chips * rows)
    whole = pl.BlockSpec(memory_space=pltpu.VMEM)
    return pl.pallas_call(
        functools.partial(down_kernel, steps),
        out_shape=(jax.ShapeDtypeStruct((chips, rows, width), BF16),) * pieces,
        in_specs=[whole, pl.BlockSpec(memory_space=pl.ANY)],
        out_specs=(whole,) * pieces,
        scratch_shapes=[pltpu.VMEM((units, width), BF16), pltpu.SemaphoreType.DMA((steps,))],
        compiler_params=params(),
        cost_estimate=cost(2 * count * width * units, 2 * width * units + 2 * count * width),
        name="expert_down",
    )(act, hbm(w_down))


def pair_kernel(a_ref, b_ref, *outs):
    total = (a_ref[...].astype(F32) + b_ref[...].astype(F32)).astype(BF16)
    size = outs[0].shape[0]
    for n, out in enumerate(outs):
        out[...] = total[n * size : (n + 1) * size]


def pair_sum(own, other, pieces=1, steps=4):
    chips, rows, width = own.shape
    wide = width // steps
    block = pl.BlockSpec((chips, rows, wide), lambda i: (0, 0, i))
    part = pl.BlockSpec((chips // pieces, rows, wide), lambda i: (0, 0, i))
    return pl.pallas_call(
        pair_kernel,
        grid=(steps,),
        out_shape=(far((chips // pieces, rows, width)),) * pieces,
        in_specs=[block, block],
        out_specs=(part,) * pieces,
        compiler_params=params(),
        cost_estimate=cost(chips * rows * width, 6 * chips * rows * width),
        name="pair_sum",
    )(own, other)


def line_kernel(*refs):
    half = len(refs) // 2
    total = refs[0][...].astype(F32)
    for ref in refs[1:half]:
        total = total + ref[...].astype(F32)
    total = total.astype(BF16)
    for n, out in enumerate(refs[half:]):
        out[...] = total[n]


def line_sum(parts, steps=2):
    n, rows, width = parts[0].shape
    wide = width // steps
    block = pl.BlockSpec((n, rows, wide), lambda i: (0, 0, i))
    return pl.pallas_call(
        line_kernel,
        grid=(steps,),
        out_shape=(far((rows, width)),) * n,
        in_specs=[block] * len(parts),
        out_specs=(pl.BlockSpec((rows, wide), lambda i: (0, i)),) * n,
        compiler_params=params(),
        cost_estimate=cost(n * n * rows * width, 2 * n * (n + 1) * rows * width),
        name="line_sum",
    )(*parts)


def chip_sum_kernel(one_ref, *refs):
    parts, out_ref = refs[:-1], refs[-1]
    one = one_ref[0].astype(F32)
    for i in range(1, one_ref.shape[0]):
        one = one + one_ref[i].astype(F32)
    two = parts[0][...].astype(F32)
    for ref in parts[1:]:
        two = two + ref[...].astype(F32)
    half = CAP // 2
    for j in range(out_ref.shape[0]):
        at = slice(j * half, (j + 1) * half)
        out_ref[j] = jnp.concatenate([one[at], two[at]], axis=0).astype(BF16)


def chip_sum(one, parts, held, steps=4):
    chips, rows, width = one.shape
    wide = width // steps
    return pl.pallas_call(
        chip_sum_kernel,
        grid=(steps,),
        out_shape=far((held, CAP, width)),
        in_specs=[pl.BlockSpec((chips, rows, wide), lambda i: (0, 0, i))]
        + [pl.BlockSpec((rows, wide), lambda i: (0, i))] * len(parts),
        out_specs=pl.BlockSpec((held, CAP, wide), lambda i: (0, 0, i)),
        compiler_params=params(),
        cost_estimate=cost(chips * rows * width, 3 * chips * rows * width),
        name="chip_sum",
    )(one, *parts)


def combine_kernel(place_ref, rows_ref, ids_ref, weights_ref, out_ref):
    held = rows_ref.shape[0]
    rows = jnp.concatenate([rows_ref[e].astype(F32) for e in range(held)], axis=0).astype(BF16)
    back = lax.dot_general(
        place_ref[...].astype(BF16), rows, (((0,), (0,)), ((), ())), preferred_element_type=F32
    )
    chosen = jnp.sum(
        jnp.where(ids_ref[...] < held, weights_ref[...], 0.0), axis=1, keepdims=True
    )
    out_ref[...] = (back * chosen).astype(BF16)


def combine_rows(place, rows, ids, weights):
    tokens = ids.shape[0]
    width = rows.shape[2]
    return pl.pallas_call(
        combine_kernel,
        out_shape=jax.ShapeDtypeStruct((tokens, width), BF16),
        compiler_params=params(),
        cost_estimate=cost(32 * tokens * width, 2 * tokens * width),
        name="combine_rows",
    )(place, rows, ids, weights)


def exchange(a, axis):
    return lax.all_to_all(a, axis, split_axis=0, concat_axis=0, tiled=True)


def shift(a, axis, by):
    n = lax.axis_size(axis)
    return lax.ppermute(a, axis, [(i, (i + by) % n) for i in range(n)])


def local(
    queries,
    key_vectors,
    values,
    log_decay,
    out_gate,
    residual,
    attn_gain,
    moe_gain,
    expert_ids,
    route_weights,
    w_gate,
    w_up,
    w_down,
):
    held = lax.axis_size("exp")
    rows, width = queries.shape
    heads = log_decay.shape[1]
    tokens = residual.shape[0]
    attn_gain = attn_gain.reshape(1, -1)
    moe_gain = moe_gain.reshape(1, -1)
    w_gate = jnp.swapaxes(w_gate, 1, 2)[0]
    w_up = jnp.swapaxes(w_up, 1, 2)[0]
    w_down = w_down[0]
    ids = expert_ids.T
    ld = hbm(log_decay.T)
    me = lax.axis_index("exp").reshape(1)
    keep = lax.optimization_barrier
    chips = lax.axis_size("z") * lax.axis_size("x")

    cum, msg = local_states(hbm(key_vectors), hbm(values), ld)
    sent = exchange(msg, CTX)
    inside, qs = inside_blocks(hbm(queries), hbm(key_vectors), hbm(values), cum, ld)
    pieces, place_own = route_rows(me, ids, hbm(residual), hbm(out_gate), held)
    sent, inside, qs, pieces = keep((sent, inside, qs, pieces))
    prior = scan_blocks(hbm(sent), lax.axis_index(CTX))
    state = exchange(prior, CTX).reshape(heads, HEAD_DIM, HEAD_DIM)
    pieces = [pieces[0]] + [shift(pieces[d], "exp", d) for d in range(1, held)]
    pieces = [hbm(a) for a in pieces]
    place = place_rows(me, pieces, tokens)

    routed, attention = carried_blocks(me, inside, hbm(qs), state, hbm(place), held)
    routed = exchange(routed.reshape(held, held * CAP, width), "exp")
    one, two = routed_norm(me, routed, pieces, attn_gain, moe_gain, chips)

    attention, two = keep((attention, two))
    one = exchange(one, ("z", "x"))
    line = jnp.stack([two] + [shift(two, "x", d) for d in range(1, 4)])
    plane = [line] + [shift(line, "z", d) for d in range(1, 4)]
    attention = [attention[0]] + [shift(attention[d], "exp", d) for d in range(1, held)]
    one, plane, attention = keep((one, plane, attention))
    near = [a.reshape(-1, a.shape[2]) for a in [one] + plane]
    act = expert_act(near + [shift(a, "core", 1) for a in near], w_gate, w_up)
    own1, own2, other1, other2 = expert_down(act, w_down, chips, two.shape[0])
    (one,) = pair_sum(own1, shift(other1, "core", 1))
    one = exchange(one, ("z", "x"))
    parts = pair_sum(own2, shift(other2, "core", 1), pieces=4)
    parts = [parts[0]] + [shift(parts[d], "z", -d) for d in range(1, 4)]
    one, parts = keep((one, parts))
    parts = line_sum(parts)
    parts = [parts[0]] + [shift(parts[d], "x", -d) for d in range(1, 4)]
    hidden = hidden_rows(me, attention, hbm(residual), hbm(out_gate), attn_gain)
    back = exchange(chip_sum(one, parts, held), "exp")
    moe_out = combine_rows(place_own, back, expert_ids, route_weights)
    return (hidden, moe_out)


def solution(mesh):
    cube = Mesh(mesh.devices.reshape(4, 4, 2, 4), ("z", "x", "core", "exp"))
    both = CTX + ("exp",)
    in_specs = (
        P(CTX, "exp"),
        P(CTX, "exp"),
        P(CTX, "exp"),
        P(CTX, "exp"),
        P(both, None),
        P(both, None),
        P(),
        P(),
        P(both, None),
        P(both, None),
        P("exp", None, CTX),
        P("exp", None, CTX),
        P("exp", CTX, None),
    )
    out_specs = (P(both, None), P(both, None))
    return jax.shard_map(local, mesh=cube, in_specs=in_specs, out_specs=out_specs, check_vma=False)
```

```python
import functools

import jax
import jax.numpy as jnp
from jax import lax
from jax.experimental import pallas as pl
from jax.experimental.pallas import tpu as pltpu
from jax.sharding import Mesh, PartitionSpec as P

HEAD_DIM = 128
CAP = 4
EPS = 1e-05
F32 = jnp.float32
BF16 = jnp.bfloat16
HIGHEST = lax.Precision.HIGHEST
CTX = ("z", "x", "core")
VMEM_LIMIT = 24 * 1024 * 1024


def iota(shape, dim):
    return lax.broadcasted_iota(jnp.int32, shape, dim)


def hbm(a):
    return pltpu.with_memory_space_constraint(a, pltpu.HBM)


def far(shape, dtype=BF16):
    return pltpu.HBM(shape, dtype)


def params(**kw):
    return pltpu.CompilerParams(vmem_limit_bytes=VMEM_LIMIT, **kw)


def cost(flops, bytes_accessed):
    return pl.CostEstimate(flops=flops, bytes_accessed=bytes_accessed, transcendentals=0)


def running_sum(ld, axis):
    rows = ld.shape[1]
    a, b = iota((rows, rows), 0), iota((rows, rows), 1)
    ones = (a >= b).astype(BF16)
    total = None
    rest = ld
    for _ in range(3):
        part = rest.astype(BF16)
        rest = rest - part.astype(F32)
        pair = (ones, part) if axis == 0 else (part, ones)
        term = lax.dot_general(*pair, (((1,), (1,)), ((), ())), preferred_element_type=F32)
        total = term if total is None else total + term
    return total


def spread(table, first, count, terms):
    n = table.shape[1]
    shape = (n, count * HEAD_DIM)
    pick = (iota(shape, 0) == first + iota(shape, 1) // HEAD_DIM).astype(BF16)
    total = None
    rest = table
    for _ in range(terms):
        part = rest.astype(BF16)
        rest = rest - part.astype(F32)
        term = jnp.dot(part, pick, preferred_element_type=F32)
        total = term if total is None else total + term
    return total


def state_kernel(group, k_ref, v_ref, ld_ref, cum_ref, msg_ref, fade_ref, decay_ref):
    heads, rows = ld_ref.shape
    per = heads * HEAD_DIM // 32
    parts = group * HEAD_DIM // per
    g = pl.program_id(0)

    @pl.when(g == 0)
    def _():
        cum = running_sum(ld_ref[...], 0)
        cum_ref[...] = cum
        final = cum[rows - 1 : rows, :]
        fade_ref[...] = jnp.exp(final - cum)
        decay_ref[...] = jnp.broadcast_to(jnp.exp(final), decay_ref.shape)

    fade = spread(fade_ref[...], g * group, group, 2)
    decay = spread(decay_ref[...], g * group, group, 2)
    row16 = iota((16, HEAD_DIM), 0)
    tiles = []
    for j in range(group):
        cols = slice(j * HEAD_DIM, (j + 1) * HEAD_DIM)
        wk = (k_ref[:, cols].astype(F32) * fade[:, cols]).astype(BF16)
        state = lax.dot_general(
            wk, v_ref[:, cols], (((0,), (0,)), ((), ())), preferred_element_type=F32
        ).astype(BF16)
        row = j * HEAD_DIM
        while row < (j + 1) * HEAD_DIM:
            part, at = row // per, row % per
            take = min(per - at, (j + 1) * HEAD_DIM - row)
            lo = row - j * HEAD_DIM
            msg_ref[part, at : at + take, :] = state[lo : lo + take, :]
            row += take
        whole = decay[:, cols]
        high = whole.astype(BF16).astype(F32)
        tiles.append((high, whole - high))
    for part in range(parts):
        first = per * part // HEAD_DIM
        last = (per * part + per - 1) // HEAD_DIM
        tile = jnp.where(
            row16 == 0,
            tiles[first][0],
            jnp.where(
                row16 == 1, tiles[first][1], jnp.where(row16 == 2, tiles[last][0], tiles[last][1])
            ),
        )
        msg_ref[part, per : per + 16, :] = tile.astype(BF16)


def local_states(k, v, ld, group=3):
    rows, width = k.shape
    heads = ld.shape[0]
    per = heads * HEAD_DIM // 32
    parts = group * HEAD_DIM // per
    block = pl.BlockSpec((rows, group * HEAD_DIM), lambda g: (0, g))
    return pl.pallas_call(
        functools.partial(state_kernel, group),
        grid=(heads // group,),
        out_shape=(
            jax.ShapeDtypeStruct((rows, heads), F32),
            far((32, per + 16, HEAD_DIM)),
        ),
        in_specs=[block, block, pl.BlockSpec((heads, rows), lambda g: (0, 0))],
        out_specs=(
            pl.BlockSpec((rows, heads), lambda g: (0, 0)),
            pl.BlockSpec((parts, per + 16, HEAD_DIM), lambda g: (g, 0, 0)),
        ),
        scratch_shapes=[pltpu.VMEM((rows, heads), F32), pltpu.VMEM((16, heads), F32)],
        compiler_params=params(),
        cost_estimate=cost(2 * rows * width * HEAD_DIM, 4 * rows * width),
        name="local_states",
    )(k, v, ld)


def scan_kernel(split_ref, in_ref, out_ref):
    parts, per, width = out_ref.shape
    first_rows = iota((per, width), 0) < split_ref[0]
    state = jnp.zeros((per, width), F32)
    for b in range(parts):
        out_ref[b, :, :] = state.astype(BF16)
        if b + 1 < parts:
            tail = in_ref[b, per : per + 16, :].astype(F32)
            d0 = tail[0:1, :] + tail[1:2, :]
            d1 = tail[2:3, :] + tail[3:4, :]
            decay = jnp.where(first_rows, d0, d1)
            state = decay * state + in_ref[b, 0:per, :].astype(F32)


def scan_blocks(msg, part):
    parts, tall, width = msg.shape
    per = tall - 16
    split = (HEAD_DIM - (per * part) % HEAD_DIM).astype(jnp.int32).reshape(1)
    return pl.pallas_call(
        scan_kernel,
        out_shape=far((parts, per, width)),
        in_specs=[
            pl.BlockSpec(memory_space=pltpu.SMEM),
            pl.BlockSpec(memory_space=pltpu.VMEM),
        ],
        out_specs=pl.BlockSpec(memory_space=pltpu.VMEM),
        compiler_params=params(),
        cost_estimate=cost(1000000, 1000000),
        name="scan_blocks",
    )(split, msg)


def inside_kernel(group, q_ref, k_ref, v_ref, cum_ref, ld_ref, inside_ref, qs_ref, cumt_ref):
    rows, heads = cum_ref.shape

    @pl.when(pl.program_id(0) == 0)
    def _():
        cumt_ref[...] = running_sum(ld_ref[...], 1)

    cum = spread(cum_ref[...], pl.program_id(0) * group, group, 3)
    size = 2 * HEAD_DIM
    causal = iota((size, size), 0) >= iota((size, size), 1)
    for j in range(group):
        h = pl.program_id(0) * group + j
        cols = slice(j * HEAD_DIM, (j + 1) * HEAD_DIM)
        col = cum[:, cols]
        row = cumt_ref[pl.ds(h, 1), :]
        q = q_ref[:, cols]
        k = k_ref[:, cols]
        v = v_ref[:, cols]
        qs_ref[:, cols] = (q.astype(F32) * jnp.exp(col)).astype(BF16)
        wide = jnp.concatenate([col, col], axis=1)
        total = None
        for lo in range(0, rows, size):
            hi = lo + size
            s = lax.dot_general(
                q[lo:], k[lo:hi], (((1,), (1,)), ((), ())), preferred_element_type=F32
            )
            decay = jnp.exp(jnp.minimum(wide[lo:] - row[:, lo:hi], 0.0))
            w = s * decay
            w = jnp.concatenate([jnp.where(causal, w[:size], 0.0), w[size:]], axis=0) if (
                hi < rows
            ) else jnp.where(causal, w, 0.0)
            part = jnp.dot(w.astype(BF16), v[lo:hi], preferred_element_type=F32)
            if total is None:
                total = part
            else:
                total = jnp.concatenate([total[:lo], total[lo:] + part], axis=0)
        inside_ref[:, cols] = total


def inside_blocks(q, k, v, cum, ld, group=3):
    rows, width = q.shape
    heads = cum.shape[1]
    block = pl.BlockSpec((rows, group * HEAD_DIM), lambda g: (0, g))
    return pl.pallas_call(
        functools.partial(inside_kernel, group),
        grid=(heads // group,),
        out_shape=(
            jax.ShapeDtypeStruct((rows, width), F32),
            far((rows, width)),
        ),
        in_specs=[
            block,
            block,
            block,
            pl.BlockSpec((rows, heads), lambda g: (0, 0)),
            pl.BlockSpec((heads, rows), lambda g: (0, 0)),
        ],
        out_specs=(block, block),
        scratch_shapes=[pltpu.VMEM((heads, rows), F32)],
        compiler_params=params(),
        cost_estimate=cost(4 * rows * rows * width, 12 * rows * width),
        name="inside_blocks",
    )(q, k, v, cum, ld)


def carried_kernel(group, me_ref, inside_ref, qs_ref, state_ref, place_ref, sel_ref, *refs):
    outs, att_ref = refs[:-1], refs[-1]
    held = len(outs)
    tokens = outs[0].shape[0]
    for j in range(group):
        cols = slice(j * HEAD_DIM, (j + 1) * HEAD_DIM)
        att_ref[:, cols] = (
            inside_ref[:, cols]
            + jnp.dot(qs_ref[:, cols], state_ref[j], preferred_element_type=F32)
        ).astype(BF16)
    sel_ref[...] = jnp.dot(
        place_ref[...], att_ref[...], preferred_element_type=F32
    ).astype(BF16)
    for d in range(held):
        at = pl.multiple_of(lax.rem(me_ref[0] + d, held) * tokens, tokens)
        outs[d][...] = att_ref[pl.ds(at, tokens), :]


def carried_blocks(me, inside, qs, state, place, held, group=3):
    rows, width = inside.shape
    heads = width // HEAD_DIM
    chosen = place.shape[0]
    wide = group * HEAD_DIM
    tokens = rows // held
    block = pl.BlockSpec((rows, wide), lambda g: (0, g))
    outs = pl.pallas_call(
        functools.partial(carried_kernel, group),
        grid=(heads // group,),
        out_shape=(far((chosen, width)),) + (far((tokens, width)),) * held,
        in_specs=[
            pl.BlockSpec(memory_space=pltpu.SMEM),
            block,
            block,
            pl.BlockSpec((group, HEAD_DIM, HEAD_DIM), lambda g: (g, 0, 0)),
            pl.BlockSpec((chosen, rows), lambda g: (0, 0)),
        ],
        out_specs=(pl.BlockSpec((chosen, wide), lambda g: (0, g)),)
        + (pl.BlockSpec((tokens, wide), lambda g: (0, g)),) * held,
        scratch_shapes=[pltpu.VMEM((rows, wide), BF16)],
        compiler_params=params(),
        cost_estimate=cost(4 * rows * width * HEAD_DIM, 8 * rows * width),
        name="carried_blocks",
    )(me, inside, qs, state, place)
    return outs[0], list(outs[1:])


def route_kernel(pieces, me_ref, ids_ref, res_hbm, gate_hbm, *refs):
    outs, (place_ref, res_ref, gate_ref, sem) = refs[:-4], refs[-4:]
    held = len(outs)
    size = res_ref.shape[0] // pieces
    copies = []
    for n, (a, b) in enumerate(((res_hbm, res_ref), (gate_hbm, gate_ref))):
        for i in range(pieces):
            at = pl.ds(i * size, size)
            copies.append(pltpu.make_async_copy(a.at[at], b.at[at], sem.at[n, i]))
    for c in copies:
        c.start()
    tokens, width = res_ref.shape
    me = me_ref[0]
    ids = ids_ref[...]
    hits = [
        ((ids[0:1, :] == e) | (ids[1:2, :] == e)).astype(F32) for e in range(held)
    ]
    m = jnp.concatenate(hits, axis=0)
    upto = (iota((tokens, tokens), 0) <= iota((tokens, tokens), 1)).astype(BF16)
    rank = jnp.dot(m.astype(BF16), upto, preferred_element_type=F32) - 1.0
    slot = iota((CAP, tokens), 0).astype(F32)
    places = [
        jnp.where(rank[e : e + 1, :] == slot, m[e : e + 1, :], 0.0) for e in range(held)
    ]
    place = jnp.concatenate(places, axis=0)
    place_ref[...] = place
    for c in copies:
        c.wait()
    ordered = []
    for d in range(held):
        expert = lax.rem(me + d, held)
        mine = places[0]
        for e in range(1, held):
            mine = jnp.where(expert == e, places[e], mine)
        ordered.append(mine)
    chosen = jnp.concatenate(ordered, axis=0).astype(BF16)
    res = jnp.dot(chosen, res_ref[...], preferred_element_type=F32)
    gate = jnp.dot(chosen, gate_ref[...], preferred_element_type=F32)
    for d in range(held):
        at = slice(d * CAP, (d + 1) * CAP)
        outs[d][:, 0:width] = jnp.concatenate([res[at], gate[at]], axis=0).astype(BF16)
        for n in range(2):
            outs[d][:, width + n * tokens : width + (n + 1) * tokens] = jnp.broadcast_to(
                ids[n : n + 1, :].astype(F32), (2 * CAP, tokens)
            ).astype(BF16)


def route_rows(me, ids, residual, out_gate, held, pieces=4):
    tokens, width = residual.shape
    whole = pl.BlockSpec(memory_space=pltpu.VMEM)
    away = pl.BlockSpec(memory_space=pl.ANY)
    piece = far((2 * CAP, width + 2 * tokens))
    outs = pl.pallas_call(
        functools.partial(route_kernel, pieces),
        out_shape=(piece,) * held + (jax.ShapeDtypeStruct((held * CAP, tokens), F32),),
        in_specs=[pl.BlockSpec(memory_space=pltpu.SMEM), whole, away, away],
        out_specs=(whole,) * (held + 1),
        scratch_shapes=[
            pltpu.VMEM((tokens, width), BF16),
            pltpu.VMEM((tokens, width), BF16),
            pltpu.SemaphoreType.DMA((2, pieces)),
        ],
        compiler_params=params(),
        cost_estimate=cost(64 * tokens * width, 5 * tokens * width),
        name="route_rows",
    )(me, ids, residual, out_gate)
    return outs[:-1], outs[-1]


def by_source(me, pieces, j):
    count = len(pieces)
    out = pieces[0]
    for d in range(1, count):
        out = jnp.where(lax.rem(me + count - d, count) == j, pieces[d], out)
    return out


def place_kernel(me_ref, *refs):
    pieces, place_ref = refs[:-1], refs[-1]
    held = len(pieces)
    tokens = pieces[0].shape[1] // 2
    total = held * tokens
    me = me_ref[0]
    tables = [p[...].astype(F32) for p in pieces]
    ordered = [by_source(me, tables, j) for j in range(held)]
    first = jnp.concatenate([a[0:1, :tokens] for a in ordered], axis=1)
    second = jnp.concatenate([a[0:1, tokens:] for a in ordered], axis=1)
    m = jnp.concatenate(
        [((first == float(e)) | (second == float(e))).astype(F32) for e in range(held)], axis=0
    )
    before = iota((total, total), 0)
    after = iota((total, total), 1)
    upto = ((before <= after) & (before // tokens == after // tokens)).astype(BF16)
    rank = jnp.dot(m.astype(BF16), upto, preferred_element_type=F32) - 1.0
    rows = held * CAP
    r = iota((rows, total), 0)
    t = iota((rows, total), 1)
    here = (t // tokens == r // CAP).astype(F32)
    slot = (r % CAP).astype(F32)
    for e in range(held):
        hit = jnp.where(rank[e : e + 1, :] == slot, m[e : e + 1, :] * here, 0.0)
        place_ref[e * rows : (e + 1) * rows, :] = hit.astype(BF16)


def place_rows(me, pieces, tokens):
    held = len(pieces)
    width = pieces[0].shape[1] - 2 * tokens
    at = width // (2 * tokens)
    return pl.pallas_call(
        place_kernel,
        grid=(1,),
        out_shape=far((held * held * CAP, held * tokens)),
        in_specs=[pl.BlockSpec(memory_space=pltpu.SMEM)]
        + [pl.BlockSpec((2 * CAP, 2 * tokens), lambda i: (0, at))] * held,
        out_specs=pl.BlockSpec((held * held * CAP, held * tokens), lambda i: (0, 0)),
        compiler_params=params(),
        cost_estimate=cost(1000000, 200000),
        name="place_rows",
    )(me, *pieces)


def gated(att, res, gate, attn_gain):
    norm = att * lax.rsqrt(jnp.mean(att * att, axis=-1, keepdims=True) + EPS) * attn_gain
    return (res + norm * jax.nn.sigmoid(gate)).astype(BF16)


def routed_norm_kernel(me_ref, att_ref, ag_ref, mg_ref, *refs):
    pieces, one_ref, two_ref = refs[:-2], refs[-2], refs[-1]
    sources, rows, part = att_ref.shape
    width = sources * part
    me = me_ref[0]
    att = jnp.concatenate([att_ref[s].astype(F32) for s in range(sources)], axis=1)
    tables = [p[...][:, :width].astype(F32) for p in pieces]
    ordered = [by_source(me, tables, j) for j in range(sources)]
    res = jnp.concatenate([a[:CAP] for a in ordered], axis=0)
    gate = jnp.concatenate([a[CAP:] for a in ordered], axis=0)
    hidden = gated(att, res, gate, ag_ref[...]).astype(F32)
    normed = (
        hidden * lax.rsqrt(jnp.mean(hidden * hidden, axis=-1, keepdims=True) + EPS) * mg_ref[...]
    ).astype(BF16)
    one_ref[...] = normed[:, : width // 2]
    for i in range(two_ref.shape[0]):
        two_ref[i] = normed[:, width // 2 :]


def routed_norm(me, att, pieces, attn_gain, moe_gain, copies):
    sources, rows, part = att.shape
    width = sources * part
    whole = pl.BlockSpec(memory_space=pltpu.VMEM)
    return pl.pallas_call(
        routed_norm_kernel,
        out_shape=(far((rows, width // 2)), far((copies, rows, width // 2))),
        in_specs=[pl.BlockSpec(memory_space=pltpu.SMEM)] + [whole] * (3 + len(pieces)),
        out_specs=(whole, whole),
        compiler_params=params(),
        cost_estimate=cost(20 * rows * width, 20 * rows * width),
        name="routed_norm",
    )(me, att, attn_gain, moe_gain, *pieces)


def hidden_kernel(me_ref, res_ref, gate_ref, ag_ref, *refs):
    pieces, out_ref = refs[:-1], refs[-1]
    me = me_ref[0]
    tables = [p[...].astype(F32) for p in pieces]
    att = jnp.concatenate([by_source(me, tables, j) for j in range(len(pieces))], axis=1)
    out_ref[...] = gated(att, res_ref[...].astype(F32), gate_ref[...].astype(F32), ag_ref[...])


def hidden_rows(me, pieces, residual, out_gate, attn_gain, tile=32):
    rows, part = pieces[0].shape
    width = len(pieces) * part
    block = pl.BlockSpec((tile, width), lambda i: (i, 0))
    return pl.pallas_call(
        hidden_kernel,
        grid=(rows // tile,),
        out_shape=jax.ShapeDtypeStruct((rows, width), BF16),
        in_specs=[
            pl.BlockSpec(memory_space=pltpu.SMEM),
            block,
            block,
            pl.BlockSpec((1, width), lambda i: (0, 0)),
        ]
        + [pl.BlockSpec((tile, part), lambda i: (i, 0))] * len(pieces),
        out_specs=block,
        compiler_params=params(),
        cost_estimate=cost(20 * rows * width, 8 * rows * width),
        name="hidden_rows",
    )(me, residual, out_gate, attn_gain, *pieces)


def repeat_kernel(*refs):
    ins, (out, sem) = refs[:-2], refs[-2:]
    copies = [
        pltpu.make_async_copy(a, out.at[n, k], sem.at[n, k])
        for n in range(out.shape[0])
        for k, a in enumerate(ins)
    ]
    for c in copies:
        c.start()
    for c in copies:
        c.wait()


def repeat(arrays, copies):
    rows, width = arrays[0].shape
    count = len(arrays)
    return pl.pallas_call(
        repeat_kernel,
        out_shape=far((copies, count, rows, width)),
        in_specs=[pl.BlockSpec(memory_space=pltpu.VMEM)] * count,
        out_specs=pl.BlockSpec(memory_space=pl.ANY),
        scratch_shapes=[pltpu.SemaphoreType.DMA((copies, count))],
        compiler_params=params(),
        cost_estimate=cost(0, 2 * (copies + 1) * count * rows * width),
        name="repeat",
    )(*arrays)


def act_kernel(steps, wg_hbm, wu_hbm, one_ref, *refs):
    twos, (act_ref, w_ref, sem) = refs[:-3], refs[-3:]
    units, width = wg_hbm.shape
    nz, nx, rows, half = one_ref.shape
    nt = (((1,), (1,)), ((), ()))
    wide = width // steps
    copies = []
    for s in range(steps):
        cols = pl.ds(s * wide, wide)
        for n, a in enumerate((wg_hbm, wu_hbm)):
            copies.append(
                pltpu.make_async_copy(a.at[:, cols], w_ref.at[n, :, cols], sem.at[s, n])
            )
    for c in copies:
        c.start()
    gate = up = None
    for s in range(steps):
        cols = slice(s * wide, (s + 1) * wide)
        copies[2 * s].wait()
        copies[2 * s + 1].wait()
        if s < steps // 2:
            x = [one_ref[z, k, :, cols] for k in range(nx) for z in range(nz)]
        else:
            near = slice(s * wide - half, (s + 1) * wide - half)
            x = [r[z, :, near] for r in twos for z in range(nz)]
        x = jnp.concatenate(x, axis=0)
        g = lax.dot_general(w_ref[0, :, cols], x, nt, preferred_element_type=F32)
        u = lax.dot_general(w_ref[1, :, cols], x, nt, preferred_element_type=F32)
        gate = g if gate is None else gate + g
        up = u if up is None else up + u
    act_ref[...] = (gate * jax.nn.sigmoid(gate) * up).T.astype(BF16)


def expert_act(one, twos, w_gate, w_up, steps=6):
    nz, nx, rows, half = one.shape
    count = nz * nx * rows
    units, width = w_gate.shape
    whole = pl.BlockSpec(memory_space=pltpu.VMEM)
    away = pl.BlockSpec(memory_space=pl.ANY)
    return pl.pallas_call(
        functools.partial(act_kernel, steps),
        out_shape=jax.ShapeDtypeStruct((count, units), BF16),
        in_specs=[away, away] + [whole] * (1 + len(twos)),
        out_specs=whole,
        scratch_shapes=[
            pltpu.VMEM((2, units, width), BF16),
            pltpu.SemaphoreType.DMA((steps, 2)),
        ],
        compiler_params=params(),
        cost_estimate=cost(4 * count * width * units, 4 * width * units + 2 * count * width),
        name="expert_act",
    )(hbm(w_gate), hbm(w_up), one, *twos)


def down_kernel(steps, act_ref, wd_hbm, one_ref, two_ref, wd_ref, sem):
    nz, nx, rows, half = one_ref.shape
    wide = 2 * half // steps
    act = act_ref[...]
    copies = []
    for s in range(steps):
        cols = pl.ds(s * wide, wide)
        copies.append(pltpu.make_async_copy(wd_hbm.at[:, cols], wd_ref.at[:, cols], sem.at[s]))
    for c in copies:
        c.start()
    for s in range(steps):
        cols = slice(s * wide, (s + 1) * wide)
        copies[s].wait()
        out = jnp.dot(act, wd_ref[:, cols], preferred_element_type=F32)
        out = out.reshape(nx, nz, rows, wide).astype(BF16)
        if s < steps // 2:
            for z in range(nz):
                one_ref[z, :, :, cols] = out[:, z]
        else:
            two_ref[:, :, :, s * wide - half : (s + 1) * wide - half] = out


def expert_down(act, w_down, nz, nx, steps=6):
    count, units = act.shape
    width = w_down.shape[1]
    rows = count // (nz * nx)
    whole = pl.BlockSpec(memory_space=pltpu.VMEM)
    return pl.pallas_call(
        functools.partial(down_kernel, steps),
        out_shape=(
            jax.ShapeDtypeStruct((nz, nx, rows, width // 2), BF16),
            jax.ShapeDtypeStruct((nx, nz, rows, width // 2), BF16),
        ),
        in_specs=[whole, pl.BlockSpec(memory_space=pl.ANY)],
        out_specs=(whole, whole),
        scratch_shapes=[pltpu.VMEM((units, width), BF16), pltpu.SemaphoreType.DMA((steps,))],
        compiler_params=params(),
        cost_estimate=cost(2 * count * width * units, 2 * width * units + 2 * count * width),
        name="expert_down",
    )(act, hbm(w_down))


def pair_kernel(a_ref, b_ref, *outs):
    total = (a_ref[...].astype(F32) + b_ref[...].astype(F32)).astype(BF16)
    if len(outs) == 1:
        outs[0][...] = total
    else:
        for n, out in enumerate(outs):
            out[...] = total[n]


def pair_sum(own, other, split, steps=3):
    n, m, rows, width = own.shape
    wide = width // steps
    block = pl.BlockSpec((n, m, rows, wide), lambda i: (0, 0, 0, i))
    part = pl.BlockSpec((m, rows, wide), lambda i: (0, 0, i))
    return pl.pallas_call(
        pair_kernel,
        grid=(steps,),
        out_shape=(far((m, rows, width)),) * n if split else (far(own.shape),),
        in_specs=[block, block],
        out_specs=(part,) * n if split else (block,),
        compiler_params=params(),
        cost_estimate=cost(n * m * rows * width, 6 * n * m * rows * width),
        name="pair_sum",
    )(own, other)


def block_kernel(in_ref, *outs):
    total = in_ref[0].astype(F32)
    for i in range(1, in_ref.shape[0]):
        total = total + in_ref[i].astype(F32)
    total = total.astype(BF16)
    for n, out in enumerate(outs):
        out[...] = total[n]


def block_sum(parts, steps=2):
    count, n, rows, width = parts.shape
    wide = width // steps
    return pl.pallas_call(
        block_kernel,
        grid=(steps,),
        out_shape=(far((rows, width)),) * n,
        in_specs=[pl.BlockSpec((count, n, rows, wide), lambda i: (0, 0, 0, i))],
        out_specs=(pl.BlockSpec((rows, wide), lambda i: (0, i)),) * n,
        compiler_params=params(),
        cost_estimate=cost(count * n * rows * width, 2 * (count + 1) * n * rows * width),
        name="block_sum",
    )(parts)


def stack_kernel(*refs):
    total = refs[0][...].astype(F32)
    for ref in refs[1:-1]:
        total = total + ref[...].astype(F32)
    refs[-1][...] = total.astype(BF16)


def stack_sum(parts, steps=2):
    n, rows, width = parts[0].shape
    wide = width // steps
    block = pl.BlockSpec((n, rows, wide), lambda i: (0, 0, i))
    return pl.pallas_call(
        stack_kernel,
        grid=(steps,),
        out_shape=far(parts[0].shape),
        in_specs=[block] * len(parts),
        out_specs=block,
        compiler_params=params(),
        cost_estimate=cost(len(parts) * n * rows * width, 2 * (len(parts) + 1) * n * rows * width),
        name="stack_sum",
    )(*parts)


def row_sum_kernel(two_ref, *refs):
    parts, out_ref = refs[:-1], refs[-1]
    one = parts[0][...].astype(F32)
    for ref in parts[1:]:
        one = one + ref[...].astype(F32)
    two = two_ref[0].astype(F32)
    for i in range(1, two_ref.shape[0]):
        two = two + two_ref[i].astype(F32)
    half = one.shape[1]
    for j in range(out_ref.shape[0]):
        at = slice(j * CAP, (j + 1) * CAP)
        out_ref[j, :, :half] = one[at].astype(BF16)
        out_ref[j, :, half:] = two[at].astype(BF16)


def row_sum(parts, two, held):
    count, rows, half = two.shape
    whole = pl.BlockSpec(memory_space=pltpu.VMEM)
    return pl.pallas_call(
        row_sum_kernel,
        out_shape=far((held, CAP, 2 * half)),
        in_specs=[whole] * (1 + len(parts)),
        out_specs=whole,
        compiler_params=params(),
        cost_estimate=cost(8 * rows * half, 20 * rows * half),
        name="row_sum",
    )(two, *parts)


def combine_kernel(place_ref, rows_ref, ids_ref, weights_ref, out_ref):
    held = rows_ref.shape[0]
    rows = jnp.concatenate([rows_ref[e].astype(F32) for e in range(held)], axis=0).astype(BF16)
    back = lax.dot_general(
        place_ref[...].astype(BF16), rows, (((0,), (0,)), ((), ())), preferred_element_type=F32
    )
    chosen = jnp.sum(
        jnp.where(ids_ref[...] < held, weights_ref[...], 0.0), axis=1, keepdims=True
    )
    out_ref[...] = (back * chosen).astype(BF16)


def combine_rows(place, rows, ids, weights):
    tokens = ids.shape[0]
    width = rows.shape[2]
    return pl.pallas_call(
        combine_kernel,
        out_shape=jax.ShapeDtypeStruct((tokens, width), BF16),
        compiler_params=params(),
        cost_estimate=cost(32 * tokens * width, 2 * tokens * width),
        name="combine_rows",
    )(place, rows, ids, weights)


def exchange(a, axis):
    return lax.all_to_all(a, axis, split_axis=0, concat_axis=0, tiled=True)


def shift(a, axis, by):
    n = lax.axis_size(axis)
    return lax.ppermute(a, axis, [(i, (i + by) % n) for i in range(n)])


def local(
    queries,
    key_vectors,
    values,
    log_decay,
    out_gate,
    residual,
    attn_gain,
    moe_gain,
    expert_ids,
    route_weights,
    w_gate,
    w_up,
    w_down,
):
    held = lax.axis_size("exp")
    rows, width = queries.shape
    heads = log_decay.shape[1]
    tokens = residual.shape[0]
    attn_gain = attn_gain.reshape(1, -1)
    moe_gain = moe_gain.reshape(1, -1)
    w_gate = jnp.swapaxes(w_gate, 1, 2)[0]
    w_up = jnp.swapaxes(w_up, 1, 2)[0]
    w_down = w_down[0]
    ids = expert_ids.T
    ld = hbm(log_decay.T)
    me = lax.axis_index("exp").reshape(1)
    keep = lax.optimization_barrier
    nz, nx = lax.axis_size("z"), lax.axis_size("x")

    cum, msg = local_states(hbm(key_vectors), hbm(values), ld)
    sent = exchange(msg, CTX)
    inside, qs = inside_blocks(hbm(queries), hbm(key_vectors), hbm(values), cum, ld)
    pieces, place_own = route_rows(me, ids, hbm(residual), hbm(out_gate), held)
    sent, inside, qs, pieces = keep((sent, inside, qs, pieces))
    prior = scan_blocks(hbm(sent), lax.axis_index(CTX))
    state = exchange(prior, CTX).reshape(heads, HEAD_DIM, HEAD_DIM)
    pieces = [pieces[0]] + [shift(pieces[d], "exp", d) for d in range(1, held)]
    pieces = [hbm(a) for a in pieces]
    place = place_rows(me, pieces, tokens)

    routed, attention = carried_blocks(me, inside, hbm(qs), state, hbm(place), held)
    routed = exchange(routed.reshape(held, held * CAP, width), "exp")
    one, two = routed_norm(me, routed, pieces, attn_gain, moe_gain, nz)

    others = range(1, nx)
    attention, one = keep((attention, one))
    ones = [one] + [shift(one, "x", d) for d in others]
    two = exchange(two, "z")
    ones, two = keep((ones, two))
    one = exchange(repeat(ones, nz), "z")
    twos = [two] + [shift(two, "x", d) for d in others]
    attention = [attention[0]] + [shift(attention[d], "exp", d) for d in range(1, held)]
    one, twos, attention = keep((one, twos, attention))

    act_own = expert_act(one, twos, w_gate, w_up)
    one, twos = shift(one, "core", 1), [shift(a, "core", 1) for a in twos]
    one, twos, act_own = keep((one, twos, act_own))
    other1, other2 = expert_down(expert_act(one, twos, w_gate, w_up), w_down, nz, nx)
    other1, other2, act_own = keep((other1, other2, act_own))
    own1, own2 = expert_down(act_own, w_down, nz, nx)
    (one,) = pair_sum(own1, shift(other1, "core", 1), False)
    twos = pair_sum(own2, shift(other2, "core", 1), True)

    one = exchange(one, "z")
    twos = [twos[0]] + [shift(twos[d], "x", -d) for d in others]
    one, twos = keep((one, twos))
    ones = block_sum(one)
    ones = [ones[0]] + [shift(ones[d], "x", -d) for d in others]
    two = exchange(stack_sum(twos), "z")
    hidden = hidden_rows(me, attention, hbm(residual), hbm(out_gate), attn_gain)
    back = exchange(row_sum(ones, two, held), "exp")
    moe_out = combine_rows(place_own, back, expert_ids, route_weights)
    return (hidden, moe_out)


def solution(mesh):
    cube = Mesh(mesh.devices.reshape(4, 4, 2, 4), ("z", "x", "core", "exp"))
    both = CTX + ("exp",)
    in_specs = (
        P(CTX, "exp"),
        P(CTX, "exp"),
        P(CTX, "exp"),
        P(CTX, "exp"),
        P(both, None),
        P(both, None),
        P(),
        P(),
        P(both, None),
        P(both, None),
        P("exp", None, CTX),
        P("exp", None, CTX),
        P("exp", CTX, None),
    )
    out_specs = (P(both, None), P(both, None))
    return jax.shard_map(local, mesh=cube, in_specs=in_specs, out_specs=out_specs, check_vma=False)
```

```python
import functools

import jax
import jax.numpy as jnp
from jax import lax
from jax.experimental import pallas as pl
from jax.experimental.pallas import tpu as pltpu
from jax.sharding import Mesh, PartitionSpec as P

HEAD_DIM = 128
CAP = 4
EPS = 1e-05
F32 = jnp.float32
BF16 = jnp.bfloat16
HIGHEST = lax.Precision.HIGHEST
CTX = ("z", "x", "core")
VMEM_LIMIT = 24 * 1024 * 1024


def iota(shape, dim):
    return lax.broadcasted_iota(jnp.int32, shape, dim)


def hbm(a):
    return pltpu.with_memory_space_constraint(a, pltpu.HBM)


def far(shape, dtype=BF16):
    return pltpu.HBM(shape, dtype)


def params(**kw):
    return pltpu.CompilerParams(vmem_limit_bytes=VMEM_LIMIT, **kw)


def cost(flops, bytes_accessed):
    return pl.CostEstimate(flops=flops, bytes_accessed=bytes_accessed, transcendentals=0)


def running_sum(ld, axis):
    rows = ld.shape[1]
    a, b = iota((rows, rows), 0), iota((rows, rows), 1)
    ones = (a >= b).astype(BF16)
    total = None
    rest = ld
    for _ in range(3):
        part = rest.astype(BF16)
        rest = rest - part.astype(F32)
        pair = (ones, part) if axis == 0 else (part, ones)
        term = lax.dot_general(*pair, (((1,), (1,)), ((), ())), preferred_element_type=F32)
        total = term if total is None else total + term
    return total


def spread(table, first, count, terms):
    n = table.shape[1]
    shape = (n, count * HEAD_DIM)
    pick = (iota(shape, 0) == first + iota(shape, 1) // HEAD_DIM).astype(BF16)
    total = None
    rest = table
    for _ in range(terms):
        part = rest.astype(BF16)
        rest = rest - part.astype(F32)
        term = jnp.dot(part, pick, preferred_element_type=F32)
        total = term if total is None else total + term
    return total


def state_kernel(group, k_ref, v_ref, ld_ref, cum_ref, msg_ref, fade_ref, decay_ref):
    heads, rows = ld_ref.shape
    per = heads * HEAD_DIM // 32
    parts = group * HEAD_DIM // per
    g = pl.program_id(0)

    @pl.when(g == 0)
    def _():
        cum = running_sum(ld_ref[...], 0)
        cum_ref[...] = cum
        final = cum[rows - 1 : rows, :]
        fade_ref[...] = jnp.exp(final - cum)
        decay_ref[...] = jnp.broadcast_to(jnp.exp(final), decay_ref.shape)

    fade = spread(fade_ref[...], g * group, group, 2)
    decay = spread(decay_ref[...], g * group, group, 2)
    row16 = iota((16, HEAD_DIM), 0)
    tiles = []
    for j in range(group):
        cols = slice(j * HEAD_DIM, (j + 1) * HEAD_DIM)
        wk = (k_ref[:, cols].astype(F32) * fade[:, cols]).astype(BF16)
        state = lax.dot_general(
            wk, v_ref[:, cols], (((0,), (0,)), ((), ())), preferred_element_type=F32
        ).astype(BF16)
        row = j * HEAD_DIM
        while row < (j + 1) * HEAD_DIM:
            part, at = row // per, row % per
            take = min(per - at, (j + 1) * HEAD_DIM - row)
            lo = row - j * HEAD_DIM
            msg_ref[part, at : at + take, :] = state[lo : lo + take, :]
            row += take
        whole = decay[:, cols]
        high = whole.astype(BF16).astype(F32)
        tiles.append((high, whole - high))
    for part in range(parts):
        first = per * part // HEAD_DIM
        last = (per * part + per - 1) // HEAD_DIM
        tile = jnp.where(
            row16 == 0,
            tiles[first][0],
            jnp.where(
                row16 == 1, tiles[first][1], jnp.where(row16 == 2, tiles[last][0], tiles[last][1])
            ),
        )
        msg_ref[part, per : per + 16, :] = tile.astype(BF16)


def local_states(k, v, ld, group=3):
    rows, width = k.shape
    heads = ld.shape[0]
    per = heads * HEAD_DIM // 32
    parts = group * HEAD_DIM // per
    block = pl.BlockSpec((rows, group * HEAD_DIM), lambda g: (0, g))
    return pl.pallas_call(
        functools.partial(state_kernel, group),
        grid=(heads // group,),
        out_shape=(
            jax.ShapeDtypeStruct((rows, heads), F32),
            far((32, per + 16, HEAD_DIM)),
        ),
        in_specs=[block, block, pl.BlockSpec((heads, rows), lambda g: (0, 0))],
        out_specs=(
            pl.BlockSpec((rows, heads), lambda g: (0, 0)),
            pl.BlockSpec((parts, per + 16, HEAD_DIM), lambda g: (g, 0, 0)),
        ),
        scratch_shapes=[pltpu.VMEM((rows, heads), F32), pltpu.VMEM((16, heads), F32)],
        compiler_params=params(),
        cost_estimate=cost(2 * rows * width * HEAD_DIM, 4 * rows * width),
        name="local_states",
    )(k, v, ld)


def scan_kernel(split_ref, in_ref, out_ref):
    parts, per, width = out_ref.shape
    first_rows = iota((per, width), 0) < split_ref[0]
    state = jnp.zeros((per, width), F32)
    for b in range(parts):
        out_ref[b, :, :] = state.astype(BF16)
        if b + 1 < parts:
            tail = in_ref[b, per : per + 16, :].astype(F32)
            d0 = tail[0:1, :] + tail[1:2, :]
            d1 = tail[2:3, :] + tail[3:4, :]
            decay = jnp.where(first_rows, d0, d1)
            state = decay * state + in_ref[b, 0:per, :].astype(F32)


def scan_blocks(msg, part):
    parts, tall, width = msg.shape
    per = tall - 16
    split = (HEAD_DIM - (per * part) % HEAD_DIM).astype(jnp.int32).reshape(1)
    return pl.pallas_call(
        scan_kernel,
        out_shape=far((parts, per, width)),
        in_specs=[
            pl.BlockSpec(memory_space=pltpu.SMEM),
            pl.BlockSpec(memory_space=pltpu.VMEM),
        ],
        out_specs=pl.BlockSpec(memory_space=pltpu.VMEM),
        compiler_params=params(),
        cost_estimate=cost(1000000, 1000000),
        name="scan_blocks",
    )(split, msg)


def inside_kernel(group, q_ref, k_ref, v_ref, cum_ref, ld_ref, inside_ref, qs_ref, cumt_ref):
    rows, heads = cum_ref.shape

    @pl.when(pl.program_id(0) == 0)
    def _():
        cumt_ref[...] = running_sum(ld_ref[...], 1)

    cum = spread(cum_ref[...], pl.program_id(0) * group, group, 3)
    size = 2 * HEAD_DIM
    causal = iota((size, size), 0) >= iota((size, size), 1)
    for j in range(group):
        h = pl.program_id(0) * group + j
        cols = slice(j * HEAD_DIM, (j + 1) * HEAD_DIM)
        col = cum[:, cols]
        row = cumt_ref[pl.ds(h, 1), :]
        q = q_ref[:, cols]
        k = k_ref[:, cols]
        v = v_ref[:, cols]
        qs_ref[:, cols] = (q.astype(F32) * jnp.exp(col)).astype(BF16)
        wide = jnp.concatenate([col, col], axis=1)
        total = None
        for lo in range(0, rows, size):
            hi = lo + size
            s = lax.dot_general(
                q[lo:], k[lo:hi], (((1,), (1,)), ((), ())), preferred_element_type=F32
            )
            decay = jnp.exp(jnp.minimum(wide[lo:] - row[:, lo:hi], 0.0))
            w = s * decay
            w = jnp.concatenate([jnp.where(causal, w[:size], 0.0), w[size:]], axis=0) if (
                hi < rows
            ) else jnp.where(causal, w, 0.0)
            part = jnp.dot(w.astype(BF16), v[lo:hi], preferred_element_type=F32)
            if total is None:
                total = part
            else:
                total = jnp.concatenate([total[:lo], total[lo:] + part], axis=0)
        inside_ref[:, cols] = total


def inside_blocks(q, k, v, cum, ld, group=3):
    rows, width = q.shape
    heads = cum.shape[1]
    block = pl.BlockSpec((rows, group * HEAD_DIM), lambda g: (0, g))
    return pl.pallas_call(
        functools.partial(inside_kernel, group),
        grid=(heads // group,),
        out_shape=(
            jax.ShapeDtypeStruct((rows, width), F32),
            far((rows, width)),
        ),
        in_specs=[
            block,
            block,
            block,
            pl.BlockSpec((rows, heads), lambda g: (0, 0)),
            pl.BlockSpec((heads, rows), lambda g: (0, 0)),
        ],
        out_specs=(block, block),
        scratch_shapes=[pltpu.VMEM((heads, rows), F32)],
        compiler_params=params(),
        cost_estimate=cost(4 * rows * rows * width, 12 * rows * width),
        name="inside_blocks",
    )(q, k, v, cum, ld)


def attend(group, inside_ref, qs_ref, state_ref, att_ref):
    for j in range(group):
        cols = slice(j * HEAD_DIM, (j + 1) * HEAD_DIM)
        att_ref[:, cols] = (
            inside_ref[:, cols]
            + jnp.dot(qs_ref[:, cols], state_ref[j], preferred_element_type=F32)
        ).astype(BF16)


def chosen_kernel(group, inside_ref, qs_ref, state_ref, place_ref, sel_ref, att_ref):
    attend(group, inside_ref, qs_ref, state_ref, att_ref)
    sel_ref[...] = jnp.dot(
        place_ref[...], att_ref[...], preferred_element_type=F32
    ).astype(BF16)


def carried_kernel(group, me_ref, inside_ref, qs_ref, state_ref, *refs):
    outs, att_ref = refs[:-1], refs[-1]
    held = len(outs)
    tokens = outs[0].shape[0]
    attend(group, inside_ref, qs_ref, state_ref, att_ref)
    for d in range(held):
        at = pl.multiple_of(lax.rem(me_ref[0] + d, held) * tokens, tokens)
        outs[d][...] = att_ref[pl.ds(at, tokens), :]


def chosen_rows(inside, qs, state, place, group=3):
    rows, width = inside.shape
    heads = width // HEAD_DIM
    chosen = place.shape[0]
    wide = group * HEAD_DIM
    block = pl.BlockSpec((rows, wide), lambda g: (0, g))
    return pl.pallas_call(
        functools.partial(chosen_kernel, group),
        grid=(heads // group,),
        out_shape=far((chosen, width)),
        in_specs=[
            block,
            block,
            pl.BlockSpec((group, HEAD_DIM, HEAD_DIM), lambda g: (g, 0, 0)),
            pl.BlockSpec((chosen, rows), lambda g: (0, 0)),
        ],
        out_specs=pl.BlockSpec((chosen, wide), lambda g: (0, g)),
        scratch_shapes=[pltpu.VMEM((rows, wide), BF16)],
        compiler_params=params(),
        cost_estimate=cost(4 * rows * width * HEAD_DIM, 8 * rows * width),
        name="chosen_rows",
    )(inside, qs, state, place)


def carried_blocks(me, inside, qs, state, held, group=3):
    rows, width = inside.shape
    heads = width // HEAD_DIM
    wide = group * HEAD_DIM
    tokens = rows // held
    block = pl.BlockSpec((rows, wide), lambda g: (0, g))
    return list(
        pl.pallas_call(
            functools.partial(carried_kernel, group),
            grid=(heads // group,),
            out_shape=(far((tokens, width)),) * held,
            in_specs=[
                pl.BlockSpec(memory_space=pltpu.SMEM),
                block,
                block,
                pl.BlockSpec((group, HEAD_DIM, HEAD_DIM), lambda g: (g, 0, 0)),
            ],
            out_specs=(pl.BlockSpec((tokens, wide), lambda g: (0, g)),) * held,
            scratch_shapes=[pltpu.VMEM((rows, wide), BF16)],
            compiler_params=params(),
            cost_estimate=cost(4 * rows * width * HEAD_DIM, 8 * rows * width),
            name="carried_blocks",
        )(me, inside, qs, state)
    )


def route_kernel(pieces, me_ref, ids_ref, res_hbm, gate_hbm, *refs):
    outs, (place_ref, res_ref, gate_ref, sem) = refs[:-4], refs[-4:]
    held = len(outs)
    size = res_ref.shape[0] // pieces
    copies = []
    for n, (a, b) in enumerate(((res_hbm, res_ref), (gate_hbm, gate_ref))):
        for i in range(pieces):
            at = pl.ds(i * size, size)
            copies.append(pltpu.make_async_copy(a.at[at], b.at[at], sem.at[n, i]))
    for c in copies:
        c.start()
    tokens, width = res_ref.shape
    me = me_ref[0]
    ids = ids_ref[...]
    hits = [
        ((ids[0:1, :] == e) | (ids[1:2, :] == e)).astype(F32) for e in range(held)
    ]
    m = jnp.concatenate(hits, axis=0)
    upto = (iota((tokens, tokens), 0) <= iota((tokens, tokens), 1)).astype(BF16)
    rank = jnp.dot(m.astype(BF16), upto, preferred_element_type=F32) - 1.0
    slot = iota((CAP, tokens), 0).astype(F32)
    places = [
        jnp.where(rank[e : e + 1, :] == slot, m[e : e + 1, :], 0.0) for e in range(held)
    ]
    place = jnp.concatenate(places, axis=0)
    place_ref[...] = place
    for c in copies:
        c.wait()
    ordered = []
    for d in range(held):
        expert = lax.rem(me + d, held)
        mine = places[0]
        for e in range(1, held):
            mine = jnp.where(expert == e, places[e], mine)
        ordered.append(mine)
    chosen = jnp.concatenate(ordered, axis=0).astype(BF16)
    res = jnp.dot(chosen, res_ref[...], preferred_element_type=F32)
    gate = jnp.dot(chosen, gate_ref[...], preferred_element_type=F32)
    for d in range(held):
        at = slice(d * CAP, (d + 1) * CAP)
        outs[d][:, 0:width] = jnp.concatenate([res[at], gate[at]], axis=0).astype(BF16)
        for n in range(2):
            outs[d][:, width + n * tokens : width + (n + 1) * tokens] = jnp.broadcast_to(
                ids[n : n + 1, :].astype(F32), (2 * CAP, tokens)
            ).astype(BF16)


def route_rows(me, ids, residual, out_gate, held, pieces=4):
    tokens, width = residual.shape
    whole = pl.BlockSpec(memory_space=pltpu.VMEM)
    away = pl.BlockSpec(memory_space=pl.ANY)
    piece = far((2 * CAP, width + 2 * tokens))
    outs = pl.pallas_call(
        functools.partial(route_kernel, pieces),
        out_shape=(piece,) * held + (jax.ShapeDtypeStruct((held * CAP, tokens), F32),),
        in_specs=[pl.BlockSpec(memory_space=pltpu.SMEM), whole, away, away],
        out_specs=(whole,) * (held + 1),
        scratch_shapes=[
            pltpu.VMEM((tokens, width), BF16),
            pltpu.VMEM((tokens, width), BF16),
            pltpu.SemaphoreType.DMA((2, pieces)),
        ],
        compiler_params=params(),
        cost_estimate=cost(64 * tokens * width, 5 * tokens * width),
        name="route_rows",
    )(me, ids, residual, out_gate)
    return outs[:-1], outs[-1]


def by_source(me, pieces, j):
    count = len(pieces)
    out = pieces[0]
    for d in range(1, count):
        out = jnp.where(lax.rem(me + count - d, count) == j, pieces[d], out)
    return out


def place_kernel(me_ref, *refs):
    pieces, place_ref = refs[:-1], refs[-1]
    held = len(pieces)
    tokens = pieces[0].shape[1] // 2
    total = held * tokens
    me = me_ref[0]
    tables = [p[...].astype(F32) for p in pieces]
    ordered = [by_source(me, tables, j) for j in range(held)]
    first = jnp.concatenate([a[0:1, :tokens] for a in ordered], axis=1)
    second = jnp.concatenate([a[0:1, tokens:] for a in ordered], axis=1)
    m = jnp.concatenate(
        [((first == float(e)) | (second == float(e))).astype(F32) for e in range(held)], axis=0
    )
    before = iota((total, total), 0)
    after = iota((total, total), 1)
    upto = ((before <= after) & (before // tokens == after // tokens)).astype(BF16)
    rank = jnp.dot(m.astype(BF16), upto, preferred_element_type=F32) - 1.0
    rows = held * CAP
    r = iota((rows, total), 0)
    t = iota((rows, total), 1)
    here = (t // tokens == r // CAP).astype(F32)
    slot = (r % CAP).astype(F32)
    for e in range(held):
        hit = jnp.where(rank[e : e + 1, :] == slot, m[e : e + 1, :] * here, 0.0)
        place_ref[e * rows : (e + 1) * rows, :] = hit.astype(BF16)


def place_rows(me, pieces, tokens):
    held = len(pieces)
    width = pieces[0].shape[1] - 2 * tokens
    at = width // (2 * tokens)
    return pl.pallas_call(
        place_kernel,
        grid=(1,),
        out_shape=far((held * held * CAP, held * tokens)),
        in_specs=[pl.BlockSpec(memory_space=pltpu.SMEM)]
        + [pl.BlockSpec((2 * CAP, 2 * tokens), lambda i: (0, at))] * held,
        out_specs=pl.BlockSpec((held * held * CAP, held * tokens), lambda i: (0, 0)),
        compiler_params=params(),
        cost_estimate=cost(1000000, 200000),
        name="place_rows",
    )(me, *pieces)


def gated(att, res, gate, attn_gain):
    norm = att * lax.rsqrt(jnp.mean(att * att, axis=-1, keepdims=True) + EPS) * attn_gain
    return (res + norm * jax.nn.sigmoid(gate)).astype(BF16)


def routed_norm_kernel(me_ref, att_ref, ag_ref, mg_ref, *refs):
    pieces, one_ref, two_ref = refs[:-2], refs[-2], refs[-1]
    sources, rows, part = att_ref.shape
    width = sources * part
    me = me_ref[0]
    att = jnp.concatenate([att_ref[s].astype(F32) for s in range(sources)], axis=1)
    tables = [p[...][:, :width].astype(F32) for p in pieces]
    ordered = [by_source(me, tables, j) for j in range(sources)]
    res = jnp.concatenate([a[:CAP] for a in ordered], axis=0)
    gate = jnp.concatenate([a[CAP:] for a in ordered], axis=0)
    hidden = gated(att, res, gate, ag_ref[...]).astype(F32)
    normed = (
        hidden * lax.rsqrt(jnp.mean(hidden * hidden, axis=-1, keepdims=True) + EPS) * mg_ref[...]
    ).astype(BF16)
    one_ref[...] = normed[:, : width // 2]
    for i in range(two_ref.shape[0]):
        two_ref[i] = normed[:, width // 2 :]


def routed_norm(me, att, pieces, attn_gain, moe_gain, copies):
    sources, rows, part = att.shape
    width = sources * part
    whole = pl.BlockSpec(memory_space=pltpu.VMEM)
    return pl.pallas_call(
        routed_norm_kernel,
        out_shape=(far((rows, width // 2)), far((copies, rows, width // 2))),
        in_specs=[pl.BlockSpec(memory_space=pltpu.SMEM)] + [whole] * (3 + len(pieces)),
        out_specs=(whole, whole),
        compiler_params=params(),
        cost_estimate=cost(20 * rows * width, 20 * rows * width),
        name="routed_norm",
    )(me, att, attn_gain, moe_gain, *pieces)


def hidden_kernel(me_ref, res_ref, gate_ref, ag_ref, *refs):
    pieces, out_ref = refs[:-1], refs[-1]
    me = me_ref[0]
    tables = [p[...].astype(F32) for p in pieces]
    att = jnp.concatenate([by_source(me, tables, j) for j in range(len(pieces))], axis=1)
    out_ref[...] = gated(att, res_ref[...].astype(F32), gate_ref[...].astype(F32), ag_ref[...])


def hidden_rows(me, pieces, residual, out_gate, attn_gain, tile=32):
    rows, part = pieces[0].shape
    width = len(pieces) * part
    block = pl.BlockSpec((tile, width), lambda i: (i, 0))
    return pl.pallas_call(
        hidden_kernel,
        grid=(rows // tile,),
        out_shape=jax.ShapeDtypeStruct((rows, width), BF16),
        in_specs=[
            pl.BlockSpec(memory_space=pltpu.SMEM),
            block,
            block,
            pl.BlockSpec((1, width), lambda i: (0, 0)),
        ]
        + [pl.BlockSpec((tile, part), lambda i: (i, 0))] * len(pieces),
        out_specs=block,
        compiler_params=params(),
        cost_estimate=cost(20 * rows * width, 8 * rows * width),
        name="hidden_rows",
    )(me, residual, out_gate, attn_gain, *pieces)


def repeat_kernel(*refs):
    ins, (out, sem) = refs[:-2], refs[-2:]
    copies = [
        pltpu.make_async_copy(a, out.at[n, k], sem.at[n, k])
        for n in range(out.shape[0])
        for k, a in enumerate(ins)
    ]
    for c in copies:
        c.start()
    for c in copies:
        c.wait()


def repeat(arrays, copies):
    rows, width = arrays[0].shape
    count = len(arrays)
    return pl.pallas_call(
        repeat_kernel,
        out_shape=far((copies, count, rows, width)),
        in_specs=[pl.BlockSpec(memory_space=pltpu.VMEM)] * count,
        out_specs=pl.BlockSpec(memory_space=pl.ANY),
        scratch_shapes=[pltpu.SemaphoreType.DMA((copies, count))],
        compiler_params=params(),
        cost_estimate=cost(0, 2 * (copies + 1) * count * rows * width),
        name="repeat",
    )(*arrays)


def act_kernel(steps, wg_hbm, wu_hbm, one_ref, *refs):
    twos, (act_ref, w_ref, sem) = refs[:-3], refs[-3:]
    units, width = wg_hbm.shape
    nz, nx, rows, half = one_ref.shape
    nt = (((1,), (1,)), ((), ()))
    wide = width // steps
    copies = []
    for s in range(steps):
        cols = pl.ds(s * wide, wide)
        for n, a in enumerate((wg_hbm, wu_hbm)):
            copies.append(
                pltpu.make_async_copy(a.at[:, cols], w_ref.at[n, :, cols], sem.at[s, n])
            )
    for c in copies:
        c.start()
    gate = up = None
    for s in range(steps):
        cols = slice(s * wide, (s + 1) * wide)
        copies[2 * s].wait()
        copies[2 * s + 1].wait()
        if s < steps // 2:
            x = [one_ref[z, k, :, cols] for k in range(nx) for z in range(nz)]
        else:
            near = slice(s * wide - half, (s + 1) * wide - half)
            x = [r[z, :, near] for r in twos for z in range(nz)]
        x = jnp.concatenate(x, axis=0)
        g = lax.dot_general(w_ref[0, :, cols], x, nt, preferred_element_type=F32)
        u = lax.dot_general(w_ref[1, :, cols], x, nt, preferred_element_type=F32)
        gate = g if gate is None else gate + g
        up = u if up is None else up + u
    act_ref[...] = (gate * jax.nn.sigmoid(gate) * up).T.astype(BF16)


def expert_act(one, twos, w_gate, w_up, steps=6):
    nz, nx, rows, half = one.shape
    count = nz * nx * rows
    units, width = w_gate.shape
    whole = pl.BlockSpec(memory_space=pltpu.VMEM)
    away = pl.BlockSpec(memory_space=pl.ANY)
    return pl.pallas_call(
        functools.partial(act_kernel, steps),
        out_shape=jax.ShapeDtypeStruct((count, units), BF16),
        in_specs=[away, away] + [whole] * (1 + len(twos)),
        out_specs=whole,
        scratch_shapes=[
            pltpu.VMEM((2, units, width), BF16),
            pltpu.SemaphoreType.DMA((steps, 2)),
        ],
        compiler_params=params(),
        cost_estimate=cost(4 * count * width * units, 4 * width * units + 2 * count * width),
        name="expert_act",
    )(hbm(w_gate), hbm(w_up), one, *twos)


def down_kernel(steps, first, by_x, act_ref, wd_hbm, *refs):
    wd_ref, sem = refs[-2:]
    half = wd_ref.shape[1]
    wide = half // steps
    copies = []
    for s in range(steps):
        cols = pl.ds(s * wide, wide)
        copies.append(
            pltpu.make_async_copy(
                wd_hbm.at[:, pl.ds(first + s * wide, wide)], wd_ref.at[:, cols], sem.at[s]
            )
        )
    for c in copies:
        c.start()
    refs = refs[:-2]
    added = refs[0] if len(refs) != 1 else None
    outs = refs[1:] if len(refs) != 1 else refs
    act = act_ref[...]
    if by_x:
        nx = outs[0].shape[0] if len(outs) == 1 else len(outs)
        nz = outs[0].shape[-3]
    else:
        nz, nx = outs[0].shape[:2]
    rows = outs[0].shape[-2]
    for s in range(steps):
        cols = slice(s * wide, (s + 1) * wide)
        copies[s].wait()
        out = jnp.dot(act, wd_ref[:, cols], preferred_element_type=F32)
        out = out.reshape(nx, nz, rows, wide)
        if by_x:
            if added is not None:
                out = out + added[:, :, :, cols].astype(F32)
            out = out.astype(BF16)
            if len(outs) == 1:
                outs[0][:, :, :, cols] = out
            else:
                for k in range(nx):
                    outs[k][:, :, cols] = out[k]
        else:
            for z in range(nz):
                part = out[:, z]
                if added is not None:
                    part = part + added[z, :, :, cols].astype(F32)
                outs[0][z, :, :, cols] = part.astype(BF16)


def expert_down(act, w_down, last, nz, nx, added=None, steps=3):
    count, units = act.shape
    half = w_down.shape[1] // 2
    rows = count // (nz * nx)
    whole = pl.BlockSpec(memory_space=pltpu.VMEM)
    if last:
        if added is None:
            shapes = (jax.ShapeDtypeStruct((nx, nz, rows, half), BF16),)
        else:
            shapes = (far((nz, rows, half)),) * nx
    elif added is None:
        shapes = (jax.ShapeDtypeStruct((nz, nx, rows, half), BF16),)
    else:
        shapes = (far((nz, nx, rows, half)),)
    more = () if added is None else (added,)
    return pl.pallas_call(
        functools.partial(down_kernel, steps, half if last else 0, last),
        out_shape=shapes,
        in_specs=[whole, pl.BlockSpec(memory_space=pl.ANY)] + [whole] * len(more),
        out_specs=(whole,) * len(shapes),
        scratch_shapes=[pltpu.VMEM((units, half), BF16), pltpu.SemaphoreType.DMA((steps,))],
        compiler_params=params(),
        cost_estimate=cost(2 * count * half * units, 2 * half * units + 2 * count * half),
        name="expert_down",
    )(act, hbm(w_down), *more)


def block_kernel(in_ref, *outs):
    total = in_ref[0].astype(F32)
    for i in range(1, in_ref.shape[0]):
        total = total + in_ref[i].astype(F32)
    total = total.astype(BF16)
    for n, out in enumerate(outs):
        out[...] = total[n]


def block_sum(parts, steps=2):
    count, n, rows, width = parts.shape
    wide = width // steps
    return pl.pallas_call(
        block_kernel,
        grid=(steps,),
        out_shape=(far((rows, width)),) * n,
        in_specs=[pl.BlockSpec((count, n, rows, wide), lambda i: (0, 0, 0, i))],
        out_specs=(pl.BlockSpec((rows, wide), lambda i: (0, i)),) * n,
        compiler_params=params(),
        cost_estimate=cost(count * n * rows * width, 2 * (count + 1) * n * rows * width),
        name="block_sum",
    )(parts)


def stack_kernel(*refs):
    total = refs[0][...].astype(F32)
    for ref in refs[1:-1]:
        total = total + ref[...].astype(F32)
    refs[-1][...] = total.astype(BF16)


def stack_sum(parts, steps=2):
    n, rows, width = parts[0].shape
    wide = width // steps
    block = pl.BlockSpec((n, rows, wide), lambda i: (0, 0, i))
    return pl.pallas_call(
        stack_kernel,
        grid=(steps,),
        out_shape=far(parts[0].shape),
        in_specs=[block] * len(parts),
        out_specs=block,
        compiler_params=params(),
        cost_estimate=cost(len(parts) * n * rows * width, 2 * (len(parts) + 1) * n * rows * width),
        name="stack_sum",
    )(*parts)


def row_sum_kernel(two_ref, *refs):
    parts, out_ref = refs[:-1], refs[-1]
    one = parts[0][...].astype(F32)
    for ref in parts[1:]:
        one = one + ref[...].astype(F32)
    two = two_ref[0].astype(F32)
    for i in range(1, two_ref.shape[0]):
        two = two + two_ref[i].astype(F32)
    half = one.shape[1]
    for j in range(out_ref.shape[0]):
        at = slice(j * CAP, (j + 1) * CAP)
        out_ref[j, :, :half] = one[at].astype(BF16)
        out_ref[j, :, half:] = two[at].astype(BF16)


def row_sum(parts, two, held):
    count, rows, half = two.shape
    whole = pl.BlockSpec(memory_space=pltpu.VMEM)
    return pl.pallas_call(
        row_sum_kernel,
        out_shape=far((held, CAP, 2 * half)),
        in_specs=[whole] * (1 + len(parts)),
        out_specs=whole,
        compiler_params=params(),
        cost_estimate=cost(8 * rows * half, 20 * rows * half),
        name="row_sum",
    )(two, *parts)


def combine_kernel(place_ref, rows_ref, ids_ref, weights_ref, out_ref):
    held = rows_ref.shape[0]
    rows = jnp.concatenate([rows_ref[e].astype(F32) for e in range(held)], axis=0).astype(BF16)
    back = lax.dot_general(
        place_ref[...].astype(BF16), rows, (((0,), (0,)), ((), ())), preferred_element_type=F32
    )
    chosen = jnp.sum(
        jnp.where(ids_ref[...] < held, weights_ref[...], 0.0), axis=1, keepdims=True
    )
    out_ref[...] = (back * chosen).astype(BF16)


def combine_rows(place, rows, ids, weights):
    tokens = ids.shape[0]
    width = rows.shape[2]
    return pl.pallas_call(
        combine_kernel,
        out_shape=jax.ShapeDtypeStruct((tokens, width), BF16),
        compiler_params=params(),
        cost_estimate=cost(32 * tokens * width, 2 * tokens * width),
        name="combine_rows",
    )(place, rows, ids, weights)


def exchange(a, axis):
    return lax.all_to_all(a, axis, split_axis=0, concat_axis=0, tiled=True)


def shift(a, axis, by):
    n = lax.axis_size(axis)
    return lax.ppermute(a, axis, [(i, (i + by) % n) for i in range(n)])


def local(
    queries,
    key_vectors,
    values,
    log_decay,
    out_gate,
    residual,
    attn_gain,
    moe_gain,
    expert_ids,
    route_weights,
    w_gate,
    w_up,
    w_down,
):
    held = lax.axis_size("exp")
    rows, width = queries.shape
    heads = log_decay.shape[1]
    tokens = residual.shape[0]
    attn_gain = attn_gain.reshape(1, -1)
    moe_gain = moe_gain.reshape(1, -1)
    w_gate = jnp.swapaxes(w_gate, 1, 2)[0]
    w_up = jnp.swapaxes(w_up, 1, 2)[0]
    w_down = w_down[0]
    ids = expert_ids.T
    ld = hbm(log_decay.T)
    me = lax.axis_index("exp").reshape(1)
    keep = lax.optimization_barrier
    nz, nx = lax.axis_size("z"), lax.axis_size("x")

    cum, msg = local_states(hbm(key_vectors), hbm(values), ld)
    sent = exchange(msg, CTX)
    inside, qs = inside_blocks(hbm(queries), hbm(key_vectors), hbm(values), cum, ld)
    pieces, place_own = route_rows(me, ids, hbm(residual), hbm(out_gate), held)
    sent, inside, qs, pieces = keep((sent, inside, qs, pieces))
    prior = scan_blocks(hbm(sent), lax.axis_index(CTX))
    state = exchange(prior, CTX).reshape(heads, HEAD_DIM, HEAD_DIM)
    pieces = [pieces[0]] + [shift(pieces[d], "exp", d) for d in range(1, held)]
    pieces = [hbm(a) for a in pieces]
    place = place_rows(me, pieces, tokens)

    routed = chosen_rows(inside, hbm(qs), state, hbm(place))
    _, inside, qs, state = keep((routed, inside, qs, state))
    routed = exchange(routed.reshape(held, held * CAP, width), "exp")
    attention = carried_blocks(me, inside, hbm(qs), state, held)
    routed, attention = keep((routed, attention))
    one, two = routed_norm(me, routed, pieces, attn_gain, moe_gain, nz)

    others = range(1, nx)
    ones = [one] + [shift(one, "x", d) for d in others]
    two = exchange(two, "z")
    across = shift(attention[2], "exp", 2)
    ones, two, across = keep((ones, two, across))
    one = exchange(repeat([hbm(ones[0])] + ones[1:], nz), "z")
    twos = [two] + [shift(two, "x", d) for d in others]
    right = shift(attention[1], "exp", 1)
    one, twos, right = keep((one, twos, right))

    act_own = expert_act(one, twos, w_gate, w_up)
    one, twos = shift(one, "core", 1), [shift(a, "core", 1) for a in twos]
    one, twos, act_own = keep((one, twos, act_own))
    act_far = expert_act(one, twos, w_gate, w_up)
    (two,) = expert_down(act_far, w_down, True, nz, nx)
    two, act_far = keep((two, act_far))
    (one,) = expert_down(act_far, w_down, False, nz, nx)
    one, two, act_own = keep((one, two, act_own))
    one, two = shift(one, "core", 1), shift(two, "core", 1)
    twos = expert_down(act_own, w_down, True, nz, nx, two)
    one, twos, act_own = keep((one, twos, act_own))
    (one,) = expert_down(act_own, w_down, False, nz, nx, one)

    one = exchange(one, "z")
    twos = [twos[0]] + [shift(twos[d], "x", -d) for d in others]
    left = shift(attention[3], "exp", 3)
    one, twos, left = keep((one, twos, left))
    attention = [attention[0], right, across, left]
    ones = block_sum(one)
    ones = [hbm(ones[0])] + [shift(ones[d], "x", -d) for d in others]
    two = exchange(stack_sum([hbm(twos[0])] + twos[1:]), "z")
    hidden = hidden_rows(me, attention, hbm(residual), hbm(out_gate), attn_gain)
    back = exchange(row_sum(ones, two, held), "exp")
    moe_out = combine_rows(place_own, back, expert_ids, route_weights)
    return (hidden, moe_out)


def solution(mesh):
    cube = Mesh(mesh.devices.reshape(4, 4, 2, 4), ("z", "x", "core", "exp"))
    both = CTX + ("exp",)
    in_specs = (
        P(CTX, "exp"),
        P(CTX, "exp"),
        P(CTX, "exp"),
        P(CTX, "exp"),
        P(both, None),
        P(both, None),
        P(),
        P(),
        P(both, None),
        P(both, None),
        P("exp", None, CTX),
        P("exp", None, CTX),
        P("exp", CTX, None),
    )
    out_specs = (P(both, None), P(both, None))
    return jax.shard_map(local, mesh=cube, in_specs=in_specs, out_specs=out_specs, check_vma=False)
```

```python
import functools

import jax
import jax.numpy as jnp
from jax import lax
from jax.experimental import pallas as pl
from jax.experimental.pallas import tpu as pltpu
from jax.sharding import Mesh, PartitionSpec as P

HEAD_DIM = 128
CAP = 4
EPS = 1e-05
F32 = jnp.float32
BF16 = jnp.bfloat16
HIGHEST = lax.Precision.HIGHEST
CTX = ("z", "x", "core")
VMEM_LIMIT = 24 * 1024 * 1024


def iota(shape, dim):
    return lax.broadcasted_iota(jnp.int32, shape, dim)


def hbm(a):
    return pltpu.with_memory_space_constraint(a, pltpu.HBM)


def far(shape, dtype=BF16):
    return pltpu.HBM(shape, dtype)


def params(**kw):
    return pltpu.CompilerParams(vmem_limit_bytes=VMEM_LIMIT, **kw)


def cost(flops, bytes_accessed):
    return pl.CostEstimate(flops=flops, bytes_accessed=bytes_accessed, transcendentals=0)


def running_sum(ld, axis):
    rows = ld.shape[1]
    a, b = iota((rows, rows), 0), iota((rows, rows), 1)
    ones = (a >= b).astype(BF16)
    total = None
    rest = ld
    for _ in range(3):
        part = rest.astype(BF16)
        rest = rest - part.astype(F32)
        pair = (ones, part) if axis == 0 else (part, ones)
        term = lax.dot_general(*pair, (((1,), (1,)), ((), ())), preferred_element_type=F32)
        total = term if total is None else total + term
    return total


def spread(table, first, count, terms):
    n = table.shape[1]
    shape = (n, count * HEAD_DIM)
    pick = (iota(shape, 0) == first + iota(shape, 1) // HEAD_DIM).astype(BF16)
    total = None
    rest = table
    for _ in range(terms):
        part = rest.astype(BF16)
        rest = rest - part.astype(F32)
        term = jnp.dot(part, pick, preferred_element_type=F32)
        total = term if total is None else total + term
    return total


def state_kernel(group, k_ref, v_ref, ld_ref, cum_ref, msg_ref, fade_ref, decay_ref):
    heads, rows = ld_ref.shape
    per = heads * HEAD_DIM // 32
    parts = group * HEAD_DIM // per
    g = pl.program_id(0)

    @pl.when(g == 0)
    def _():
        cum = running_sum(ld_ref[...], 0)
        cum_ref[...] = cum
        final = cum[rows - 1 : rows, :]
        fade_ref[...] = jnp.exp(final - cum)
        decay_ref[...] = jnp.broadcast_to(jnp.exp(final), decay_ref.shape)

    fade = spread(fade_ref[...], g * group, group, 2)
    decay = spread(decay_ref[...], g * group, group, 2)
    row16 = iota((16, HEAD_DIM), 0)
    tiles = []
    for j in range(group):
        cols = slice(j * HEAD_DIM, (j + 1) * HEAD_DIM)
        wk = (k_ref[:, cols].astype(F32) * fade[:, cols]).astype(BF16)
        state = lax.dot_general(
            wk, v_ref[:, cols], (((0,), (0,)), ((), ())), preferred_element_type=F32
        ).astype(BF16)
        row = j * HEAD_DIM
        while row < (j + 1) * HEAD_DIM:
            part, at = row // per, row % per
            take = min(per - at, (j + 1) * HEAD_DIM - row)
            lo = row - j * HEAD_DIM
            msg_ref[part, at : at + take, :] = state[lo : lo + take, :]
            row += take
        whole = decay[:, cols]
        high = whole.astype(BF16).astype(F32)
        tiles.append((high, whole - high))
    for part in range(parts):
        first = per * part // HEAD_DIM
        last = (per * part + per - 1) // HEAD_DIM
        tile = jnp.where(
            row16 == 0,
            tiles[first][0],
            jnp.where(
                row16 == 1, tiles[first][1], jnp.where(row16 == 2, tiles[last][0], tiles[last][1])
            ),
        )
        msg_ref[part, per : per + 16, :] = tile.astype(BF16)


def local_states(k, v, ld, group=3):
    rows, width = k.shape
    heads = ld.shape[0]
    per = heads * HEAD_DIM // 32
    parts = group * HEAD_DIM // per
    block = pl.BlockSpec((rows, group * HEAD_DIM), lambda g: (0, g))
    return pl.pallas_call(
        functools.partial(state_kernel, group),
        grid=(heads // group,),
        out_shape=(
            jax.ShapeDtypeStruct((rows, heads), F32),
            far((32, per + 16, HEAD_DIM)),
        ),
        in_specs=[block, block, pl.BlockSpec((heads, rows), lambda g: (0, 0))],
        out_specs=(
            pl.BlockSpec((rows, heads), lambda g: (0, 0)),
            pl.BlockSpec((parts, per + 16, HEAD_DIM), lambda g: (g, 0, 0)),
        ),
        scratch_shapes=[pltpu.VMEM((rows, heads), F32), pltpu.VMEM((16, heads), F32)],
        compiler_params=params(),
        cost_estimate=cost(2 * rows * width * HEAD_DIM, 4 * rows * width),
        name="local_states",
    )(k, v, ld)


def scan_kernel(split_ref, in_ref, out_ref):
    parts, per, width = out_ref.shape
    first_rows = iota((per, width), 0) < split_ref[0]
    state = jnp.zeros((per, width), F32)
    for b in range(parts):
        out_ref[b, :, :] = state.astype(BF16)
        if b + 1 < parts:
            tail = in_ref[b, per : per + 16, :].astype(F32)
            d0 = tail[0:1, :] + tail[1:2, :]
            d1 = tail[2:3, :] + tail[3:4, :]
            decay = jnp.where(first_rows, d0, d1)
            state = decay * state + in_ref[b, 0:per, :].astype(F32)


def scan_blocks(msg, part):
    parts, tall, width = msg.shape
    per = tall - 16
    split = (HEAD_DIM - (per * part) % HEAD_DIM).astype(jnp.int32).reshape(1)
    return pl.pallas_call(
        scan_kernel,
        out_shape=far((parts, per, width)),
        in_specs=[
            pl.BlockSpec(memory_space=pltpu.SMEM),
            pl.BlockSpec(memory_space=pltpu.VMEM),
        ],
        out_specs=pl.BlockSpec(memory_space=pltpu.VMEM),
        compiler_params=params(),
        cost_estimate=cost(1000000, 1000000),
        name="scan_blocks",
    )(split, msg)


def inside_kernel(group, q_ref, k_ref, v_ref, cum_ref, ld_ref, inside_ref, qs_ref, cumt_ref):
    rows, heads = cum_ref.shape

    @pl.when(pl.program_id(0) == 0)
    def _():
        cumt_ref[...] = running_sum(ld_ref[...], 1)

    cum = spread(cum_ref[...], pl.program_id(0) * group, group, 3)
    size = 2 * HEAD_DIM
    causal = iota((size, size), 0) >= iota((size, size), 1)
    for j in range(group):
        h = pl.program_id(0) * group + j
        cols = slice(j * HEAD_DIM, (j + 1) * HEAD_DIM)
        col = cum[:, cols]
        row = cumt_ref[pl.ds(h, 1), :]
        q = q_ref[:, cols]
        k = k_ref[:, cols]
        v = v_ref[:, cols]
        qs_ref[:, cols] = (q.astype(F32) * jnp.exp(col)).astype(BF16)
        wide = jnp.concatenate([col, col], axis=1)
        total = None
        for lo in range(0, rows, size):
            hi = lo + size
            s = lax.dot_general(
                q[lo:], k[lo:hi], (((1,), (1,)), ((), ())), preferred_element_type=F32
            )
            decay = jnp.exp(jnp.minimum(wide[lo:] - row[:, lo:hi], 0.0))
            w = s * decay
            w = jnp.concatenate([jnp.where(causal, w[:size], 0.0), w[size:]], axis=0) if (
                hi < rows
            ) else jnp.where(causal, w, 0.0)
            part = jnp.dot(w.astype(BF16), v[lo:hi], preferred_element_type=F32)
            if total is None:
                total = part
            else:
                total = jnp.concatenate([total[:lo], total[lo:] + part], axis=0)
        inside_ref[:, cols] = total


def inside_blocks(q, k, v, cum, ld, group=3):
    rows, width = q.shape
    heads = cum.shape[1]
    block = pl.BlockSpec((rows, group * HEAD_DIM), lambda g: (0, g))
    return pl.pallas_call(
        functools.partial(inside_kernel, group),
        grid=(heads // group,),
        out_shape=(
            jax.ShapeDtypeStruct((rows, width), F32),
            far((rows, width)),
        ),
        in_specs=[
            block,
            block,
            block,
            pl.BlockSpec((rows, heads), lambda g: (0, 0)),
            pl.BlockSpec((heads, rows), lambda g: (0, 0)),
        ],
        out_specs=(block, block),
        scratch_shapes=[pltpu.VMEM((heads, rows), F32)],
        compiler_params=params(),
        cost_estimate=cost(4 * rows * rows * width, 12 * rows * width),
        name="inside_blocks",
    )(q, k, v, cum, ld)


def attend(group, inside_ref, qs_ref, state_ref, att_ref):
    for j in range(group):
        cols = slice(j * HEAD_DIM, (j + 1) * HEAD_DIM)
        att_ref[:, cols] = (
            inside_ref[:, cols]
            + jnp.dot(qs_ref[:, cols], state_ref[j], preferred_element_type=F32)
        ).astype(BF16)


def chosen_kernel(group, inside_ref, qs_hbm, state_ref, place_ref, sel_ref, att_ref, qs_ref, sem):
    wide = group * HEAD_DIM
    steps = sel_ref.shape[1] // wide
    copies = []
    for g in range(steps):
        cols = pl.ds(g * wide, wide)
        copies.append(pltpu.make_async_copy(qs_hbm.at[:, cols], qs_ref.at[:, cols], sem.at[g]))
    for c in copies:
        c.start()
    for g in range(steps):
        cols = slice(g * wide, (g + 1) * wide)
        copies[g].wait()
        attend(
            group,
            inside_ref.at[:, cols],
            qs_ref.at[:, cols],
            state_ref.at[g * group : (g + 1) * group],
            att_ref,
        )
        sel_ref[:, cols] = jnp.dot(
            place_ref[...], att_ref[...], preferred_element_type=F32
        ).astype(BF16)


def carried_kernel(group, me_ref, inside_ref, qs_ref, state_ref, *refs):
    outs, att_ref = refs[:-1], refs[-1]
    held = len(outs)
    tokens = outs[0].shape[0]
    attend(group, inside_ref, qs_ref, state_ref, att_ref)
    for d in range(held):
        at = pl.multiple_of(lax.rem(me_ref[0] + d, held) * tokens, tokens)
        outs[d][...] = att_ref[pl.ds(at, tokens), :]


def chosen_rows(inside, qs, state, place, group=3):
    rows, width = inside.shape
    chosen = place.shape[0]
    wide = group * HEAD_DIM
    whole = pl.BlockSpec(memory_space=pltpu.VMEM)
    return pl.pallas_call(
        functools.partial(chosen_kernel, group),
        out_shape=far((chosen, width)),
        in_specs=[whole, pl.BlockSpec(memory_space=pl.ANY), whole, whole],
        out_specs=whole,
        scratch_shapes=[
            pltpu.VMEM((rows, wide), BF16),
            pltpu.VMEM((rows, width), BF16),
            pltpu.SemaphoreType.DMA((width // wide,)),
        ],
        compiler_params=params(),
        cost_estimate=cost(4 * rows * width * HEAD_DIM, 8 * rows * width),
        name="chosen_rows",
    )(inside, qs, state, place)


def carried_blocks(me, inside, qs, state, held, group=3):
    rows, width = inside.shape
    heads = width // HEAD_DIM
    wide = group * HEAD_DIM
    tokens = rows // held
    block = pl.BlockSpec((rows, wide), lambda g: (0, g))
    return list(
        pl.pallas_call(
            functools.partial(carried_kernel, group),
            grid=(heads // group,),
            out_shape=(far((tokens, width)),) * held,
            in_specs=[
                pl.BlockSpec(memory_space=pltpu.SMEM),
                block,
                block,
                pl.BlockSpec((group, HEAD_DIM, HEAD_DIM), lambda g: (g, 0, 0)),
            ],
            out_specs=(pl.BlockSpec((tokens, wide), lambda g: (0, g)),) * held,
            scratch_shapes=[pltpu.VMEM((rows, wide), BF16)],
            compiler_params=params(),
            cost_estimate=cost(4 * rows * width * HEAD_DIM, 8 * rows * width),
            name="carried_blocks",
        )(me, inside, qs, state)
    )


def route_kernel(pieces, me_ref, ids_ref, res_hbm, gate_hbm, *refs):
    outs, (place_ref, res_ref, gate_ref, sem) = refs[:-4], refs[-4:]
    held = len(outs)
    size = res_ref.shape[0] // pieces
    copies = []
    for n, (a, b) in enumerate(((res_hbm, res_ref), (gate_hbm, gate_ref))):
        for i in range(pieces):
            at = pl.ds(i * size, size)
            copies.append(pltpu.make_async_copy(a.at[at], b.at[at], sem.at[n, i]))
    for c in copies:
        c.start()
    tokens, width = res_ref.shape
    me = me_ref[0]
    ids = ids_ref[...]
    hits = [
        ((ids[0:1, :] == e) | (ids[1:2, :] == e)).astype(F32) for e in range(held)
    ]
    m = jnp.concatenate(hits, axis=0)
    upto = (iota((tokens, tokens), 0) <= iota((tokens, tokens), 1)).astype(BF16)
    rank = jnp.dot(m.astype(BF16), upto, preferred_element_type=F32) - 1.0
    slot = iota((CAP, tokens), 0).astype(F32)
    places = [
        jnp.where(rank[e : e + 1, :] == slot, m[e : e + 1, :], 0.0) for e in range(held)
    ]
    place = jnp.concatenate(places, axis=0)
    place_ref[...] = place
    for c in copies:
        c.wait()
    ordered = []
    for d in range(held):
        expert = lax.rem(me + d, held)
        mine = places[0]
        for e in range(1, held):
            mine = jnp.where(expert == e, places[e], mine)
        ordered.append(mine)
    chosen = jnp.concatenate(ordered, axis=0).astype(BF16)
    res = jnp.dot(chosen, res_ref[...], preferred_element_type=F32)
    gate = jnp.dot(chosen, gate_ref[...], preferred_element_type=F32)
    for d in range(held):
        at = slice(d * CAP, (d + 1) * CAP)
        outs[d][:, 0:width] = jnp.concatenate([res[at], gate[at]], axis=0).astype(BF16)
        for n in range(2):
            outs[d][:, width + n * tokens : width + (n + 1) * tokens] = jnp.broadcast_to(
                ids[n : n + 1, :].astype(F32), (2 * CAP, tokens)
            ).astype(BF16)


def route_rows(me, ids, residual, out_gate, held, pieces=4):
    tokens, width = residual.shape
    whole = pl.BlockSpec(memory_space=pltpu.VMEM)
    away = pl.BlockSpec(memory_space=pl.ANY)
    piece = far((2 * CAP, width + 2 * tokens))
    outs = pl.pallas_call(
        functools.partial(route_kernel, pieces),
        out_shape=(piece,) * held + (jax.ShapeDtypeStruct((held * CAP, tokens), F32),),
        in_specs=[pl.BlockSpec(memory_space=pltpu.SMEM), whole, away, away],
        out_specs=(whole,) * (held + 1),
        scratch_shapes=[
            pltpu.VMEM((tokens, width), BF16),
            pltpu.VMEM((tokens, width), BF16),
            pltpu.SemaphoreType.DMA((2, pieces)),
        ],
        compiler_params=params(),
        cost_estimate=cost(64 * tokens * width, 5 * tokens * width),
        name="route_rows",
    )(me, ids, residual, out_gate)
    return outs[:-1], outs[-1]


def by_source(me, pieces, j):
    count = len(pieces)
    out = pieces[0]
    for d in range(1, count):
        out = jnp.where(lax.rem(me + count - d, count) == j, pieces[d], out)
    return out


def place_kernel(me_ref, *refs):
    pieces, place_ref = refs[:-1], refs[-1]
    held = len(pieces)
    tokens = pieces[0].shape[1] // 2
    total = held * tokens
    me = me_ref[0]
    tables = [p[...].astype(F32) for p in pieces]
    ordered = [by_source(me, tables, j) for j in range(held)]
    first = jnp.concatenate([a[0:1, :tokens] for a in ordered], axis=1)
    second = jnp.concatenate([a[0:1, tokens:] for a in ordered], axis=1)
    m = jnp.concatenate(
        [((first == float(e)) | (second == float(e))).astype(F32) for e in range(held)], axis=0
    )
    before = iota((total, total), 0)
    after = iota((total, total), 1)
    upto = ((before <= after) & (before // tokens == after // tokens)).astype(BF16)
    rank = jnp.dot(m.astype(BF16), upto, preferred_element_type=F32) - 1.0
    rows = held * CAP
    r = iota((rows, total), 0)
    t = iota((rows, total), 1)
    here = (t // tokens == r // CAP).astype(F32)
    slot = (r % CAP).astype(F32)
    for e in range(held):
        hit = jnp.where(rank[e : e + 1, :] == slot, m[e : e + 1, :] * here, 0.0)
        place_ref[e * rows : (e + 1) * rows, :] = hit.astype(BF16)


def place_rows(me, pieces, tokens):
    held = len(pieces)
    width = pieces[0].shape[1] - 2 * tokens
    at = width // (2 * tokens)
    return pl.pallas_call(
        place_kernel,
        grid=(1,),
        out_shape=far((held * held * CAP, held * tokens)),
        in_specs=[pl.BlockSpec(memory_space=pltpu.SMEM)]
        + [pl.BlockSpec((2 * CAP, 2 * tokens), lambda i: (0, at))] * held,
        out_specs=pl.BlockSpec((held * held * CAP, held * tokens), lambda i: (0, 0)),
        compiler_params=params(),
        cost_estimate=cost(1000000, 200000),
        name="place_rows",
    )(me, *pieces)


def gated(att, res, gate, attn_gain):
    norm = att * lax.rsqrt(jnp.mean(att * att, axis=-1, keepdims=True) + EPS) * attn_gain
    return (res + norm * jax.nn.sigmoid(gate)).astype(BF16)


def routed_norm_kernel(me_ref, att_ref, ag_ref, mg_ref, *refs):
    pieces, one_ref, two_ref = refs[:-2], refs[-2], refs[-1]
    sources, rows, part = att_ref.shape
    width = sources * part
    me = me_ref[0]
    att = jnp.concatenate([att_ref[s].astype(F32) for s in range(sources)], axis=1)
    tables = [p[...][:, :width].astype(F32) for p in pieces]
    ordered = [by_source(me, tables, j) for j in range(sources)]
    res = jnp.concatenate([a[:CAP] for a in ordered], axis=0)
    gate = jnp.concatenate([a[CAP:] for a in ordered], axis=0)
    hidden = gated(att, res, gate, ag_ref[...]).astype(F32)
    normed = (
        hidden * lax.rsqrt(jnp.mean(hidden * hidden, axis=-1, keepdims=True) + EPS) * mg_ref[...]
    ).astype(BF16)
    one_ref[...] = normed[:, : width // 2]
    for i in range(two_ref.shape[0]):
        two_ref[i] = normed[:, width // 2 :]


def routed_norm(me, att, pieces, attn_gain, moe_gain, copies):
    sources, rows, part = att.shape
    width = sources * part
    whole = pl.BlockSpec(memory_space=pltpu.VMEM)
    return pl.pallas_call(
        routed_norm_kernel,
        out_shape=(far((rows, width // 2)), far((copies, rows, width // 2))),
        in_specs=[pl.BlockSpec(memory_space=pltpu.SMEM)] + [whole] * (3 + len(pieces)),
        out_specs=(whole, whole),
        compiler_params=params(),
        cost_estimate=cost(20 * rows * width, 20 * rows * width),
        name="routed_norm",
    )(me, att, attn_gain, moe_gain, *pieces)


def hidden_kernel(me_ref, res_ref, gate_ref, ag_ref, *refs):
    pieces, out_ref = refs[:-1], refs[-1]
    me = me_ref[0]
    tables = [p[...].astype(F32) for p in pieces]
    att = jnp.concatenate([by_source(me, tables, j) for j in range(len(pieces))], axis=1)
    out_ref[...] = gated(att, res_ref[...].astype(F32), gate_ref[...].astype(F32), ag_ref[...])


def hidden_rows(me, pieces, residual, out_gate, attn_gain, tile=32):
    rows, part = pieces[0].shape
    width = len(pieces) * part
    block = pl.BlockSpec((tile, width), lambda i: (i, 0))
    return pl.pallas_call(
        hidden_kernel,
        grid=(rows // tile,),
        out_shape=jax.ShapeDtypeStruct((rows, width), BF16),
        in_specs=[
            pl.BlockSpec(memory_space=pltpu.SMEM),
            block,
            block,
            pl.BlockSpec((1, width), lambda i: (0, 0)),
        ]
        + [pl.BlockSpec((tile, part), lambda i: (i, 0))] * len(pieces),
        out_specs=block,
        compiler_params=params(),
        cost_estimate=cost(20 * rows * width, 8 * rows * width),
        name="hidden_rows",
    )(me, residual, out_gate, attn_gain, *pieces)


def repeat_kernel(*refs):
    ins, (out, sem) = refs[:-2], refs[-2:]
    copies = [
        pltpu.make_async_copy(a, out.at[n, k], sem.at[n, k])
        for n in range(out.shape[0])
        for k, a in enumerate(ins)
    ]
    for c in copies:
        c.start()
    for c in copies:
        c.wait()


def repeat(arrays, copies):
    rows, width = arrays[0].shape
    count = len(arrays)
    return pl.pallas_call(
        repeat_kernel,
        out_shape=far((copies, count, rows, width)),
        in_specs=[pl.BlockSpec(memory_space=pltpu.VMEM)] * count,
        out_specs=pl.BlockSpec(memory_space=pl.ANY),
        scratch_shapes=[pltpu.SemaphoreType.DMA((copies, count))],
        compiler_params=params(),
        cost_estimate=cost(0, 2 * (copies + 1) * count * rows * width),
        name="repeat",
    )(*arrays)


def act_rows(steps, w_ref, one_ref, twos, arrived):
    width = w_ref.shape[2]
    nz, nx, rows, half = one_ref.shape
    nt = (((1,), (1,)), ((), ()))
    wide = width // steps
    gate = up = None
    for s in range(steps):
        cols = slice(s * wide, (s + 1) * wide)
        arrived(s)
        if s < steps // 2:
            x = [one_ref[z, k, :, cols] for k in range(nx) for z in range(nz)]
        else:
            near = slice(s * wide - half, (s + 1) * wide - half)
            x = [r[z, :, near] for r in twos for z in range(nz)]
        x = jnp.concatenate(x, axis=0)
        g = lax.dot_general(w_ref[0, :, cols], x, nt, preferred_element_type=F32)
        u = lax.dot_general(w_ref[1, :, cols], x, nt, preferred_element_type=F32)
        gate = g if gate is None else gate + g
        up = u if up is None else up + u
    return (gate * jax.nn.sigmoid(gate) * up).T.astype(BF16)


def first_act_kernel(steps, wg_hbm, wu_hbm, one_ref, *refs):
    twos, (act_ref, w_ref, sem) = refs[:-3], refs[-3:]
    wide = w_ref.shape[2] // steps
    copies = []
    for s in range(steps):
        cols = pl.ds(s * wide, wide)
        for n, a in enumerate((wg_hbm, wu_hbm)):
            copies.append(
                pltpu.make_async_copy(a.at[:, cols], w_ref.at[n, :, cols], sem.at[s, n])
            )
    for c in copies:
        c.start()

    def arrived(s):
        copies[2 * s].wait()
        copies[2 * s + 1].wait()

    act_ref[...] = act_rows(steps, w_ref, one_ref, twos, arrived)


def next_act_kernel(steps, w_ref, one_ref, *refs):
    refs[-1][...] = act_rows(steps, w_ref, one_ref, refs[:-1], lambda s: None)


def expert_act(one, twos, weights, steps=6):
    nz, nx, rows, half = one.shape
    count = nz * nx * rows
    whole = pl.BlockSpec(memory_space=pltpu.VMEM)
    away = pl.BlockSpec(memory_space=pl.ANY)
    if isinstance(weights, tuple):
        units, width = weights[0].shape
        return pl.pallas_call(
            functools.partial(first_act_kernel, steps),
            out_shape=(
                jax.ShapeDtypeStruct((count, units), BF16),
                pltpu.VMEM((2, units, width), BF16),
            ),
            in_specs=[away, away] + [whole] * (1 + len(twos)),
            out_specs=(whole, whole),
            scratch_shapes=[pltpu.SemaphoreType.DMA((steps, 2))],
            compiler_params=params(),
            cost_estimate=cost(4 * count * width * units, 4 * width * units + 2 * count * width),
            name="first_act",
        )(hbm(weights[0]), hbm(weights[1]), one, *twos)
    _, units, width = weights.shape
    return pl.pallas_call(
        functools.partial(next_act_kernel, steps),
        out_shape=jax.ShapeDtypeStruct((count, units), BF16),
        in_specs=[whole] * (2 + len(twos)),
        out_specs=whole,
        compiler_params=params(),
        cost_estimate=cost(4 * count * width * units, 2 * count * width),
        name="next_act",
    )(pltpu.with_memory_space_constraint(weights, pltpu.VMEM), one, *twos)


def down_kernel(steps, first, by_x, act_ref, wd_hbm, *refs):
    wd_ref, sem = refs[-2:]
    half = wd_ref.shape[1]
    wide = half // steps
    copies = []
    for s in range(steps):
        cols = pl.ds(s * wide, wide)
        copies.append(
            pltpu.make_async_copy(
                wd_hbm.at[:, pl.ds(first + s * wide, wide)], wd_ref.at[:, cols], sem.at[s]
            )
        )
    for c in copies:
        c.start()
    refs = refs[:-2]
    added = refs[0] if len(refs) != 1 else None
    outs = refs[1:] if len(refs) != 1 else refs
    act = act_ref[...]
    if by_x:
        nx = outs[0].shape[0] if len(outs) == 1 else len(outs)
        nz = outs[0].shape[-3]
    else:
        nz, nx = outs[0].shape[:2]
    rows = outs[0].shape[-2]
    for s in range(steps):
        cols = slice(s * wide, (s + 1) * wide)
        copies[s].wait()
        out = jnp.dot(act, wd_ref[:, cols], preferred_element_type=F32)
        out = out.reshape(nx, nz, rows, wide)
        if by_x:
            if added is not None:
                out = out + added[:, :, :, cols].astype(F32)
            out = out.astype(BF16)
            if len(outs) == 1:
                outs[0][:, :, :, cols] = out
            else:
                for k in range(nx):
                    outs[k][:, :, cols] = out[k]
        else:
            for z in range(nz):
                part = out[:, z]
                if added is not None:
                    part = part + added[z, :, :, cols].astype(F32)
                outs[0][z, :, :, cols] = part.astype(BF16)


def expert_down(act, w_down, cut, last, nz, nx, added=None, steps=2):
    count, units = act.shape
    half = w_down.shape[1] - cut if last else cut
    rows = count // (nz * nx)
    whole = pl.BlockSpec(memory_space=pltpu.VMEM)
    if last:
        if added is None:
            shapes = (jax.ShapeDtypeStruct((nx, nz, rows, half), BF16),)
        else:
            shapes = (far((nz, rows, half)),) * nx
    elif added is None:
        shapes = (jax.ShapeDtypeStruct((nz, nx, rows, half), BF16),)
    else:
        shapes = (far((nz, nx, rows, half)),)
    more = () if added is None else (added,)
    return pl.pallas_call(
        functools.partial(down_kernel, steps, cut if last else 0, last),
        out_shape=shapes,
        in_specs=[whole, pl.BlockSpec(memory_space=pl.ANY)] + [whole] * len(more),
        out_specs=(whole,) * len(shapes),
        scratch_shapes=[pltpu.VMEM((units, half), BF16), pltpu.SemaphoreType.DMA((steps,))],
        compiler_params=params(),
        cost_estimate=cost(2 * count * half * units, 2 * half * units + 2 * count * half),
        name="expert_down",
    )(act, hbm(w_down), *more)


def block_kernel(in_ref, *outs):
    total = in_ref[0].astype(F32)
    for i in range(1, in_ref.shape[0]):
        total = total + in_ref[i].astype(F32)
    total = total.astype(BF16)
    for n, out in enumerate(outs):
        out[...] = total[n]


def block_sum(parts, steps=2):
    count, n, rows, width = parts.shape
    wide = width // steps
    return pl.pallas_call(
        block_kernel,
        grid=(steps,),
        out_shape=(far((rows, width)),) * n,
        in_specs=[pl.BlockSpec((count, n, rows, wide), lambda i: (0, 0, 0, i))],
        out_specs=(pl.BlockSpec((rows, wide), lambda i: (0, i)),) * n,
        compiler_params=params(),
        cost_estimate=cost(count * n * rows * width, 2 * (count + 1) * n * rows * width),
        name="block_sum",
    )(parts)


def stack_kernel(*refs):
    total = refs[0][...].astype(F32)
    for ref in refs[1:-1]:
        total = total + ref[...].astype(F32)
    refs[-1][...] = total.astype(BF16)


def stack_sum(parts, steps=2):
    n, rows, width = parts[0].shape
    wide = width // steps
    block = pl.BlockSpec((n, rows, wide), lambda i: (0, 0, i))
    return pl.pallas_call(
        stack_kernel,
        grid=(steps,),
        out_shape=far(parts[0].shape),
        in_specs=[block] * len(parts),
        out_specs=block,
        compiler_params=params(),
        cost_estimate=cost(len(parts) * n * rows * width, 2 * (len(parts) + 1) * n * rows * width),
        name="stack_sum",
    )(*parts)


def row_sum_kernel(two_ref, *refs):
    parts, out_ref = refs[:-1], refs[-1]
    one = parts[0][...].astype(F32)
    for ref in parts[1:]:
        one = one + ref[...].astype(F32)
    two = two_ref[0].astype(F32)
    for i in range(1, two_ref.shape[0]):
        two = two + two_ref[i].astype(F32)
    cut = one.shape[1]
    for j in range(out_ref.shape[0]):
        at = slice(j * CAP, (j + 1) * CAP)
        out_ref[j, :, :cut] = one[at].astype(BF16)
        out_ref[j, :, cut:] = two[at].astype(BF16)


def row_sum(parts, two, held):
    count, rows, half = two.shape
    whole = pl.BlockSpec(memory_space=pltpu.VMEM)
    return pl.pallas_call(
        row_sum_kernel,
        out_shape=far((held, CAP, parts[0].shape[1] + half)),
        in_specs=[whole] * (1 + len(parts)),
        out_specs=whole,
        compiler_params=params(),
        cost_estimate=cost(8 * rows * half, 20 * rows * half),
        name="row_sum",
    )(two, *parts)


def combine_kernel(place_ref, rows_ref, ids_ref, weights_ref, out_ref):
    held = rows_ref.shape[0]
    rows = jnp.concatenate([rows_ref[e].astype(F32) for e in range(held)], axis=0).astype(BF16)
    back = lax.dot_general(
        place_ref[...].astype(BF16), rows, (((0,), (0,)), ((), ())), preferred_element_type=F32
    )
    chosen = jnp.sum(
        jnp.where(ids_ref[...] < held, weights_ref[...], 0.0), axis=1, keepdims=True
    )
    out_ref[...] = (back * chosen).astype(BF16)


def combine_rows(place, rows, ids, weights):
    tokens = ids.shape[0]
    width = rows.shape[2]
    return pl.pallas_call(
        combine_kernel,
        out_shape=jax.ShapeDtypeStruct((tokens, width), BF16),
        compiler_params=params(),
        cost_estimate=cost(32 * tokens * width, 2 * tokens * width),
        name="combine_rows",
    )(place, rows, ids, weights)


def exchange(a, axis):
    return lax.all_to_all(a, axis, split_axis=0, concat_axis=0, tiled=True)


def shift(a, axis, by):
    n = lax.axis_size(axis)
    return lax.ppermute(a, axis, [(i, (i + by) % n) for i in range(n)])


def local(
    queries,
    key_vectors,
    values,
    log_decay,
    out_gate,
    residual,
    attn_gain,
    moe_gain,
    expert_ids,
    route_weights,
    w_gate,
    w_up,
    w_down,
):
    held = lax.axis_size("exp")
    rows, width = queries.shape
    heads = log_decay.shape[1]
    tokens = residual.shape[0]
    attn_gain = hbm(attn_gain.reshape(1, -1))
    moe_gain = hbm(moe_gain.reshape(1, -1))
    w_gate = jnp.swapaxes(w_gate, 1, 2)[0]
    w_up = jnp.swapaxes(w_up, 1, 2)[0]
    w_down = w_down[0]
    ids = expert_ids.T
    ld = hbm(log_decay.T)
    me = lax.axis_index("exp").reshape(1)
    keep = lax.optimization_barrier
    nz, nx = lax.axis_size("z"), lax.axis_size("x")

    cum, msg = local_states(hbm(key_vectors), hbm(values), ld)
    sent = exchange(msg, CTX)
    inside, qs = inside_blocks(hbm(queries), hbm(key_vectors), hbm(values), cum, ld)
    pieces, place_own = route_rows(me, ids, hbm(residual), hbm(out_gate), held)
    sent, inside, qs, pieces = keep((sent, inside, qs, pieces))
    prior = scan_blocks(hbm(sent), lax.axis_index(CTX))
    state = exchange(prior, CTX).reshape(heads, HEAD_DIM, HEAD_DIM)
    pieces = [pieces[0]] + [shift(pieces[d], "exp", d) for d in range(1, held)]
    pieces = [hbm(a) for a in pieces]
    place = place_rows(me, pieces, tokens)

    routed = chosen_rows(inside, hbm(qs), state, hbm(place))
    _, inside, qs, state = keep((routed, inside, qs, state))
    routed = exchange(routed.reshape(held, held * CAP, width), "exp")
    attention = carried_blocks(me, inside, hbm(qs), state, held)
    routed, attention = keep((routed, attention))
    one, two = routed_norm(me, routed, pieces, attn_gain, moe_gain, nz)

    others = range(1, nx)
    ones = [one] + [shift(one, "x", d) for d in others]
    two = exchange(two, "z")
    across = shift(attention[2], "exp", 2)
    ones, two, across = keep((ones, two, across))
    one = exchange(repeat([hbm(ones[0])] + ones[1:], nz), "z")
    twos = [two] + [shift(two, "x", d) for d in others]
    right, left = shift(attention[1], "exp", 1), shift(attention[3], "exp", 3)
    one, twos, right, left = keep((one, twos, right, left))

    cut = moe_gain.shape[1] * 7 // 12
    act_own, weights = expert_act(one, twos, (w_gate, w_up))
    one, twos = shift(one, "core", 1), [shift(a, "core", 1) for a in twos]
    one, twos, weights = keep((one, twos, weights))
    act_far = expert_act(one, twos, weights)
    (one,) = expert_down(act_far, w_down, cut, False, nz, nx)
    one, act_far = keep((one, act_far))
    (two,) = expert_down(act_far, w_down, cut, True, nz, nx)
    one, two, act_own = keep((one, two, act_own))
    one, two = shift(one, "core", 1), shift(two, "core", 1)
    (one,) = expert_down(act_own, w_down, cut, False, nz, nx, one)
    one, two, act_own = keep((one, two, act_own))
    twos = expert_down(act_own, w_down, cut, True, nz, nx, two)

    one = exchange(one, "z")
    twos = [twos[0]] + [shift(twos[d], "x", -d) for d in others]
    one, twos = keep((one, twos))
    attention = [attention[0], right, across, left]
    ones = block_sum(one)
    ones = [hbm(ones[0])] + [shift(ones[d], "x", -d) for d in others]
    two = exchange(stack_sum([hbm(twos[0])] + twos[1:]), "z")
    hidden = hidden_rows(me, attention, hbm(residual), hbm(out_gate), attn_gain)
    back = exchange(row_sum(ones, two, held), "exp")
    moe_out = combine_rows(place_own, back, expert_ids, route_weights)
    return (hidden, moe_out)


def solution(mesh):
    cube = Mesh(mesh.devices.reshape(4, 4, 2, 4), ("z", "x", "core", "exp"))
    both = CTX + ("exp",)
    in_specs = (
        P(CTX, "exp"),
        P(CTX, "exp"),
        P(CTX, "exp"),
        P(CTX, "exp"),
        P(both, None),
        P(both, None),
        P(),
        P(),
        P(both, None),
        P(both, None),
        P("exp", None, CTX),
        P("exp", None, CTX),
        P("exp", CTX, None),
    )
    out_specs = (P(both, None), P(both, None))
    return jax.shard_map(local, mesh=cube, in_specs=in_specs, out_specs=out_specs, check_vma=False)
```

```python
import functools

import jax
import jax.numpy as jnp
from jax import lax
from jax.experimental import pallas as pl
from jax.experimental.pallas import tpu as pltpu
from jax.sharding import Mesh, PartitionSpec as P

HEAD_DIM = 128
CAP = 4
EPS = 1e-05
F32 = jnp.float32
BF16 = jnp.bfloat16
HIGHEST = lax.Precision.HIGHEST
CTX = ("z", "x", "core")
VMEM_LIMIT = 24 * 1024 * 1024


def iota(shape, dim):
    return lax.broadcasted_iota(jnp.int32, shape, dim)


def hbm(a):
    return pltpu.with_memory_space_constraint(a, pltpu.HBM)


def far(shape, dtype=BF16):
    return pltpu.HBM(shape, dtype)


def params(**kw):
    return pltpu.CompilerParams(vmem_limit_bytes=VMEM_LIMIT, **kw)


def cost(flops, bytes_accessed):
    return pl.CostEstimate(flops=flops, bytes_accessed=bytes_accessed, transcendentals=0)


def running_sum(ld, axis):
    rows = ld.shape[1]
    a, b = iota((rows, rows), 0), iota((rows, rows), 1)
    ones = (a >= b).astype(BF16)
    total = None
    rest = ld
    for _ in range(3):
        part = rest.astype(BF16)
        rest = rest - part.astype(F32)
        pair = (ones, part) if axis == 0 else (part, ones)
        term = lax.dot_general(*pair, (((1,), (1,)), ((), ())), preferred_element_type=F32)
        total = term if total is None else total + term
    return total


def spread(table, first, count, terms):
    n = table.shape[1]
    shape = (n, count * HEAD_DIM)
    pick = (iota(shape, 0) == first + iota(shape, 1) // HEAD_DIM).astype(BF16)
    total = None
    rest = table
    for _ in range(terms):
        part = rest.astype(BF16)
        rest = rest - part.astype(F32)
        term = jnp.dot(part, pick, preferred_element_type=F32)
        total = term if total is None else total + term
    return total


def state_kernel(group, k_ref, v_ref, ld_ref, cum_ref, msg_ref, fade_ref, decay_ref):
    heads, rows = ld_ref.shape
    per = heads * HEAD_DIM // 32
    parts = group * HEAD_DIM // per
    g = pl.program_id(0)

    @pl.when(g == 0)
    def _():
        cum = running_sum(ld_ref[...], 0)
        cum_ref[...] = cum
        final = cum[rows - 1 : rows, :]
        fade_ref[...] = jnp.exp(final - cum)
        decay_ref[...] = jnp.broadcast_to(jnp.exp(final), decay_ref.shape)

    fade = spread(fade_ref[...], g * group, group, 2)
    decay = spread(decay_ref[...], g * group, group, 2)
    row16 = iota((16, HEAD_DIM), 0)
    tiles = []
    for j in range(group):
        cols = slice(j * HEAD_DIM, (j + 1) * HEAD_DIM)
        wk = (k_ref[:, cols].astype(F32) * fade[:, cols]).astype(BF16)
        state = lax.dot_general(
            wk, v_ref[:, cols], (((0,), (0,)), ((), ())), preferred_element_type=F32
        ).astype(BF16)
        row = j * HEAD_DIM
        while row < (j + 1) * HEAD_DIM:
            part, at = row // per, row % per
            take = min(per - at, (j + 1) * HEAD_DIM - row)
            lo = row - j * HEAD_DIM
            msg_ref[part, at : at + take, :] = state[lo : lo + take, :]
            row += take
        whole = decay[:, cols]
        high = whole.astype(BF16).astype(F32)
        tiles.append((high, whole - high))
    for part in range(parts):
        first = per * part // HEAD_DIM
        last = (per * part + per - 1) // HEAD_DIM
        tile = jnp.where(
            row16 == 0,
            tiles[first][0],
            jnp.where(
                row16 == 1, tiles[first][1], jnp.where(row16 == 2, tiles[last][0], tiles[last][1])
            ),
        )
        msg_ref[part, per : per + 16, :] = tile.astype(BF16)


def local_states(k, v, ld, group=3):
    rows, width = k.shape
    heads = ld.shape[0]
    per = heads * HEAD_DIM // 32
    parts = group * HEAD_DIM // per
    block = pl.BlockSpec((rows, group * HEAD_DIM), lambda g: (0, g))
    return pl.pallas_call(
        functools.partial(state_kernel, group),
        grid=(heads // group,),
        out_shape=(
            jax.ShapeDtypeStruct((rows, heads), F32),
            far((32, per + 16, HEAD_DIM)),
        ),
        in_specs=[block, block, pl.BlockSpec((heads, rows), lambda g: (0, 0))],
        out_specs=(
            pl.BlockSpec((rows, heads), lambda g: (0, 0)),
            pl.BlockSpec((parts, per + 16, HEAD_DIM), lambda g: (g, 0, 0)),
        ),
        scratch_shapes=[pltpu.VMEM((rows, heads), F32), pltpu.VMEM((16, heads), F32)],
        compiler_params=params(),
        cost_estimate=cost(2 * rows * width * HEAD_DIM, 4 * rows * width),
        name="local_states",
    )(k, v, ld)


def scan_kernel(split_ref, in_ref, out_ref):
    parts, per, width = out_ref.shape
    first_rows = iota((per, width), 0) < split_ref[0]
    state = jnp.zeros((per, width), F32)
    for b in range(parts):
        out_ref[b, :, :] = state.astype(BF16)
        if b + 1 < parts:
            tail = in_ref[b, per : per + 16, :].astype(F32)
            d0 = tail[0:1, :] + tail[1:2, :]
            d1 = tail[2:3, :] + tail[3:4, :]
            decay = jnp.where(first_rows, d0, d1)
            state = decay * state + in_ref[b, 0:per, :].astype(F32)


def scan_blocks(msg, part):
    parts, tall, width = msg.shape
    per = tall - 16
    split = (HEAD_DIM - (per * part) % HEAD_DIM).astype(jnp.int32).reshape(1)
    return pl.pallas_call(
        scan_kernel,
        out_shape=far((parts, per, width)),
        in_specs=[
            pl.BlockSpec(memory_space=pltpu.SMEM),
            pl.BlockSpec(memory_space=pltpu.VMEM),
        ],
        out_specs=pl.BlockSpec(memory_space=pltpu.VMEM),
        compiler_params=params(),
        cost_estimate=cost(1000000, 1000000),
        name="scan_blocks",
    )(split, msg)


def inside_kernel(group, q_ref, k_ref, v_ref, cum_ref, ld_ref, inside_ref, qs_ref, cumt_ref):
    rows, heads = cum_ref.shape

    @pl.when(pl.program_id(0) == 0)
    def _():
        cumt_ref[...] = running_sum(ld_ref[...], 1)

    cum = spread(cum_ref[...], pl.program_id(0) * group, group, 3)
    size = 2 * HEAD_DIM
    causal = iota((size, size), 0) >= iota((size, size), 1)
    for j in range(group):
        h = pl.program_id(0) * group + j
        cols = slice(j * HEAD_DIM, (j + 1) * HEAD_DIM)
        col = cum[:, cols]
        row = cumt_ref[pl.ds(h, 1), :]
        q = q_ref[:, cols]
        k = k_ref[:, cols]
        v = v_ref[:, cols]
        qs_ref[:, cols] = (q.astype(F32) * jnp.exp(col)).astype(BF16)
        wide = jnp.concatenate([col, col], axis=1)
        total = None
        for lo in range(0, rows, size):
            hi = lo + size
            s = lax.dot_general(
                q[lo:], k[lo:hi], (((1,), (1,)), ((), ())), preferred_element_type=F32
            )
            decay = jnp.exp(jnp.minimum(wide[lo:] - row[:, lo:hi], 0.0))
            w = s * decay
            w = jnp.concatenate([jnp.where(causal, w[:size], 0.0), w[size:]], axis=0) if (
                hi < rows
            ) else jnp.where(causal, w, 0.0)
            part = jnp.dot(w.astype(BF16), v[lo:hi], preferred_element_type=F32)
            if total is None:
                total = part
            else:
                total = jnp.concatenate([total[:lo], total[lo:] + part], axis=0)
        inside_ref[:, cols] = total


def inside_blocks(q, k, v, cum, ld, group=3):
    rows, width = q.shape
    heads = cum.shape[1]
    block = pl.BlockSpec((rows, group * HEAD_DIM), lambda g: (0, g))
    return pl.pallas_call(
        functools.partial(inside_kernel, group),
        grid=(heads // group,),
        out_shape=(
            jax.ShapeDtypeStruct((rows, width), F32),
            far((rows, width)),
        ),
        in_specs=[
            block,
            block,
            block,
            pl.BlockSpec((rows, heads), lambda g: (0, 0)),
            pl.BlockSpec((heads, rows), lambda g: (0, 0)),
        ],
        out_specs=(block, block),
        scratch_shapes=[pltpu.VMEM((heads, rows), F32)],
        compiler_params=params(),
        cost_estimate=cost(4 * rows * rows * width, 12 * rows * width),
        name="inside_blocks",
    )(q, k, v, cum, ld)


def attend(group, inside_ref, qs_ref, state_ref, att_ref):
    for j in range(group):
        cols = slice(j * HEAD_DIM, (j + 1) * HEAD_DIM)
        att_ref[:, cols] = (
            inside_ref[:, cols]
            + jnp.dot(qs_ref[:, cols], state_ref[j], preferred_element_type=F32)
        ).astype(BF16)


def chosen_kernel(inside_ref, qs_ref, state_ref, sel_ref):
    for h in range(state_ref.shape[0]):
        cols = slice(h * HEAD_DIM, (h + 1) * HEAD_DIM)
        sel_ref[:, cols] = (
            inside_ref[:, cols]
            + jnp.dot(qs_ref[:, cols], state_ref[h], preferred_element_type=F32)
        ).astype(BF16)


def carried_kernel(group, me_ref, inside_ref, qs_ref, state_ref, *refs):
    outs, att_ref = refs[:-1], refs[-1]
    held = len(outs)
    tokens = outs[0].shape[0]
    attend(group, inside_ref, qs_ref, state_ref, att_ref)
    for d in range(held):
        at = pl.multiple_of(lax.rem(me_ref[0] + d, held) * tokens, tokens)
        outs[d][...] = att_ref[pl.ds(at, tokens), :]


def chosen_rows(inside, qs, state):
    chosen, width = inside.shape
    return pl.pallas_call(
        chosen_kernel,
        out_shape=far((chosen, width)),
        compiler_params=params(),
        cost_estimate=cost(2 * chosen * width * HEAD_DIM, 8 * chosen * width),
        name="chosen_rows",
    )(inside, qs, state)


def carried_blocks(me, inside, qs, state, held, group=3):
    rows, width = inside.shape
    heads = width // HEAD_DIM
    wide = group * HEAD_DIM
    tokens = rows // held
    block = pl.BlockSpec((rows, wide), lambda g: (0, g))
    return list(
        pl.pallas_call(
            functools.partial(carried_kernel, group),
            grid=(heads // group,),
            out_shape=(far((tokens, width)),) * held,
            in_specs=[
                pl.BlockSpec(memory_space=pltpu.SMEM),
                block,
                block,
                pl.BlockSpec((group, HEAD_DIM, HEAD_DIM), lambda g: (g, 0, 0)),
            ],
            out_specs=(pl.BlockSpec((tokens, wide), lambda g: (0, g)),) * held,
            scratch_shapes=[pltpu.VMEM((rows, wide), BF16)],
            compiler_params=params(),
            cost_estimate=cost(4 * rows * width * HEAD_DIM, 8 * rows * width),
            name="carried_blocks",
        )(me, inside, qs, state)
    )


def route_kernel(pieces, me_ref, ids_ref, res_hbm, gate_hbm, *refs):
    outs, (place_ref, res_ref, gate_ref, sem) = refs[:-4], refs[-4:]
    held = len(outs)
    size = res_ref.shape[0] // pieces
    copies = []
    for n, (a, b) in enumerate(((res_hbm, res_ref), (gate_hbm, gate_ref))):
        for i in range(pieces):
            at = pl.ds(i * size, size)
            copies.append(pltpu.make_async_copy(a.at[at], b.at[at], sem.at[n, i]))
    for c in copies:
        c.start()
    tokens, width = res_ref.shape
    me = me_ref[0]
    ids = ids_ref[...]
    hits = [
        ((ids[0:1, :] == e) | (ids[1:2, :] == e)).astype(F32) for e in range(held)
    ]
    m = jnp.concatenate(hits, axis=0)
    upto = (iota((tokens, tokens), 0) <= iota((tokens, tokens), 1)).astype(BF16)
    rank = jnp.dot(m.astype(BF16), upto, preferred_element_type=F32) - 1.0
    slot = iota((CAP, tokens), 0).astype(F32)
    places = [
        jnp.where(rank[e : e + 1, :] == slot, m[e : e + 1, :], 0.0) for e in range(held)
    ]
    place = jnp.concatenate(places, axis=0)
    place_ref[...] = place
    for c in copies:
        c.wait()
    ordered = []
    for d in range(held):
        expert = lax.rem(me + d, held)
        mine = places[0]
        for e in range(1, held):
            mine = jnp.where(expert == e, places[e], mine)
        ordered.append(mine)
    chosen = jnp.concatenate(ordered, axis=0).astype(BF16)
    res = jnp.dot(chosen, res_ref[...], preferred_element_type=F32)
    gate = jnp.dot(chosen, gate_ref[...], preferred_element_type=F32)
    for d in range(held):
        at = slice(d * CAP, (d + 1) * CAP)
        outs[d][:, 0:width] = jnp.concatenate([res[at], gate[at]], axis=0).astype(BF16)
        for n in range(2):
            outs[d][:, width + n * tokens : width + (n + 1) * tokens] = jnp.broadcast_to(
                ids[n : n + 1, :].astype(F32), (2 * CAP, tokens)
            ).astype(BF16)


def route_rows(me, ids, residual, out_gate, held, pieces=4):
    tokens, width = residual.shape
    whole = pl.BlockSpec(memory_space=pltpu.VMEM)
    away = pl.BlockSpec(memory_space=pl.ANY)
    piece = far((2 * CAP, width + 2 * tokens))
    outs = pl.pallas_call(
        functools.partial(route_kernel, pieces),
        out_shape=(piece,) * held + (jax.ShapeDtypeStruct((held * CAP, tokens), F32),),
        in_specs=[pl.BlockSpec(memory_space=pltpu.SMEM), whole, away, away],
        out_specs=(whole,) * (held + 1),
        scratch_shapes=[
            pltpu.VMEM((tokens, width), BF16),
            pltpu.VMEM((tokens, width), BF16),
            pltpu.SemaphoreType.DMA((2, pieces)),
        ],
        compiler_params=params(),
        cost_estimate=cost(64 * tokens * width, 5 * tokens * width),
        name="route_rows",
    )(me, ids, residual, out_gate)
    return outs[:-1], outs[-1]


def by_source(me, pieces, j):
    count = len(pieces)
    out = pieces[0]
    for d in range(1, count):
        out = jnp.where(lax.rem(me + count - d, count) == j, pieces[d], out)
    return out


def place_kernel(group, me_ref, inside_ref, qs_ref, *refs):
    pieces, (some_inside_ref, some_qs_ref, place_ref) = refs[:-3], refs[-3:]
    held = len(pieces)
    tokens = pieces[0].shape[1] // 2
    total = held * tokens
    me = me_ref[0]
    tables = [p[...].astype(F32) for p in pieces]
    ordered = [by_source(me, tables, j) for j in range(held)]
    first = jnp.concatenate([a[0:1, :tokens] for a in ordered], axis=1)
    second = jnp.concatenate([a[0:1, tokens:] for a in ordered], axis=1)
    m = jnp.concatenate(
        [((first == float(e)) | (second == float(e))).astype(F32) for e in range(held)], axis=0
    )
    before = iota((total, total), 0)
    after = iota((total, total), 1)
    upto = ((before <= after) & (before // tokens == after // tokens)).astype(BF16)
    rank = jnp.dot(m.astype(BF16), upto, preferred_element_type=F32) - 1.0
    rows = held * CAP
    r = iota((rows, total), 0)
    t = iota((rows, total), 1)
    here = (t // tokens == r // CAP).astype(F32)
    slot = (r % CAP).astype(F32)
    for e in range(held):
        hit = jnp.where(rank[e : e + 1, :] == slot, m[e : e + 1, :] * here, 0.0)
        place_ref[e * rows : (e + 1) * rows, :] = hit.astype(BF16)
    place = place_ref[...]
    wide = group * HEAD_DIM
    for g in range(qs_ref.shape[1] // wide):
        cols = slice(g * wide, (g + 1) * wide)
        some_qs_ref[:, cols] = jnp.dot(
            place, qs_ref[:, cols], preferred_element_type=F32
        ).astype(BF16)
        rest = inside_ref[:, cols]
        picked = None
        for _ in range(3):
            part = rest.astype(BF16)
            rest = rest - part.astype(F32)
            term = jnp.dot(place, part, preferred_element_type=F32)
            picked = term if picked is None else picked + term
        some_inside_ref[:, cols] = picked


def place_rows(me, inside, qs, pieces, tokens, group=3):
    held = len(pieces)
    chosen = held * held * CAP
    width = pieces[0].shape[1] - 2 * tokens
    at = width // (2 * tokens)
    whole = pl.BlockSpec(memory_space=pltpu.VMEM)
    return pl.pallas_call(
        functools.partial(place_kernel, group),
        grid=(1,),
        out_shape=(
            far((chosen, inside.shape[1]), F32),
            far((chosen, inside.shape[1])),
        ),
        in_specs=[pl.BlockSpec(memory_space=pltpu.SMEM), whole, whole]
        + [pl.BlockSpec((2 * CAP, 2 * tokens), lambda i: (0, at))] * held,
        out_specs=(whole, whole),
        scratch_shapes=[pltpu.VMEM((chosen, held * tokens), BF16)],
        compiler_params=params(),
        cost_estimate=cost(1000000, 200000),
        name="place_rows",
    )(me, inside, qs, *pieces)


def gated(att, res, gate, attn_gain):
    norm = att * lax.rsqrt(jnp.mean(att * att, axis=-1, keepdims=True) + EPS) * attn_gain
    return (res + norm * jax.nn.sigmoid(gate)).astype(BF16)


def routed_norm_kernel(me_ref, att_ref, ag_ref, mg_ref, *refs):
    pieces, one_ref, two_ref = refs[:-2], refs[-2], refs[-1]
    sources, rows, part = att_ref.shape
    width = sources * part
    me = me_ref[0]
    att = jnp.concatenate([att_ref[s].astype(F32) for s in range(sources)], axis=1)
    tables = [p[...][:, :width].astype(F32) for p in pieces]
    ordered = [by_source(me, tables, j) for j in range(sources)]
    res = jnp.concatenate([a[:CAP] for a in ordered], axis=0)
    gate = jnp.concatenate([a[CAP:] for a in ordered], axis=0)
    hidden = gated(att, res, gate, ag_ref[...]).astype(F32)
    normed = (
        hidden * lax.rsqrt(jnp.mean(hidden * hidden, axis=-1, keepdims=True) + EPS) * mg_ref[...]
    ).astype(BF16)
    cut = one_ref.shape[1]
    one_ref[...] = normed[:, :cut]
    for i in range(two_ref.shape[0]):
        two_ref[i] = normed[:, cut:]


def routed_norm(me, att, pieces, attn_gain, moe_gain, copies):
    sources, rows, part = att.shape
    width = sources * part
    cut = width * 7 // 12
    whole = pl.BlockSpec(memory_space=pltpu.VMEM)
    return pl.pallas_call(
        routed_norm_kernel,
        out_shape=(far((rows, cut)), far((copies, rows, width - cut))),
        in_specs=[pl.BlockSpec(memory_space=pltpu.SMEM)] + [whole] * (3 + len(pieces)),
        out_specs=(whole, whole),
        compiler_params=params(),
        cost_estimate=cost(20 * rows * width, 20 * rows * width),
        name="routed_norm",
    )(me, att, attn_gain, moe_gain, *pieces)


def hidden_kernel(me_ref, res_ref, gate_ref, ag_ref, *refs):
    pieces, out_ref = refs[:-1], refs[-1]
    me = me_ref[0]
    tables = [p[...].astype(F32) for p in pieces]
    att = jnp.concatenate([by_source(me, tables, j) for j in range(len(pieces))], axis=1)
    out_ref[...] = gated(att, res_ref[...].astype(F32), gate_ref[...].astype(F32), ag_ref[...])


def hidden_rows(me, pieces, residual, out_gate, attn_gain, tile=32):
    rows, part = pieces[0].shape
    width = len(pieces) * part
    block = pl.BlockSpec((tile, width), lambda i: (i, 0))
    return pl.pallas_call(
        hidden_kernel,
        grid=(rows // tile,),
        out_shape=jax.ShapeDtypeStruct((rows, width), BF16),
        in_specs=[
            pl.BlockSpec(memory_space=pltpu.SMEM),
            block,
            block,
            pl.BlockSpec((1, width), lambda i: (0, 0)),
        ]
        + [pl.BlockSpec((tile, part), lambda i: (i, 0))] * len(pieces),
        out_specs=block,
        compiler_params=params(),
        cost_estimate=cost(20 * rows * width, 8 * rows * width),
        name="hidden_rows",
    )(me, residual, out_gate, attn_gain, *pieces)


def repeat_kernel(*refs):
    ins, (out, sem) = refs[:-2], refs[-2:]
    copies = [
        pltpu.make_async_copy(a, out.at[n, k], sem.at[n, k])
        for n in range(out.shape[0])
        for k, a in enumerate(ins)
    ]
    for c in copies:
        c.start()
    for c in copies:
        c.wait()


def repeat(arrays, copies):
    rows, width = arrays[0].shape
    count = len(arrays)
    return pl.pallas_call(
        repeat_kernel,
        out_shape=far((copies, count, rows, width)),
        in_specs=[pl.BlockSpec(memory_space=pltpu.VMEM)] * count,
        out_specs=pl.BlockSpec(memory_space=pl.ANY),
        scratch_shapes=[pltpu.SemaphoreType.DMA((copies, count))],
        compiler_params=params(),
        cost_estimate=cost(0, 2 * (copies + 1) * count * rows * width),
        name="repeat",
    )(*arrays)


def act_rows(steps, w_ref, one_ref, twos, arrived):
    width = w_ref.shape[2]
    nz, nx, rows, half = one_ref.shape
    nt = (((1,), (1,)), ((), ()))
    wide = width // steps
    gate = up = None
    for s in range(steps):
        cols = slice(s * wide, (s + 1) * wide)
        arrived(s)
        if s * wide < half:
            x = [one_ref[z, k, :, cols] for k in range(nx) for z in range(nz)]
        else:
            near = slice(s * wide - half, (s + 1) * wide - half)
            x = [r[z, :, near] for r in twos for z in range(nz)]
        x = jnp.concatenate(x, axis=0)
        g = lax.dot_general(w_ref[0, :, cols], x, nt, preferred_element_type=F32)
        u = lax.dot_general(w_ref[1, :, cols], x, nt, preferred_element_type=F32)
        gate = g if gate is None else gate + g
        up = u if up is None else up + u
    return (gate * jax.nn.sigmoid(gate) * up).T.astype(BF16)


def first_act_kernel(steps, wg_hbm, wu_hbm, one_ref, *refs):
    twos, (act_ref, w_ref, sem) = refs[:-3], refs[-3:]
    wide = w_ref.shape[2] // steps
    copies = []
    for s in range(steps):
        cols = pl.ds(s * wide, wide)
        for n, a in enumerate((wg_hbm, wu_hbm)):
            copies.append(
                pltpu.make_async_copy(a.at[:, cols], w_ref.at[n, :, cols], sem.at[s, n])
            )
    for c in copies:
        c.start()

    def arrived(s):
        copies[2 * s].wait()
        copies[2 * s + 1].wait()

    act_ref[...] = act_rows(steps, w_ref, one_ref, twos, arrived)


def next_act_kernel(steps, w_ref, one_ref, *refs):
    refs[-1][...] = act_rows(steps, w_ref, one_ref, refs[:-1], lambda s: None)


def expert_act(one, twos, weights, steps=12):
    nz, nx, rows, half = one.shape
    count = nz * nx * rows
    whole = pl.BlockSpec(memory_space=pltpu.VMEM)
    away = pl.BlockSpec(memory_space=pl.ANY)
    if isinstance(weights, tuple):
        units, width = weights[0].shape
        return pl.pallas_call(
            functools.partial(first_act_kernel, steps),
            out_shape=(
                jax.ShapeDtypeStruct((count, units), BF16),
                pltpu.VMEM((2, units, width), BF16),
            ),
            in_specs=[away, away] + [whole] * (1 + len(twos)),
            out_specs=(whole, whole),
            scratch_shapes=[pltpu.SemaphoreType.DMA((steps, 2))],
            compiler_params=params(),
            cost_estimate=cost(4 * count * width * units, 4 * width * units + 2 * count * width),
            name="first_act",
        )(hbm(weights[0]), hbm(weights[1]), one, *twos)
    _, units, width = weights.shape
    return pl.pallas_call(
        functools.partial(next_act_kernel, steps),
        out_shape=jax.ShapeDtypeStruct((count, units), BF16),
        in_specs=[whole] * (2 + len(twos)),
        out_specs=whole,
        compiler_params=params(),
        cost_estimate=cost(4 * count * width * units, 2 * count * width),
        name="next_act",
    )(pltpu.with_memory_space_constraint(weights, pltpu.VMEM), one, *twos)


def down_kernel(steps, first, by_x, act_ref, wd_hbm, *refs):
    wd_ref, sem = refs[-2:]
    half = wd_ref.shape[1]
    wide = half // steps
    copies = []
    for s in range(steps):
        cols = pl.ds(s * wide, wide)
        copies.append(
            pltpu.make_async_copy(
                wd_hbm.at[:, pl.ds(first + s * wide, wide)], wd_ref.at[:, cols], sem.at[s]
            )
        )
    for c in copies:
        c.start()
    refs = refs[:-2]
    added, kept, ends = (refs[0], refs[-2], refs[-1]) if len(refs) != 1 else (None,) * 3
    outs = refs[1:-2] if len(refs) != 1 else refs
    leaving = []

    def send(s, cols):
        n = s * len(outs)
        if len(outs) == 1:
            leaving.append(
                pltpu.make_async_copy(kept.at[:, :, :, cols], outs[0].at[:, :, :, cols], ends.at[n])
            )
            leaving[-1].start()
            return
        for k, ref in enumerate(outs):
            leaving.append(
                pltpu.make_async_copy(kept.at[k, :, :, cols], ref.at[:, :, cols], ends.at[n + k])
            )
            leaving[-1].start()

    act = act_ref[...]
    if by_x:
        nx = outs[0].shape[0] if len(outs) == 1 else len(outs)
        nz = outs[0].shape[-3]
    else:
        nz, nx = outs[0].shape[:2]
    rows = outs[0].shape[-2]
    for s in range(steps):
        cols = slice(s * wide, (s + 1) * wide)
        copies[s].wait()
        out = jnp.dot(act, wd_ref[:, cols], preferred_element_type=F32)
        out = out.reshape(nx, nz, rows, wide)
        if by_x:
            if added is not None:
                out = out + added[:, :, :, cols].astype(F32)
            target = outs[0] if added is None else kept
            target[:, :, :, cols] = out.astype(BF16)
        else:
            for z in range(nz):
                part = out[:, z]
                if added is not None:
                    part = part + added[z, :, :, cols].astype(F32)
                target = outs[0] if added is None else kept
                target[z, :, :, cols] = part.astype(BF16)
        if added is not None:
            send(s, pl.ds(s * wide, wide))
    for c in leaving:
        c.wait()


def expert_down(act, w_down, cut, last, nz, nx, added=None, steps=2):
    count, units = act.shape
    half = w_down.shape[1] - cut if last else cut
    rows = count // (nz * nx)
    whole = pl.BlockSpec(memory_space=pltpu.VMEM)
    if last:
        if added is None:
            shapes = (jax.ShapeDtypeStruct((nx, nz, rows, half), BF16),)
        else:
            shapes = (far((nz, rows, half)),) * nx
    elif added is None:
        shapes = (jax.ShapeDtypeStruct((nz, nx, rows, half), BF16),)
    else:
        shapes = (far((nz, nx, rows, half)),)
    more = () if added is None else (added,)
    away = pl.BlockSpec(memory_space=pl.ANY)
    scratch = [pltpu.VMEM((units, half), BF16), pltpu.SemaphoreType.DMA((steps,))]
    if added is not None:
        scratch = [
            pltpu.VMEM(added.shape, BF16),
            pltpu.SemaphoreType.DMA((steps * len(shapes),)),
        ] + scratch
    return pl.pallas_call(
        functools.partial(down_kernel, steps, cut if last else 0, last),
        out_shape=shapes,
        in_specs=[whole, away] + [whole] * len(more),
        out_specs=(whole if added is None else away,) * len(shapes),
        scratch_shapes=scratch,
        compiler_params=params(),
        cost_estimate=cost(2 * count * half * units, 2 * half * units + 2 * count * half),
        name="expert_down",
    )(act, hbm(w_down), *more)


def block_kernel(in_ref, *outs):
    total = in_ref[0].astype(F32)
    for i in range(1, in_ref.shape[0]):
        total = total + in_ref[i].astype(F32)
    total = total.astype(BF16)
    for n, out in enumerate(outs):
        out[...] = total[n]


def block_sum(parts, steps=2):
    count, n, rows, width = parts.shape
    wide = width // steps
    return pl.pallas_call(
        block_kernel,
        grid=(steps,),
        out_shape=(far((rows, width)),) * n,
        in_specs=[pl.BlockSpec((count, n, rows, wide), lambda i: (0, 0, 0, i))],
        out_specs=(pl.BlockSpec((rows, wide), lambda i: (0, i)),) * n,
        compiler_params=params(),
        cost_estimate=cost(count * n * rows * width, 2 * (count + 1) * n * rows * width),
        name="block_sum",
    )(parts)


def stack_kernel(*refs):
    total = refs[0][...].astype(F32)
    for ref in refs[1:-1]:
        total = total + ref[...].astype(F32)
    refs[-1][...] = total.astype(BF16)


def stack_sum(parts, steps=2):
    n, rows, width = parts[0].shape
    wide = width // steps
    block = pl.BlockSpec((n, rows, wide), lambda i: (0, 0, i))
    return pl.pallas_call(
        stack_kernel,
        grid=(steps,),
        out_shape=far(parts[0].shape),
        in_specs=[block] * len(parts),
        out_specs=block,
        compiler_params=params(),
        cost_estimate=cost(len(parts) * n * rows * width, 2 * (len(parts) + 1) * n * rows * width),
        name="stack_sum",
    )(*parts)


def row_sum_kernel(two_ref, *refs):
    parts, out_ref = refs[:-1], refs[-1]
    one = parts[0][...].astype(F32)
    for ref in parts[1:]:
        one = one + ref[...].astype(F32)
    two = two_ref[0].astype(F32)
    for i in range(1, two_ref.shape[0]):
        two = two + two_ref[i].astype(F32)
    cut = one.shape[1]
    for j in range(out_ref.shape[0]):
        at = slice(j * CAP, (j + 1) * CAP)
        out_ref[j, :, :cut] = one[at].astype(BF16)
        out_ref[j, :, cut:] = two[at].astype(BF16)


def row_sum(parts, two, held):
    count, rows, half = two.shape
    whole = pl.BlockSpec(memory_space=pltpu.VMEM)
    return pl.pallas_call(
        row_sum_kernel,
        out_shape=far((held, CAP, parts[0].shape[1] + half)),
        in_specs=[whole] * (1 + len(parts)),
        out_specs=whole,
        compiler_params=params(),
        cost_estimate=cost(8 * rows * half, 20 * rows * half),
        name="row_sum",
    )(two, *parts)


def combine_kernel(place_ref, rows_ref, ids_ref, weights_ref, out_ref):
    held = rows_ref.shape[0]
    rows = jnp.concatenate([rows_ref[e].astype(F32) for e in range(held)], axis=0).astype(BF16)
    back = lax.dot_general(
        place_ref[...].astype(BF16), rows, (((0,), (0,)), ((), ())), preferred_element_type=F32
    )
    chosen = jnp.sum(
        jnp.where(ids_ref[...] < held, weights_ref[...], 0.0), axis=1, keepdims=True
    )
    out_ref[...] = (back * chosen).astype(BF16)


def combine_rows(place, rows, ids, weights):
    tokens = ids.shape[0]
    width = rows.shape[2]
    return pl.pallas_call(
        combine_kernel,
        out_shape=jax.ShapeDtypeStruct((tokens, width), BF16),
        compiler_params=params(),
        cost_estimate=cost(32 * tokens * width, 2 * tokens * width),
        name="combine_rows",
    )(place, rows, ids, weights)


def exchange(a, axis):
    return lax.all_to_all(a, axis, split_axis=0, concat_axis=0, tiled=True)


def shift(a, axis, by):
    n = lax.axis_size(axis)
    return lax.ppermute(a, axis, [(i, (i + by) % n) for i in range(n)])


def local(
    queries,
    key_vectors,
    values,
    log_decay,
    out_gate,
    residual,
    attn_gain,
    moe_gain,
    expert_ids,
    route_weights,
    w_gate,
    w_up,
    w_down,
):
    held = lax.axis_size("exp")
    rows, width = queries.shape
    heads = log_decay.shape[1]
    tokens = residual.shape[0]
    attn_gain = hbm(attn_gain.reshape(1, -1))
    moe_gain = hbm(moe_gain.reshape(1, -1))
    w_gate = jnp.swapaxes(w_gate, 1, 2)[0]
    w_up = jnp.swapaxes(w_up, 1, 2)[0]
    w_down = w_down[0]
    ids = expert_ids.T
    ld = hbm(log_decay.T)
    me = lax.axis_index("exp").reshape(1)
    keep = lax.optimization_barrier
    nz, nx = lax.axis_size("z"), lax.axis_size("x")

    cum, msg = local_states(hbm(key_vectors), hbm(values), ld)
    sent = exchange(msg, CTX)
    inside, qs = inside_blocks(hbm(queries), hbm(key_vectors), hbm(values), cum, ld)
    pieces, place_own = route_rows(me, ids, hbm(residual), hbm(out_gate), held)
    sent, inside, qs, pieces = keep((sent, inside, qs, pieces))
    prior = scan_blocks(hbm(sent), lax.axis_index(CTX))
    state = exchange(prior, CTX).reshape(heads, HEAD_DIM, HEAD_DIM)
    pieces = [pieces[0]] + [shift(pieces[d], "exp", d) for d in range(1, held)]
    pieces = [hbm(a) for a in pieces]
    some_inside, some_qs = place_rows(me, inside, hbm(qs), pieces, tokens)

    routed = chosen_rows(hbm(some_inside), hbm(some_qs), state)
    _, inside, qs, state = keep((routed, inside, qs, state))
    routed = exchange(routed.reshape(held, held * CAP, width), "exp")
    attention = carried_blocks(me, inside, hbm(qs), state, held)
    routed, attention = keep((routed, attention))
    one, two = routed_norm(me, routed, pieces, attn_gain, moe_gain, nz)

    others = range(1, nx)
    ones = [one] + [shift(one, "x", d) for d in others]
    two = exchange(two, "z")
    across = shift(attention[2], "exp", 2)
    ones, two, across = keep((ones, two, across))
    one = exchange(repeat([hbm(ones[0])] + ones[1:], nz), "z")
    twos = [two] + [shift(two, "x", d) for d in others]
    right, left = shift(attention[1], "exp", 1), shift(attention[3], "exp", 3)
    one, twos, right, left = keep((one, twos, right, left))

    cut = moe_gain.shape[1] * 2 // 3
    act_own, weights = expert_act(one, twos, (w_gate, w_up))
    one, twos = shift(one, "core", 1), [shift(a, "core", 1) for a in twos]
    one, twos, weights = keep((one, twos, weights))
    act_far = expert_act(one, twos, weights)
    (one,) = expert_down(act_far, w_down, cut, False, nz, nx)
    one, act_far = keep((one, act_far))
    (two,) = expert_down(act_far, w_down, cut, True, nz, nx)
    one, two, act_own = keep((one, two, act_own))
    one, two = shift(one, "core", 1), shift(two, "core", 1)
    (one,) = expert_down(act_own, w_down, cut, False, nz, nx, one)
    one, two, act_own = keep((one, two, act_own))
    twos = expert_down(act_own, w_down, cut, True, nz, nx, two)

    one = exchange(one, "z")
    twos = [twos[0]] + [shift(twos[d], "x", -d) for d in others]
    one, twos = keep((one, twos))
    attention = [attention[0], right, across, left]
    ones = block_sum(one)
    ones = [hbm(ones[0])] + [shift(ones[d], "x", -d) for d in others]
    two = exchange(stack_sum([hbm(twos[0])] + twos[1:]), "z")
    hidden = hidden_rows(me, attention, hbm(residual), hbm(out_gate), attn_gain)
    back = exchange(row_sum(ones, two, held), "exp")
    moe_out = combine_rows(place_own, back, expert_ids, route_weights)
    return (hidden, moe_out)


def solution(mesh):
    cube = Mesh(mesh.devices.reshape(4, 4, 2, 4), ("z", "x", "core", "exp"))
    both = CTX + ("exp",)
    in_specs = (
        P(CTX, "exp"),
        P(CTX, "exp"),
        P(CTX, "exp"),
        P(CTX, "exp"),
        P(both, None),
        P(both, None),
        P(),
        P(),
        P(both, None),
        P(both, None),
        P("exp", None, CTX),
        P("exp", None, CTX),
        P("exp", CTX, None),
    )
    out_specs = (P(both, None), P(both, None))
    return jax.shard_map(local, mesh=cube, in_specs=in_specs, out_specs=out_specs, check_vma=False)
```

```python
import functools

import jax
import jax.numpy as jnp
from jax import lax
from jax.experimental import pallas as pl
from jax.experimental.pallas import tpu as pltpu
from jax.sharding import Mesh, PartitionSpec as P

HEAD_DIM = 128
CAP = 4
EPS = 1e-05
F32 = jnp.float32
BF16 = jnp.bfloat16
HIGHEST = lax.Precision.HIGHEST
CTX = ("z", "x", "core")
VMEM_LIMIT = 24 * 1024 * 1024


def iota(shape, dim):
    return lax.broadcasted_iota(jnp.int32, shape, dim)


def hbm(a):
    return pltpu.with_memory_space_constraint(a, pltpu.HBM)


def far(shape, dtype=BF16):
    return pltpu.HBM(shape, dtype)


def params(**kw):
    return pltpu.CompilerParams(vmem_limit_bytes=VMEM_LIMIT, **kw)


def cost(flops, bytes_accessed):
    return pl.CostEstimate(flops=flops, bytes_accessed=bytes_accessed, transcendentals=0)


def running_sum(ld, axis):
    rows = ld.shape[1]
    a, b = iota((rows, rows), 0), iota((rows, rows), 1)
    ones = (a >= b).astype(BF16)
    total = None
    rest = ld
    for _ in range(3):
        part = rest.astype(BF16)
        rest = rest - part.astype(F32)
        pair = (ones, part) if axis == 0 else (part, ones)
        term = lax.dot_general(*pair, (((1,), (1,)), ((), ())), preferred_element_type=F32)
        total = term if total is None else total + term
    return total


def spread(table, first, count, terms):
    n = table.shape[1]
    shape = (n, count * HEAD_DIM)
    pick = (iota(shape, 0) == first + iota(shape, 1) // HEAD_DIM).astype(BF16)
    total = None
    rest = table
    for _ in range(terms):
        part = rest.astype(BF16)
        rest = rest - part.astype(F32)
        term = jnp.dot(part, pick, preferred_element_type=F32)
        total = term if total is None else total + term
    return total


def state_kernel(
    group, k_hbm, v_hbm, ld_ref, cum_ref, out_hbm, k_ref, v_ref, msg_ref, arrive, leave
):
    heads, rows = ld_ref.shape
    per = heads * HEAD_DIM // 32
    parts = group * HEAD_DIM // per
    wide = group * HEAD_DIM
    arriving = []
    for g in range(heads // group):
        cols = pl.ds(g * wide, wide)
        for n, (a, b) in enumerate(((k_hbm, k_ref), (v_hbm, v_ref))):
            arriving.append(pltpu.make_async_copy(a.at[:, cols], b.at[:, cols], arrive.at[g, n]))
    for c in arriving:
        c.start()
    cum = running_sum(ld_ref[...], 0)
    cum_ref[...] = cum
    final = cum[rows - 1 : rows, :]
    fades = jnp.exp(final - cum)
    decays = jnp.broadcast_to(jnp.exp(final), (16, heads))
    row16 = iota((16, HEAD_DIM), 0)
    leaving = []
    for g in range(heads // group):
        fade = spread(fades, g * group, group, 2)
        decay = spread(decays, g * group, group, 2)
        arriving[2 * g].wait()
        arriving[2 * g + 1].wait()
        tiles = []
        for j in range(group):
            cols = slice(j * HEAD_DIM, (j + 1) * HEAD_DIM)
            here = slice((g * group + j) * HEAD_DIM, (g * group + j + 1) * HEAD_DIM)
            wk = (k_ref[:, here].astype(F32) * fade[:, cols]).astype(BF16)
            state = lax.dot_general(
                wk, v_ref[:, here], (((0,), (0,)), ((), ())), preferred_element_type=F32
            ).astype(BF16)
            row = (g * group + j) * HEAD_DIM
            end = row + HEAD_DIM
            lo = 0
            while row < end:
                part, at = row // per, row % per
                take = min(per - at, end - row)
                msg_ref[part, at : at + take, :] = state[lo : lo + take, :]
                row += take
                lo += take
            whole = decay[:, cols]
            high = whole.astype(BF16).astype(F32)
            tiles.append((high, whole - high))
        for part in range(parts):
            first = per * part // HEAD_DIM
            last = (per * part + per - 1) // HEAD_DIM
            tile = jnp.where(
                row16 == 0,
                tiles[first][0],
                jnp.where(
                    row16 == 1,
                    tiles[first][1],
                    jnp.where(row16 == 2, tiles[last][0], tiles[last][1]),
                ),
            )
            msg_ref[g * parts + part, per : per + 16, :] = tile.astype(BF16)
        at = pl.ds(g * parts, parts)
        leaving.append(pltpu.make_async_copy(msg_ref.at[at], out_hbm.at[at], leave.at[g]))
        leaving[-1].start()
    for c in leaving:
        c.wait()


def local_states(k, v, ld, group=3):
    rows, width = k.shape
    heads = ld.shape[0]
    per = heads * HEAD_DIM // 32
    whole = pl.BlockSpec(memory_space=pltpu.VMEM)
    away = pl.BlockSpec(memory_space=pl.ANY)
    steps = heads // group
    return pl.pallas_call(
        functools.partial(state_kernel, group),
        out_shape=(
            jax.ShapeDtypeStruct((rows, heads), F32),
            far((32, per + 16, HEAD_DIM)),
        ),
        in_specs=[away, away, whole],
        out_specs=(whole, away),
        scratch_shapes=[
            pltpu.VMEM((rows, width), BF16),
            pltpu.VMEM((rows, width), BF16),
            pltpu.VMEM((32, per + 16, HEAD_DIM), BF16),
            pltpu.SemaphoreType.DMA((steps, 2)),
            pltpu.SemaphoreType.DMA((steps,)),
        ],
        compiler_params=params(),
        cost_estimate=cost(2 * rows * width * HEAD_DIM, 4 * rows * width),
        name="local_states",
    )(k, v, ld)


def scan_kernel(split_ref, in_ref, out_ref):
    parts, per, width = out_ref.shape
    first_rows = iota((per, width), 0) < split_ref[0]
    state = jnp.zeros((per, width), F32)
    for b in range(parts):
        out_ref[b, :, :] = state.astype(BF16)
        if b + 1 < parts:
            tail = in_ref[b, per : per + 16, :].astype(F32)
            d0 = tail[0:1, :] + tail[1:2, :]
            d1 = tail[2:3, :] + tail[3:4, :]
            decay = jnp.where(first_rows, d0, d1)
            state = decay * state + in_ref[b, 0:per, :].astype(F32)


def scan_blocks(msg, part):
    parts, tall, width = msg.shape
    per = tall - 16
    split = (HEAD_DIM - (per * part) % HEAD_DIM).astype(jnp.int32).reshape(1)
    return pl.pallas_call(
        scan_kernel,
        out_shape=far((parts, per, width)),
        in_specs=[
            pl.BlockSpec(memory_space=pltpu.SMEM),
            pl.BlockSpec(memory_space=pltpu.VMEM),
        ],
        out_specs=pl.BlockSpec(memory_space=pltpu.VMEM),
        compiler_params=params(),
        cost_estimate=cost(1000000, 1000000),
        name="scan_blocks",
    )(split, msg)


def inside_kernel(group, q_ref, k_ref, v_ref, cum_ref, ld_ref, inside_ref, qs_ref, cumt_ref):
    rows, heads = cum_ref.shape

    @pl.when(pl.program_id(0) == 0)
    def _():
        cumt_ref[...] = running_sum(ld_ref[...], 1)

    cum = spread(cum_ref[...], pl.program_id(0) * group, group, 3)
    size = 2 * HEAD_DIM
    causal = iota((size, size), 0) >= iota((size, size), 1)
    for j in range(group):
        h = pl.program_id(0) * group + j
        cols = slice(j * HEAD_DIM, (j + 1) * HEAD_DIM)
        col = cum[:, cols]
        row = cumt_ref[pl.ds(h, 1), :]
        q = q_ref[:, cols]
        k = k_ref[:, cols]
        v = v_ref[:, cols]
        qs_ref[:, cols] = (q.astype(F32) * jnp.exp(col)).astype(BF16)
        wide = jnp.concatenate([col, col], axis=1)
        total = None
        for lo in range(0, rows, size):
            hi = lo + size
            s = lax.dot_general(
                q[lo:], k[lo:hi], (((1,), (1,)), ((), ())), preferred_element_type=F32
            )
            decay = jnp.exp(jnp.minimum(wide[lo:] - row[:, lo:hi], 0.0))
            w = s * decay
            w = jnp.concatenate([jnp.where(causal, w[:size], 0.0), w[size:]], axis=0) if (
                hi < rows
            ) else jnp.where(causal, w, 0.0)
            part = jnp.dot(w.astype(BF16), v[lo:hi], preferred_element_type=F32)
            if total is None:
                total = part
            else:
                total = jnp.concatenate([total[:lo], total[lo:] + part], axis=0)
        inside_ref[:, cols] = total


def inside_blocks(q, k, v, cum, ld, group=3):
    rows, width = q.shape
    heads = cum.shape[1]
    block = pl.BlockSpec((rows, group * HEAD_DIM), lambda g: (0, g))
    return pl.pallas_call(
        functools.partial(inside_kernel, group),
        grid=(heads // group,),
        out_shape=(
            jax.ShapeDtypeStruct((rows, width), F32),
            far((rows, width)),
        ),
        in_specs=[
            block,
            block,
            block,
            pl.BlockSpec((rows, heads), lambda g: (0, 0)),
            pl.BlockSpec((heads, rows), lambda g: (0, 0)),
        ],
        out_specs=(block, block),
        scratch_shapes=[pltpu.VMEM((heads, rows), F32)],
        compiler_params=params(),
        cost_estimate=cost(4 * rows * rows * width, 12 * rows * width),
        name="inside_blocks",
    )(q, k, v, cum, ld)


def attend(group, inside_ref, qs_ref, state_ref, att_ref):
    for j in range(group):
        cols = slice(j * HEAD_DIM, (j + 1) * HEAD_DIM)
        att_ref[:, cols] = (
            inside_ref[:, cols]
            + jnp.dot(qs_ref[:, cols], state_ref[j], preferred_element_type=F32)
        ).astype(BF16)


def chosen_kernel(inside_ref, qs_ref, state_ref, sel_ref):
    for h in range(state_ref.shape[0]):
        cols = slice(h * HEAD_DIM, (h + 1) * HEAD_DIM)
        sel_ref[:, cols] = (
            inside_ref[:, cols]
            + jnp.dot(qs_ref[:, cols], state_ref[h], preferred_element_type=F32)
        ).astype(BF16)


def carried_kernel(group, me_ref, inside_ref, qs_ref, state_ref, *refs):
    outs, att_ref = refs[:-1], refs[-1]
    held = len(outs)
    tokens = outs[0].shape[0]
    attend(group, inside_ref, qs_ref, state_ref, att_ref)
    for d in range(held):
        at = pl.multiple_of(lax.rem(me_ref[0] + d, held) * tokens, tokens)
        outs[d][...] = att_ref[pl.ds(at, tokens), :]


def chosen_rows(inside, qs, state):
    chosen, width = inside.shape
    return pl.pallas_call(
        chosen_kernel,
        out_shape=far((chosen, width)),
        compiler_params=params(),
        cost_estimate=cost(2 * chosen * width * HEAD_DIM, 8 * chosen * width),
        name="chosen_rows",
    )(inside, qs, state)


def carried_blocks(me, inside, qs, state, held, group=3):
    rows, width = inside.shape
    heads = width // HEAD_DIM
    wide = group * HEAD_DIM
    tokens = rows // held
    block = pl.BlockSpec((rows, wide), lambda g: (0, g))
    return list(
        pl.pallas_call(
            functools.partial(carried_kernel, group),
            grid=(heads // group,),
            out_shape=(far((tokens, width)),) * held,
            in_specs=[
                pl.BlockSpec(memory_space=pltpu.SMEM),
                block,
                block,
                pl.BlockSpec((group, HEAD_DIM, HEAD_DIM), lambda g: (g, 0, 0)),
            ],
            out_specs=(pl.BlockSpec((tokens, wide), lambda g: (0, g)),) * held,
            scratch_shapes=[pltpu.VMEM((rows, wide), BF16)],
            compiler_params=params(),
            cost_estimate=cost(4 * rows * width * HEAD_DIM, 8 * rows * width),
            name="carried_blocks",
        )(me, inside, qs, state)
    )


def route_kernel(pieces, me_ref, ids_ref, res_hbm, gate_hbm, *refs):
    outs, (place_ref, res_ref, gate_ref, sem) = refs[:-4], refs[-4:]
    held = len(outs)
    size = res_ref.shape[0] // pieces
    copies = []
    for n, (a, b) in enumerate(((res_hbm, res_ref), (gate_hbm, gate_ref))):
        for i in range(pieces):
            at = pl.ds(i * size, size)
            copies.append(pltpu.make_async_copy(a.at[at], b.at[at], sem.at[n, i]))
    for c in copies:
        c.start()
    tokens, width = res_ref.shape
    me = me_ref[0]
    ids = ids_ref[...]
    hits = [
        ((ids[0:1, :] == e) | (ids[1:2, :] == e)).astype(F32) for e in range(held)
    ]
    m = jnp.concatenate(hits, axis=0)
    upto = (iota((tokens, tokens), 0) <= iota((tokens, tokens), 1)).astype(BF16)
    rank = jnp.dot(m.astype(BF16), upto, preferred_element_type=F32) - 1.0
    slot = iota((CAP, tokens), 0).astype(F32)
    places = [
        jnp.where(rank[e : e + 1, :] == slot, m[e : e + 1, :], 0.0) for e in range(held)
    ]
    place = jnp.concatenate(places, axis=0)
    place_ref[...] = place
    for c in copies:
        c.wait()
    ordered = []
    for d in range(held):
        expert = lax.rem(me + d, held)
        mine = places[0]
        for e in range(1, held):
            mine = jnp.where(expert == e, places[e], mine)
        ordered.append(mine)
    chosen = jnp.concatenate(ordered, axis=0).astype(BF16)
    res = jnp.dot(chosen, res_ref[...], preferred_element_type=F32)
    gate = jnp.dot(chosen, gate_ref[...], preferred_element_type=F32)
    for d in range(held):
        at = slice(d * CAP, (d + 1) * CAP)
        outs[d][:, 0:width] = jnp.concatenate([res[at], gate[at]], axis=0).astype(BF16)
        for n in range(2):
            outs[d][:, width + n * tokens : width + (n + 1) * tokens] = jnp.broadcast_to(
                ids[n : n + 1, :].astype(F32), (2 * CAP, tokens)
            ).astype(BF16)


def route_rows(me, ids, residual, out_gate, held, pieces=4):
    tokens, width = residual.shape
    whole = pl.BlockSpec(memory_space=pltpu.VMEM)
    away = pl.BlockSpec(memory_space=pl.ANY)
    piece = far((2 * CAP, width + 2 * tokens))
    outs = pl.pallas_call(
        functools.partial(route_kernel, pieces),
        out_shape=(piece,) * held + (jax.ShapeDtypeStruct((held * CAP, tokens), F32),),
        in_specs=[pl.BlockSpec(memory_space=pltpu.SMEM), whole, away, away],
        out_specs=(whole,) * (held + 1),
        scratch_shapes=[
            pltpu.VMEM((tokens, width), BF16),
            pltpu.VMEM((tokens, width), BF16),
            pltpu.SemaphoreType.DMA((2, pieces)),
        ],
        compiler_params=params(),
        cost_estimate=cost(64 * tokens * width, 5 * tokens * width),
        name="route_rows",
    )(me, ids, residual, out_gate)
    return outs[:-1], outs[-1]


def by_source(me, pieces, j):
    count = len(pieces)
    out = pieces[0]
    for d in range(1, count):
        out = jnp.where(lax.rem(me + count - d, count) == j, pieces[d], out)
    return out


def place_kernel(group, me_ref, inside_ref, qs_ref, *refs):
    pieces, (some_inside_ref, some_qs_ref, place_ref) = refs[:-3], refs[-3:]
    held = len(pieces)
    tokens = pieces[0].shape[1] // 2
    total = held * tokens
    me = me_ref[0]
    tables = [p[...].astype(F32) for p in pieces]
    ordered = [by_source(me, tables, j) for j in range(held)]
    first = jnp.concatenate([a[0:1, :tokens] for a in ordered], axis=1)
    second = jnp.concatenate([a[0:1, tokens:] for a in ordered], axis=1)
    m = jnp.concatenate(
        [((first == float(e)) | (second == float(e))).astype(F32) for e in range(held)], axis=0
    )
    before = iota((total, total), 0)
    after = iota((total, total), 1)
    upto = ((before <= after) & (before // tokens == after // tokens)).astype(BF16)
    rank = jnp.dot(m.astype(BF16), upto, preferred_element_type=F32) - 1.0
    rows = held * CAP
    r = iota((rows, total), 0)
    t = iota((rows, total), 1)
    here = (t // tokens == r // CAP).astype(F32)
    slot = (r % CAP).astype(F32)
    for e in range(held):
        hit = jnp.where(rank[e : e + 1, :] == slot, m[e : e + 1, :] * here, 0.0)
        place_ref[e * rows : (e + 1) * rows, :] = hit.astype(BF16)
    place = place_ref[...]
    wide = group * HEAD_DIM
    for g in range(qs_ref.shape[1] // wide):
        cols = slice(g * wide, (g + 1) * wide)
        some_qs_ref[:, cols] = jnp.dot(
            place, qs_ref[:, cols], preferred_element_type=F32
        ).astype(BF16)
        rest = inside_ref[:, cols]
        picked = None
        for _ in range(3):
            part = rest.astype(BF16)
            rest = rest - part.astype(F32)
            term = jnp.dot(place, part, preferred_element_type=F32)
            picked = term if picked is None else picked + term
        some_inside_ref[:, cols] = picked


def place_rows(me, inside, qs, pieces, tokens, group=3):
    held = len(pieces)
    chosen = held * held * CAP
    width = pieces[0].shape[1] - 2 * tokens
    at = width // (2 * tokens)
    whole = pl.BlockSpec(memory_space=pltpu.VMEM)
    return pl.pallas_call(
        functools.partial(place_kernel, group),
        grid=(1,),
        out_shape=(
            far((chosen, inside.shape[1]), F32),
            far((chosen, inside.shape[1])),
        ),
        in_specs=[pl.BlockSpec(memory_space=pltpu.SMEM), whole, whole]
        + [pl.BlockSpec((2 * CAP, 2 * tokens), lambda i: (0, at))] * held,
        out_specs=(whole, whole),
        scratch_shapes=[pltpu.VMEM((chosen, held * tokens), BF16)],
        compiler_params=params(),
        cost_estimate=cost(1000000, 200000),
        name="place_rows",
    )(me, inside, qs, *pieces)


def gated(att, res, gate, attn_gain):
    norm = att * lax.rsqrt(jnp.mean(att * att, axis=-1, keepdims=True) + EPS) * attn_gain
    return (res + norm * jax.nn.sigmoid(gate)).astype(BF16)


def routed_norm_kernel(me_ref, att_ref, ag_ref, mg_ref, *refs):
    pieces, one_ref, two_ref = refs[:-2], refs[-2], refs[-1]
    sources, rows, part = att_ref.shape
    width = sources * part
    me = me_ref[0]
    att = jnp.concatenate([att_ref[s].astype(F32) for s in range(sources)], axis=1)
    tables = [p[...][:, :width].astype(F32) for p in pieces]
    ordered = [by_source(me, tables, j) for j in range(sources)]
    res = jnp.concatenate([a[:CAP] for a in ordered], axis=0)
    gate = jnp.concatenate([a[CAP:] for a in ordered], axis=0)
    hidden = gated(att, res, gate, ag_ref[...]).astype(F32)
    normed = (
        hidden * lax.rsqrt(jnp.mean(hidden * hidden, axis=-1, keepdims=True) + EPS) * mg_ref[...]
    ).astype(BF16)
    cut = one_ref.shape[1]
    one_ref[...] = normed[:, :cut]
    for i in range(two_ref.shape[0]):
        two_ref[i] = normed[:, cut:]


def routed_norm(me, att, pieces, attn_gain, moe_gain, copies):
    sources, rows, part = att.shape
    width = sources * part
    cut = width // 2
    whole = pl.BlockSpec(memory_space=pltpu.VMEM)
    return pl.pallas_call(
        routed_norm_kernel,
        out_shape=(far((rows, cut)), far((copies, rows, width - cut))),
        in_specs=[pl.BlockSpec(memory_space=pltpu.SMEM)] + [whole] * (3 + len(pieces)),
        out_specs=(whole, whole),
        compiler_params=params(),
        cost_estimate=cost(20 * rows * width, 20 * rows * width),
        name="routed_norm",
    )(me, att, attn_gain, moe_gain, *pieces)


def hidden_kernel(me_ref, res_ref, gate_ref, ag_ref, *refs):
    pieces, out_ref = refs[:-1], refs[-1]
    me = me_ref[0]
    tables = [p[...].astype(F32) for p in pieces]
    att = jnp.concatenate([by_source(me, tables, j) for j in range(len(pieces))], axis=1)
    out_ref[...] = gated(att, res_ref[...].astype(F32), gate_ref[...].astype(F32), ag_ref[...])


def hidden_rows(me, pieces, residual, out_gate, attn_gain, tile=32):
    rows, part = pieces[0].shape
    width = len(pieces) * part
    block = pl.BlockSpec((tile, width), lambda i: (i, 0))
    return pl.pallas_call(
        hidden_kernel,
        grid=(rows // tile,),
        out_shape=jax.ShapeDtypeStruct((rows, width), BF16),
        in_specs=[
            pl.BlockSpec(memory_space=pltpu.SMEM),
            block,
            block,
            pl.BlockSpec((1, width), lambda i: (0, 0)),
        ]
        + [pl.BlockSpec((tile, part), lambda i: (i, 0))] * len(pieces),
        out_specs=block,
        compiler_params=params(),
        cost_estimate=cost(20 * rows * width, 8 * rows * width),
        name="hidden_rows",
    )(me, residual, out_gate, attn_gain, *pieces)


def repeat_kernel(*refs):
    ins, (out, sem) = refs[:-2], refs[-2:]
    copies = [
        pltpu.make_async_copy(a, out.at[n, k], sem.at[n, k])
        for n in range(out.shape[0])
        for k, a in enumerate(ins)
    ]
    for c in copies:
        c.start()
    for c in copies:
        c.wait()


def repeat(arrays, copies):
    rows, width = arrays[0].shape
    count = len(arrays)
    return pl.pallas_call(
        repeat_kernel,
        out_shape=far((copies, count, rows, width)),
        in_specs=[pl.BlockSpec(memory_space=pl.ANY)]
        + [pl.BlockSpec(memory_space=pltpu.VMEM)] * (count - 1),
        out_specs=pl.BlockSpec(memory_space=pl.ANY),
        scratch_shapes=[pltpu.SemaphoreType.DMA((copies, count))],
        compiler_params=params(),
        cost_estimate=cost(0, 2 * (copies + 1) * count * rows * width),
        name="repeat",
    )(*arrays)


def act_rows(steps, w_ref, one_ref, twos, arrived):
    width = w_ref.shape[2]
    nz, nx, rows, half = one_ref.shape
    nt = (((1,), (1,)), ((), ()))
    wide = width // steps
    gate = up = None
    for s in range(steps):
        cols = slice(s * wide, (s + 1) * wide)
        arrived(s)
        if s * wide < half:
            x = [one_ref[z, k, :, cols] for k in range(nx) for z in range(nz)]
        else:
            near = slice(s * wide - half, (s + 1) * wide - half)
            x = [r[z, :, near] for r in twos for z in range(nz)]
        x = jnp.concatenate(x, axis=0)
        g = lax.dot_general(w_ref[0, :, cols], x, nt, preferred_element_type=F32)
        u = lax.dot_general(w_ref[1, :, cols], x, nt, preferred_element_type=F32)
        gate = g if gate is None else gate + g
        up = u if up is None else up + u
    return (gate * jax.nn.sigmoid(gate) * up).T.astype(BF16)


def first_act_kernel(steps, wg_hbm, wu_hbm, one_ref, *refs):
    twos, (act_ref, w_ref, sem) = refs[:-3], refs[-3:]
    wide = w_ref.shape[2] // steps
    copies = []
    for s in range(steps):
        cols = pl.ds(s * wide, wide)
        for n, a in enumerate((wg_hbm, wu_hbm)):
            copies.append(
                pltpu.make_async_copy(a.at[:, cols], w_ref.at[n, :, cols], sem.at[s, n])
            )
    for c in copies:
        c.start()

    def arrived(s):
        copies[2 * s].wait()
        copies[2 * s + 1].wait()

    act_ref[...] = act_rows(steps, w_ref, one_ref, twos, arrived)


def next_act_kernel(steps, w_ref, one_ref, *refs):
    refs[-1][...] = act_rows(steps, w_ref, one_ref, refs[:-1], lambda s: None)


def expert_act(one, twos, weights, steps=6):
    nz, nx, rows, half = one.shape
    count = nz * nx * rows
    whole = pl.BlockSpec(memory_space=pltpu.VMEM)
    away = pl.BlockSpec(memory_space=pl.ANY)
    if isinstance(weights, tuple):
        units, width = weights[0].shape
        return pl.pallas_call(
            functools.partial(first_act_kernel, steps),
            out_shape=(
                jax.ShapeDtypeStruct((count, units), BF16),
                pltpu.VMEM((2, units, width), BF16),
            ),
            in_specs=[away, away] + [whole] * (1 + len(twos)),
            out_specs=(whole, whole),
            scratch_shapes=[pltpu.SemaphoreType.DMA((steps, 2))],
            compiler_params=params(),
            cost_estimate=cost(4 * count * width * units, 4 * width * units + 2 * count * width),
            name="first_act",
        )(hbm(weights[0]), hbm(weights[1]), one, *twos)
    _, units, width = weights.shape
    return pl.pallas_call(
        functools.partial(next_act_kernel, steps),
        out_shape=jax.ShapeDtypeStruct((count, units), BF16),
        in_specs=[whole] * (2 + len(twos)),
        out_specs=whole,
        compiler_params=params(),
        cost_estimate=cost(4 * count * width * units, 2 * count * width),
        name="next_act",
    )(pltpu.with_memory_space_constraint(weights, pltpu.VMEM), one, *twos)


def down_kernel(steps, first, by_x, act_ref, wd_hbm, *refs):
    wd_ref, sem = refs[-2:]
    half = wd_ref.shape[1]
    wide = half // steps
    copies = []
    for s in range(steps):
        cols = pl.ds(s * wide, wide)
        copies.append(
            pltpu.make_async_copy(
                wd_hbm.at[:, pl.ds(first + s * wide, wide)], wd_ref.at[:, cols], sem.at[s]
            )
        )
    for c in copies:
        c.start()
    refs = refs[:-2]
    added, kept, ends = (refs[0], refs[-2], refs[-1]) if len(refs) != 1 else (None,) * 3
    outs = refs[1:-2] if len(refs) != 1 else refs
    leaving = []

    def send(s, cols):
        n = s * len(outs)
        if len(outs) == 1:
            leaving.append(
                pltpu.make_async_copy(kept.at[:, :, :, cols], outs[0].at[:, :, :, cols], ends.at[n])
            )
            leaving[-1].start()
            return
        for k, ref in enumerate(outs):
            leaving.append(
                pltpu.make_async_copy(kept.at[k, :, :, cols], ref.at[:, :, cols], ends.at[n + k])
            )
            leaving[-1].start()

    act = act_ref[...]
    if by_x:
        nx = outs[0].shape[0] if len(outs) == 1 else len(outs)
        nz = outs[0].shape[-3]
    else:
        nz, nx = outs[0].shape[:2]
    rows = outs[0].shape[-2]
    for s in range(steps):
        cols = slice(s * wide, (s + 1) * wide)
        copies[s].wait()
        out = jnp.dot(act, wd_ref[:, cols], preferred_element_type=F32)
        out = out.reshape(nx, nz, rows, wide)
        if by_x:
            if added is not None:
                out = out + added[:, :, :, cols].astype(F32)
            target = outs[0] if added is None else kept
            target[:, :, :, cols] = out.astype(BF16)
        else:
            for z in range(nz):
                part = out[:, z]
                if added is not None:
                    part = part + added[z, :, :, cols].astype(F32)
                target = outs[0] if added is None else kept
                target[z, :, :, cols] = part.astype(BF16)
        if added is not None:
            send(s, pl.ds(s * wide, wide))
    for c in leaving:
        c.wait()


def expert_down(act, w_down, cut, last, nz, nx, added=None, steps=2):
    count, units = act.shape
    half = w_down.shape[1] - cut if last else cut
    rows = count // (nz * nx)
    whole = pl.BlockSpec(memory_space=pltpu.VMEM)
    if last:
        if added is None:
            shapes = (jax.ShapeDtypeStruct((nx, nz, rows, half), BF16),)
        else:
            shapes = (far((nz, rows, half)),) * nx
    elif added is None:
        shapes = (jax.ShapeDtypeStruct((nz, nx, rows, half), BF16),)
    else:
        shapes = (far((nz, nx, rows, half)),)
    more = () if added is None else (added,)
    away = pl.BlockSpec(memory_space=pl.ANY)
    scratch = [pltpu.VMEM((units, half), BF16), pltpu.SemaphoreType.DMA((steps,))]
    if added is not None:
        scratch = [
            pltpu.VMEM(added.shape, BF16),
            pltpu.SemaphoreType.DMA((steps * len(shapes),)),
        ] + scratch
    return pl.pallas_call(
        functools.partial(down_kernel, steps, cut if last else 0, last),
        out_shape=shapes,
        in_specs=[whole, away] + [whole] * len(more),
        out_specs=(whole if added is None else away,) * len(shapes),
        scratch_shapes=scratch,
        compiler_params=params(),
        cost_estimate=cost(2 * count * half * units, 2 * half * units + 2 * count * half),
        name="expert_down",
    )(act, hbm(w_down), *more)


def block_kernel(in_ref, *outs):
    total = in_ref[0].astype(F32)
    for i in range(1, in_ref.shape[0]):
        total = total + in_ref[i].astype(F32)
    total = total.astype(BF16)
    for n, out in enumerate(outs):
        out[...] = total[n]


def block_sum(parts, steps=2):
    count, n, rows, width = parts.shape
    wide = width // steps
    return pl.pallas_call(
        block_kernel,
        grid=(steps,),
        out_shape=(far((rows, width)),) * n,
        in_specs=[pl.BlockSpec((count, n, rows, wide), lambda i: (0, 0, 0, i))],
        out_specs=(pl.BlockSpec((rows, wide), lambda i: (0, i)),) * n,
        compiler_params=params(),
        cost_estimate=cost(count * n * rows * width, 2 * (count + 1) * n * rows * width),
        name="block_sum",
    )(parts)


def stack_kernel(*refs):
    total = refs[0][...].astype(F32)
    for ref in refs[1:-1]:
        total = total + ref[...].astype(F32)
    refs[-1][...] = total.astype(BF16)


def stack_sum(parts, steps=2):
    n, rows, width = parts[0].shape
    wide = width // steps
    block = pl.BlockSpec((n, rows, wide), lambda i: (0, 0, i))
    return pl.pallas_call(
        stack_kernel,
        grid=(steps,),
        out_shape=far(parts[0].shape),
        in_specs=[block] * len(parts),
        out_specs=block,
        compiler_params=params(),
        cost_estimate=cost(len(parts) * n * rows * width, 2 * (len(parts) + 1) * n * rows * width),
        name="stack_sum",
    )(*parts)


def row_sum_kernel(two_ref, *refs):
    parts, out_ref = refs[:-1], refs[-1]
    one = parts[0][...].astype(F32)
    for ref in parts[1:]:
        one = one + ref[...].astype(F32)
    two = two_ref[0].astype(F32)
    for i in range(1, two_ref.shape[0]):
        two = two + two_ref[i].astype(F32)
    cut = one.shape[1]
    for j in range(out_ref.shape[0]):
        at = slice(j * CAP, (j + 1) * CAP)
        out_ref[j, :, :cut] = one[at].astype(BF16)
        out_ref[j, :, cut:] = two[at].astype(BF16)


def row_sum(parts, two, held):
    count, rows, half = two.shape
    whole = pl.BlockSpec(memory_space=pltpu.VMEM)
    return pl.pallas_call(
        row_sum_kernel,
        out_shape=far((held, CAP, parts[0].shape[1] + half)),
        in_specs=[whole] * (1 + len(parts)),
        out_specs=whole,
        compiler_params=params(),
        cost_estimate=cost(8 * rows * half, 20 * rows * half),
        name="row_sum",
    )(two, *parts)


def combine_kernel(place_ref, rows_ref, ids_ref, weights_ref, out_ref):
    held = rows_ref.shape[0]
    rows = jnp.concatenate([rows_ref[e].astype(F32) for e in range(held)], axis=0).astype(BF16)
    back = lax.dot_general(
        place_ref[...].astype(BF16), rows, (((0,), (0,)), ((), ())), preferred_element_type=F32
    )
    chosen = jnp.sum(
        jnp.where(ids_ref[...] < held, weights_ref[...], 0.0), axis=1, keepdims=True
    )
    out_ref[...] = (back * chosen).astype(BF16)


def combine_rows(place, rows, ids, weights):
    tokens = ids.shape[0]
    width = rows.shape[2]
    return pl.pallas_call(
        combine_kernel,
        out_shape=jax.ShapeDtypeStruct((tokens, width), BF16),
        compiler_params=params(),
        cost_estimate=cost(32 * tokens * width, 2 * tokens * width),
        name="combine_rows",
    )(place, rows, ids, weights)


def exchange(a, axis):
    return lax.all_to_all(a, axis, split_axis=0, concat_axis=0, tiled=True)


def shift(a, axis, by):
    n = lax.axis_size(axis)
    return lax.ppermute(a, axis, [(i, (i + by) % n) for i in range(n)])


def local(
    queries,
    key_vectors,
    values,
    log_decay,
    out_gate,
    residual,
    attn_gain,
    moe_gain,
    expert_ids,
    route_weights,
    w_gate,
    w_up,
    w_down,
):
    held = lax.axis_size("exp")
    rows, width = queries.shape
    heads = log_decay.shape[1]
    tokens = residual.shape[0]
    attn_gain = hbm(attn_gain.reshape(1, -1))
    moe_gain = hbm(moe_gain.reshape(1, -1))
    w_gate = jnp.swapaxes(w_gate, 1, 2)[0]
    w_up = jnp.swapaxes(w_up, 1, 2)[0]
    w_down = w_down[0]
    ids = expert_ids.T
    ld = hbm(log_decay.T)
    me = lax.axis_index("exp").reshape(1)
    keep = lax.optimization_barrier
    nz, nx = lax.axis_size("z"), lax.axis_size("x")

    cum, msg = local_states(hbm(key_vectors), hbm(values), ld)
    sent = exchange(msg, CTX)
    inside, qs = inside_blocks(hbm(queries), hbm(key_vectors), hbm(values), cum, ld)
    pieces, place_own = route_rows(me, ids, hbm(residual), hbm(out_gate), held)
    sent, inside, qs, pieces = keep((sent, inside, qs, pieces))
    prior = scan_blocks(hbm(sent), lax.axis_index(CTX))
    state = exchange(prior, CTX).reshape(heads, HEAD_DIM, HEAD_DIM)
    pieces = [pieces[0]] + [shift(pieces[d], "exp", d) for d in range(1, held)]
    pieces = [hbm(a) for a in pieces]
    some_inside, some_qs = place_rows(me, inside, hbm(qs), pieces, tokens)

    routed = chosen_rows(hbm(some_inside), hbm(some_qs), state)
    _, inside, qs, state = keep((routed, inside, qs, state))
    routed = exchange(routed.reshape(held, held * CAP, width), "exp")
    attention = carried_blocks(me, inside, hbm(qs), state, held)
    routed, attention = keep((routed, attention))
    one, two = routed_norm(me, routed, pieces, attn_gain, moe_gain, nz)

    others = range(1, nx)
    ones = [one] + [shift(one, "x", d) for d in others]
    two = exchange(two, "z")
    across = shift(attention[2], "exp", 2)
    ones, two, across = keep((ones, two, across))
    one = exchange(repeat([hbm(ones[0])] + ones[1:], nz), "z")
    twos = [two] + [shift(two, "x", d) for d in others]
    right, left = shift(attention[1], "exp", 1), shift(attention[3], "exp", 3)
    one, twos, right, left = keep((one, twos, right, left))

    cut = moe_gain.shape[1] * 7 // 12
    act_own, weights = expert_act(one, twos, (w_gate, w_up))
    one, twos = shift(one, "core", 1), [shift(a, "core", 1) for a in twos]
    one, twos, weights = keep((one, twos, weights))
    act_far = expert_act(one, twos, weights)
    (one,) = expert_down(act_far, w_down, cut, False, nz, nx)
    one, act_far = keep((one, act_far))
    (two,) = expert_down(act_far, w_down, cut, True, nz, nx)
    one, two, act_own = keep((one, two, act_own))
    one, two = shift(one, "core", 1), shift(two, "core", 1)
    (one,) = expert_down(act_own, w_down, cut, False, nz, nx, one)
    one, two, act_own = keep((one, two, act_own))
    twos = expert_down(act_own, w_down, cut, True, nz, nx, two)

    one = exchange(one, "z")
    twos = [twos[0]] + [shift(twos[d], "x", -d) for d in others]
    one, twos = keep((one, twos))
    attention = [attention[0], right, across, left]
    ones = block_sum(one)
    ones = [hbm(ones[0])] + [shift(ones[d], "x", -d) for d in others]
    two = exchange(stack_sum([hbm(twos[0])] + twos[1:]), "z")
    hidden = hidden_rows(me, attention, hbm(residual), hbm(out_gate), attn_gain)
    back = exchange(row_sum(ones, two, held), "exp")
    moe_out = combine_rows(place_own, back, expert_ids, route_weights)
    return (hidden, moe_out)


def solution(mesh):
    cube = Mesh(mesh.devices.reshape(4, 4, 2, 4), ("z", "x", "core", "exp"))
    both = CTX + ("exp",)
    in_specs = (
        P(CTX, "exp"),
        P(CTX, "exp"),
        P(CTX, "exp"),
        P(CTX, "exp"),
        P(both, None),
        P(both, None),
        P(),
        P(),
        P(both, None),
        P(both, None),
        P("exp", None, CTX),
        P("exp", None, CTX),
        P("exp", CTX, None),
    )
    out_specs = (P(both, None), P(both, None))
    return jax.shard_map(local, mesh=cube, in_specs=in_specs, out_specs=out_specs, check_vma=False)
```

```python
import functools

import jax
import jax.numpy as jnp
from jax import lax
from jax.experimental import pallas as pl
from jax.experimental.pallas import tpu as pltpu
from jax.sharding import Mesh, PartitionSpec as P

HEAD_DIM = 128
CAP = 4
EPS = 1e-05
F32 = jnp.float32
BF16 = jnp.bfloat16
HIGHEST = lax.Precision.HIGHEST
CTX = ("z", "x", "core")
VMEM_LIMIT = 24 * 1024 * 1024


def iota(shape, dim):
    return lax.broadcasted_iota(jnp.int32, shape, dim)


def hbm(a):
    return pltpu.with_memory_space_constraint(a, pltpu.HBM)


def far(shape, dtype=BF16):
    return pltpu.HBM(shape, dtype)


def params(**kw):
    return pltpu.CompilerParams(vmem_limit_bytes=VMEM_LIMIT, **kw)


def cost(flops, bytes_accessed):
    return pl.CostEstimate(flops=flops, bytes_accessed=bytes_accessed, transcendentals=0)


def running_sum(ld, axis):
    rows = ld.shape[1]
    a, b = iota((rows, rows), 0), iota((rows, rows), 1)
    ones = (a >= b).astype(BF16)
    total = None
    rest = ld
    for _ in range(3):
        part = rest.astype(BF16)
        rest = rest - part.astype(F32)
        pair = (ones, part) if axis == 0 else (part, ones)
        term = lax.dot_general(*pair, (((1,), (1,)), ((), ())), preferred_element_type=F32)
        total = term if total is None else total + term
    return total


def spread(table, first, count, terms):
    n = table.shape[1]
    shape = (n, count * HEAD_DIM)
    pick = (iota(shape, 0) == first + iota(shape, 1) // HEAD_DIM).astype(BF16)
    total = None
    rest = table
    for _ in range(terms):
        part = rest.astype(BF16)
        rest = rest - part.astype(F32)
        term = jnp.dot(part, pick, preferred_element_type=F32)
        total = term if total is None else total + term
    return total


def state_kernel(
    group, k_hbm, v_hbm, ld_ref, cum_ref, out_hbm, k_ref, v_ref, msg_ref, arrive, leave
):
    heads, rows = ld_ref.shape
    per = heads * HEAD_DIM // 32
    parts = group * HEAD_DIM // per
    wide = group * HEAD_DIM
    arriving = []
    for g in range(heads // group):
        cols = pl.ds(g * wide, wide)
        for n, (a, b) in enumerate(((k_hbm, k_ref), (v_hbm, v_ref))):
            arriving.append(pltpu.make_async_copy(a.at[:, cols], b.at[:, cols], arrive.at[g, n]))
    for c in arriving:
        c.start()
    cum = running_sum(ld_ref[...], 0)
    cum_ref[...] = cum
    final = cum[rows - 1 : rows, :]
    fades = jnp.exp(final - cum)
    decays = jnp.broadcast_to(jnp.exp(final), (16, heads))
    row16 = iota((16, HEAD_DIM), 0)
    leaving = []
    for g in range(heads // group):
        fade = spread(fades, g * group, group, 2)
        decay = spread(decays, g * group, group, 2)
        arriving[2 * g].wait()
        arriving[2 * g + 1].wait()
        tiles = []
        for j in range(group):
            cols = slice(j * HEAD_DIM, (j + 1) * HEAD_DIM)
            if j % 2 == 0:
                two = slice(j * HEAD_DIM, (j + 2) * HEAD_DIM)
                both = slice((g * group + j) * HEAD_DIM, (g * group + j + 2) * HEAD_DIM)
                wk = (k_ref[:, both].astype(F32) * fade[:, two]).astype(BF16)
                pair = lax.dot_general(
                    wk, v_ref[:, both], (((0,), (0,)), ((), ())), preferred_element_type=F32
                )
            at = slice((j % 2) * HEAD_DIM, (j % 2 + 1) * HEAD_DIM)
            state = pair[at, at].astype(BF16)
            row = (g * group + j) * HEAD_DIM
            end = row + HEAD_DIM
            lo = 0
            while row < end:
                part, at = row // per, row % per
                take = min(per - at, end - row)
                msg_ref[part, at : at + take, :] = state[lo : lo + take, :]
                row += take
                lo += take
            whole = decay[:, cols]
            high = whole.astype(BF16).astype(F32)
            tiles.append((high, whole - high))
        for part in range(parts):
            first = per * part // HEAD_DIM
            last = (per * part + per - 1) // HEAD_DIM
            tile = jnp.where(
                row16 == 0,
                tiles[first][0],
                jnp.where(
                    row16 == 1,
                    tiles[first][1],
                    jnp.where(row16 == 2, tiles[last][0], tiles[last][1]),
                ),
            )
            msg_ref[g * parts + part, per : per + 16, :] = tile.astype(BF16)
        at = pl.ds(g * parts, parts)
        leaving.append(pltpu.make_async_copy(msg_ref.at[at], out_hbm.at[at], leave.at[g]))
        leaving[-1].start()
    for c in leaving:
        c.wait()


def local_states(k, v, ld, group=6):
    rows, width = k.shape
    heads = ld.shape[0]
    per = heads * HEAD_DIM // 32
    whole = pl.BlockSpec(memory_space=pltpu.VMEM)
    away = pl.BlockSpec(memory_space=pl.ANY)
    steps = heads // group
    return pl.pallas_call(
        functools.partial(state_kernel, group),
        out_shape=(
            jax.ShapeDtypeStruct((rows, heads), F32),
            far((32, per + 16, HEAD_DIM)),
        ),
        in_specs=[away, away, whole],
        out_specs=(whole, away),
        scratch_shapes=[
            pltpu.VMEM((rows, width), BF16),
            pltpu.VMEM((rows, width), BF16),
            pltpu.VMEM((32, per + 16, HEAD_DIM), BF16),
            pltpu.SemaphoreType.DMA((steps, 2)),
            pltpu.SemaphoreType.DMA((steps,)),
        ],
        compiler_params=params(),
        cost_estimate=cost(2 * rows * width * HEAD_DIM, 4 * rows * width),
        name="local_states",
    )(k, v, ld)


def scan_kernel(split_ref, in_ref, out_ref):
    parts, per, width = out_ref.shape
    first_rows = iota((per, width), 0) < split_ref[0]
    state = jnp.zeros((per, width), F32)
    for b in range(parts):
        out_ref[b, :, :] = state.astype(BF16)
        if b + 1 < parts:
            tail = in_ref[b, per : per + 16, :].astype(F32)
            d0 = tail[0:1, :] + tail[1:2, :]
            d1 = tail[2:3, :] + tail[3:4, :]
            decay = jnp.where(first_rows, d0, d1)
            state = decay * state + in_ref[b, 0:per, :].astype(F32)


def scan_blocks(msg, part):
    parts, tall, width = msg.shape
    per = tall - 16
    split = (HEAD_DIM - (per * part) % HEAD_DIM).astype(jnp.int32).reshape(1)
    return pl.pallas_call(
        scan_kernel,
        out_shape=far((parts, per, width)),
        in_specs=[
            pl.BlockSpec(memory_space=pltpu.SMEM),
            pl.BlockSpec(memory_space=pltpu.VMEM),
        ],
        out_specs=pl.BlockSpec(memory_space=pltpu.VMEM),
        compiler_params=params(),
        cost_estimate=cost(1000000, 1000000),
        name="scan_blocks",
    )(split, msg)


def inside_kernel(group, q_ref, k_ref, v_ref, cum_ref, ld_ref, inside_ref, qs_ref, cumt_ref):
    rows, heads = cum_ref.shape

    @pl.when(pl.program_id(0) == 0)
    def _():
        cumt_ref[...] = running_sum(ld_ref[...], 1)

    cum = spread(cum_ref[...], pl.program_id(0) * group, group, 3)
    size = 2 * HEAD_DIM
    causal = iota((size, size), 0) >= iota((size, size), 1)
    for j in range(group):
        h = pl.program_id(0) * group + j
        cols = slice(j * HEAD_DIM, (j + 1) * HEAD_DIM)
        col = cum[:, cols]
        row = cumt_ref[pl.ds(h, 1), :]
        q = q_ref[:, cols]
        k = k_ref[:, cols]
        v = v_ref[:, cols]
        qs_ref[:, cols] = (q.astype(F32) * jnp.exp(col)).astype(BF16)
        wide = jnp.concatenate([col, col], axis=1)
        total = None
        for lo in range(0, rows, size):
            hi = lo + size
            s = lax.dot_general(
                q[lo:], k[lo:hi], (((1,), (1,)), ((), ())), preferred_element_type=F32
            )
            decay = jnp.exp(jnp.minimum(wide[lo:] - row[:, lo:hi], 0.0))
            w = s * decay
            w = jnp.concatenate([jnp.where(causal, w[:size], 0.0), w[size:]], axis=0) if (
                hi < rows
            ) else jnp.where(causal, w, 0.0)
            part = jnp.dot(w.astype(BF16), v[lo:hi], preferred_element_type=F32)
            if total is None:
                total = part
            else:
                total = jnp.concatenate([total[:lo], total[lo:] + part], axis=0)
        inside_ref[:, cols] = total


def inside_blocks(q, k, v, cum, ld, group=3):
    rows, width = q.shape
    heads = cum.shape[1]
    block = pl.BlockSpec((rows, group * HEAD_DIM), lambda g: (0, g))
    return pl.pallas_call(
        functools.partial(inside_kernel, group),
        grid=(heads // group,),
        out_shape=(
            jax.ShapeDtypeStruct((rows, width), F32),
            far((rows, width)),
        ),
        in_specs=[
            block,
            block,
            block,
            pl.BlockSpec((rows, heads), lambda g: (0, 0)),
            pl.BlockSpec((heads, rows), lambda g: (0, 0)),
        ],
        out_specs=(block, block),
        scratch_shapes=[pltpu.VMEM((heads, rows), F32)],
        compiler_params=params(),
        cost_estimate=cost(4 * rows * rows * width, 12 * rows * width),
        name="inside_blocks",
    )(q, k, v, cum, ld)


def attend(group, inside_ref, qs_ref, state_ref, att_ref):
    for j in range(group):
        cols = slice(j * HEAD_DIM, (j + 1) * HEAD_DIM)
        att_ref[:, cols] = (
            inside_ref[:, cols]
            + jnp.dot(qs_ref[:, cols], state_ref[j], preferred_element_type=F32)
        ).astype(BF16)


def chosen_kernel(inside_ref, qs_ref, state_ref, sel_ref):
    for h in range(state_ref.shape[0]):
        cols = slice(h * HEAD_DIM, (h + 1) * HEAD_DIM)
        sel_ref[:, cols] = (
            inside_ref[:, cols]
            + jnp.dot(qs_ref[:, cols], state_ref[h], preferred_element_type=F32)
        ).astype(BF16)


def carried_kernel(group, me_ref, inside_ref, qs_ref, state_ref, *refs):
    outs, att_ref = refs[:-1], refs[-1]
    held = len(outs)
    tokens = outs[0].shape[0]
    attend(group, inside_ref, qs_ref, state_ref, att_ref)
    for d in range(held):
        at = pl.multiple_of(lax.rem(me_ref[0] + d, held) * tokens, tokens)
        outs[d][...] = att_ref[pl.ds(at, tokens), :]


def chosen_rows(inside, qs, state):
    chosen, width = inside.shape
    return pl.pallas_call(
        chosen_kernel,
        out_shape=far((chosen, width)),
        compiler_params=params(),
        cost_estimate=cost(2 * chosen * width * HEAD_DIM, 8 * chosen * width),
        name="chosen_rows",
    )(inside, qs, state)


def carried_blocks(me, inside, qs, state, held, group=3):
    rows, width = inside.shape
    heads = width // HEAD_DIM
    wide = group * HEAD_DIM
    tokens = rows // held
    block = pl.BlockSpec((rows, wide), lambda g: (0, g))
    return list(
        pl.pallas_call(
            functools.partial(carried_kernel, group),
            grid=(heads // group,),
            out_shape=(far((tokens, width)),) * held,
            in_specs=[
                pl.BlockSpec(memory_space=pltpu.SMEM),
                block,
                block,
                pl.BlockSpec((group, HEAD_DIM, HEAD_DIM), lambda g: (g, 0, 0)),
            ],
            out_specs=(pl.BlockSpec((tokens, wide), lambda g: (0, g)),) * held,
            scratch_shapes=[pltpu.VMEM((rows, wide), BF16)],
            compiler_params=params(),
            cost_estimate=cost(4 * rows * width * HEAD_DIM, 8 * rows * width),
            name="carried_blocks",
        )(me, inside, qs, state)
    )


def route_kernel(pieces, me_ref, ids_ref, res_hbm, gate_hbm, *refs):
    outs, (place_ref, res_ref, gate_ref, sem) = refs[:-4], refs[-4:]
    held = len(outs)
    size = res_ref.shape[0] // pieces
    copies = []
    for n, (a, b) in enumerate(((res_hbm, res_ref), (gate_hbm, gate_ref))):
        for i in range(pieces):
            at = pl.ds(i * size, size)
            copies.append(pltpu.make_async_copy(a.at[at], b.at[at], sem.at[n, i]))
    for c in copies:
        c.start()
    tokens, width = res_ref.shape
    me = me_ref[0]
    ids = ids_ref[...]
    hits = [
        ((ids[0:1, :] == e) | (ids[1:2, :] == e)).astype(F32) for e in range(held)
    ]
    m = jnp.concatenate(hits, axis=0)
    upto = (iota((tokens, tokens), 0) <= iota((tokens, tokens), 1)).astype(BF16)
    rank = jnp.dot(m.astype(BF16), upto, preferred_element_type=F32) - 1.0
    slot = iota((CAP, tokens), 0).astype(F32)
    places = [
        jnp.where(rank[e : e + 1, :] == slot, m[e : e + 1, :], 0.0) for e in range(held)
    ]
    place = jnp.concatenate(places, axis=0)
    place_ref[...] = place
    for c in copies:
        c.wait()
    ordered = []
    for d in range(held):
        expert = lax.rem(me + d, held)
        mine = places[0]
        for e in range(1, held):
            mine = jnp.where(expert == e, places[e], mine)
        ordered.append(mine)
    chosen = jnp.concatenate(ordered, axis=0).astype(BF16)
    res = jnp.dot(chosen, res_ref[...], preferred_element_type=F32)
    gate = jnp.dot(chosen, gate_ref[...], preferred_element_type=F32)
    for d in range(held):
        at = slice(d * CAP, (d + 1) * CAP)
        outs[d][:, 0:width] = jnp.concatenate([res[at], gate[at]], axis=0).astype(BF16)
        for n in range(2):
            outs[d][:, width + n * tokens : width + (n + 1) * tokens] = jnp.broadcast_to(
                ids[n : n + 1, :].astype(F32), (2 * CAP, tokens)
            ).astype(BF16)


def route_rows(me, ids, residual, out_gate, held, pieces=4):
    tokens, width = residual.shape
    whole = pl.BlockSpec(memory_space=pltpu.VMEM)
    away = pl.BlockSpec(memory_space=pl.ANY)
    piece = far((2 * CAP, width + 2 * tokens))
    outs = pl.pallas_call(
        functools.partial(route_kernel, pieces),
        out_shape=(piece,) * held + (jax.ShapeDtypeStruct((held * CAP, tokens), F32),),
        in_specs=[pl.BlockSpec(memory_space=pltpu.SMEM), whole, away, away],
        out_specs=(whole,) * (held + 1),
        scratch_shapes=[
            pltpu.VMEM((tokens, width), BF16),
            pltpu.VMEM((tokens, width), BF16),
            pltpu.SemaphoreType.DMA((2, pieces)),
        ],
        compiler_params=params(),
        cost_estimate=cost(64 * tokens * width, 5 * tokens * width),
        name="route_rows",
    )(me, ids, residual, out_gate)
    return outs[:-1], outs[-1]


def by_source(me, pieces, j):
    count = len(pieces)
    out = pieces[0]
    for d in range(1, count):
        out = jnp.where(lax.rem(me + count - d, count) == j, pieces[d], out)
    return out


def place_kernel(group, me_ref, inside_ref, qs_ref, *refs):
    pieces, (some_inside_ref, some_qs_ref, place_ref) = refs[:-3], refs[-3:]
    held = len(pieces)
    tokens = pieces[0].shape[1] // 2
    total = held * tokens
    me = me_ref[0]
    tables = [p[...].astype(F32) for p in pieces]
    ordered = [by_source(me, tables, j) for j in range(held)]
    first = jnp.concatenate([a[0:1, :tokens] for a in ordered], axis=1)
    second = jnp.concatenate([a[0:1, tokens:] for a in ordered], axis=1)
    m = jnp.concatenate(
        [((first == float(e)) | (second == float(e))).astype(F32) for e in range(held)], axis=0
    )
    before = iota((total, total), 0)
    after = iota((total, total), 1)
    upto = ((before <= after) & (before // tokens == after // tokens)).astype(BF16)
    rank = jnp.dot(m.astype(BF16), upto, preferred_element_type=F32) - 1.0
    rows = held * CAP
    r = iota((rows, total), 0)
    t = iota((rows, total), 1)
    here = (t // tokens == r // CAP).astype(F32)
    slot = (r % CAP).astype(F32)
    for e in range(held):
        hit = jnp.where(rank[e : e + 1, :] == slot, m[e : e + 1, :] * here, 0.0)
        place_ref[e * rows : (e + 1) * rows, :] = hit.astype(BF16)
    place = place_ref[...]
    wide = group * HEAD_DIM
    for g in range(qs_ref.shape[1] // wide):
        cols = slice(g * wide, (g + 1) * wide)
        some_qs_ref[:, cols] = jnp.dot(
            place, qs_ref[:, cols], preferred_element_type=F32
        ).astype(BF16)
        rest = inside_ref[:, cols]
        picked = None
        for _ in range(3):
            part = rest.astype(BF16)
            rest = rest - part.astype(F32)
            term = jnp.dot(place, part, preferred_element_type=F32)
            picked = term if picked is None else picked + term
        some_inside_ref[:, cols] = picked


def place_rows(me, inside, qs, pieces, tokens, group=3):
    held = len(pieces)
    chosen = held * held * CAP
    width = pieces[0].shape[1] - 2 * tokens
    at = width // (2 * tokens)
    whole = pl.BlockSpec(memory_space=pltpu.VMEM)
    return pl.pallas_call(
        functools.partial(place_kernel, group),
        grid=(1,),
        out_shape=(
            far((chosen, inside.shape[1]), F32),
            far((chosen, inside.shape[1])),
        ),
        in_specs=[pl.BlockSpec(memory_space=pltpu.SMEM), whole, whole]
        + [pl.BlockSpec((2 * CAP, 2 * tokens), lambda i: (0, at))] * held,
        out_specs=(whole, whole),
        scratch_shapes=[pltpu.VMEM((chosen, held * tokens), BF16)],
        compiler_params=params(),
        cost_estimate=cost(1000000, 200000),
        name="place_rows",
    )(me, inside, qs, *pieces)


def gated(att, res, gate, attn_gain):
    norm = att * lax.rsqrt(jnp.mean(att * att, axis=-1, keepdims=True) + EPS) * attn_gain
    return (res + norm * jax.nn.sigmoid(gate)).astype(BF16)


def routed_norm_kernel(me_ref, att_ref, ag_ref, mg_ref, *refs):
    pieces, one_ref, two_ref = refs[:-2], refs[-2], refs[-1]
    sources, rows, part = att_ref.shape
    width = sources * part
    me = me_ref[0]
    att = jnp.concatenate([att_ref[s].astype(F32) for s in range(sources)], axis=1)
    tables = [p[...][:, :width].astype(F32) for p in pieces]
    ordered = [by_source(me, tables, j) for j in range(sources)]
    res = jnp.concatenate([a[:CAP] for a in ordered], axis=0)
    gate = jnp.concatenate([a[CAP:] for a in ordered], axis=0)
    hidden = gated(att, res, gate, ag_ref[...]).astype(F32)
    normed = (
        hidden * lax.rsqrt(jnp.mean(hidden * hidden, axis=-1, keepdims=True) + EPS) * mg_ref[...]
    ).astype(BF16)
    cut = one_ref.shape[1]
    one_ref[...] = normed[:, :cut]
    for i in range(two_ref.shape[0]):
        two_ref[i] = normed[:, cut:]


def routed_norm(me, att, pieces, attn_gain, moe_gain, copies):
    sources, rows, part = att.shape
    width = sources * part
    cut = width // 2
    whole = pl.BlockSpec(memory_space=pltpu.VMEM)
    return pl.pallas_call(
        routed_norm_kernel,
        out_shape=(far((rows, cut)), far((copies, rows, width - cut))),
        in_specs=[pl.BlockSpec(memory_space=pltpu.SMEM)] + [whole] * (3 + len(pieces)),
        out_specs=(whole, whole),
        compiler_params=params(),
        cost_estimate=cost(20 * rows * width, 20 * rows * width),
        name="routed_norm",
    )(me, att, attn_gain, moe_gain, *pieces)


def hidden_kernel(me_ref, res_ref, gate_ref, ag_ref, *refs):
    pieces, out_ref = refs[:-1], refs[-1]
    me = me_ref[0]
    tables = [p[...].astype(F32) for p in pieces]
    att = jnp.concatenate([by_source(me, tables, j) for j in range(len(pieces))], axis=1)
    out_ref[...] = gated(att, res_ref[...].astype(F32), gate_ref[...].astype(F32), ag_ref[...])


def hidden_rows(me, pieces, residual, out_gate, attn_gain, tile=32):
    rows, part = pieces[0].shape
    width = len(pieces) * part
    block = pl.BlockSpec((tile, width), lambda i: (i, 0))
    return pl.pallas_call(
        hidden_kernel,
        grid=(rows // tile,),
        out_shape=jax.ShapeDtypeStruct((rows, width), BF16),
        in_specs=[
            pl.BlockSpec(memory_space=pltpu.SMEM),
            block,
            block,
            pl.BlockSpec((1, width), lambda i: (0, 0)),
        ]
        + [pl.BlockSpec((tile, part), lambda i: (i, 0))] * len(pieces),
        out_specs=block,
        compiler_params=params(),
        cost_estimate=cost(20 * rows * width, 8 * rows * width),
        name="hidden_rows",
    )(me, residual, out_gate, attn_gain, *pieces)


def repeat_kernel(*refs):
    ins, (out, sem) = refs[:-2], refs[-2:]
    copies = [
        pltpu.make_async_copy(a, out.at[n, k], sem.at[n, k])
        for n in range(out.shape[0])
        for k, a in enumerate(ins)
    ]
    for c in copies:
        c.start()
    for c in copies:
        c.wait()


def repeat(arrays, copies):
    rows, width = arrays[0].shape
    count = len(arrays)
    return pl.pallas_call(
        repeat_kernel,
        out_shape=far((copies, count, rows, width)),
        in_specs=[pl.BlockSpec(memory_space=pltpu.VMEM)] * count,
        out_specs=pl.BlockSpec(memory_space=pl.ANY),
        scratch_shapes=[pltpu.SemaphoreType.DMA((copies, count))],
        compiler_params=params(),
        cost_estimate=cost(0, 2 * (copies + 1) * count * rows * width),
        name="repeat",
    )(*arrays)


def act_rows(steps, w_ref, one_ref, twos, arrived):
    width = w_ref.shape[2]
    nz, nx, rows, half = one_ref.shape
    nt = (((1,), (1,)), ((), ()))
    wide = width // steps
    gate = up = None
    for s in range(steps):
        cols = slice(s * wide, (s + 1) * wide)
        arrived(s)
        if s * wide < half:
            x = [one_ref[z, k, :, cols] for k in range(nx) for z in range(nz)]
        else:
            near = slice(s * wide - half, (s + 1) * wide - half)
            x = [r[z, :, near] for r in twos for z in range(nz)]
        x = jnp.concatenate(x, axis=0)
        g = lax.dot_general(w_ref[0, :, cols], x, nt, preferred_element_type=F32)
        u = lax.dot_general(w_ref[1, :, cols], x, nt, preferred_element_type=F32)
        gate = g if gate is None else gate + g
        up = u if up is None else up + u
    return (gate * jax.nn.sigmoid(gate) * up).T.astype(BF16)


def first_act_kernel(steps, wg_hbm, wu_hbm, one_ref, *refs):
    twos, (act_ref, w_ref, sem) = refs[:-3], refs[-3:]
    wide = w_ref.shape[2] // steps
    copies = []
    for s in range(steps):
        cols = pl.ds(s * wide, wide)
        for n, a in enumerate((wg_hbm, wu_hbm)):
            copies.append(
                pltpu.make_async_copy(a.at[:, cols], w_ref.at[n, :, cols], sem.at[s, n])
            )
    for c in copies:
        c.start()

    def arrived(s):
        copies[2 * s].wait()
        copies[2 * s + 1].wait()

    act_ref[...] = act_rows(steps, w_ref, one_ref, twos, arrived)


def next_act_kernel(steps, w_ref, one_ref, *refs):
    refs[-1][...] = act_rows(steps, w_ref, one_ref, refs[:-1], lambda s: None)


def expert_act(one, twos, weights, steps=6):
    nz, nx, rows, half = one.shape
    count = nz * nx * rows
    whole = pl.BlockSpec(memory_space=pltpu.VMEM)
    away = pl.BlockSpec(memory_space=pl.ANY)
    if isinstance(weights, tuple):
        units, width = weights[0].shape
        return pl.pallas_call(
            functools.partial(first_act_kernel, steps),
            out_shape=(
                jax.ShapeDtypeStruct((count, units), BF16),
                pltpu.VMEM((2, units, width), BF16),
            ),
            in_specs=[away, away] + [whole] * (1 + len(twos)),
            out_specs=(whole, whole),
            scratch_shapes=[pltpu.SemaphoreType.DMA((steps, 2))],
            compiler_params=params(),
            cost_estimate=cost(4 * count * width * units, 4 * width * units + 2 * count * width),
            name="first_act",
        )(hbm(weights[0]), hbm(weights[1]), one, *twos)
    _, units, width = weights.shape
    return pl.pallas_call(
        functools.partial(next_act_kernel, steps),
        out_shape=jax.ShapeDtypeStruct((count, units), BF16),
        in_specs=[whole] * (2 + len(twos)),
        out_specs=whole,
        compiler_params=params(),
        cost_estimate=cost(4 * count * width * units, 2 * count * width),
        name="next_act",
    )(pltpu.with_memory_space_constraint(weights, pltpu.VMEM), one, *twos)


def down_kernel(steps, first, by_x, act_ref, wd_hbm, *refs):
    wd_ref, sem = refs[-2:]
    half = wd_ref.shape[1]
    wide = half // steps
    copies = []
    for s in range(steps):
        cols = pl.ds(s * wide, wide)
        copies.append(
            pltpu.make_async_copy(
                wd_hbm.at[:, pl.ds(first + s * wide, wide)], wd_ref.at[:, cols], sem.at[s]
            )
        )
    for c in copies:
        c.start()
    refs = refs[:-2]
    added, kept, ends = (refs[0], refs[-2], refs[-1]) if len(refs) != 1 else (None,) * 3
    outs = refs[1:-2] if len(refs) != 1 else refs
    leaving = []

    def send(s, cols):
        n = s * len(outs)
        if len(outs) == 1:
            leaving.append(
                pltpu.make_async_copy(kept.at[:, :, :, cols], outs[0].at[:, :, :, cols], ends.at[n])
            )
            leaving[-1].start()
            return
        for k, ref in enumerate(outs):
            leaving.append(
                pltpu.make_async_copy(kept.at[k, :, :, cols], ref.at[:, :, cols], ends.at[n + k])
            )
            leaving[-1].start()

    act = act_ref[...]
    if by_x:
        nx = outs[0].shape[0] if len(outs) == 1 else len(outs)
        nz = outs[0].shape[-3]
    else:
        nz, nx = outs[0].shape[:2]
    rows = outs[0].shape[-2]
    for s in range(steps):
        cols = slice(s * wide, (s + 1) * wide)
        copies[s].wait()
        out = jnp.dot(act, wd_ref[:, cols], preferred_element_type=F32)
        out = out.reshape(nx, nz, rows, wide)
        if by_x:
            if added is not None:
                out = out + added[:, :, :, cols].astype(F32)
            target = outs[0] if added is None else kept
            target[:, :, :, cols] = out.astype(BF16)
        else:
            for z in range(nz):
                part = out[:, z]
                if added is not None:
                    part = part + added[z, :, :, cols].astype(F32)
                target = outs[0] if added is None else kept
                target[z, :, :, cols] = part.astype(BF16)
        if added is not None:
            send(s, pl.ds(s * wide, wide))
    for c in leaving:
        c.wait()


def expert_down(act, w_down, cut, last, nz, nx, added=None, steps=2):
    count, units = act.shape
    half = w_down.shape[1] - cut if last else cut
    rows = count // (nz * nx)
    whole = pl.BlockSpec(memory_space=pltpu.VMEM)
    if last:
        if added is None:
            shapes = (jax.ShapeDtypeStruct((nx, nz, rows, half), BF16),)
        else:
            shapes = (far((nz, rows, half)),) * nx
    elif added is None:
        shapes = (jax.ShapeDtypeStruct((nz, nx, rows, half), BF16),)
    else:
        shapes = (far((nz, nx, rows, half)),)
    more = () if added is None else (added,)
    away = pl.BlockSpec(memory_space=pl.ANY)
    scratch = [pltpu.VMEM((units, half), BF16), pltpu.SemaphoreType.DMA((steps,))]
    if added is not None:
        scratch = [
            pltpu.VMEM(added.shape, BF16),
            pltpu.SemaphoreType.DMA((steps * len(shapes),)),
        ] + scratch
    return pl.pallas_call(
        functools.partial(down_kernel, steps, cut if last else 0, last),
        out_shape=shapes,
        in_specs=[whole, away] + [whole] * len(more),
        out_specs=(whole if added is None else away,) * len(shapes),
        scratch_shapes=scratch,
        compiler_params=params(),
        cost_estimate=cost(2 * count * half * units, 2 * half * units + 2 * count * half),
        name="expert_down",
    )(act, hbm(w_down), *more)


def block_kernel(in_ref, *outs):
    total = in_ref[0].astype(F32)
    for i in range(1, in_ref.shape[0]):
        total = total + in_ref[i].astype(F32)
    total = total.astype(BF16)
    for n, out in enumerate(outs):
        out[...] = total[n]


def block_sum(parts, steps=2):
    count, n, rows, width = parts.shape
    wide = width // steps
    return pl.pallas_call(
        block_kernel,
        grid=(steps,),
        out_shape=(far((rows, width)),) * n,
        in_specs=[pl.BlockSpec((count, n, rows, wide), lambda i: (0, 0, 0, i))],
        out_specs=(pl.BlockSpec((rows, wide), lambda i: (0, i)),) * n,
        compiler_params=params(),
        cost_estimate=cost(count * n * rows * width, 2 * (count + 1) * n * rows * width),
        name="block_sum",
    )(parts)


def stack_kernel(*refs):
    total = refs[0][...].astype(F32)
    for ref in refs[1:-1]:
        total = total + ref[...].astype(F32)
    refs[-1][...] = total.astype(BF16)


def stack_sum(parts, steps=2):
    n, rows, width = parts[0].shape
    wide = width // steps
    block = pl.BlockSpec((n, rows, wide), lambda i: (0, 0, i))
    return pl.pallas_call(
        stack_kernel,
        grid=(steps,),
        out_shape=far(parts[0].shape),
        in_specs=[block] * len(parts),
        out_specs=block,
        compiler_params=params(),
        cost_estimate=cost(len(parts) * n * rows * width, 2 * (len(parts) + 1) * n * rows * width),
        name="stack_sum",
    )(*parts)


def row_sum_kernel(two_ref, *refs):
    parts, out_ref = refs[:-1], refs[-1]
    one = parts[0][...].astype(F32)
    for ref in parts[1:]:
        one = one + ref[...].astype(F32)
    two = two_ref[0].astype(F32)
    for i in range(1, two_ref.shape[0]):
        two = two + two_ref[i].astype(F32)
    cut = one.shape[1]
    for j in range(out_ref.shape[0]):
        at = slice(j * CAP, (j + 1) * CAP)
        out_ref[j, :, :cut] = one[at].astype(BF16)
        out_ref[j, :, cut:] = two[at].astype(BF16)


def row_sum(parts, two, held):
    count, rows, half = two.shape
    whole = pl.BlockSpec(memory_space=pltpu.VMEM)
    return pl.pallas_call(
        row_sum_kernel,
        out_shape=far((held, CAP, parts[0].shape[1] + half)),
        in_specs=[whole] * (1 + len(parts)),
        out_specs=whole,
        compiler_params=params(),
        cost_estimate=cost(8 * rows * half, 20 * rows * half),
        name="row_sum",
    )(two, *parts)


def combine_kernel(place_ref, rows_ref, ids_ref, weights_ref, out_ref):
    held = rows_ref.shape[0]
    rows = jnp.concatenate([rows_ref[e].astype(F32) for e in range(held)], axis=0).astype(BF16)
    back = lax.dot_general(
        place_ref[...].astype(BF16), rows, (((0,), (0,)), ((), ())), preferred_element_type=F32
    )
    chosen = jnp.sum(
        jnp.where(ids_ref[...] < held, weights_ref[...], 0.0), axis=1, keepdims=True
    )
    out_ref[...] = (back * chosen).astype(BF16)


def combine_rows(place, rows, ids, weights):
    tokens = ids.shape[0]
    width = rows.shape[2]
    return pl.pallas_call(
        combine_kernel,
        out_shape=jax.ShapeDtypeStruct((tokens, width), BF16),
        compiler_params=params(),
        cost_estimate=cost(32 * tokens * width, 2 * tokens * width),
        name="combine_rows",
    )(place, rows, ids, weights)


def exchange(a, axis):
    return lax.all_to_all(a, axis, split_axis=0, concat_axis=0, tiled=True)


def shift(a, axis, by):
    n = lax.axis_size(axis)
    return lax.ppermute(a, axis, [(i, (i + by) % n) for i in range(n)])


def local(
    queries,
    key_vectors,
    values,
    log_decay,
    out_gate,
    residual,
    attn_gain,
    moe_gain,
    expert_ids,
    route_weights,
    w_gate,
    w_up,
    w_down,
):
    held = lax.axis_size("exp")
    rows, width = queries.shape
    heads = log_decay.shape[1]
    tokens = residual.shape[0]
    attn_gain = hbm(attn_gain.reshape(1, -1))
    moe_gain = hbm(moe_gain.reshape(1, -1))
    w_gate = jnp.swapaxes(w_gate, 1, 2)[0]
    w_up = jnp.swapaxes(w_up, 1, 2)[0]
    w_down = w_down[0]
    ids = expert_ids.T
    ld = hbm(log_decay.T)
    me = lax.axis_index("exp").reshape(1)
    keep = lax.optimization_barrier
    nz, nx = lax.axis_size("z"), lax.axis_size("x")

    cum, msg = local_states(hbm(key_vectors), hbm(values), ld)
    sent = exchange(msg, CTX)
    inside, qs = inside_blocks(hbm(queries), hbm(key_vectors), hbm(values), cum, ld)
    pieces, place_own = route_rows(me, ids, hbm(residual), hbm(out_gate), held)
    sent, inside, qs, pieces = keep((sent, inside, qs, pieces))
    prior = scan_blocks(hbm(sent), lax.axis_index(CTX))
    state = exchange(prior, CTX).reshape(heads, HEAD_DIM, HEAD_DIM)
    pieces = [pieces[0]] + [shift(pieces[d], "exp", d) for d in range(1, held)]
    pieces = [hbm(a) for a in pieces]
    some_inside, some_qs = place_rows(me, inside, hbm(qs), pieces, tokens)

    routed = chosen_rows(hbm(some_inside), hbm(some_qs), state)
    _, inside, qs, state = keep((routed, inside, qs, state))
    routed = exchange(routed.reshape(held, held * CAP, width), "exp")
    attention = carried_blocks(me, inside, hbm(qs), state, held)
    routed, attention = keep((routed, attention))
    one, two = routed_norm(me, routed, pieces, attn_gain, moe_gain, nz)

    others = range(1, nx)
    ones = [one] + [shift(one, "x", d) for d in others]
    two = exchange(two, "z")
    across = shift(attention[2], "exp", 2)
    ones, two, across = keep((ones, two, across))
    one = exchange(repeat([hbm(ones[0])] + ones[1:], nz), "z")
    twos = [two] + [shift(two, "x", d) for d in others]
    right, left = shift(attention[1], "exp", 1), shift(attention[3], "exp", 3)
    one, twos, right, left = keep((one, twos, right, left))

    cut = moe_gain.shape[1] * 7 // 12
    act_own, weights = expert_act(one, twos, (w_gate, w_up))
    one, twos = shift(one, "core", 1), [shift(a, "core", 1) for a in twos]
    one, twos, weights = keep((one, twos, weights))
    act_far = expert_act(one, twos, weights)
    (one,) = expert_down(act_far, w_down, cut, False, nz, nx)
    one, act_far = keep((one, act_far))
    (two,) = expert_down(act_far, w_down, cut, True, nz, nx)
    one, two, act_own = keep((one, two, act_own))
    one, two = shift(one, "core", 1), shift(two, "core", 1)
    (one,) = expert_down(act_own, w_down, cut, False, nz, nx, one)
    one, two, act_own = keep((one, two, act_own))
    twos = expert_down(act_own, w_down, cut, True, nz, nx, two)

    one = exchange(one, "z")
    twos = [twos[0]] + [shift(twos[d], "x", -d) for d in others]
    one, twos = keep((one, twos))
    attention = [attention[0], right, across, left]
    ones = block_sum(one)
    ones = [hbm(ones[0])] + [shift(ones[d], "x", -d) for d in others]
    two = exchange(stack_sum([hbm(twos[0])] + twos[1:]), "z")
    hidden = hidden_rows(me, attention, hbm(residual), hbm(out_gate), attn_gain)
    back = exchange(row_sum(ones, two, held), "exp")
    moe_out = combine_rows(place_own, back, expert_ids, route_weights)
    return (hidden, moe_out)


def solution(mesh):
    cube = Mesh(mesh.devices.reshape(4, 4, 2, 4), ("z", "x", "core", "exp"))
    both = CTX + ("exp",)
    in_specs = (
        P(CTX, "exp"),
        P(CTX, "exp"),
        P(CTX, "exp"),
        P(CTX, "exp"),
        P(both, None),
        P(both, None),
        P(),
        P(),
        P(both, None),
        P(both, None),
        P("exp", None, CTX),
        P("exp", None, CTX),
        P("exp", CTX, None),
    )
    out_specs = (P(both, None), P(both, None))
    return jax.shard_map(local, mesh=cube, in_specs=in_specs, out_specs=out_specs, check_vma=False)
```

```python
import functools

import jax
import jax.numpy as jnp
from jax import lax
from jax.experimental import pallas as pl
from jax.experimental.pallas import tpu as pltpu
from jax.sharding import Mesh, PartitionSpec as P

HEAD_DIM = 128
CAP = 4
EPS = 1e-05
F32 = jnp.float32
BF16 = jnp.bfloat16
HIGHEST = lax.Precision.HIGHEST
CTX = ("z", "x", "core")
VMEM_LIMIT = 24 * 1024 * 1024


def iota(shape, dim):
    return lax.broadcasted_iota(jnp.int32, shape, dim)


def hbm(a):
    return pltpu.with_memory_space_constraint(a, pltpu.HBM)


def far(shape, dtype=BF16):
    return pltpu.HBM(shape, dtype)


def params(**kw):
    return pltpu.CompilerParams(vmem_limit_bytes=VMEM_LIMIT, **kw)


def cost(flops, bytes_accessed):
    return pl.CostEstimate(flops=flops, bytes_accessed=bytes_accessed, transcendentals=0)


def running_sum(ld, axis):
    rows = ld.shape[1]
    a, b = iota((rows, rows), 0), iota((rows, rows), 1)
    ones = (a >= b).astype(BF16)
    total = None
    rest = ld
    for _ in range(3):
        part = rest.astype(BF16)
        rest = rest - part.astype(F32)
        pair = (ones, part) if axis == 0 else (part, ones)
        term = lax.dot_general(*pair, (((1,), (1,)), ((), ())), preferred_element_type=F32)
        total = term if total is None else total + term
    return total


def spread(table, first, count, terms):
    n = table.shape[1]
    shape = (n, count * HEAD_DIM)
    pick = (iota(shape, 0) == first + iota(shape, 1) // HEAD_DIM).astype(BF16)
    total = None
    rest = table
    for _ in range(terms):
        part = rest.astype(BF16)
        rest = rest - part.astype(F32)
        term = jnp.dot(part, pick, preferred_element_type=F32)
        total = term if total is None else total + term
    return total


def state_kernel(
    group, k_hbm, v_hbm, ld_ref, cum_ref, out_hbm, k_ref, v_ref, msg_ref, arrive, leave
):
    heads, rows = ld_ref.shape
    per = heads * HEAD_DIM // 32
    parts = group * HEAD_DIM // per
    wide = group * HEAD_DIM
    arriving = []
    for g in range(heads // group):
        cols = pl.ds(g * wide, wide)
        for n, (a, b) in enumerate(((k_hbm, k_ref), (v_hbm, v_ref))):
            arriving.append(pltpu.make_async_copy(a.at[:, cols], b.at[:, cols], arrive.at[g, n]))
    for c in arriving:
        c.start()
    cum = running_sum(ld_ref[...], 0)
    cum_ref[...] = cum
    final = cum[rows - 1 : rows, :]
    fades = jnp.exp(final - cum)
    decays = jnp.broadcast_to(jnp.exp(final), (16, heads))
    row16 = iota((16, HEAD_DIM), 0)
    leaving = []
    for g in range(heads // group):
        fade = spread(fades, g * group, group, 2)
        decay = spread(decays, g * group, group, 2)
        arriving[2 * g].wait()
        arriving[2 * g + 1].wait()
        tiles = []
        for j in range(group):
            cols = slice(j * HEAD_DIM, (j + 1) * HEAD_DIM)
            if j % 2 == 0:
                two = slice(j * HEAD_DIM, (j + 2) * HEAD_DIM)
                both = slice((g * group + j) * HEAD_DIM, (g * group + j + 2) * HEAD_DIM)
                wk = (k_ref[:, both].astype(F32) * fade[:, two]).astype(BF16)
                pair = lax.dot_general(
                    wk, v_ref[:, both], (((0,), (0,)), ((), ())), preferred_element_type=F32
                )
            at = slice((j % 2) * HEAD_DIM, (j % 2 + 1) * HEAD_DIM)
            state = pair[at, at].astype(BF16)
            row = (g * group + j) * HEAD_DIM
            end = row + HEAD_DIM
            lo = 0
            while row < end:
                part, at = row // per, row % per
                take = min(per - at, end - row)
                msg_ref[part, at : at + take, :] = state[lo : lo + take, :]
                row += take
                lo += take
            whole = decay[:, cols]
            high = whole.astype(BF16).astype(F32)
            tiles.append((high, whole - high))
        for part in range(parts):
            first = per * part // HEAD_DIM
            last = (per * part + per - 1) // HEAD_DIM
            tile = jnp.where(
                row16 == 0,
                tiles[first][0],
                jnp.where(
                    row16 == 1,
                    tiles[first][1],
                    jnp.where(row16 == 2, tiles[last][0], tiles[last][1]),
                ),
            )
            msg_ref[g * parts + part, per : per + 16, :] = tile.astype(BF16)
        at = pl.ds(g * parts, parts)
        leaving.append(pltpu.make_async_copy(msg_ref.at[at], out_hbm.at[at], leave.at[g]))
        leaving[-1].start()
    for c in leaving:
        c.wait()


def local_states(k, v, ld, group=6):
    rows, width = k.shape
    heads = ld.shape[0]
    per = heads * HEAD_DIM // 32
    whole = pl.BlockSpec(memory_space=pltpu.VMEM)
    away = pl.BlockSpec(memory_space=pl.ANY)
    steps = heads // group
    return pl.pallas_call(
        functools.partial(state_kernel, group),
        out_shape=(
            jax.ShapeDtypeStruct((rows, heads), F32),
            far((32, per + 16, HEAD_DIM)),
        ),
        in_specs=[away, away, whole],
        out_specs=(whole, away),
        scratch_shapes=[
            pltpu.VMEM((rows, width), BF16),
            pltpu.VMEM((rows, width), BF16),
            pltpu.VMEM((32, per + 16, HEAD_DIM), BF16),
            pltpu.SemaphoreType.DMA((steps, 2)),
            pltpu.SemaphoreType.DMA((steps,)),
        ],
        compiler_params=params(),
        cost_estimate=cost(2 * rows * width * HEAD_DIM, 4 * rows * width),
        name="local_states",
    )(k, v, ld)


def scan_kernel(split_ref, in_ref, out_ref):
    parts, per, width = out_ref.shape
    first_rows = iota((per, width), 0) < split_ref[0]
    state = jnp.zeros((per, width), F32)
    for b in range(parts):
        out_ref[b, :, :] = state.astype(BF16)
        if b + 1 < parts:
            tail = in_ref[b, per : per + 16, :].astype(F32)
            d0 = tail[0:1, :] + tail[1:2, :]
            d1 = tail[2:3, :] + tail[3:4, :]
            decay = jnp.where(first_rows, d0, d1)
            state = decay * state + in_ref[b, 0:per, :].astype(F32)


def scan_blocks(msg, part):
    parts, tall, width = msg.shape
    per = tall - 16
    split = (HEAD_DIM - (per * part) % HEAD_DIM).astype(jnp.int32).reshape(1)
    return pl.pallas_call(
        scan_kernel,
        out_shape=far((parts, per, width)),
        in_specs=[
            pl.BlockSpec(memory_space=pltpu.SMEM),
            pl.BlockSpec(memory_space=pltpu.VMEM),
        ],
        out_specs=pl.BlockSpec(memory_space=pltpu.VMEM),
        compiler_params=params(),
        cost_estimate=cost(1000000, 1000000),
        name="scan_blocks",
    )(split, msg)


def inside_kernel(group, q_ref, k_ref, v_ref, cum_ref, ld_ref, inside_ref, qs_ref, cumt_ref):
    rows, heads = cum_ref.shape

    @pl.when(pl.program_id(0) == 0)
    def _():
        cumt_ref[...] = running_sum(ld_ref[...], 1)

    cum = spread(cum_ref[...], pl.program_id(0) * group, group, 3)
    size = 2 * HEAD_DIM
    causal = iota((size, size), 0) >= iota((size, size), 1)
    for j in range(group):
        h = pl.program_id(0) * group + j
        cols = slice(j * HEAD_DIM, (j + 1) * HEAD_DIM)
        col = cum[:, cols]
        row = cumt_ref[pl.ds(h, 1), :]
        q = q_ref[:, cols]
        k = k_ref[:, cols]
        v = v_ref[:, cols]
        qs_ref[:, cols] = (q.astype(F32) * jnp.exp(col)).astype(BF16)
        wide = jnp.concatenate([col, col], axis=1)
        total = None
        for lo in range(0, rows, size):
            hi = lo + size
            s = lax.dot_general(
                q[lo:], k[lo:hi], (((1,), (1,)), ((), ())), preferred_element_type=F32
            )
            decay = jnp.exp(jnp.minimum(wide[lo:] - row[:, lo:hi], 0.0))
            w = s * decay
            w = jnp.concatenate([jnp.where(causal, w[:size], 0.0), w[size:]], axis=0) if (
                hi < rows
            ) else jnp.where(causal, w, 0.0)
            part = jnp.dot(w.astype(BF16), v[lo:hi], preferred_element_type=F32)
            if total is None:
                total = part
            else:
                total = jnp.concatenate([total[:lo], total[lo:] + part], axis=0)
        inside_ref[:, cols] = total


def inside_blocks(q, k, v, cum, ld, group=3):
    rows, width = q.shape
    heads = cum.shape[1]
    block = pl.BlockSpec((rows, group * HEAD_DIM), lambda g: (0, g))
    return pl.pallas_call(
        functools.partial(inside_kernel, group),
        grid=(heads // group,),
        out_shape=(
            jax.ShapeDtypeStruct((rows, width), F32),
            far((rows, width)),
        ),
        in_specs=[
            block,
            block,
            block,
            pl.BlockSpec((rows, heads), lambda g: (0, 0)),
            pl.BlockSpec((heads, rows), lambda g: (0, 0)),
        ],
        out_specs=(block, block),
        scratch_shapes=[pltpu.VMEM((heads, rows), F32)],
        compiler_params=params(),
        cost_estimate=cost(4 * rows * rows * width, 12 * rows * width),
        name="inside_blocks",
    )(q, k, v, cum, ld)


def attend(group, inside_ref, qs_ref, state_ref, att_ref):
    for j in range(group):
        cols = slice(j * HEAD_DIM, (j + 1) * HEAD_DIM)
        att_ref[:, cols] = (
            inside_ref[:, cols]
            + jnp.dot(qs_ref[:, cols], state_ref[j], preferred_element_type=F32)
        ).astype(BF16)


def chosen_kernel(inside_ref, qs_ref, state_ref, sel_ref):
    for h in range(state_ref.shape[0]):
        cols = slice(h * HEAD_DIM, (h + 1) * HEAD_DIM)
        sel_ref[:, cols] = (
            inside_ref[:, cols]
            + jnp.dot(qs_ref[:, cols], state_ref[h], preferred_element_type=F32)
        ).astype(BF16)


def carried_kernel(group, me_ref, inside_ref, qs_ref, state_ref, *refs):
    outs, att_ref = refs[:-1], refs[-1]
    held = len(outs)
    tokens = outs[0].shape[0]
    attend(group, inside_ref, qs_ref, state_ref, att_ref)
    for d in range(held):
        at = pl.multiple_of(lax.rem(me_ref[0] + d, held) * tokens, tokens)
        outs[d][...] = att_ref[pl.ds(at, tokens), :]


def chosen_rows(inside, qs, state):
    chosen, width = inside.shape
    return pl.pallas_call(
        chosen_kernel,
        out_shape=far((chosen, width)),
        compiler_params=params(),
        cost_estimate=cost(2 * chosen * width * HEAD_DIM, 8 * chosen * width),
        name="chosen_rows",
    )(inside, qs, state)


def carried_blocks(me, inside, qs, state, held, group=3):
    rows, width = inside.shape
    heads = width // HEAD_DIM
    wide = group * HEAD_DIM
    tokens = rows // held
    block = pl.BlockSpec((rows, wide), lambda g: (0, g))
    return list(
        pl.pallas_call(
            functools.partial(carried_kernel, group),
            grid=(heads // group,),
            out_shape=(far((tokens, width)),) * held,
            in_specs=[
                pl.BlockSpec(memory_space=pltpu.SMEM),
                block,
                block,
                pl.BlockSpec((group, HEAD_DIM, HEAD_DIM), lambda g: (g, 0, 0)),
            ],
            out_specs=(pl.BlockSpec((tokens, wide), lambda g: (0, g)),) * held,
            scratch_shapes=[pltpu.VMEM((rows, wide), BF16)],
            compiler_params=params(),
            cost_estimate=cost(4 * rows * width * HEAD_DIM, 8 * rows * width),
            name="carried_blocks",
        )(me, inside, qs, state)
    )


def route_kernel(pieces, me_ref, ids_ref, res_hbm, gate_hbm, *refs):
    outs, (place_ref, res_ref, gate_ref, sem) = refs[:-4], refs[-4:]
    held = len(outs)
    size = res_ref.shape[0] // pieces
    copies = []
    for n, (a, b) in enumerate(((res_hbm, res_ref), (gate_hbm, gate_ref))):
        for i in range(pieces):
            at = pl.ds(i * size, size)
            copies.append(pltpu.make_async_copy(a.at[at], b.at[at], sem.at[n, i]))
    for c in copies:
        c.start()
    tokens, width = res_ref.shape
    me = me_ref[0]
    ids = ids_ref[...]
    hits = [
        ((ids[0:1, :] == e) | (ids[1:2, :] == e)).astype(F32) for e in range(held)
    ]
    m = jnp.concatenate(hits, axis=0)
    upto = (iota((tokens, tokens), 0) <= iota((tokens, tokens), 1)).astype(BF16)
    rank = jnp.dot(m.astype(BF16), upto, preferred_element_type=F32) - 1.0
    slot = iota((CAP, tokens), 0).astype(F32)
    places = [
        jnp.where(rank[e : e + 1, :] == slot, m[e : e + 1, :], 0.0) for e in range(held)
    ]
    place = jnp.concatenate(places, axis=0)
    place_ref[...] = place
    for c in copies:
        c.wait()
    ordered = []
    for d in range(held):
        expert = lax.rem(me + d, held)
        mine = places[0]
        for e in range(1, held):
            mine = jnp.where(expert == e, places[e], mine)
        ordered.append(mine)
    chosen = jnp.concatenate(ordered, axis=0).astype(BF16)
    res = jnp.dot(chosen, res_ref[...], preferred_element_type=F32)
    gate = jnp.dot(chosen, gate_ref[...], preferred_element_type=F32)
    for d in range(held):
        at = slice(d * CAP, (d + 1) * CAP)
        outs[d][:, 0:width] = jnp.concatenate([res[at], gate[at]], axis=0).astype(BF16)
        for n in range(2):
            outs[d][:, width + n * tokens : width + (n + 1) * tokens] = jnp.broadcast_to(
                ids[n : n + 1, :].astype(F32), (2 * CAP, tokens)
            ).astype(BF16)


def route_rows(me, ids, residual, out_gate, held, pieces=4):
    tokens, width = residual.shape
    whole = pl.BlockSpec(memory_space=pltpu.VMEM)
    away = pl.BlockSpec(memory_space=pl.ANY)
    piece = far((2 * CAP, width + 2 * tokens))
    outs = pl.pallas_call(
        functools.partial(route_kernel, pieces),
        out_shape=(piece,) * held + (jax.ShapeDtypeStruct((held * CAP, tokens), F32),),
        in_specs=[pl.BlockSpec(memory_space=pltpu.SMEM), whole, away, away],
        out_specs=(whole,) * (held + 1),
        scratch_shapes=[
            pltpu.VMEM((tokens, width), BF16),
            pltpu.VMEM((tokens, width), BF16),
            pltpu.SemaphoreType.DMA((2, pieces)),
        ],
        compiler_params=params(),
        cost_estimate=cost(64 * tokens * width, 5 * tokens * width),
        name="route_rows",
    )(me, ids, residual, out_gate)
    return outs[:-1], outs[-1]


def by_source(me, pieces, j):
    count = len(pieces)
    out = pieces[0]
    for d in range(1, count):
        out = jnp.where(lax.rem(me + count - d, count) == j, pieces[d], out)
    return out


def place_kernel(group, me_ref, inside_ref, qs_ref, *refs):
    pieces, (some_inside_ref, some_qs_ref, place_ref) = refs[:-3], refs[-3:]
    held = len(pieces)
    tokens = pieces[0].shape[1] // 2
    total = held * tokens
    me = me_ref[0]
    tables = [p[...].astype(F32) for p in pieces]
    ordered = [by_source(me, tables, j) for j in range(held)]
    first = jnp.concatenate([a[0:1, :tokens] for a in ordered], axis=1)
    second = jnp.concatenate([a[0:1, tokens:] for a in ordered], axis=1)
    m = jnp.concatenate(
        [((first == float(e)) | (second == float(e))).astype(F32) for e in range(held)], axis=0
    )
    before = iota((total, total), 0)
    after = iota((total, total), 1)
    upto = ((before <= after) & (before // tokens == after // tokens)).astype(BF16)
    rank = jnp.dot(m.astype(BF16), upto, preferred_element_type=F32) - 1.0
    rows = held * CAP
    r = iota((rows, total), 0)
    t = iota((rows, total), 1)
    here = (t // tokens == r // CAP).astype(F32)
    slot = (r % CAP).astype(F32)
    for e in range(held):
        hit = jnp.where(rank[e : e + 1, :] == slot, m[e : e + 1, :] * here, 0.0)
        place_ref[e * rows : (e + 1) * rows, :] = hit.astype(BF16)
    place = place_ref[...]
    wide = group * HEAD_DIM
    for g in range(qs_ref.shape[1] // wide):
        cols = slice(g * wide, (g + 1) * wide)
        some_qs_ref[:, cols] = jnp.dot(
            place, qs_ref[:, cols], preferred_element_type=F32
        ).astype(BF16)
        rest = inside_ref[:, cols]
        picked = None
        for _ in range(3):
            part = rest.astype(BF16)
            rest = rest - part.astype(F32)
            term = jnp.dot(place, part, preferred_element_type=F32)
            picked = term if picked is None else picked + term
        some_inside_ref[:, cols] = picked


def place_rows(me, inside, qs, pieces, tokens, group=3):
    held = len(pieces)
    chosen = held * held * CAP
    width = pieces[0].shape[1] - 2 * tokens
    at = width // (2 * tokens)
    whole = pl.BlockSpec(memory_space=pltpu.VMEM)
    return pl.pallas_call(
        functools.partial(place_kernel, group),
        grid=(1,),
        out_shape=(
            far((chosen, inside.shape[1]), F32),
            far((chosen, inside.shape[1])),
        ),
        in_specs=[pl.BlockSpec(memory_space=pltpu.SMEM), whole, whole]
        + [pl.BlockSpec((2 * CAP, 2 * tokens), lambda i: (0, at))] * held,
        out_specs=(whole, whole),
        scratch_shapes=[pltpu.VMEM((chosen, held * tokens), BF16)],
        compiler_params=params(),
        cost_estimate=cost(1000000, 200000),
        name="place_rows",
    )(me, inside, qs, *pieces)


def gated(att, res, gate, attn_gain):
    norm = att * lax.rsqrt(jnp.mean(att * att, axis=-1, keepdims=True) + EPS) * attn_gain
    return (res + norm * jax.nn.sigmoid(gate)).astype(BF16)


def routed_norm_kernel(me_ref, att_ref, ag_ref, mg_ref, *refs):
    pieces, one_ref, two_ref = refs[:-2], refs[-2], refs[-1]
    sources, rows, part = att_ref.shape
    width = sources * part
    me = me_ref[0]
    att = jnp.concatenate([att_ref[s].astype(F32) for s in range(sources)], axis=1)
    tables = [p[...][:, :width].astype(F32) for p in pieces]
    ordered = [by_source(me, tables, j) for j in range(sources)]
    res = jnp.concatenate([a[:CAP] for a in ordered], axis=0)
    gate = jnp.concatenate([a[CAP:] for a in ordered], axis=0)
    hidden = gated(att, res, gate, ag_ref[...]).astype(F32)
    normed = (
        hidden * lax.rsqrt(jnp.mean(hidden * hidden, axis=-1, keepdims=True) + EPS) * mg_ref[...]
    ).astype(BF16)
    cut = one_ref.shape[1]
    one_ref[...] = normed[:, :cut]
    for i in range(two_ref.shape[0]):
        two_ref[i] = normed[:, cut:]


def routed_norm(me, att, pieces, attn_gain, moe_gain, copies):
    sources, rows, part = att.shape
    width = sources * part
    cut = width // 2
    whole = pl.BlockSpec(memory_space=pltpu.VMEM)
    return pl.pallas_call(
        routed_norm_kernel,
        out_shape=(far((rows, cut)), far((copies, rows, width - cut))),
        in_specs=[pl.BlockSpec(memory_space=pltpu.SMEM)] + [whole] * (3 + len(pieces)),
        out_specs=(whole, whole),
        compiler_params=params(),
        cost_estimate=cost(20 * rows * width, 20 * rows * width),
        name="routed_norm",
    )(me, att, attn_gain, moe_gain, *pieces)


def hidden_kernel(me_ref, res_ref, gate_ref, ag_ref, *refs):
    pieces, out_ref = refs[:-1], refs[-1]
    me = me_ref[0]
    tables = [p[...].astype(F32) for p in pieces]
    att = jnp.concatenate([by_source(me, tables, j) for j in range(len(pieces))], axis=1)
    out_ref[...] = gated(att, res_ref[...].astype(F32), gate_ref[...].astype(F32), ag_ref[...])


def hidden_rows(me, pieces, residual, out_gate, attn_gain, tile=32):
    rows, part = pieces[0].shape
    width = len(pieces) * part
    block = pl.BlockSpec((tile, width), lambda i: (i, 0))
    return pl.pallas_call(
        hidden_kernel,
        grid=(rows // tile,),
        out_shape=jax.ShapeDtypeStruct((rows, width), BF16),
        in_specs=[
            pl.BlockSpec(memory_space=pltpu.SMEM),
            block,
            block,
            pl.BlockSpec((1, width), lambda i: (0, 0)),
        ]
        + [pl.BlockSpec((tile, part), lambda i: (i, 0))] * len(pieces),
        out_specs=block,
        compiler_params=params(),
        cost_estimate=cost(20 * rows * width, 8 * rows * width),
        name="hidden_rows",
    )(me, residual, out_gate, attn_gain, *pieces)


def repeat_kernel(*refs):
    ins, (out, sem) = refs[:-2], refs[-2:]
    copies = [
        pltpu.make_async_copy(a, out.at[n, k], sem.at[n, k])
        for n in range(out.shape[0])
        for k, a in enumerate(ins)
    ]
    for c in copies:
        c.start()
    for c in copies:
        c.wait()


def repeat(arrays, copies):
    rows, width = arrays[0].shape
    count = len(arrays)
    return pl.pallas_call(
        repeat_kernel,
        out_shape=far((copies, count, rows, width)),
        in_specs=[pl.BlockSpec(memory_space=pltpu.VMEM)] * count,
        out_specs=pl.BlockSpec(memory_space=pl.ANY),
        scratch_shapes=[pltpu.SemaphoreType.DMA((copies, count))],
        compiler_params=params(),
        cost_estimate=cost(0, 2 * (copies + 1) * count * rows * width),
        name="repeat",
    )(*arrays)


def act_rows(steps, w_ref, one_ref, twos, arrived):
    width = w_ref.shape[2]
    nz, nx, rows, half = one_ref.shape
    nt = (((1,), (1,)), ((), ()))
    wide = width // steps
    gate = up = None
    for s in range(steps):
        cols = slice(s * wide, (s + 1) * wide)
        arrived(s)
        if s * wide < half:
            x = [one_ref[z, k, :, cols] for k in range(nx) for z in range(nz)]
        else:
            near = slice(s * wide - half, (s + 1) * wide - half)
            x = [r[z, :, near] for r in twos for z in range(nz)]
        x = jnp.concatenate(x, axis=0)
        g = lax.dot_general(w_ref[0, :, cols], x, nt, preferred_element_type=F32)
        u = lax.dot_general(w_ref[1, :, cols], x, nt, preferred_element_type=F32)
        gate = g if gate is None else gate + g
        up = u if up is None else up + u
    return (gate * jax.nn.sigmoid(gate) * up).T.astype(BF16)


def first_act_kernel(steps, wg_hbm, wu_hbm, one_ref, *refs):
    twos, (act_ref, w_ref, sem) = refs[:-3], refs[-3:]
    wide = w_ref.shape[2] // steps
    copies = []
    for s in range(steps):
        cols = pl.ds(s * wide, wide)
        for n, a in enumerate((wg_hbm, wu_hbm)):
            copies.append(
                pltpu.make_async_copy(a.at[:, cols], w_ref.at[n, :, cols], sem.at[s, n])
            )
    for c in copies:
        c.start()

    def arrived(s):
        copies[2 * s].wait()
        copies[2 * s + 1].wait()

    act_ref[...] = act_rows(steps, w_ref, one_ref, twos, arrived)


def next_act_kernel(steps, w_ref, one_ref, *refs):
    refs[-1][...] = act_rows(steps, w_ref, one_ref, refs[:-1], lambda s: None)


def expert_act(one, twos, weights, steps=6):
    nz, nx, rows, half = one.shape
    count = nz * nx * rows
    whole = pl.BlockSpec(memory_space=pltpu.VMEM)
    away = pl.BlockSpec(memory_space=pl.ANY)
    if isinstance(weights, tuple):
        units, width = weights[0].shape
        return pl.pallas_call(
            functools.partial(first_act_kernel, steps),
            out_shape=(
                jax.ShapeDtypeStruct((count, units), BF16),
                pltpu.VMEM((2, units, width), BF16),
            ),
            in_specs=[away, away] + [whole] * (1 + len(twos)),
            out_specs=(whole, whole),
            scratch_shapes=[pltpu.SemaphoreType.DMA((steps, 2))],
            compiler_params=params(),
            cost_estimate=cost(4 * count * width * units, 4 * width * units + 2 * count * width),
            name="first_act",
        )(hbm(weights[0]), hbm(weights[1]), one, *twos)
    _, units, width = weights.shape
    return pl.pallas_call(
        functools.partial(next_act_kernel, steps),
        out_shape=jax.ShapeDtypeStruct((count, units), BF16),
        in_specs=[whole] * (2 + len(twos)),
        out_specs=whole,
        compiler_params=params(),
        cost_estimate=cost(4 * count * width * units, 2 * count * width),
        name="next_act",
    )(pltpu.with_memory_space_constraint(weights, pltpu.VMEM), one, *twos)


def down_kernel(steps, first, by_x, act_ref, wd_hbm, *refs):
    wd_ref, sem = refs[-2:]
    half = wd_ref.shape[1]
    wide = half // steps
    copies = []
    for s in range(steps):
        cols = pl.ds(s * wide, wide)
        copies.append(
            pltpu.make_async_copy(
                wd_hbm.at[:, pl.ds(first + s * wide, wide)], wd_ref.at[:, cols], sem.at[s]
            )
        )
    for c in copies:
        c.start()
    refs = refs[:-2]
    added, kept, ends = (refs[0], refs[-2], refs[-1]) if len(refs) != 1 else (None,) * 3
    outs = refs[1:-2] if len(refs) != 1 else refs
    leaving = []

    def send(s, cols):
        n = s * len(outs)
        if len(outs) == 1:
            leaving.append(
                pltpu.make_async_copy(kept.at[:, :, :, cols], outs[0].at[:, :, :, cols], ends.at[n])
            )
            leaving[-1].start()
            return
        for k, ref in enumerate(outs):
            leaving.append(
                pltpu.make_async_copy(kept.at[k, :, :, cols], ref.at[:, :, cols], ends.at[n + k])
            )
            leaving[-1].start()

    act = act_ref[...]
    if by_x:
        nx = outs[0].shape[0] if len(outs) == 1 else len(outs)
        nz = outs[0].shape[-3]
    else:
        nz, nx = outs[0].shape[:2]
    rows = outs[0].shape[-2]
    for s in range(steps):
        cols = slice(s * wide, (s + 1) * wide)
        copies[s].wait()
        out = jnp.dot(act, wd_ref[:, cols], preferred_element_type=F32)
        out = out.reshape(nx, nz, rows, wide)
        if by_x:
            if added is not None:
                out = out + added[:, :, :, cols].astype(F32)
            target = outs[0] if added is None else kept
            target[:, :, :, cols] = out.astype(BF16)
        else:
            for z in range(nz):
                part = out[:, z]
                if added is not None:
                    part = part + added[z, :, :, cols].astype(F32)
                target = outs[0] if added is None else kept
                target[z, :, :, cols] = part.astype(BF16)
        if added is not None:
            send(s, pl.ds(s * wide, wide))
    for c in leaving:
        c.wait()


def expert_down(act, w_down, cut, last, nz, nx, added=None, steps=2):
    count, units = act.shape
    half = w_down.shape[1] - cut if last else cut
    rows = count // (nz * nx)
    whole = pl.BlockSpec(memory_space=pltpu.VMEM)
    if last:
        if added is None:
            shapes = (jax.ShapeDtypeStruct((nx, nz, rows, half), BF16),)
        else:
            shapes = (far((nz, rows, half)),) * nx
    elif added is None:
        shapes = (jax.ShapeDtypeStruct((nz, nx, rows, half), BF16),)
    else:
        shapes = (far((nz, nx, rows, half)),)
    more = () if added is None else (added,)
    away = pl.BlockSpec(memory_space=pl.ANY)
    scratch = [pltpu.VMEM((units, half), BF16), pltpu.SemaphoreType.DMA((steps,))]
    if added is not None:
        scratch = [
            pltpu.VMEM(added.shape, BF16),
            pltpu.SemaphoreType.DMA((steps * len(shapes),)),
        ] + scratch
    return pl.pallas_call(
        functools.partial(down_kernel, steps, cut if last else 0, last),
        out_shape=shapes,
        in_specs=[whole, away] + [whole] * len(more),
        out_specs=(whole if added is None else away,) * len(shapes),
        scratch_shapes=scratch,
        compiler_params=params(),
        cost_estimate=cost(2 * count * half * units, 2 * half * units + 2 * count * half),
        name="expert_down",
    )(act, hbm(w_down), *more)


def block_kernel(in_ref, *outs):
    total = in_ref[0].astype(F32)
    for i in range(1, in_ref.shape[0]):
        total = total + in_ref[i].astype(F32)
    total = total.astype(BF16)
    for n, out in enumerate(outs):
        out[...] = total[n]


def block_sum(parts, steps=2):
    count, n, rows, width = parts.shape
    wide = width // steps
    return pl.pallas_call(
        block_kernel,
        grid=(steps,),
        out_shape=(far((rows, width)),) * n,
        in_specs=[pl.BlockSpec((count, n, rows, wide), lambda i: (0, 0, 0, i))],
        out_specs=(pl.BlockSpec((rows, wide), lambda i: (0, i)),) * n,
        compiler_params=params(),
        cost_estimate=cost(count * n * rows * width, 2 * (count + 1) * n * rows * width),
        name="block_sum",
    )(parts)


def stack_kernel(*refs):
    total = refs[0][...].astype(F32)
    for ref in refs[1:-1]:
        total = total + ref[...].astype(F32)
    refs[-1][...] = total.astype(BF16)


def stack_sum(parts, steps=2):
    n, rows, width = parts[0].shape
    wide = width // steps
    block = pl.BlockSpec((n, rows, wide), lambda i: (0, 0, i))
    return pl.pallas_call(
        stack_kernel,
        grid=(steps,),
        out_shape=far(parts[0].shape),
        in_specs=[block] * len(parts),
        out_specs=block,
        compiler_params=params(),
        cost_estimate=cost(len(parts) * n * rows * width, 2 * (len(parts) + 1) * n * rows * width),
        name="stack_sum",
    )(*parts)


def row_sum_kernel(two_ref, *refs):
    parts, out_ref = refs[:-1], refs[-1]
    one = parts[0][...].astype(F32)
    for ref in parts[1:]:
        one = one + ref[...].astype(F32)
    two = two_ref[0].astype(F32)
    for i in range(1, two_ref.shape[0]):
        two = two + two_ref[i].astype(F32)
    cut = one.shape[1]
    for j in range(out_ref.shape[0]):
        at = slice(j * CAP, (j + 1) * CAP)
        out_ref[j, :, :cut] = one[at].astype(BF16)
        out_ref[j, :, cut:] = two[at].astype(BF16)


def row_sum(parts, two, held):
    count, rows, half = two.shape
    whole = pl.BlockSpec(memory_space=pltpu.VMEM)
    return pl.pallas_call(
        row_sum_kernel,
        out_shape=far((held, CAP, parts[0].shape[1] + half)),
        in_specs=[whole] * (1 + len(parts)),
        out_specs=whole,
        compiler_params=params(),
        cost_estimate=cost(8 * rows * half, 20 * rows * half),
        name="row_sum",
    )(two, *parts)


def combine_kernel(place_ref, rows_ref, ids_ref, weights_ref, out_ref):
    held = rows_ref.shape[0]
    rows = jnp.concatenate([rows_ref[e].astype(F32) for e in range(held)], axis=0).astype(BF16)
    back = lax.dot_general(
        place_ref[...].astype(BF16), rows, (((0,), (0,)), ((), ())), preferred_element_type=F32
    )
    chosen = jnp.sum(
        jnp.where(ids_ref[...] < held, weights_ref[...], 0.0), axis=1, keepdims=True
    )
    out_ref[...] = (back * chosen).astype(BF16)


def combine_rows(place, rows, ids, weights):
    tokens = ids.shape[0]
    width = rows.shape[2]
    return pl.pallas_call(
        combine_kernel,
        out_shape=jax.ShapeDtypeStruct((tokens, width), BF16),
        compiler_params=params(),
        cost_estimate=cost(32 * tokens * width, 2 * tokens * width),
        name="combine_rows",
    )(place, rows, ids, weights)


def exchange(a, axis):
    return lax.all_to_all(a, axis, split_axis=0, concat_axis=0, tiled=True)


def shift(a, axis, by):
    n = lax.axis_size(axis)
    return lax.ppermute(a, axis, [(i, (i + by) % n) for i in range(n)])


def local(
    queries,
    key_vectors,
    values,
    log_decay,
    out_gate,
    residual,
    attn_gain,
    moe_gain,
    expert_ids,
    route_weights,
    w_gate,
    w_up,
    w_down,
):
    held = lax.axis_size("exp")
    rows, width = queries.shape
    heads = log_decay.shape[1]
    tokens = residual.shape[0]
    attn_gain = hbm(attn_gain.reshape(1, -1))
    moe_gain = hbm(moe_gain.reshape(1, -1))
    w_gate = jnp.swapaxes(w_gate, 1, 2)[0]
    w_up = jnp.swapaxes(w_up, 1, 2)[0]
    w_down = w_down[0]
    ids = expert_ids.T
    ld = hbm(log_decay.T)
    me = lax.axis_index("exp").reshape(1)
    keep = lax.optimization_barrier
    nz, nx = lax.axis_size("z"), lax.axis_size("x")

    cum, msg = local_states(hbm(key_vectors), hbm(values), ld)
    sent = exchange(msg, CTX)
    inside, qs = inside_blocks(hbm(queries), hbm(key_vectors), hbm(values), cum, ld)
    pieces, place_own = route_rows(me, ids, hbm(residual), hbm(out_gate), held)
    sent, inside, qs, pieces = keep((sent, inside, qs, pieces))
    prior = scan_blocks(hbm(sent), lax.axis_index(CTX))
    state = exchange(prior, CTX).reshape(heads, HEAD_DIM, HEAD_DIM)
    pieces = [pieces[0]] + [shift(pieces[d], "exp", d) for d in range(1, held)]
    pieces = [hbm(a) for a in pieces]
    some_inside, some_qs = place_rows(me, inside, hbm(qs), pieces, tokens)

    routed = chosen_rows(hbm(some_inside), hbm(some_qs), state)
    _, inside, qs, state = keep((routed, inside, qs, state))
    routed = exchange(routed.reshape(held, held * CAP, width), "exp")
    attention = carried_blocks(me, inside, hbm(qs), state, held)
    routed, attention = keep((routed, attention))
    one, two = routed_norm(me, routed, pieces, attn_gain, moe_gain, nz)

    others = range(1, nx)
    ones = [one] + [shift(one, "x", d) for d in others]
    two = exchange(two, "z")
    across = shift(attention[2], "exp", 2)
    ones, two, across = keep((ones, two, across))
    one = exchange(repeat([hbm(ones[0])] + ones[1:], nz), "z")
    twos = [two] + [shift(two, "x", d) for d in others]
    right = shift(attention[1], "exp", 1)
    last, arrived = keep((attention[3], twos[1]))
    twos = [twos[0], arrived] + twos[2:]
    one, twos, right, last = keep((one, twos, right, last))
    left = shift(last, "exp", 3)

    cut = moe_gain.shape[1] * 7 // 12
    act_own, weights = expert_act(one, twos, (w_gate, w_up))
    one, twos = shift(one, "core", 1), [shift(a, "core", 1) for a in twos]
    one, twos, weights = keep((one, twos, weights))
    act_far = expert_act(one, twos, weights)
    (one,) = expert_down(act_far, w_down, cut, False, nz, nx)
    one, act_far = keep((one, act_far))
    (two,) = expert_down(act_far, w_down, cut, True, nz, nx)
    one, two, act_own, left = keep((one, two, act_own, left))
    one, two = shift(one, "core", 1), shift(two, "core", 1)
    (one,) = expert_down(act_own, w_down, cut, False, nz, nx, one)
    one, two, act_own = keep((one, two, act_own))
    twos = expert_down(act_own, w_down, cut, True, nz, nx, two)

    one = exchange(one, "z")
    twos = [twos[0]] + [shift(twos[d], "x", -d) for d in others]
    one, twos = keep((one, twos))
    attention = [attention[0], right, across, left]
    ones = block_sum(one)
    ones = [hbm(ones[0])] + [shift(ones[d], "x", -d) for d in others]
    two = exchange(stack_sum([hbm(twos[0])] + twos[1:]), "z")
    hidden = hidden_rows(me, attention, hbm(residual), hbm(out_gate), attn_gain)
    back = exchange(row_sum(ones, two, held), "exp")
    moe_out = combine_rows(place_own, back, expert_ids, route_weights)
    return (hidden, moe_out)


def solution(mesh):
    cube = Mesh(mesh.devices.reshape(4, 4, 2, 4), ("z", "x", "core", "exp"))
    both = CTX + ("exp",)
    in_specs = (
        P(CTX, "exp"),
        P(CTX, "exp"),
        P(CTX, "exp"),
        P(CTX, "exp"),
        P(both, None),
        P(both, None),
        P(),
        P(),
        P(both, None),
        P(both, None),
        P("exp", None, CTX),
        P("exp", None, CTX),
        P("exp", CTX, None),
    )
    out_specs = (P(both, None), P(both, None))
    return jax.shard_map(local, mesh=cube, in_specs=in_specs, out_specs=out_specs, check_vma=False)
```
